32 devices in a mesh: gx: 8 (over z, y), gy: 4 (over x, core).
Axes of the slice: x: 2, y: 2, z: 4, core: 2. Of those that a mesh axis runs over, the one named last changes fastest.
Arguments:
- layer_in: bfloat16 [2048, 1536], P('gx', 'gy'), may hold values from -40 to 40
- first_gain: float32 [1536], P('gy'), may hold values from 0.5 to 1.5
- query_weight: bfloat16 [1536, 1536], P('gx', 'gy'), may hold values from -0.21875 to 0.21875
- key_matrix: bfloat16 [1536, 768], P('gx', 'gy'), may hold values from -0.21875 to 0.21875
- value_matrix: bfloat16 [1536, 768], P('gx', 'gy'), may hold values from -0.15625 to 0.15625
- out_weight: bfloat16 [1536, 1536], P('gy', 'gx'), may hold values from -0.875 to 0.875
- second_gain: float32 [1536], P('gy'), may hold values from 0.5 to 1.5
- gate_weight: bfloat16 [1536, 4096], P('gx', 'gy'), may hold values from -0.15625 to 0.15625
- up_weight: bfloat16 [1536, 4096], P('gx', 'gy'), may hold values from -0.15625 to 0.15625
- down_weight: bfloat16 [4096, 1536], P('gy', 'gx'), may hold values from -0.1875 to 0.1875
- out_grad: bfloat16 [2048, 1536], P('gx', 'gy'), may hold values from -6 to 6
Outputs:
- layer_out: bfloat16 [2048, 1536], P('gx', 'gy')
- in_grad: float32 [2048, 1536], P('gx', 'gy')
- first_gain_grad: float32 [1536], P('gy')
- query_grad: float32 [1536, 1536], P('gx', 'gy')
- key_grad: float32 [1536, 768], P('gx', 'gy')
- value_grad: float32 [1536, 768], P('gx', 'gy')
- out_proj_grad: float32 [1536, 1536], P('gy', 'gx')
- second_gain_grad: float32 [1536], P('gy')
- gate_grad: float32 [1536, 4096], P('gx', 'gy')
- up_grad: float32 [1536, 4096], P('gx', 'gy')
- down_grad: float32 [4096, 1536], P('gy', 'gx')
The draws below stay inside these ranges and needn't reach their ends.
All inputs are finite; a program needn't handle non-finite values.
Results may differ from the reference program's by a relative error of at most 0.024.
Values may be sent and summed in bfloat16 or wider, within the bound.
No kernel may reach another device: no remote copies, remote signals or barrier semaphores. Data moves between devices by JAX's collectives and lax.ppermute only.
A program may use at most 128 MiB of HBM per device.

```python
import jax
import jax.numpy as jnp
from jax import lax

MODEL_DIM = 1536
QUERY_HEADS = 16
KEY_VALUE_HEADS = 8
HEAD_DIM = 96
FF = 4096
BLOCK_TOKENS = 256
PROMPT_DEV = 4
CONT_DEV = 4
TOKENS = 2048


def draw_layer_in(key, part):
    splits = jax.random.split(key, 3)
    column = jnp.arange(MODEL_DIM, dtype=jnp.float32) / (MODEL_DIM - 1)
    base = jnp.clip(jax.random.normal(splits[0], (TOKENS, MODEL_DIM), jnp.float32), -4.5, 4.5)
    ramp = 0.6 * 3.0 ** column
    col_scale = ramp * jnp.exp(jax.random.uniform(splits[1], (MODEL_DIM,), jnp.float32, -0.7, 0.7))
    row_scale = jnp.exp(jax.random.uniform(splits[2], (TOKENS, 1), jnp.float32, -1.15, 1.15))
    return (0.5 * base * col_scale[None, :] * row_scale).astype(jnp.bfloat16)


def strengthened(entries, own_key, source, target, parts, factor):
    owner, partner = [(jnp.arange(entries.shape[position]) // (entries.shape[position] // parts)).reshape([-1 if axis == position else 1 for axis in range(entries.ndim)]) for position in (source, target)]
    chosen = jax.random.permutation(own_key, parts)[partner]
    strong = (owner == chosen) | (owner == (partner + parts // 2) % parts)
    return jnp.where(strong, factor * entries, entries)


def block_scale(rng, extent, cuts, least, top_value):
    def one(position, shards_of):
        draws = jax.random.uniform(jax.random.fold_in(jax.random.fold_in(rng, 6), position), (shards_of,), jnp.float32, least / len(cuts), top_value / len(cuts))
        return jnp.repeat(jnp.exp(draws), extent[position] // shards_of).reshape((-1,) + (1,) * (len(extent) - position - 1))

    gain = one(*cuts[0])
    for cut in cuts[1:]:
        gain = gain * one(*cut)
    return gain


def normal_values(own_key, dims, width, bound, shards=(), held_as=jnp.bfloat16):
    entries = jax.random.normal(own_key, dims, jnp.float32) * width
    if len(shards) > 0:
        entries = block_scale(own_key, dims, shards, -0.22, 0.18) * entries
    return jnp.clip(entries, min=-bound, max=bound).astype(held_as)


def bell_draw_with(rng, dims, deviation, limit, shards, heavy, kind=jnp.bfloat16):
    entries = deviation * jax.random.normal(rng, dims, jnp.float32)
    if shards:
        entries = entries * block_scale(rng, dims, shards, -0.22, 0.18)
    return jnp.clip(strengthened(entries, jax.random.fold_in(rng, 3), *heavy), -limit, limit).astype(kind)


def setup_inputs(seed: int = 0) -> dict:
    key_list = jax.random.split(jax.random.key(seed), 12)
    layer_in = draw_layer_in(jax.random.fold_in(key_list[11], 71), 0)
    first_gain = jnp.clip(1.0 + 0.1 * jax.random.normal(key_list[1], (MODEL_DIM,), jnp.float32), 0.5, 1.5)
    query_weight = normal_values(key_list[2], (MODEL_DIM, QUERY_HEADS * HEAD_DIM), (MODEL_DIM // 2) ** -0.5, 0.21875, ((0, 8), (1, 4)))
    key_matrix = normal_values(key_list[3], (MODEL_DIM, KEY_VALUE_HEADS * HEAD_DIM), (MODEL_DIM // 2) ** -0.5, 0.21875, ((0, 8), (1, 4)))
    value_matrix = normal_values(key_list[4], (MODEL_DIM, KEY_VALUE_HEADS * HEAD_DIM), MODEL_DIM ** -0.5, 0.15625, ((0, 8), (1, 4)))
    out_weight = normal_values(key_list[5], (QUERY_HEADS * HEAD_DIM, MODEL_DIM), (QUERY_HEADS * HEAD_DIM // 32) ** -0.5, 0.875, ((0, 4), (1, 8)))
    second_gain = jnp.clip(1.0 + 0.1 * jax.random.normal(key_list[6], (MODEL_DIM,), jnp.float32), 0.5, 1.5)
    gate_weight = normal_values(key_list[7], (MODEL_DIM, FF), MODEL_DIM ** -0.5, 0.15625, ((0, 8), (1, 4)))
    up_weight = normal_values(key_list[8], (MODEL_DIM, FF), MODEL_DIM ** -0.5, 0.15625, ((0, 8), (1, 4)))
    down_weight = normal_values(key_list[9], (FF, MODEL_DIM), (FF // 4) ** -0.5, 0.1875, ((0, 4), (1, 8)))
    out_grad = bell_draw_with(key_list[10], (TOKENS, MODEL_DIM), 1.0, 6.0, ((0, 8), (1, 4)), (0, 1, 8, 2.0))
    return {"layer_in": layer_in, "first_gain": first_gain, "query_weight": query_weight, "key_matrix": key_matrix, "value_matrix": value_matrix, "out_weight": out_weight, "second_gain": second_gain, "gate_weight": gate_weight, "up_weight": up_weight, "down_weight": down_weight, "out_grad": out_grad}


eps = 1e-05
neg_big = -1e+30
rope_base = 100000.0
highest = lax.Precision.HIGHEST

@jax.custom_vjp
def low(v):
    return lax.optimization_barrier(v.astype(jnp.bfloat16)).astype(jnp.float32)

@jax.custom_vjp
def low_back(v):
    return v

def low_keep(v):
    return (low(v), None)

def low_pass(kept, grad):
    return (grad,)

def back_keep(v):
    return (v, None)

def back_low(kept, grad):
    return (low(grad),)
low.defvjp(low_keep, low_pass)
low_back.defvjp(back_keep, back_low)

def rope_tables(positions, half):
    freq = rope_base ** (-(2.0 * jnp.arange(half, dtype=jnp.float32)) / (2.0 * half))
    angle = positions.astype(jnp.float32)[:, None] * freq[None, :]
    return (jnp.cos(angle), jnp.sin(angle))

def apply_rotary(values, cosine_table, sine_table, sign):
    half = values.shape[-1] // 2
    first = values[..., :half]
    second = values[..., half:]
    cos_part = cosine_table[:, None, :]
    sin_part = sine_table[:, None, :] * sign
    return jnp.concatenate([first * cos_part - second * sin_part, second * cos_part + first * sin_part], axis=-1)

def attend(split_keys, split_values, query_block, row_positions):
    col_ids = jnp.arange(split_keys.shape[0], dtype=jnp.int32)
    row_block = (row_positions // BLOCK_TOKENS)[:, None]
    col_block = (col_ids // BLOCK_TOKENS)[None, :]
    allowed = (row_block == col_block) & (col_ids[None, :] <= row_positions[:, None]) | (col_block < jnp.minimum(row_block, PROMPT_DEV))
    scores = jnp.einsum('tkgd,skd->kgts', query_block, split_keys, precision=highest) * HEAD_DIM ** (-0.5)
    scores = jnp.where(allowed[None, None], low_back(scores), neg_big)
    prob_rows = low(jax.nn.softmax(scores, axis=-1))
    return jnp.einsum('kgts,skd->tkgd', prob_rows, split_values, precision=highest)

def group_layer(rows_in, first_gain, query_weight, key_matrix, value_matrix, out_weight, second_gain, gate_weight, up_weight, down_weight):
    count_of_rows = rows_in.shape[0]
    row_positions = jnp.arange(count_of_rows, dtype=jnp.int32)
    within = row_positions % BLOCK_TOKENS
    positions = jnp.where(row_positions // BLOCK_TOKENS < PROMPT_DEV, row_positions, PROMPT_DEV * BLOCK_TOKENS + within)
    cosine_table, sine_table = rope_tables(positions, HEAD_DIM // 2)
    inverse = lax.rsqrt(lax.optimization_barrier(jnp.mean(rows_in * rows_in, axis=-1, keepdims=True)) + eps)
    normed = low(rows_in * inverse * first_gain)
    split_queries = low_back(jnp.dot(normed, query_weight, precision=highest))
    split_keys = low_back(jnp.dot(normed, key_matrix, precision=highest))
    split_values = low_back(jnp.dot(normed, value_matrix, precision=highest))
    split_queries = low(apply_rotary(split_queries.reshape(count_of_rows, QUERY_HEADS, HEAD_DIM), cosine_table, sine_table, 1.0))
    split_queries = split_queries.reshape(count_of_rows, KEY_VALUE_HEADS, QUERY_HEADS // KEY_VALUE_HEADS, HEAD_DIM)
    split_keys = low(apply_rotary(split_keys.reshape(count_of_rows, KEY_VALUE_HEADS, HEAD_DIM), cosine_table, sine_table, 1.0))
    split_values = low(split_values.reshape(count_of_rows, KEY_VALUE_HEADS, HEAD_DIM))
    block_list = count_of_rows // BLOCK_TOKENS
    verified = jax.checkpoint(attend)
    attended_rows = lax.map(lambda block_entry: verified(split_keys, split_values, block_entry[0], block_entry[1]), (split_queries.reshape(block_list, BLOCK_TOKENS, KEY_VALUE_HEADS, QUERY_HEADS // KEY_VALUE_HEADS, HEAD_DIM), row_positions.reshape(block_list, BLOCK_TOKENS)))
    attended_rows = low(low_back(attended_rows.reshape(count_of_rows, QUERY_HEADS * HEAD_DIM)))
    hidden = rows_in + low_back(jnp.dot(attended_rows, out_weight, precision=highest))
    inverse_mid = lax.rsqrt(lax.optimization_barrier(jnp.mean(hidden * hidden, axis=-1, keepdims=True)) + eps)
    normed_mid = low(hidden * inverse_mid * second_gain)
    gate = low_back(jnp.dot(normed_mid, gate_weight, precision=highest))
    upper = low_back(jnp.dot(normed_mid, up_weight, precision=highest))
    active = low(jax.nn.silu(gate) * upper)
    return hidden + low_back(jnp.dot(active, down_weight, precision=highest))

def forward(layer_in, first_gain, query_weight, key_matrix, value_matrix, out_weight, second_gain, gate_weight, up_weight, down_weight):
    groups = layer_in.shape[0] // (BLOCK_TOKENS * (PROMPT_DEV + CONT_DEV))
    verified = jax.checkpoint(group_layer)

    def one_group(carry, rows_in):
        return (carry, verified(rows_in, first_gain, query_weight, key_matrix, value_matrix, out_weight, second_gain, gate_weight, up_weight, down_weight))
    unused, outputs = lax.scan(one_group, jnp.zeros((), jnp.float32), layer_in.reshape(groups, -1, layer_in.shape[1]))
    return outputs.reshape(-1, layer_in.shape[1])

def reference(layer_in, first_gain, query_weight, key_matrix, value_matrix, out_weight, second_gain, gate_weight, up_weight, down_weight, out_grad):
    inputs = tuple((operand.astype(jnp.float32) for operand in (layer_in, first_gain, query_weight, key_matrix, value_matrix, out_weight, second_gain, gate_weight, up_weight, down_weight)))
    result, pullback = jax.vjp(forward, *inputs)
    gradients = pullback(out_grad.astype(jnp.float32))
    return (result.astype(jnp.bfloat16), gradients[0], gradients[1], gradients[2], gradients[3], gradients[4], gradients[5], gradients[6], gradients[7], gradients[8], gradients[9])
```

```python
import jax
import jax.numpy as jnp
from jax import lax
from jax.experimental import pallas as pl
from jax.experimental.pallas import tpu as pltpu
from jax.sharding import PartitionSpec as P

HEAD_DIM = 96
PROMPT_DEV = 4
CONT_DEV = 4
LINE_MAX = 8

eps = 1e-05
neg_big = -1e30
rope_base = 100000.0
f32 = jnp.float32
bf16 = jnp.bfloat16


def dims(left, right, left_axis, right_axis):
    return lax.dot_general(
        left, right, (((left_axis,), (right_axis,)), ((), ())), preferred_element_type=f32
    )


class Place:
    def __init__(self):
        self.nx = lax.axis_size("gx")
        self.ny = lax.axis_size("gy")
        assert self.ny == 4 and self.nx % (PROMPT_DEV + CONT_DEV) == 0
        self.n = self.nx // 2
        gx = lax.axis_index("gx")
        gy = lax.axis_index("gy")
        self.z, self.y = gx // 2, gx % 2
        self.x, self.c = gy // 2, gy % 2
        self.gx, self.gy = gx, gy

    def swap_y(self, value):
        return lax.ppermute(value, "gx", [(i, i ^ 1) for i in range(self.nx)])

    def swap_gx(self, value, bit):
        return lax.ppermute(value, "gx", [(i, i ^ bit) for i in range(self.nx)])

    def swap_x(self, value):
        return lax.ppermute(value, "gy", [(i, i ^ 2) for i in range(self.ny)])

    def swap_c(self, value):
        return lax.ppermute(value, "gy", [(i, i ^ 1) for i in range(self.ny)])

    def shift(self, value, sources, step):
        pairs = [(2 * s + y, 2 * (s + step) + y) for s in sources for y in range(2)]
        return lax.ppermute(value, "gx", pairs)


def pair(flag, mine, other):
    return jnp.where(flag == 0, mine, other), jnp.where(flag == 0, other, mine)


def groups_by_y(place):
    return [[2 * z + y for z in range(place.n)] for y in range(2)]


def gather_line(place, piece):
    n, z = place.n, place.z
    if n > LINE_MAX:
        return lax.all_gather(piece, "gx", axis_index_groups=groups_by_y(place))
    ups, downs = {}, {}
    up = down = piece
    for k in range(1, n):
        up = place.shift(up, range(k - 1, n - 1), 1)
        down = place.shift(down, range(1, n - k + 1), -1)
        ups[k], downs[k] = up, down
    whole = jnp.zeros((n,) + piece.shape, piece.dtype)
    whole = lax.dynamic_update_index_in_dim(whole, piece, z, 0)
    for k in range(1, n):
        taken = jnp.where(z >= k, ups[k], downs[n - k])
        whole = lax.dynamic_update_index_in_dim(whole, taken, (z - k) % n, 0)
    return whole


def scatter_line(place, parts):
    n, z = place.n, place.z
    if n > LINE_MAX:
        return lax.psum_scatter(
            parts.astype(bf16), "gx", axis_index_groups=groups_by_y(place)
        ).astype(f32)

    def part(index):
        chosen = lax.dynamic_index_in_dim(parts, jnp.clip(index, 0, n - 1), 0, keepdims=False)
        return chosen.astype(f32)

    down = up = None
    for k in range(n - 1, 0, -1):
        send_down, send_up = part(z - k), part(z + k)
        if down is not None:
            send_down, send_up = send_down + down, send_up + up
        down = place.shift(send_down.astype(bf16), range(k, n), -1).astype(f32)
        up = place.shift(send_up.astype(bf16), range(0, n - k), 1).astype(f32)
    return part(z) + down + up


def split_y(place, rows_of_y):
    half = rows_of_y.shape[1] // 2
    low, high = rows_of_y[:, :half], rows_of_y[:, half:]
    mine = jnp.where(place.y == 0, low, high)
    other = jnp.where(place.y == 0, high, low)
    return mine, other


def join_y(place, summed):
    rows = summed.shape[0] // 2
    low, high = summed[:rows], summed[rows:]
    mine = jnp.where(place.y == 0, low, high)
    other = jnp.where(place.y == 0, high, low)
    return mine, place.swap_y(other.astype(bf16)).astype(f32)


def reduce_core(place, partial_rows):
    width = partial_rows.shape[1] // 4
    blocks = [partial_rows[:, i * width : (i + 1) * width] for i in range(4)]
    keep = [jnp.where(place.c == 0, blocks[2 * i], blocks[2 * i + 1]) for i in range(2)]
    send = [jnp.where(place.c == 0, blocks[2 * i + 1], blocks[2 * i]) for i in range(2)]
    got = place.swap_c(jnp.stack([s.astype(bf16) for s in send]))
    return [keep[i] + got[i].astype(f32) for i in range(2)]


def all_sum(place, partial_rows):
    first, second = reduce_core(place, partial_rows)
    first_got = place.swap_x(first.astype(bf16))
    second_got = place.swap_y(second.astype(bf16))
    first, second = first + first_got.astype(f32), second + second_got.astype(f32)
    first_got = place.swap_y(first.astype(bf16))
    second_got = place.swap_x(second.astype(bf16))
    first, second = first + first_got.astype(f32), second + second_got.astype(f32)
    both = jnp.stack([first.astype(bf16), second.astype(bf16)])
    other = place.swap_c(both)
    low, high = pair(place.c, both, other)
    whole = jnp.concatenate([low[0], high[0], low[1], high[1]], axis=1)
    return whole, own_rows(place, jnp.where(place.x == 0, first, second))


def own_rows(place, rows):
    half = rows.shape[0] // 2
    return jnp.where(place.y == 0, rows[:half], rows[half:])


def own_sum(place, partial_rows):
    first, second = reduce_core(place, partial_rows)
    mine = jnp.where(place.x == 0, first, second)
    other = jnp.where(place.x == 0, second, first)
    mine = mine + place.swap_x(other.astype(bf16)).astype(f32)
    half = mine.shape[0] // 2
    low, high = mine[:half], mine[half:]
    other = jnp.where(place.y == 0, high, low)
    return jnp.where(place.y == 0, low, high) + place.swap_y(other.astype(bf16)).astype(f32)


def spread(place, blocks):
    count, rows, cols = blocks.shape
    by_x = jnp.stack(pair(place.x, blocks, place.swap_x(blocks)))
    by_y = jnp.stack(pair(place.y, by_x, place.swap_y(by_x)))
    by_c = jnp.stack(pair(place.c, by_y, place.swap_c(by_y)))
    return jnp.transpose(by_c, (3, 1, 4, 2, 0, 5)).reshape(count, 2 * rows, 4 * cols)


def rope_tables(positions, half):
    freq = rope_base ** (-(2.0 * jnp.arange(half, dtype=f32)) / (2.0 * half))
    angle = freq[:, None] * positions.astype(f32)[None, :]
    return (jnp.cos(angle), jnp.sin(angle))


def rotate(values, cosine, sine):
    half = values.shape[1] // 2
    first, second = values[:, :half], values[:, half:]
    return jnp.concatenate(
        [first * cosine - second * sine, second * cosine + first * sine], axis=1
    )


def attend_kernel(count_ref, q_ref, own_ref, far_ref, out_ref, log_ref, *, block, scale):
    head = HEAD_DIM
    far = far_ref[...]
    key_far, value_far = far[:head].T, far[head:]
    key_own = own_ref[:head].T
    total = far.shape[1]
    for part in range(q_ref.shape[2] // block):
        cols = slice(part * block, (part + 1) * block)
        key_near, value_near = key_own[cols], own_ref[head:, cols]
        row = lax.broadcasted_iota(jnp.int32, (total, block), 0)
        seen = row < count_ref[part] * block
        near_row = lax.broadcasted_iota(jnp.int32, (block, block), 0)
        near_col = lax.broadcasted_iota(jnp.int32, (block, block), 1)
        causal = near_row <= near_col
        for h in range(q_ref.shape[0]):
            query = q_ref[h, :, cols]
            score_far = jnp.where(seen, dims(key_far, query, 1, 0) * scale, neg_big)
            score_near = jnp.where(causal, dims(key_near, query, 1, 0) * scale, neg_big)
            top = jnp.maximum(
                jnp.max(score_far, axis=0, keepdims=True), jnp.max(score_near, axis=0, keepdims=True)
            )
            weight_far = jnp.exp(score_far - top)
            weight_near = jnp.exp(score_near - top)
            total_weight = jnp.sum(weight_far, axis=0, keepdims=True) + jnp.sum(
                weight_near, axis=0, keepdims=True
            )
            out = dims(value_far, weight_far.astype(bf16), 1, 0) + dims(
                value_near, weight_near.astype(bf16), 1, 0
            )
            out_ref[h, :, cols] = out / total_weight
            log_ref[h, :, cols] = top + jnp.log(total_weight)


def attend_back_kernel(
    count_ref,
    q_ref,
    own_ref,
    far_ref,
    grad_ref,
    out_ref,
    log_ref,
    dq_ref,
    down_ref,
    dfar_ref,
    *,
    block,
    scale,
):
    head = HEAD_DIM
    far = far_ref[...]
    key_far_t, value_far_t = far[:head], far[head:]
    key_far, value_far = key_far_t.T, value_far_t.T
    key_own, value_own = own_ref[:head].T, own_ref[head:].T
    total = far.shape[1]
    for part in range(q_ref.shape[2] // block):
        cols = slice(part * block, (part + 1) * block)
        key_near, value_near = key_own[cols], value_own[cols]
        key_near_t = own_ref[:head, cols]
        row = lax.broadcasted_iota(jnp.int32, (total, block), 0)
        seen = row < count_ref[part] * block
        near_row = lax.broadcasted_iota(jnp.int32, (block, block), 0)
        near_col = lax.broadcasted_iota(jnp.int32, (block, block), 1)
        causal = near_row <= near_col
        dk_near = jnp.zeros((head, block), f32)
        dv_near = jnp.zeros((head, block), f32)
        for h in range(q_ref.shape[0]):
            query, grad = q_ref[h, :, cols], grad_ref[h, :, cols]
            delta = jnp.sum(grad.astype(f32) * out_ref[h, :, cols], axis=0, keepdims=True)
            log_total = log_ref[h, :, cols]

            def one(key, value, allowed):
                score = dims(key, query, 1, 0) * scale
                prob = jnp.where(allowed, jnp.exp(score - log_total), 0.0)
                change = (prob * (dims(value, grad, 1, 0) - delta)).astype(bf16)
                return prob.astype(bf16), change

            prob_far, change_far = one(key_far, value_far, seen)
            prob_near, change_near = one(key_near, value_near, causal)
            dq_ref[h, :, cols] = (
                dims(key_far_t, change_far, 1, 0) + dims(key_near_t, change_near, 1, 0)
            ) * scale
            dk_far = dims(query, change_far, 1, 1) * scale
            dv_far = dims(grad, prob_far, 1, 1)
            if part == 0 and h == 0:
                dfar_ref[:head] = dk_far
                dfar_ref[head:] = dv_far
            else:
                dfar_ref[:head] += dk_far
                dfar_ref[head:] += dv_far
            dk_near += dims(query, change_near, 1, 1) * scale
            dv_near += dims(grad, prob_near, 1, 1)
        down_ref[:head, cols] = dk_near
        down_ref[head:, cols] = dv_near


def on_core(kernel, out_shape, count, *operands):
    whole = pl.BlockSpec(memory_space=pltpu.VMEM)
    return pl.pallas_call(
        kernel,
        out_shape=out_shape,
        in_specs=[pl.BlockSpec(memory_space=pltpu.SMEM)] + [whole] * len(operands),
        out_specs=jax.tree.map(lambda s: whole, out_shape),
    )(count, *operands)


def shards(
    layer_in,
    first_gain,
    query_weight,
    key_matrix,
    value_matrix,
    out_weight,
    second_gain,
    gate_weight,
    up_weight,
    down_weight,
    out_grad,
):
    place = Place()
    n, z, y = place.n, place.z, place.y
    block = layer_in.shape[0]
    tokens = 2 * block
    width = layer_in.shape[1]
    model_width = width * place.ny
    scale = HEAD_DIM ** (-0.5)
    group = (PROMPT_DEV + CONT_DEV) // 2
    prompts = PROMPT_DEV // 2
    z_in = z % group

    def halves(*matrices):
        mine, other = zip(*(split_y(place, m) for m in matrices))
        return jnp.concatenate(mine, axis=1), jnp.concatenate(other, axis=1)

    def rows_of_z(mine, got):
        low, high = pair(y, mine, got)
        return jnp.concatenate([low, high], axis=0)

    qkv_mine, qkv_other = halves(query_weight, key_matrix, value_matrix)
    out_mine, out_other = halves(out_weight.T)
    gu_mine, gu_other = halves(gate_weight, up_weight)
    down_mine, down_other = halves(down_weight.T)
    qkv_full = gather_line(place, rows_of_z(qkv_mine, place.swap_y(qkv_other)))
    out_full = gather_line(place, rows_of_z(out_mine, place.swap_y(out_other)))
    gu_full = gather_line(place, rows_of_z(gu_mine, place.swap_y(gu_other)))
    down_full = gather_line(place, rows_of_z(down_mine, place.swap_y(down_other)))
    qkv_full = qkv_full.reshape(model_width, -1)
    out_full = out_full.reshape(model_width, -1)
    gu_full = gu_full.reshape(model_width, -1)
    down_full = down_full.reshape(model_width, -1)
    hidden_dev = down_full.shape[1]
    heads = out_full.shape[1] // HEAD_DIM

    both = spread(place, jnp.stack([layer_in, out_grad]))
    rows_in, grad_low = both[0].astype(f32), both[1]
    gains = jnp.stack([first_gain, second_gain])
    gains = jnp.stack(pair(place.x, gains, place.swap_x(gains)))
    gains = jnp.stack(pair(place.c, gains, place.swap_c(gains)))
    gains = jnp.transpose(gains, (2, 1, 0, 3)).reshape(2, 1, model_width)

    inverse_in = lax.rsqrt(jnp.mean(rows_in * rows_in, axis=1, keepdims=True) + eps)
    normed_in = (rows_in * inverse_in * gains[0]).astype(bf16)

    qkv = dims(qkv_full, normed_in, 0, 1).reshape(-1, HEAD_DIM, tokens)
    offset = 2 * z_in + jnp.arange(2, dtype=jnp.int32)
    within = jnp.arange(block, dtype=jnp.int32)
    positions = (jnp.minimum(offset, PROMPT_DEV)[:, None] * block + within[None, :]).reshape(-1)
    cosine, sine = rope_tables(positions, HEAD_DIM // 2)
    turned = rotate(qkv[: heads + 1], cosine, sine).astype(bf16)
    query = turned[:heads]
    own = jnp.concatenate([turned[heads], qkv[heads + 1].astype(bf16)], axis=0)
    slots = [own] * prompts
    moving = own
    for k in range(1, group):
        sources = [
            s for s in range(n) if 0 <= s % group - (k - 1) < prompts and s % group + 1 < group
        ]
        moving = place.shift(moving, sources, 1)
        slots = [jnp.where(z_in == i + k, moving, slots[i]) for i in range(prompts)]
    far = jnp.concatenate(slots, axis=1)
    count = jnp.minimum(offset, PROMPT_DEV)

    def kernel(body):
        return lambda *refs: body(*refs, block=block, scale=scale)

    attended, log_total = on_core(
        kernel(attend_kernel),
        (
            jax.ShapeDtypeStruct((heads, HEAD_DIM, tokens), f32),
            jax.ShapeDtypeStruct((heads, 1, tokens), f32),
        ),
        count,
        query,
        own,
        far,
    )
    attended_low = attended.astype(bf16).reshape(heads * HEAD_DIM, tokens)
    branch, branch_own = all_sum(place, dims(attended_low, out_full, 0, 1))

    hidden = rows_in + branch.astype(f32)
    hidden_own = layer_in.astype(f32) + branch_own
    inverse_mid = lax.rsqrt(jnp.mean(hidden * hidden, axis=1, keepdims=True) + eps)
    normed_mid = (hidden * inverse_mid * gains[1]).astype(bf16)
    gate_up = dims(normed_mid, gu_full, 1, 0)
    gate, up = gate_up[:, :hidden_dev], gate_up[:, hidden_dev:]
    sigmoid = jax.nn.sigmoid(gate)
    active = (gate * sigmoid * up).astype(bf16)
    layer_out = (hidden_own + own_sum(place, dims(active, down_full, 1, 1))).astype(bf16)

    def scattered(parts):
        parts = parts.astype(bf16).reshape(n, model_width // n, -1)
        return join_y(place, scatter_line(place, parts))

    down_grad = scattered(dims(grad_low, active, 0, 0))
    active_grad = dims(grad_low, down_full, 1, 0)
    gate_low = (active_grad * up * sigmoid * (1.0 + gate * (1.0 - sigmoid))).astype(bf16)
    up_low = (active_grad * gate * sigmoid).astype(bf16)
    gu_low = jnp.concatenate([gate_low, up_low], axis=1)
    gu_grad = scattered(dims(normed_mid, gu_low, 0, 0))
    mid_grad, mid_grad_own = all_sum(place, dims(gu_low, gu_full, 1, 1))

    def norm_back(rows, inverse, gain, grad):
        scaled = grad * gain
        inner = jnp.sum(scaled * rows, axis=1, keepdims=True)
        return scaled, inverse**3 * inner / model_width

    mid_grad = mid_grad.astype(f32)
    scaled, pull = norm_back(hidden, inverse_mid, gains[1], mid_grad)
    through = (grad_low.astype(f32) + inverse_mid * scaled - hidden * pull).astype(bf16)
    inverse_own, pull_own = own_rows(place, inverse_mid), own_rows(place, pull)
    through_own = (
        out_grad.astype(f32)
        + inverse_own * mid_grad_own * second_gain[None, :]
        - hidden_own * pull_own
    )
    second_term = jnp.sum(mid_grad_own * hidden_own * inverse_own, axis=0)

    out_parts = dims(through, attended_low, 0, 1)
    branch_grad = dims(out_full, through, 0, 1).astype(bf16).reshape(heads, HEAD_DIM, tokens)
    query_back, own_back, far_back = on_core(
        kernel(attend_back_kernel),
        (
            jax.ShapeDtypeStruct((heads, HEAD_DIM, tokens), f32),
            jax.ShapeDtypeStruct(own.shape, f32),
            jax.ShapeDtypeStruct(far.shape, f32),
        ),
        count,
        query,
        own,
        far,
        branch_grad,
        attended,
        log_total,
    )
    query_low = rotate(query_back, cosine, -sine).astype(bf16).reshape(heads * HEAD_DIM, tokens)
    query_out = scattered(
        jnp.concatenate([dims(normed_in, query_low, 0, 1), out_parts], axis=1)
    )
    slots_back = [far_back[:, i * tokens : (i + 1) * tokens] for i in range(prompts)]
    for i in range(prompts):
        own_back = own_back + jnp.where(z_in == i, slots_back[i], 0.0)
    moving = None
    for k in range(group - 1, 0, -1):
        sources = [s for s in range(n) if 0 <= s % group - k < prompts]
        send = slots_back[0]
        for i in range(1, prompts):
            send = jnp.where(z_in - k == i, slots_back[i], send)
        if moving is not None:
            send = send + moving
        moving = place.shift(send.astype(bf16), sources, -1).astype(f32)
    own_back = own_back + moving
    key_low = rotate(own_back[None, :HEAD_DIM], cosine, -sine)[0].astype(bf16)
    key_value_low = jnp.concatenate([key_low, own_back[HEAD_DIM:].astype(bf16)], axis=0)
    key_value = scattered(dims(normed_in, key_value_low, 0, 1))
    qkv_low = jnp.concatenate([query_low, key_value_low], axis=0)
    first_own = own_sum(place, dims(qkv_low, qkv_full, 0, 1))
    input_own = layer_in.astype(f32)
    inverse_own = own_rows(place, inverse_in)
    scaled = first_own * first_gain[None, :]
    inner = jnp.sum(scaled * input_own, axis=1, keepdims=True)
    inner = inner + place.swap_c(inner)
    inner = inner + place.swap_x(inner)
    in_grad = (
        through_own + inverse_own * scaled - input_own * (inverse_own**3 * inner / model_width)
    )
    first_term = jnp.sum(first_own * input_own * inverse_own, axis=0)
    terms = jnp.stack([first_term, second_term])
    bit = 1
    while bit < place.nx:
        terms = terms + place.swap_gx(terms, bit)
        bit *= 2

    def columns(summed, start, stop):
        low, high = pair(y, summed[0][:, start:stop], summed[1][:, start:stop])
        return jnp.concatenate([low, high], axis=1)

    query_cols = heads * HEAD_DIM
    return (
        layer_out,
        in_grad,
        terms[0],
        columns(query_out, 0, query_cols),
        columns(key_value, 0, HEAD_DIM),
        columns(key_value, HEAD_DIM, 2 * HEAD_DIM),
        columns(query_out, query_cols, 2 * query_cols).T,
        terms[1],
        columns(gu_grad, 0, hidden_dev),
        columns(gu_grad, hidden_dev, 2 * hidden_dev),
        columns(down_grad, 0, hidden_dev).T,
    )


def solution(mesh):
    rows, cols, gain = P("gx", "gy"), P("gy", "gx"), P("gy")
    return jax.shard_map(
        shards,
        mesh=mesh,
        in_specs=(rows, gain, rows, rows, rows, cols, gain, rows, rows, cols, rows),
        out_specs=(rows, rows, gain, rows, rows, rows, cols, gain, rows, rows, cols),
        check_vma=False,
    )
```

```python
import jax
import jax.numpy as jnp
from jax import lax
from jax.experimental import pallas as pl
from jax.experimental.pallas import tpu as pltpu
from jax.sharding import PartitionSpec as P

HEAD_DIM = 96
PROMPT_DEV = 4
CONT_DEV = 4
GROUP = (PROMPT_DEV + CONT_DEV) // 2
PROMPTS = PROMPT_DEV // 2

eps = 1e-05
neg_big = -1e30
rope_base = 100000.0
score_scale = HEAD_DIM ** (-0.5)
f32 = jnp.float32
bf16 = jnp.bfloat16


def dims(left, right, left_axis, right_axis):
    return lax.dot_general(
        left, right, (((left_axis,), (right_axis,)), ((), ())), preferred_element_type=f32
    )


class Place:
    def __init__(self):
        self.nx = lax.axis_size("gx")
        self.ny = lax.axis_size("gy")
        assert self.ny == 4 and self.nx % (PROMPT_DEV + CONT_DEV) == 0
        self.n = self.nx // 2
        self.gx = lax.axis_index("gx")
        self.gy = lax.axis_index("gy")
        self.z, self.y = self.gx // 2, self.gx % 2
        self.x, self.c = self.gy // 2, self.gy % 2
        self.z_in = self.z % GROUP
        offset = 2 * self.z_in + jnp.arange(2, dtype=jnp.int32)
        self.offset = offset
        first = jnp.stack([self.z, self.y, self.x, self.c, self.z_in]).astype(jnp.int32)
        self.table = jnp.concatenate([first, jnp.minimum(offset, PROMPT_DEV)])

    def swap_gx(self, value, bit):
        return lax.ppermute(value, "gx", [(i, i ^ bit) for i in range(self.nx)])

    def swap_y(self, value):
        return self.swap_gx(value, 1)

    def swap_x(self, value):
        return lax.ppermute(value, "gy", [(i, i ^ 2) for i in range(self.ny)])

    def swap_c(self, value):
        return lax.ppermute(value, "gy", [(i, i ^ 1) for i in range(self.ny)])

    def shift(self, value, sources, step):
        pairs = [(2 * s + y, 2 * (s + step) + y) for s in sources for y in range(2)]
        return lax.ppermute(value, "gx", pairs)

    def by_y(self):
        return [[2 * z + y for z in range(self.n)] for y in range(2)]


def pair(flag, mine, other):
    return jnp.where(flag == 0, mine, other), jnp.where(flag == 0, other, mine)


def part_of(flag, whole, axis):
    low, high = jnp.split(whole, 2, axis)
    return jnp.where(flag == 0, low, high), jnp.where(flag == 0, high, low)


def gather_pieces(place, piece):
    n = place.n
    ups, downs = [], []
    up = down = piece
    for k in range(1, n):
        up = place.shift(up, range(k - 1, n - 1), 1)
        down = place.shift(down, range(1, n - k + 1), -1)
        ups.append(up)
        downs.append(down)
    return [piece] + ups + downs


def gather_whole(place, piece, by_rows):
    every = lax.all_gather(piece, "gx", axis_index_groups=place.by_y())
    inner = place.n // place.ny
    rows, cols = piece.shape
    if by_rows:
        return every.reshape(place.ny, inner * rows, cols)
    every = every.reshape(place.ny, inner, rows, cols)
    return jnp.swapaxes(every, 1, 2).reshape(place.ny, rows, inner * cols)


def scatter_sum(place, parts, by_rows):
    n, z = place.n, place.z
    if n != place.ny:
        inner = n // place.ny
        count, rows, cols = parts.shape
        if by_rows:
            parts = parts.reshape(n, rows // inner, cols)
        else:
            parts = jnp.swapaxes(parts.reshape(count, rows, inner, cols // inner), 1, 2)
            parts = parts.reshape(n, rows, cols // inner)
        return lax.psum_scatter(parts, "gx", axis_index_groups=place.by_y()).astype(f32)

    def part(index):
        return lax.dynamic_index_in_dim(
            parts, jnp.clip(index, 0, n - 1), 0, keepdims=False
        ).astype(f32)

    down = up = None
    for k in range(n - 1, 0, -1):
        send_down, send_up = part(z - k), part(z + k)
        if down is not None:
            send_down, send_up = send_down + down, send_up + up
        down = place.shift(send_down.astype(bf16), range(k, n), -1).astype(f32)
        up = place.shift(send_up.astype(bf16), range(0, n - k), 1).astype(f32)
    return part(z) + down + up


def all_sum(place, keep, send):
    got = place.swap_c(send)
    first, second = keep[0] + got[0].astype(f32), keep[1] + got[1].astype(f32)
    first_got = place.swap_x(first.astype(bf16))
    second_got = place.swap_y(second.astype(bf16))
    first, second = first + first_got.astype(f32), second + second_got.astype(f32)
    first_got = place.swap_y(first.astype(bf16))
    second_got = place.swap_x(second.astype(bf16))
    first, second = first + first_got.astype(f32), second + second_got.astype(f32)
    own = jnp.stack([first.astype(bf16), second.astype(bf16)])
    return own, place.swap_c(own)


def own_sum(place, keep, send):
    got = place.swap_c(send)
    first, second = keep[0] + got[0].astype(f32), keep[1] + got[1].astype(f32)
    mine, other = jnp.where(place.x == 0, first, second), jnp.where(place.x == 0, second, first)
    mine = mine + place.swap_x(other.astype(bf16)).astype(f32)
    mine, other = part_of(place.y, mine, 0)
    return mine + place.swap_y(other.astype(bf16)).astype(f32)


def own_block(place, blocks):
    rows = blocks.shape[1] // 2
    return lax.dynamic_slice(
        blocks, (place.gy, place.y * rows, 0), (1, rows, blocks.shape[2])
    )[0]


Z, Y, X, C, Z_IN, COUNT = range(6)


def call(body, outs, table, operands, pieces=(), scratch=(), limit=40):
    lengths = [len(p) for p in pieces]
    flat = [a for p in pieces for a in p]
    vmem = pl.BlockSpec(memory_space=pltpu.VMEM)

    def kernel(table_ref, *refs):
        plain, rest = refs[: len(operands)], refs[len(operands) :]
        lists = []
        for length in lengths:
            lists.append(rest[:length])
            rest = rest[length:]
        body(table_ref, *plain, *lists, *rest)

    return pl.pallas_call(
        kernel,
        out_shape=[jax.ShapeDtypeStruct(shape, dtype) for shape, dtype in outs],
        in_specs=[pl.BlockSpec(memory_space=pltpu.SMEM)]
        + [vmem] * len(operands)
        + [pl.BlockSpec(memory_space=pl.ANY)] * len(flat),
        out_specs=[vmem] * len(outs),
        scratch_shapes=list(scratch),
        compiler_params=pltpu.CompilerParams(vmem_limit_bytes=limit << 20),
    )(table, *operands, *flat)


def start_pieces(table, pieces, whole, sems):
    if len(pieces) == 1:
        copy = pltpu.make_async_copy(pieces[0], whole, sems.at[0])
        copy.start()
        return copy.wait
    n = (len(pieces) + 1) // 2
    z = table[Z]
    pltpu.make_async_copy(pieces[0], whole.at[z], sems.at[0]).start()
    for k in range(1, n):
        below, above = pieces[k], pieces[n - 1 + n - k]

        @pl.when(z >= k)
        def _():
            pltpu.make_async_copy(below, whole.at[z - k], sems.at[k]).start()

        @pl.when(z < k)
        def _():
            pltpu.make_async_copy(above, whole.at[z + n - k], sems.at[k]).start()

    def wait():
        for k in range(n):
            pltpu.make_async_copy(pieces[0], whole.at[0], sems.at[k]).wait()

    return wait


def keep_and_send(table, block_of, keep_first, keep_second, send):
    core = table[C]
    keep_first[...] = block_of(core)
    keep_second[...] = block_of(2 + core)

    def one(i, _):
        send[i] = block_of(2 * i + 1 - core).astype(bf16)
        return 0

    lax.fori_loop(0, 2, one, 0)


def rows_body(table, *refs):
    rows, gains = refs[:8], refs[8:12]
    raw, grad, normed, inverse, gain_first, gain_second = refs[12:]
    x, y, c = table[X], table[Y], table[C]
    tokens = rows[0].shape[1]
    for dc in range(2):
        for dx in range(2):
            block = 2 * (x + dx - 2 * x * dx) + c + dc - 2 * c * dc
            gain = gains[2 * dc + dx][...]
            gain_first[block] = gain[0:1]
            gain_second[block] = gain[1:2]
            for dy in range(2):
                at = pl.ds(pl.multiple_of(tokens * (y + dy - 2 * y * dy), tokens), tokens)
                piece = rows[4 * dc + 2 * dy + dx]
                raw[block, at, :] = piece[0]
                grad[block, at, :] = piece[1]

    def square(b, total):
        values = raw[b].astype(f32)
        return total + jnp.sum(values * values, axis=1, keepdims=True)

    count = raw.shape[0]
    total = lax.fori_loop(0, count, square, jnp.zeros((raw.shape[1], 1), f32))
    scale = lax.rsqrt(total / (count * raw.shape[2]) + eps)
    inverse[...] = scale

    def norm(b, _):
        normed[b] = (raw[b].astype(f32) * scale * gain_first[b]).astype(bf16)
        return 0

    lax.fori_loop(0, count, norm, 0)


def turn(values, cosine, sine):
    half = values.shape[0] // 2
    first, second = values[:half], values[half:]
    return jnp.concatenate(
        [first * cosine - second * sine, second * cosine + first * sine], axis=0
    )


def qkv_body(table, normed, cosine, sine, pieces, query, own, weights, acc, sems):
    start_pieces(table, pieces, weights, sems)()
    model = normed.shape[2]
    acc[...] = jnp.zeros_like(acc)

    def one(b, _):
        acc[...] += dims(normed[b], weights[b, :model], 1, 0)
        return 0

    lax.fori_loop(0, normed.shape[0], one, 0)
    flipped = acc[...].T
    head = HEAD_DIM
    heads = query.shape[0] // head
    cos, sin = cosine[...], sine[...]
    for h in range(heads):
        at = slice(h * head, (h + 1) * head)
        query[at] = turn(flipped[at], cos, sin).astype(bf16)
    at = slice(heads * head, (heads + 1) * head)
    own[:head] = turn(flipped[at], cos, sin).astype(bf16)
    own[head:] = flipped[(heads + 1) * head :].astype(bf16)


def attend_body(
    table, query, own, *refs
):
    moved = refs[: GROUP - 1]
    weights, attended, attended_low, log_total, far, keep_first, keep_second, send = refs[
        GROUP - 1 :
    ]
    tokens = own.shape[1]
    for place in range(GROUP):

        @pl.when(table[Z_IN] == place)
        def _():
            for slot in range(PROMPTS):
                k = place - slot
                far[:, slot * tokens : (slot + 1) * tokens] = (
                    moved[k - 1][...] if k > 0 else own[...]
                )

    head = HEAD_DIM
    block = tokens // 2
    key_far, value_far = far[:head].T, far[head:]
    key_own = own[:head].T
    total = far.shape[1]
    near_row = lax.broadcasted_iota(jnp.int32, (block, block), 0)
    near_col = lax.broadcasted_iota(jnp.int32, (block, block), 1)
    causal = near_row <= near_col
    row = lax.broadcasted_iota(jnp.int32, (total, block), 0)
    for part in range(2):
        cols = slice(part * block, (part + 1) * block)
        key_near, value_near = key_own[cols], own[head:, cols]
        seen = row < table[COUNT + part] * block

        def one(h, _):
            at = pl.ds(pl.multiple_of(h * head, head), head)
            rows = query[at, cols]
            score_far = jnp.where(seen, dims(key_far, rows, 1, 0) * score_scale, neg_big)
            score_near = jnp.where(causal, dims(key_near, rows, 1, 0) * score_scale, neg_big)
            top = jnp.maximum(
                jnp.max(score_far, axis=0, keepdims=True), jnp.max(score_near, axis=0, keepdims=True)
            )
            weight_far = jnp.exp(score_far - top)
            weight_near = jnp.exp(score_near - top)
            weight = jnp.sum(weight_far, axis=0, keepdims=True) + jnp.sum(
                weight_near, axis=0, keepdims=True
            )
            out = dims(value_far, weight_far.astype(bf16), 1, 0) + dims(
                value_near, weight_near.astype(bf16), 1, 0
            )
            attended[at, cols] = out / weight
            log_total[h, :, cols] = top + jnp.log(weight)
            return 0

        lax.fori_loop(0, query.shape[0] // head, one, 0)
    values = attended[...]
    attended_low[...] = values.astype(bf16)
    flipped = values.T.astype(bf16)
    model = weights.shape[2]
    keep_and_send(
        table,
        lambda b: dims(flipped, weights[b, model:], 1, 0),
        keep_first,
        keep_second,
        send,
    )


def hidden_body(table, raw, summed, other, gain, hidden, normed, inverse):
    core = table[C]
    for i in range(2):
        b = 2 * i + core
        hidden[b] = raw[b].astype(f32) + summed[i].astype(f32)
        b = 2 * i + 1 - core
        hidden[b] = raw[b].astype(f32) + other[i].astype(f32)

    def square(b, total):
        values = hidden[b]
        return total + jnp.sum(values * values, axis=1, keepdims=True)

    count = raw.shape[0]
    total = lax.fori_loop(0, count, square, jnp.zeros((raw.shape[1], 1), f32))
    scale = lax.rsqrt(total / (count * raw.shape[2]) + eps)
    inverse[...] = scale

    def norm(b, _):
        normed[b] = (hidden[b] * scale * gain[b]).astype(bf16)
        return 0

    lax.fori_loop(0, count, norm, 0)


def gate_body(table, normed, pieces, active, gate_slope, up_slope, weights, acc, sems):
    start_pieces(table, pieces, weights, sems)()
    acc[...] = jnp.zeros_like(acc)

    def one(b, _):
        acc[...] += dims(normed[b], weights[b], 1, 0)
        return 0

    lax.fori_loop(0, normed.shape[0], one, 0)
    half = acc.shape[1] // 2
    rows = acc.shape[0] // 4

    def part(i, _):
        at = pl.ds(pl.multiple_of(i * rows, rows), rows)
        gate, up = acc[at, :half], acc[at, half:]
        sigmoid = jax.nn.sigmoid(gate)
        active[at] = (gate * sigmoid * up).astype(bf16)
        gate_slope[at] = up * sigmoid * (1.0 + gate * (1.0 - sigmoid))
        up_slope[at] = gate * sigmoid
        return 0

    lax.fori_loop(0, 4, part, 0)


def down_parts_body(table, active, grad, parts):
    flipped = active[...].T

    def one(b, _):
        parts[b] = dims(flipped, grad[b], 1, 0).astype(bf16)
        return 0

    lax.fori_loop(0, grad.shape[0], one, 0)


def gate_back_body(
    table,
    grad,
    gate_slope,
    up_slope,
    gate_pieces,
    down_pieces,
    change,
    keep_first,
    keep_second,
    send,
    gate_weights,
    down_weights,
    acc,
    gate_sems,
    down_sems,
):
    down_wait = start_pieces(table, down_pieces, down_weights, down_sems)
    gate_wait = start_pieces(table, gate_pieces, gate_weights, gate_sems)
    down_wait()
    acc[...] = jnp.zeros_like(acc)

    def one(b, _):
        acc[...] += dims(grad[b], down_weights[b], 1, 1)
        return 0

    lax.fori_loop(0, grad.shape[0], one, 0)
    half = acc.shape[1]
    change[:, :half] = (acc[...] * gate_slope[...]).astype(bf16)
    change[:, half:] = (acc[...] * up_slope[...]).astype(bf16)
    gate_wait()
    values = change[...]
    keep_and_send(
        table, lambda b: dims(values, gate_weights[b], 1, 1), keep_first, keep_second, send
    )


def down_body(table, active, pieces, keep_first, keep_second, send, weights, sems):
    start_pieces(table, pieces, weights, sems)()
    values = active[...]
    keep_and_send(table, lambda b: dims(values, weights[b], 1, 0), keep_first, keep_second, send)


def gate_parts_body(table, normed, change, parts):
    def one(b, _):
        parts[b] = dims(normed[b], change[...], 0, 0).astype(bf16)
        return 0

    lax.fori_loop(0, normed.shape[0], one, 0)


def attend_back_body(
    table,
    hidden,
    inverse,
    summed,
    other,
    grad,
    gain,
    weights,
    query,
    own,
    far,
    attended,
    log_total,
    cosine,
    sine,
    through,
    pull,
    query_low,
    own_back,
    far_back,
    change,
):
    core = table[C]
    count, tokens, model = hidden.shape
    for i in range(2):
        change[2 * i + core] = summed[i].astype(f32) * gain[2 * i + core]
        change[2 * i + 1 - core] = other[i].astype(f32) * gain[2 * i + 1 - core]

    def product(b, total):
        return total + jnp.sum(change[b] * hidden[b], axis=1, keepdims=True)

    inner = lax.fori_loop(0, count, product, jnp.zeros((tokens, 1), f32))
    scale = inverse[...]
    back = scale * scale * scale * inner / (count * model)
    pull[...] = back

    def rows(b, total):
        values = grad[b].astype(f32) + scale * change[b] - hidden[b] * back
        low = values.astype(bf16)
        through[b] = low
        return total + dims(low, weights[b, model:], 1, 1)

    heads_cols = query.shape[0]
    branch = lax.fori_loop(0, count, rows, jnp.zeros((tokens, heads_cols), f32))
    branch = branch.T.astype(bf16)

    head = HEAD_DIM
    block = tokens // 2
    key_far_t = far[:head]
    key_far, value_far = key_far_t.T, far[head:].T
    key_own, value_own = own[:head].T, own[head:].T
    total = far.shape[1]
    near_row = lax.broadcasted_iota(jnp.int32, (block, block), 0)
    near_col = lax.broadcasted_iota(jnp.int32, (block, block), 1)
    causal = near_row <= near_col
    row = lax.broadcasted_iota(jnp.int32, (total, block), 0)
    far_back[...] = jnp.zeros_like(far_back)
    own_back[...] = jnp.zeros_like(own_back)
    for part in range(2):
        cols = slice(part * block, (part + 1) * block)
        key_near, value_near = key_own[cols], value_own[cols]
        key_near_t = own[:head, cols]
        seen = row < table[COUNT + part] * block
        for h in range(heads_cols // head):
            at = slice(h * head, (h + 1) * head)
            rows_q, rows_grad = query[at, cols], branch[at, cols]
            delta = jnp.sum(
                rows_grad.astype(f32) * attended[at, cols], axis=0, keepdims=True
            )
            logs = log_total[h, :, cols]

            def one(key, value, allowed):
                score = dims(key, rows_q, 1, 0) * score_scale
                prob = jnp.where(allowed, jnp.exp(score - logs), 0.0)
                moved = (prob * (dims(value, rows_grad, 1, 0) - delta)).astype(bf16)
                return prob.astype(bf16), moved

            prob_far, moved_far = one(key_far, value_far, seen)
            prob_near, moved_near = one(key_near, value_near, causal)
            query_back = (
                dims(key_far_t, moved_far, 1, 0) + dims(key_near_t, moved_near, 1, 0)
            ) * score_scale
            query_low[at, cols] = turn(query_back, cosine[:, cols], -sine[:, cols]).astype(bf16)
            far_back[:head] += dims(rows_q, moved_far, 1, 1) * score_scale
            far_back[head:] += dims(rows_grad, prob_far, 1, 1)
            own_back[:head, cols] += dims(rows_q, moved_near, 1, 1) * score_scale
            own_back[head:, cols] += dims(rows_grad, prob_near, 1, 1)
    for slot in range(PROMPTS):

        @pl.when(table[Z_IN] == slot)
        def _():
            own_back[...] += far_back[:, slot * tokens : (slot + 1) * tokens]


def query_parts_body(table, query_low, normed, attended_low, through, parts):
    rows = query_low.shape[0]

    def one(b, _):
        parts[b, :rows] = dims(query_low[...], normed[b], 1, 0).astype(bf16)
        parts[b, rows:] = dims(attended_low[...], through[b], 1, 0).astype(bf16)
        return 0

    lax.fori_loop(0, normed.shape[0], one, 0)


def qkv_back_body(
    table, own_back, query_low, normed, weights, cosine, sine, parts, keep_first, keep_second, send
):
    head = HEAD_DIM
    key = turn(own_back[:head], cosine[...], -sine[...])
    low = jnp.concatenate([key, own_back[head:]], axis=0)
    low_16 = low.astype(bf16)

    def one(b, _):
        parts[b] = dims(low_16, normed[b], 1, 0).astype(bf16)
        return 0

    lax.fori_loop(0, normed.shape[0], one, 0)
    flipped = jnp.concatenate([query_low[...].T, low.T.astype(bf16)], axis=1)
    model = weights.shape[2]
    keep_and_send(
        table,
        lambda b: dims(flipped, weights[b, :model], 1, 1),
        keep_first,
        keep_second,
        send,
    )


def rope_tables(positions, half):
    freq = rope_base ** (-(2.0 * jnp.arange(half, dtype=f32)) / (2.0 * half))
    angle = freq[:, None] * positions.astype(f32)[None, :]
    return (jnp.cos(angle), jnp.sin(angle))


def shards(
    layer_in,
    first_gain,
    query_weight,
    key_matrix,
    value_matrix,
    out_weight,
    second_gain,
    gate_weight,
    up_weight,
    down_weight,
    out_grad,
):
    place = Place()
    n, ny, y, z_in, table = place.n, place.ny, place.y, place.z_in, place.table
    lined = n == ny
    block, width = layer_in.shape
    tokens = 2 * block
    model_width = width * ny
    hidden_dev = gate_weight.shape[1] // 2
    query_rows = query_weight.shape[1] // 2
    kv_rows = key_matrix.shape[1]
    qkv_cols = query_rows + kv_rows
    full = (ny, tokens, width)
    wide = [(full[1:], f32), (full[1:], f32), ((2,) + full[1:], bf16)]

    def by_columns(*matrices):
        mine, other = zip(*(part_of(y, m, 1) for m in matrices))
        got = place.swap_y(jnp.concatenate(other, axis=1))
        return jnp.concatenate(pair(y, jnp.concatenate(mine, axis=1), got), axis=0)

    def by_rows(matrix):
        mine, other = part_of(y, matrix, 0)
        return jnp.concatenate(pair(y, mine, place.swap_y(other)), axis=1)

    def gathered(piece, rows_first):
        if lined:
            return gather_pieces(place, piece)
        return [gather_whole(place, piece, rows_first)]

    qkv_piece = by_columns(query_weight, key_matrix, value_matrix)
    out_piece = by_rows(out_weight)
    if lined:
        attend_pieces = gather_pieces(place, jnp.concatenate([qkv_piece, out_piece], axis=0))
    else:
        attend_pieces = [
            jnp.concatenate(
                [gather_whole(place, qkv_piece, True), gather_whole(place, out_piece, False)],
                axis=1,
            )
        ]
    gate_pieces = gathered(by_columns(gate_weight, up_weight), True)
    down_pieces = gathered(by_rows(down_weight), False)
    attend_shape = (ny, width + query_rows, width)
    gate_shape = (ny, width, 2 * hidden_dev)
    down_shape = (ny, hidden_dev, width)
    sems = pltpu.SemaphoreType.DMA((ny,))

    rows = jnp.stack([layer_in, out_grad])
    rows_x = place.swap_x(rows)
    four = [rows, rows_x, place.swap_y(rows), place.swap_y(rows_x)]
    eight = four + [place.swap_c(r) for r in four]
    gains = jnp.stack([first_gain, second_gain])
    two = [gains, place.swap_x(gains)]
    gains = two + [place.swap_c(g) for g in two]
    raw, grad, normed_in, inverse_in, gain_in, gain_mid = call(
        rows_body,
        [(full, bf16), (full, bf16), (full, bf16), ((tokens, 1), f32)]
        + [((ny, 1, width), f32)] * 2,
        table,
        eight + gains,
    )

    within = jnp.arange(block, dtype=jnp.int32)
    positions = jnp.minimum(place.offset, PROMPT_DEV)[:, None] * block + within[None, :]
    cosine, sine = rope_tables(positions.reshape(-1), HEAD_DIM // 2)
    query, own, attend_weights = call(
        qkv_body,
        [((query_rows, tokens), bf16), ((kv_rows, tokens), bf16), (attend_shape, bf16)],
        table,
        [normed_in, cosine, sine],
        [attend_pieces],
        [pltpu.VMEM((tokens, qkv_cols), f32), sems],
    )
    moved = []
    moving = own
    for k in range(1, GROUP):
        sources = [
            s for s in range(n) if 0 <= s % GROUP - (k - 1) < PROMPTS and s % GROUP + 1 < GROUP
        ]
        moving = place.shift(moving, sources, 1)
        moved.append(moving)
    attended, attended_low, log_total, far, keep_first, keep_second, send = call(
        attend_body,
        [
            ((query_rows, tokens), f32),
            ((query_rows, tokens), bf16),
            ((query_rows // HEAD_DIM, 1, tokens), f32),
            ((kv_rows, PROMPTS * tokens), bf16),
        ]
        + wide,
        table,
        [query, own] + moved + [attend_weights],
    )
    summed, other = all_sum(place, (keep_first, keep_second), send)

    hidden, normed_mid, inverse_mid = call(
        hidden_body,
        [(full, f32), (full, bf16), ((tokens, 1), f32)],
        table,
        [raw, summed, other, gain_mid],
    )
    active, gate_slope, up_slope = call(
        gate_body,
        [((tokens, hidden_dev), bf16)] + [((tokens, hidden_dev), f32)] * 2,
        table,
        [normed_mid],
        [gate_pieces],
        [
            pltpu.VMEM(gate_shape, bf16),
            pltpu.VMEM((tokens, 2 * hidden_dev), f32),
            sems,
        ],
    )
    (down_parts,) = call(down_parts_body, [(down_shape, bf16)], table, [active, grad])
    change, keep_first, keep_second, send = call(
        gate_back_body,
        [((tokens, 2 * hidden_dev), bf16)] + wide,
        table,
        [grad, gate_slope, up_slope],
        [gate_pieces, down_pieces],
        [
            pltpu.VMEM(gate_shape, bf16),
            pltpu.VMEM(down_shape, bf16),
            pltpu.VMEM((tokens, hidden_dev), f32),
            sems,
            sems,
        ],
    )
    summed, other = all_sum(place, (keep_first, keep_second), send)
    keep_first, keep_second, send = call(
        down_body, wide, table, [active], [down_pieces], [pltpu.VMEM(down_shape, bf16), sems]
    )
    hidden_own = own_block(place, hidden)
    layer_out = (hidden_own + own_sum(place, (keep_first, keep_second), send)).astype(bf16)
    down_grad = scatter_sum(place, down_parts, False)
    (gate_parts,) = call(gate_parts_body, [(gate_shape, bf16)], table, [normed_mid, change])
    gate_grad = scatter_sum(place, gate_parts, True)

    through, pull, query_low, own_back, far_back = call(
        attend_back_body,
        [
            (full, bf16),
            ((tokens, 1), f32),
            ((query_rows, tokens), bf16),
            ((kv_rows, tokens), f32),
            ((kv_rows, PROMPTS * tokens), f32),
        ],
        table,
        [
            hidden,
            inverse_mid,
            summed,
            other,
            grad,
            gain_mid,
            attend_weights,
            query,
            own,
            far,
            attended,
            log_total,
            cosine,
            sine,
        ],
        scratch=[pltpu.VMEM(full, f32)],
    )
    inverse_own, _ = part_of(y, inverse_mid, 0)
    pull_own, _ = part_of(y, pull, 0)
    mid_own = lax.dynamic_index_in_dim(summed, place.x, 0, keepdims=False)
    mid_own = part_of(y, mid_own, 0)[0].astype(f32)
    through_own = (
        out_grad.astype(f32)
        + inverse_own * mid_own * second_gain[None, :]
        - hidden_own * pull_own
    )
    second_term = jnp.sum(mid_own * hidden_own * inverse_own, axis=0)

    (query_parts,) = call(
        query_parts_body,
        [((ny, 2 * query_rows, width), bf16)],
        table,
        [query_low, normed_in, attended_low, through],
    )
    query_grad = scatter_sum(place, query_parts, False)

    moving = None
    for k in range(GROUP - 1, 0, -1):
        sources = [s for s in range(n) if 0 <= s % GROUP - k < PROMPTS]
        send = far_back[:, :tokens]
        for i in range(1, PROMPTS):
            send = jnp.where(z_in - k == i, far_back[:, i * tokens : (i + 1) * tokens], send)
        if moving is not None:
            send = send + moving
        moving = place.shift(send.astype(bf16), sources, -1).astype(f32)
    own_back = own_back + moving
    kv_parts, keep_first, keep_second, send = call(
        qkv_back_body,
        [((ny, kv_rows, width), bf16)] + wide,
        table,
        [own_back, query_low, normed_in, attend_weights, cosine, sine],
    )
    kv_grad = scatter_sum(place, kv_parts, False)
    first_own = own_sum(place, (keep_first, keep_second), send)
    input_own = layer_in.astype(f32)
    inverse_own, _ = part_of(y, inverse_in, 0)
    scaled = first_own * first_gain[None, :]
    inner = jnp.sum(scaled * input_own, axis=1, keepdims=True)
    inner = inner + place.swap_c(inner)
    inner = inner + place.swap_x(inner)
    in_grad = (
        through_own + inverse_own * scaled - input_own * (inverse_own**3 * inner / model_width)
    )
    first_term = jnp.sum(first_own * input_own * inverse_own, axis=0)
    terms = jnp.stack([first_term, second_term])
    bit = 1
    while bit < place.nx:
        terms = terms + place.swap_gx(terms, bit)
        bit *= 2

    def joined(summed_part, axis):
        mine, other = part_of(y, summed_part, axis)
        return pair(y, mine, place.swap_y(other.astype(bf16)).astype(f32))

    gate_low, gate_high = joined(gate_grad, 0)
    down_grad = jnp.concatenate(joined(down_grad, 1), axis=0)
    query_low, query_high = joined(query_grad, 1)
    kv_low, kv_high = joined(kv_grad, 1)

    def stacked(low, high, start, stop):
        return jnp.concatenate([low[start:stop], high[start:stop]], axis=0)

    half_kv = kv_rows // 2
    return (
        layer_out,
        in_grad,
        terms[0],
        stacked(query_low, query_high, 0, query_rows).T,
        stacked(kv_low, kv_high, 0, half_kv).T,
        stacked(kv_low, kv_high, half_kv, kv_rows).T,
        stacked(query_low, query_high, query_rows, 2 * query_rows),
        terms[1],
        jnp.concatenate([gate_low[:, :hidden_dev], gate_high[:, :hidden_dev]], axis=1),
        jnp.concatenate([gate_low[:, hidden_dev:], gate_high[:, hidden_dev:]], axis=1),
        down_grad,
    )


def solution(mesh):
    rows, cols, gain = P("gx", "gy"), P("gy", "gx"), P("gy")
    return jax.shard_map(
        shards,
        mesh=mesh,
        in_specs=(rows, gain, rows, rows, rows, cols, gain, rows, rows, cols, rows),
        out_specs=(rows, rows, gain, rows, rows, rows, cols, gain, rows, rows, cols),
        check_vma=False,
    )
```

```python
import jax
import jax.numpy as jnp
from jax import lax
from jax.experimental import pallas as pl
from jax.experimental.pallas import tpu as pltpu
from jax.sharding import PartitionSpec as P

HEAD_DIM = 96
PROMPT_DEV = 4
CONT_DEV = 4
GROUP = (PROMPT_DEV + CONT_DEV) // 2
PROMPTS = PROMPT_DEV // 2

eps = 1e-05
neg_big = -1e30
rope_base = 100000.0
score_scale = HEAD_DIM ** (-0.5)
f32 = jnp.float32
bf16 = jnp.bfloat16


def dims(left, right, left_axis, right_axis):
    return lax.dot_general(
        left, right, (((left_axis,), (right_axis,)), ((), ())), preferred_element_type=f32
    )


class Place:
    def __init__(self):
        self.nx = lax.axis_size("gx")
        self.ny = lax.axis_size("gy")
        assert self.ny == 4 and self.nx % (PROMPT_DEV + CONT_DEV) == 0
        self.n = self.nx // 2
        self.gx = lax.axis_index("gx")
        self.gy = lax.axis_index("gy")
        self.z, self.y = self.gx // 2, self.gx % 2
        self.x, self.c = self.gy // 2, self.gy % 2
        self.z_in = self.z % GROUP
        offset = 2 * self.z_in + jnp.arange(2, dtype=jnp.int32)
        self.offset = offset
        self.lined = self.n == self.ny
        blocks = jnp.arange(self.ny, dtype=jnp.int32)
        first = jnp.stack([self.z, self.y, self.x, self.c, self.z_in]).astype(jnp.int32)
        self.table = jnp.concatenate(
            [first, jnp.minimum(offset, PROMPT_DEV), blocks ^ self.z if self.lined else blocks]
        )

    def swap_gx(self, value, bit):
        return lax.ppermute(value, "gx", [(i, i ^ bit) for i in range(self.nx)])

    def swap_y(self, value):
        return self.swap_gx(value, 1)

    def swap_x(self, value):
        return lax.ppermute(value, "gy", [(i, i ^ 2) for i in range(self.ny)])

    def swap_c(self, value):
        return lax.ppermute(value, "gy", [(i, i ^ 1) for i in range(self.ny)])

    def send_z(self, value, moves):
        pairs = [(2 * s + y, 2 * t + y) for s, t in moves for y in range(2)]
        return lax.ppermute(value, "gx", pairs)

    def by_y(self):
        return [[2 * z + y for z in range(self.n)] for y in range(2)]


def pair(flag, mine, other):
    return jnp.where(flag == 0, mine, other), jnp.where(flag == 0, other, mine)


def part_of(flag, whole, axis):
    low, high = jnp.split(whole, 2, axis)
    return jnp.where(flag == 0, low, high), jnp.where(flag == 0, high, low)


def after(value, *earlier):
    return lax.optimization_barrier((value,) + earlier)[0]


NEAR = [(0, 1), (1, 0), (2, 3), (3, 2)]
SECOND = [(0, 2), (1, 3), (2, 0), (3, 1)]
MIDDLE = [(1, 2), (2, 1)]
INWARD = [(0, 1), (3, 2)]
OUTWARD = [(1, 0), (2, 3)]


def gather_pieces(place, piece):
    near = place.send_z(piece, NEAR)
    second = place.send_z(piece, SECOND)
    middle = place.send_z(piece, MIDDLE)
    return [piece, near, second, middle, place.send_z(second, OUTWARD)]


def gather_whole(place, piece, by_rows):
    every = lax.all_gather(piece, "gx", axis_index_groups=place.by_y())
    inner = place.n // place.ny
    rows, cols = piece.shape
    if by_rows:
        return every.reshape(place.ny, inner * rows, cols)
    every = every.reshape(place.ny, inner, rows, cols)
    return jnp.swapaxes(every, 1, 2).reshape(place.ny, rows, inner * cols)


def scatter_sum(place, parts, by_rows):
    if not place.lined:
        n = place.n
        inner = n // place.ny
        parts = jnp.stack(parts)
        count, rows, cols = parts.shape
        if by_rows:
            parts = parts.reshape(n, rows // inner, cols)
        else:
            parts = jnp.swapaxes(parts.reshape(count, rows, inner, cols // inner), 1, 2)
            parts = parts.reshape(n, rows, cols // inner)
        return lax.psum_scatter(parts, "gx", axis_index_groups=place.by_y()).astype(f32)
    own, near, second, third = parts
    far = place.send_z(third, INWARD)
    near = place.send_z(near, NEAR)
    middle = place.send_z(third, MIDDLE)
    second = place.send_z((second.astype(f32) + far.astype(f32)).astype(bf16), SECOND)
    return own.astype(f32) + near.astype(f32) + middle.astype(f32) + second.astype(f32)


def all_sum(place, keep, send, *earlier):
    got = place.swap_c(send)
    first, second = keep[0] + got[0].astype(f32), keep[1] + got[1].astype(f32)
    first_got = place.swap_x(first.astype(bf16))
    second_got = place.swap_y(second.astype(bf16))
    first, second = first + first_got.astype(f32), second + second_got.astype(f32)
    first_low, second_low = first.astype(bf16), second.astype(bf16)
    if earlier:
        first_low, second_low = lax.optimization_barrier((first_low, second_low) + earlier)[:2]
    first_got = place.swap_y(first_low)
    second_got = place.swap_x(second_low)
    own = [
        (first + first_got.astype(f32)).astype(bf16),
        (second + second_got.astype(f32)).astype(bf16),
    ]
    return own + [place.swap_c(part) for part in own]


def own_sum(place, keep, send):
    got = place.swap_c(send)
    first, second = keep[0] + got[0].astype(f32), keep[1] + got[1].astype(f32)
    mine, other = jnp.where(place.x == 0, first, second), jnp.where(place.x == 0, second, first)
    mine = mine + place.swap_x(other.astype(bf16)).astype(f32)
    mine, other = part_of(place.y, mine, 0)
    return mine + place.swap_y(other.astype(bf16)).astype(f32)


def own_block(place, blocks):
    rows = blocks.shape[1] // 2
    return lax.dynamic_slice(
        blocks, (place.gy, place.y * rows, 0), (1, rows, blocks.shape[2])
    )[0]


Z, Y, X, C, Z_IN, COUNT = range(6)
ORDER = COUNT + 2


def call(body, outs, table, operands, pieces=(), scratch=(), earlier=(), limit=24):
    lengths = [len(p) for p in pieces]
    flat = [a for p in pieces for a in p] + list(earlier)
    vmem = pl.BlockSpec(memory_space=pltpu.VMEM)

    def kernel(table_ref, *refs):
        plain, rest = refs[: len(operands)], refs[len(operands) :]
        lists = []
        for length in lengths:
            lists.append(rest[:length])
            rest = rest[length:]
        rest = rest[len(earlier) :]
        body(table_ref, *plain, *lists, *rest)

    return pl.pallas_call(
        kernel,
        out_shape=[jax.ShapeDtypeStruct(shape, dtype) for shape, dtype in outs],
        in_specs=[pl.BlockSpec(memory_space=pltpu.SMEM)]
        + [vmem] * len(operands)
        + [pl.BlockSpec(memory_space=pl.ANY)] * len(flat),
        out_specs=[vmem] * len(outs),
        scratch_shapes=list(scratch),
        compiler_params=pltpu.CompilerParams(vmem_limit_bytes=limit << 20),
    )(table, *operands, *flat)


def start_pieces(table, pieces, whole, sems):
    if len(pieces) == 1:
        copy = pltpu.make_async_copy(pieces[0], whole, sems.at[0])
        copy.start()
        return copy.wait
    z = table[Z]
    own, near, second, middle, end = pieces
    inside = jnp.logical_or(z == 1, z == 2)
    pltpu.make_async_copy(own, whole.at[table[ORDER]], sems.at[0]).start()
    pltpu.make_async_copy(near, whole.at[table[ORDER + 1]], sems.at[1]).start()
    pltpu.make_async_copy(second, whole.at[table[ORDER + 2]], sems.at[2]).start()

    @pl.when(inside)
    def _():
        pltpu.make_async_copy(middle, whole.at[table[ORDER + 3]], sems.at[3]).start()

    @pl.when(jnp.logical_not(inside))
    def _():
        pltpu.make_async_copy(end, whole.at[table[ORDER + 3]], sems.at[3]).start()

    def wait():
        for k in range(4):
            pltpu.make_async_copy(own, whole.at[0], sems.at[k]).wait()

    return wait


def keep_and_send(table, block_of, keep_first, keep_second, send):
    core = table[C]
    keep_first[...] = block_of(core)
    keep_second[...] = block_of(2 + core)

    def one(i, _):
        send[i] = block_of(2 * i + 1 - core).astype(bf16)
        return 0

    lax.fori_loop(0, 2, one, 0)


def place_rows(table, pieces, whole):
    x, y, c = table[X], table[Y], table[C]
    tokens = pieces[0].shape[0]
    for dc in range(2):
        for dx in range(2):
            block = 2 * (x + dx - 2 * x * dx) + c + dc - 2 * c * dc
            for dy in range(2):
                at = pl.ds(pl.multiple_of(tokens * (y + dy - 2 * y * dy), tokens), tokens)
                whole[block, at, :] = pieces[4 * dc + 2 * dy + dx][...]


def grad_body(table, *refs):
    place_rows(table, refs[:8], refs[8])


def rows_body(table, *refs):
    rows, gains = refs[:8], refs[8:12]
    raw, normed, inverse, gain_first, gain_second = refs[12:]
    place_rows(table, rows, raw)
    x, c = table[X], table[C]
    for dc in range(2):
        for dx in range(2):
            block = 2 * (x + dx - 2 * x * dx) + c + dc - 2 * c * dc
            gain = gains[2 * dc + dx][...]
            gain_first[block] = gain[0:1]
            gain_second[block] = gain[1:2]

    def square(b, total):
        values = raw[b].astype(f32)
        return total + jnp.sum(values * values, axis=1, keepdims=True)

    count = raw.shape[0]
    total = lax.fori_loop(0, count, square, jnp.zeros((raw.shape[1], 1), f32))
    scale = lax.rsqrt(total / (count * raw.shape[2]) + eps)
    inverse[...] = scale

    def norm(b, _):
        normed[b] = (raw[b].astype(f32) * scale * gain_first[b]).astype(bf16)
        return 0

    lax.fori_loop(0, count, norm, 0)


def turn(values, cosine, sine):
    half = values.shape[0] // 2
    first, second = values[:half], values[half:]
    return jnp.concatenate(
        [first * cosine - second * sine, second * cosine + first * sine], axis=0
    )


def qkv_body(table, normed, cosine, sine, pieces, query, own, weights, acc, sems):
    start_pieces(table, pieces, weights, sems)()
    model = normed.shape[2]
    acc[...] = jnp.zeros_like(acc)

    def one(b, _):
        acc[...] += dims(normed[b], weights[b, :model], 1, 0)
        return 0

    lax.fori_loop(0, normed.shape[0], one, 0)
    flipped = acc[...].T
    head = HEAD_DIM
    heads = query.shape[0] // head
    cos, sin = cosine[...], sine[...]
    for h in range(heads):
        at = slice(h * head, (h + 1) * head)
        query[at] = turn(flipped[at], cos, sin).astype(bf16)
    at = slice(heads * head, (heads + 1) * head)
    own[:head] = turn(flipped[at], cos, sin).astype(bf16)
    own[head:] = flipped[(heads + 1) * head :].astype(bf16)


def attend_body(
    table, query, own, *refs
):
    moved = refs[: GROUP - 1]
    weights, attended, attended_low, log_total, far, keep_first, keep_second, send = refs[
        GROUP - 1 :
    ]
    tokens = own.shape[1]
    for place in range(GROUP):

        @pl.when(table[Z_IN] == place)
        def _():
            for slot in range(PROMPTS):
                k = place - slot
                far[:, slot * tokens : (slot + 1) * tokens] = (
                    moved[k - 1][...] if k > 0 else own[...]
                )

    head = HEAD_DIM
    block = tokens // 2
    key_far, value_far = far[:head].T, far[head:]
    key_own = own[:head].T
    total = far.shape[1]
    near_row = lax.broadcasted_iota(jnp.int32, (block, block), 0)
    near_col = lax.broadcasted_iota(jnp.int32, (block, block), 1)
    causal = near_row <= near_col
    row = lax.broadcasted_iota(jnp.int32, (total, block), 0)
    for part in range(2):
        cols = slice(part * block, (part + 1) * block)
        key_near, value_near = key_own[cols], own[head:, cols]
        seen = row < table[COUNT + part] * block

        def one(h, _):
            at = pl.ds(pl.multiple_of(h * head, head), head)
            rows = query[at, cols]
            score_far = jnp.where(seen, dims(key_far, rows, 1, 0) * score_scale, neg_big)
            score_near = jnp.where(causal, dims(key_near, rows, 1, 0) * score_scale, neg_big)
            top = jnp.maximum(
                jnp.max(score_far, axis=0, keepdims=True), jnp.max(score_near, axis=0, keepdims=True)
            )
            weight_far = jnp.exp(score_far - top)
            weight_near = jnp.exp(score_near - top)
            weight = jnp.sum(weight_far, axis=0, keepdims=True) + jnp.sum(
                weight_near, axis=0, keepdims=True
            )
            out = dims(value_far, weight_far.astype(bf16), 1, 0) + dims(
                value_near, weight_near.astype(bf16), 1, 0
            )
            attended[at, cols] = out / weight
            log_total[h, :, cols] = top + jnp.log(weight)
            return 0

        lax.fori_loop(0, query.shape[0] // head, one, 0)
    values = attended[...]
    attended_low[...] = values.astype(bf16)
    flipped = values.T.astype(bf16)
    model = weights.shape[2]
    keep_and_send(
        table,
        lambda b: dims(flipped, weights[b, model:], 1, 0),
        keep_first,
        keep_second,
        send,
    )


def hidden_body(
    table, raw, own_first, own_second, other_first, other_second, gain, hidden, normed, inverse
):
    core = table[C]
    summed, other = (own_first, own_second), (other_first, other_second)
    for i in range(2):
        b = 2 * i + core
        hidden[b] = raw[b].astype(f32) + summed[i][...].astype(f32)
        b = 2 * i + 1 - core
        hidden[b] = raw[b].astype(f32) + other[i][...].astype(f32)

    def square(b, total):
        values = hidden[b]
        return total + jnp.sum(values * values, axis=1, keepdims=True)

    count = raw.shape[0]
    total = lax.fori_loop(0, count, square, jnp.zeros((raw.shape[1], 1), f32))
    scale = lax.rsqrt(total / (count * raw.shape[2]) + eps)
    inverse[...] = scale

    def norm(b, _):
        normed[b] = (hidden[b] * scale * gain[b]).astype(bf16)
        return 0

    lax.fori_loop(0, count, norm, 0)


def gate_body(table, normed, pieces, active, gate_slope, up_slope, weights, acc, sems):
    start_pieces(table, pieces, weights, sems)()
    acc[...] = jnp.zeros_like(acc)

    def one(b, _):
        acc[...] += dims(normed[b], weights[b], 1, 0)
        return 0

    lax.fori_loop(0, normed.shape[0], one, 0)
    half = acc.shape[1] // 2
    rows = acc.shape[0] // 4

    def part(i, _):
        at = pl.ds(pl.multiple_of(i * rows, rows), rows)
        gate, up = acc[at, :half], acc[at, half:]
        sigmoid = jax.nn.sigmoid(gate)
        active[at] = (gate * sigmoid * up).astype(bf16)
        gate_slope[at] = up * sigmoid * (1.0 + gate * (1.0 - sigmoid))
        up_slope[at] = gate * sigmoid
        return 0

    lax.fori_loop(0, 4, part, 0)


def down_parts_body(table, active, grad, *parts):
    flipped = active[...].T
    for k, part in enumerate(parts):
        part[...] = dims(flipped, grad[table[ORDER + k]], 1, 0).astype(bf16)


def gate_back_body(
    table,
    grad,
    gate_slope,
    up_slope,
    gate_pieces,
    down_pieces,
    change,
    keep_first,
    keep_second,
    send,
    gate_weights,
    down_weights,
    acc,
    gate_sems,
    down_sems,
):
    down_wait = start_pieces(table, down_pieces, down_weights, down_sems)
    gate_wait = start_pieces(table, gate_pieces, gate_weights, gate_sems)
    down_wait()
    acc[...] = jnp.zeros_like(acc)

    def one(b, _):
        acc[...] += dims(grad[b], down_weights[b], 1, 1)
        return 0

    lax.fori_loop(0, grad.shape[0], one, 0)
    half = acc.shape[1]
    change[:, :half] = (acc[...] * gate_slope[...]).astype(bf16)
    change[:, half:] = (acc[...] * up_slope[...]).astype(bf16)
    gate_wait()
    values = change[...]
    keep_and_send(
        table, lambda b: dims(values, gate_weights[b], 1, 1), keep_first, keep_second, send
    )


def down_body(table, active, pieces, keep_first, keep_second, send, weights, sems):
    start_pieces(table, pieces, weights, sems)()
    values = active[...]
    keep_and_send(table, lambda b: dims(values, weights[b], 1, 0), keep_first, keep_second, send)


def gate_parts_body(table, normed, change, *parts):
    for k, part in enumerate(parts):
        part[...] = dims(normed[table[ORDER + k]], change[...], 0, 0).astype(bf16)


def attend_back_body(
    table,
    hidden,
    inverse,
    own_first,
    own_second,
    other_first,
    other_second,
    grad,
    gain,
    weights,
    query,
    own,
    far,
    attended,
    log_total,
    cosine,
    sine,
    through,
    pull,
    query_low,
    own_back,
    *rest,
):
    sends, far_back, change = rest[: GROUP - 1], rest[-2], rest[-1]
    core = table[C]
    count, tokens, model = hidden.shape
    for i, (mine, theirs) in enumerate(((own_first, other_first), (own_second, other_second))):
        change[2 * i + core] = mine[...].astype(f32) * gain[2 * i + core]
        change[2 * i + 1 - core] = theirs[...].astype(f32) * gain[2 * i + 1 - core]

    def product(b, total):
        return total + jnp.sum(change[b] * hidden[b], axis=1, keepdims=True)

    inner = lax.fori_loop(0, count, product, jnp.zeros((tokens, 1), f32))
    scale = inverse[...]
    back = scale * scale * scale * inner / (count * model)
    pull[...] = back

    def rows(b, total):
        values = grad[b].astype(f32) + scale * change[b] - hidden[b] * back
        low = values.astype(bf16)
        through[b] = low
        return total + dims(low, weights[b, model:], 1, 1)

    heads_cols = query.shape[0]
    branch = lax.fori_loop(0, count, rows, jnp.zeros((tokens, heads_cols), f32))
    branch = branch.T.astype(bf16)

    head = HEAD_DIM
    block = tokens // 2
    key_far_t = far[:head]
    key_far, value_far = key_far_t.T, far[head:].T
    key_own, value_own = own[:head].T, own[head:].T
    total = far.shape[1]
    near_row = lax.broadcasted_iota(jnp.int32, (block, block), 0)
    near_col = lax.broadcasted_iota(jnp.int32, (block, block), 1)
    causal = near_row <= near_col
    row = lax.broadcasted_iota(jnp.int32, (total, block), 0)
    far_back[...] = jnp.zeros_like(far_back)
    own_back[...] = jnp.zeros_like(own_back)
    for part in range(2):
        cols = slice(part * block, (part + 1) * block)
        key_near, value_near = key_own[cols], value_own[cols]
        key_near_t = own[:head, cols]
        seen = row < table[COUNT + part] * block
        for h in range(heads_cols // head):
            at = slice(h * head, (h + 1) * head)
            rows_q, rows_grad = query[at, cols], branch[at, cols]
            delta = jnp.sum(
                rows_grad.astype(f32) * attended[at, cols], axis=0, keepdims=True
            )
            logs = log_total[h, :, cols]

            def one(key, value, allowed):
                score = dims(key, rows_q, 1, 0) * score_scale
                prob = jnp.where(allowed, jnp.exp(score - logs), 0.0)
                moved = (prob * (dims(value, rows_grad, 1, 0) - delta)).astype(bf16)
                return prob.astype(bf16), moved

            prob_far, moved_far = one(key_far, value_far, seen)
            prob_near, moved_near = one(key_near, value_near, causal)
            query_back = (
                dims(key_far_t, moved_far, 1, 0) + dims(key_near_t, moved_near, 1, 0)
            ) * score_scale
            query_low[at, cols] = turn(query_back, cosine[:, cols], -sine[:, cols]).astype(bf16)
            far_back[:head] += dims(rows_q, moved_far, 1, 1) * score_scale
            far_back[head:] += dims(rows_grad, prob_far, 1, 1)
            own_back[:head, cols] += dims(rows_q, moved_near, 1, 1) * score_scale
            own_back[head:, cols] += dims(rows_grad, prob_near, 1, 1)
    for slot in range(PROMPTS):

        @pl.when(table[Z_IN] == slot)
        def _():
            own_back[...] += far_back[:, slot * tokens : (slot + 1) * tokens]

    for k in range(1, GROUP):
        sends[k - 1][...] = far_back[:, :tokens].astype(bf16)
        for slot in range(1, PROMPTS):

            @pl.when(table[Z_IN] == slot + k)
            def _():
                sends[k - 1][...] = far_back[:, slot * tokens : (slot + 1) * tokens].astype(bf16)


def query_parts_body(table, query_low, normed, attended_low, through, *parts):
    rows = query_low.shape[0]
    for k, part in enumerate(parts):
        b = table[ORDER + k]
        part[:rows] = dims(query_low[...], normed[b], 1, 0).astype(bf16)
        part[rows:] = dims(attended_low[...], through[b], 1, 0).astype(bf16)


def qkv_back_body(table, own_back, *refs):
    moved, refs = refs[: GROUP - 1], refs[GROUP - 1 :]
    query_low, normed, weights, cosine, sine = refs[:5]
    parts, (keep_first, keep_second, send) = refs[5:-3], refs[-3:]
    head = HEAD_DIM
    total = own_back[...]
    for part in moved:
        total = total + part[...].astype(f32)
    key = turn(total[:head], cosine[...], -sine[...])
    low = jnp.concatenate([key, total[head:]], axis=0)
    low_16 = low.astype(bf16)
    for k, part in enumerate(parts):
        part[...] = dims(low_16, normed[table[ORDER + k]], 1, 0).astype(bf16)
    flipped = jnp.concatenate([query_low[...].T, low.T.astype(bf16)], axis=1)
    model = weights.shape[2]
    keep_and_send(
        table,
        lambda b: dims(flipped, weights[b, :model], 1, 1),
        keep_first,
        keep_second,
        send,
    )


def rope_tables(positions, half):
    freq = rope_base ** (-(2.0 * jnp.arange(half, dtype=f32)) / (2.0 * half))
    angle = freq[:, None] * positions.astype(f32)[None, :]
    return (jnp.cos(angle), jnp.sin(angle))


def shards(
    layer_in,
    first_gain,
    query_weight,
    key_matrix,
    value_matrix,
    out_weight,
    second_gain,
    gate_weight,
    up_weight,
    down_weight,
    out_grad,
):
    place = Place()
    n, ny, y, z_in, table = place.n, place.ny, place.y, place.z_in, place.table
    lined = place.lined
    block, width = layer_in.shape
    tokens = 2 * block
    model_width = width * ny
    hidden_dev = gate_weight.shape[1] // 2
    query_rows = query_weight.shape[1] // 2
    kv_rows = key_matrix.shape[1]
    qkv_cols = query_rows + kv_rows
    full = (ny, tokens, width)
    wide = [(full[1:], f32), (full[1:], f32), ((2,) + full[1:], bf16)]

    def by_columns(*matrices):
        mine, other = zip(*(part_of(y, m, 1) for m in matrices))
        got = place.swap_y(jnp.concatenate(other, axis=1))
        return jnp.concatenate(pair(y, jnp.concatenate(mine, axis=1), got), axis=0)

    def by_rows(matrix):
        mine, other = part_of(y, matrix, 0)
        return jnp.concatenate(pair(y, mine, place.swap_y(other)), axis=1)

    def gathered(piece, rows_first):
        if lined:
            return gather_pieces(place, piece)
        return [gather_whole(place, piece, rows_first)]

    qkv_piece = by_columns(query_weight, key_matrix, value_matrix)
    out_piece = by_rows(out_weight)
    if lined:
        attend_pieces = gather_pieces(place, jnp.concatenate([qkv_piece, out_piece], axis=0))
    else:
        attend_pieces = [
            jnp.concatenate(
                [gather_whole(place, qkv_piece, True), gather_whole(place, out_piece, False)],
                axis=1,
            )
        ]
    gate_piece = by_columns(gate_weight, up_weight)
    down_piece = by_rows(down_weight)
    gate_pieces = gathered(after(gate_piece, attend_pieces[len(attend_pieces) // 2]), True)
    down_pieces = gathered(after(down_piece, gate_pieces[len(gate_pieces) // 2]), False)
    attend_shape = (ny, width + query_rows, width)
    gate_shape = (ny, width, 2 * hidden_dev)
    down_shape = (ny, hidden_dev, width)
    sems = pltpu.SemaphoreType.DMA((ny,))

    def spread(value):
        by_x = place.swap_x(value)
        four = [value, by_x, place.swap_y(value), place.swap_y(by_x)]
        return four + [place.swap_c(r) for r in four]

    gains = jnp.stack([first_gain, second_gain])
    two = [gains, place.swap_x(gains)]
    gains = two + [place.swap_c(g) for g in two]
    raw, normed_in, inverse_in, gain_in, gain_mid = call(
        rows_body,
        [(full, bf16), (full, bf16), ((tokens, 1), f32)] + [((ny, 1, width), f32)] * 2,
        table,
        spread(layer_in) + gains,
        earlier=[gate_piece, down_piece],
    )

    within = jnp.arange(block, dtype=jnp.int32)
    positions = jnp.minimum(place.offset, PROMPT_DEV)[:, None] * block + within[None, :]
    cosine, sine = rope_tables(positions.reshape(-1), HEAD_DIM // 2)
    query, own, attend_weights = call(
        qkv_body,
        [((query_rows, tokens), bf16), ((kv_rows, tokens), bf16), (attend_shape, bf16)],
        table,
        [normed_in, cosine, sine],
        [attend_pieces],
        [pltpu.VMEM((tokens, qkv_cols), f32), sems],
    )
    moved = [
        place.send_z(
            own,
            [(s, s + k) for s in range(n) if s % GROUP < PROMPTS and s % GROUP + k < GROUP],
        )
        for k in range(1, GROUP)
    ]
    (grad,) = call(grad_body, [(full, bf16)], table, spread(after(out_grad, normed_in)))
    attended, attended_low, log_total, far, keep_first, keep_second, send = call(
        attend_body,
        [
            ((query_rows, tokens), f32),
            ((query_rows, tokens), bf16),
            ((query_rows // HEAD_DIM, 1, tokens), f32),
            ((kv_rows, PROMPTS * tokens), bf16),
        ]
        + wide,
        table,
        [query, own] + moved + [attend_weights],
        earlier=[grad, gate_pieces[len(gate_pieces) // 4]],
    )
    summed = all_sum(place, (keep_first, keep_second), send, gate_pieces[len(gate_pieces) // 2])

    hidden, normed_mid, inverse_mid = call(
        hidden_body,
        [(full, f32), (full, bf16), ((tokens, 1), f32)],
        table,
        [raw] + summed + [gain_mid],
        earlier=[gate_pieces[-1], down_pieces[len(down_pieces) // 4]],
    )
    active, gate_slope, up_slope = call(
        gate_body,
        [((tokens, hidden_dev), bf16)] + [((tokens, hidden_dev), f32)] * 2,
        table,
        [normed_mid],
        [gate_pieces],
        [
            pltpu.VMEM(gate_shape, bf16),
            pltpu.VMEM((tokens, 2 * hidden_dev), f32),
            sems,
        ],
        earlier=[down_pieces[len(down_pieces) // 2]],
    )
    down_parts = call(down_parts_body, [(down_shape[1:], bf16)] * ny, table, [active, grad])
    change, keep_first, keep_second, send = call(
        gate_back_body,
        [((tokens, 2 * hidden_dev), bf16)] + wide,
        table,
        [grad, gate_slope, up_slope],
        [gate_pieces, down_pieces],
        [
            pltpu.VMEM(gate_shape, bf16),
            pltpu.VMEM(down_shape, bf16),
            pltpu.VMEM((tokens, hidden_dev), f32),
            sems,
            sems,
        ],
        earlier=[down_parts[0]],
    )
    summed = all_sum(place, (keep_first, keep_second), send)
    keep_first, keep_second, send = call(
        down_body,
        wide,
        table,
        [active],
        [down_pieces],
        [pltpu.VMEM(down_shape, bf16), sems],
        earlier=[summed[-1]],
    )
    hidden_own = own_block(place, hidden)
    layer_out = (hidden_own + own_sum(place, (keep_first, keep_second), send)).astype(bf16)
    down_grad = scatter_sum(place, down_parts, False)
    gate_parts = call(gate_parts_body, [(gate_shape[1:], bf16)] * ny, table, [normed_mid, change])
    gate_grad = scatter_sum(place, gate_parts, True)

    through, pull, query_low, own_back, *sends = call(
        attend_back_body,
        [
            (full, bf16),
            ((tokens, 1), f32),
            ((query_rows, tokens), bf16),
            ((kv_rows, tokens), f32),
        ]
        + [((kv_rows, tokens), bf16)] * (GROUP - 1),
        table,
        [hidden, inverse_mid]
        + summed
        + [
            grad,
            gain_mid,
            attend_weights,
            query,
            own,
            far,
            attended,
            log_total,
            cosine,
            sine,
        ],
        scratch=[pltpu.VMEM((kv_rows, PROMPTS * tokens), f32), pltpu.VMEM(full, f32)],
    )
    inverse_own, _ = part_of(y, inverse_mid, 0)
    pull_own, _ = part_of(y, pull, 0)
    mid_own = jnp.where(place.x == 0, summed[0], summed[1])
    mid_own = part_of(y, mid_own, 0)[0].astype(f32)
    through_own = (
        out_grad.astype(f32)
        + inverse_own * mid_own * second_gain[None, :]
        - hidden_own * pull_own
    )
    second_term = jnp.sum(mid_own * hidden_own * inverse_own, axis=0)

    query_parts = call(
        query_parts_body,
        [((2 * query_rows, width), bf16)] * ny,
        table,
        [query_low, normed_in, attended_low, through],
    )
    query_grad = scatter_sum(place, query_parts, False)

    moved = [
        place.send_z(
            sends[k - 1],
            [(s, s - k) for s in range(n) if 0 <= s % GROUP - k < PROMPTS],
        )
        for k in range(1, GROUP)
    ]
    *kv_parts, keep_first, keep_second, send = call(
        qkv_back_body,
        [((kv_rows, width), bf16)] * ny + wide,
        table,
        [own_back] + moved + [query_low, normed_in, attend_weights, cosine, sine],
    )
    kv_grad = scatter_sum(place, kv_parts, False)
    first_own = own_sum(place, (keep_first, keep_second), send)
    input_own = layer_in.astype(f32)
    inverse_own, _ = part_of(y, inverse_in, 0)
    scaled = first_own * first_gain[None, :]
    inner = jnp.sum(scaled * input_own, axis=1, keepdims=True)
    inner = inner + place.swap_c(inner)
    inner = inner + place.swap_x(inner)
    in_grad = (
        through_own + inverse_own * scaled - input_own * (inverse_own**3 * inner / model_width)
    )
    first_term = jnp.sum(first_own * input_own * inverse_own, axis=0)
    terms = jnp.stack([first_term, second_term])
    bit = 1
    while bit < place.nx:
        terms = terms + place.swap_gx(terms, bit)
        bit *= 2

    def joined(summed_part, axis):
        mine, other = part_of(y, summed_part, axis)
        return pair(y, mine, place.swap_y(other.astype(bf16)).astype(f32))

    gate_low, gate_high = joined(gate_grad, 0)
    down_grad = jnp.concatenate(joined(down_grad, 1), axis=0)
    query_low, query_high = joined(query_grad, 1)
    kv_low, kv_high = joined(kv_grad, 1)

    def stacked(low, high, start, stop):
        return jnp.concatenate([low[start:stop], high[start:stop]], axis=0)

    half_kv = kv_rows // 2
    return (
        layer_out,
        in_grad,
        terms[0],
        stacked(query_low, query_high, 0, query_rows).T,
        stacked(kv_low, kv_high, 0, half_kv).T,
        stacked(kv_low, kv_high, half_kv, kv_rows).T,
        stacked(query_low, query_high, query_rows, 2 * query_rows),
        terms[1],
        jnp.concatenate([gate_low[:, :hidden_dev], gate_high[:, :hidden_dev]], axis=1),
        jnp.concatenate([gate_low[:, hidden_dev:], gate_high[:, hidden_dev:]], axis=1),
        down_grad,
    )


def solution(mesh):
    rows, cols, gain = P("gx", "gy"), P("gy", "gx"), P("gy")
    return jax.shard_map(
        shards,
        mesh=mesh,
        in_specs=(rows, gain, rows, rows, rows, cols, gain, rows, rows, cols, rows),
        out_specs=(rows, rows, gain, rows, rows, rows, cols, gain, rows, rows, cols),
        check_vma=False,
    )
```

```python
from functools import partial

import jax
import jax.numpy as jnp
from jax import lax
from jax.experimental import pallas as pl
from jax.experimental.pallas import tpu as pltpu
from jax.sharding import PartitionSpec as P

HEAD_DIM = 96
PROMPT_DEV = 4
CONT_DEV = 4
GROUP = (PROMPT_DEV + CONT_DEV) // 2
PROMPTS = PROMPT_DEV // 2

eps = 1e-05
neg_big = -1e30
rope_base = 100000.0
score_scale = HEAD_DIM ** (-0.5)
f32 = jnp.float32
bf16 = jnp.bfloat16


def dims(left, right, left_axis, right_axis):
    return lax.dot_general(
        left, right, (((left_axis,), (right_axis,)), ((), ())), preferred_element_type=f32
    )


class Place:
    def __init__(self):
        self.nx = lax.axis_size("gx")
        self.ny = lax.axis_size("gy")
        assert self.ny == 4 and self.nx % (PROMPT_DEV + CONT_DEV) == 0
        self.n = self.nx // 2
        self.gx = lax.axis_index("gx")
        self.gy = lax.axis_index("gy")
        self.z, self.y = self.gx // 2, self.gx % 2
        self.x, self.c = self.gy // 2, self.gy % 2
        self.z_in = self.z % GROUP
        offset = 2 * self.z_in + jnp.arange(2, dtype=jnp.int32)
        self.offset = offset
        self.lined = self.n == self.ny
        blocks = jnp.arange(self.ny, dtype=jnp.int32)
        first = jnp.stack([self.z, self.y, self.x, self.c, self.z_in]).astype(jnp.int32)
        self.table = jnp.concatenate(
            [first, jnp.minimum(offset, PROMPT_DEV), blocks ^ self.z if self.lined else blocks]
        )

    def swap_gx(self, value, bit):
        return lax.ppermute(value, "gx", [(i, i ^ bit) for i in range(self.nx)])

    def swap_y(self, value):
        return self.swap_gx(value, 1)

    def swap_x(self, value):
        return lax.ppermute(value, "gy", [(i, i ^ 2) for i in range(self.ny)])

    def swap_c(self, value):
        return lax.ppermute(value, "gy", [(i, i ^ 1) for i in range(self.ny)])

    def send_z(self, value, moves):
        pairs = [(2 * s + y, 2 * t + y) for s, t in moves for y in range(2)]
        return lax.ppermute(value, "gx", pairs)

    def by_y(self):
        return [[2 * z + y for z in range(self.n)] for y in range(2)]


def pair(flag, mine, other):
    return jnp.where(flag == 0, mine, other), jnp.where(flag == 0, other, mine)


def part_of(flag, whole, axis):
    low, high = jnp.split(whole, 2, axis)
    return jnp.where(flag == 0, low, high), jnp.where(flag == 0, high, low)


def after(value, *earlier):
    return lax.optimization_barrier((value,) + earlier)[0]


NEAR = [(0, 1), (1, 0), (2, 3), (3, 2)]
SECOND = [(0, 2), (1, 3), (2, 0), (3, 1)]
MIDDLE = [(1, 2), (2, 1)]
INWARD = [(0, 1), (3, 2)]
OUTWARD = [(1, 0), (2, 3)]


def gather_pieces(place, piece):
    near = place.send_z(piece, NEAR)
    second = place.send_z(piece, SECOND)
    middle = place.send_z(piece, MIDDLE)
    return [piece, near, second, middle, place.send_z(second, OUTWARD)]


def gather_whole(place, piece):
    every = lax.all_gather(piece, "gx", axis_index_groups=place.by_y())
    inner = place.n // place.ny
    if inner == 1:
        return every
    rows, cols = piece.shape
    every = every.reshape(place.ny, inner, rows, cols)
    return jnp.swapaxes(every, 1, 2).reshape(place.ny, rows, inner * cols)


def scatter_whole(place, parts):
    inner = place.n // place.ny
    if inner > 1:
        count, rows, cols = parts.shape
        parts = jnp.swapaxes(parts.reshape(count, rows, inner, cols // inner), 1, 2)
        parts = parts.reshape(place.n, rows, cols // inner)
    return lax.psum_scatter(parts, "gx", axis_index_groups=place.by_y())


def scatter_sum(place, parts):
    if not place.lined:
        return scatter_whole(place, jnp.stack(parts)).astype(f32)
    own, near, second, third = parts
    far = place.send_z(third, INWARD)
    near = place.send_z(near, NEAR)
    middle = place.send_z(third, MIDDLE)
    second = place.send_z((second.astype(f32) + far.astype(f32)).astype(bf16), SECOND)
    return own.astype(f32) + near.astype(f32) + middle.astype(f32) + second.astype(f32)


def all_sum(place, keep, send):
    got = place.swap_c(send)
    first, second = keep[0] + got[0].astype(f32), keep[1] + got[1].astype(f32)
    first_got = place.swap_x(first.astype(bf16))
    second_got = place.swap_y(second.astype(bf16))
    first, second = first + first_got.astype(f32), second + second_got.astype(f32)
    first_low, second_low = first.astype(bf16), second.astype(bf16)
    first_got = place.swap_y(first_low)
    second_got = place.swap_x(second_low)
    own = [
        (first + first_got.astype(f32)).astype(bf16),
        (second + second_got.astype(f32)).astype(bf16),
    ]
    return own + [place.swap_c(part) for part in own]


def own_sum(place, keep, send):
    got = place.swap_c(send)
    first, second = keep[0] + got[0].astype(f32), keep[1] + got[1].astype(f32)
    mine, other = jnp.where(place.x == 0, first, second), jnp.where(place.x == 0, second, first)
    mine = mine + place.swap_x(other.astype(bf16)).astype(f32)
    mine, other = part_of(place.y, mine, 0)
    return mine + place.swap_y(other.astype(bf16)).astype(f32)


def own_block(place, blocks):
    rows = blocks.shape[1] // 2
    return lax.dynamic_slice(
        blocks, (place.gy, place.y * rows, 0), (1, rows, blocks.shape[2])
    )[0]


Z, Y, X, C, Z_IN, COUNT = range(6)
ORDER = COUNT + 2


def call(body, outs, table, operands, pieces=(), scratch=(), earlier=(), limit=24):
    lengths = [len(p) for p in pieces]
    flat = [a for p in pieces for a in p] + list(earlier)
    vmem = pl.BlockSpec(memory_space=pltpu.VMEM)

    def kernel(table_ref, *refs):
        plain, rest = refs[: len(operands)], refs[len(operands) :]
        lists = []
        for length in lengths:
            lists.append(rest[:length])
            rest = rest[length:]
        rest = rest[len(earlier) :]
        body(table_ref, *plain, *lists, *rest)

    return pl.pallas_call(
        kernel,
        out_shape=[jax.ShapeDtypeStruct(shape, dtype) for shape, dtype in outs],
        in_specs=[pl.BlockSpec(memory_space=pltpu.SMEM)]
        + [vmem] * len(operands)
        + [pl.BlockSpec(memory_space=pl.ANY)] * len(flat),
        out_specs=[vmem] * len(outs),
        scratch_shapes=list(scratch),
        compiler_params=pltpu.CompilerParams(vmem_limit_bytes=limit << 20),
    )(table, *operands, *flat)


def start_pieces(table, pieces, whole, sems):
    if len(pieces) == 1:
        copy = pltpu.make_async_copy(pieces[0], whole, sems.at[0])
        copy.start()
        return copy.wait
    z = table[Z]
    own, near, second, middle, end = pieces
    inside = jnp.logical_or(z == 1, z == 2)
    pltpu.make_async_copy(own, whole.at[table[ORDER]], sems.at[0]).start()
    pltpu.make_async_copy(near, whole.at[table[ORDER + 1]], sems.at[1]).start()
    pltpu.make_async_copy(second, whole.at[table[ORDER + 2]], sems.at[2]).start()

    @pl.when(inside)
    def _():
        pltpu.make_async_copy(middle, whole.at[table[ORDER + 3]], sems.at[3]).start()

    @pl.when(jnp.logical_not(inside))
    def _():
        pltpu.make_async_copy(end, whole.at[table[ORDER + 3]], sems.at[3]).start()

    def wait():
        for k in range(4):
            pltpu.make_async_copy(own, whole.at[0], sems.at[k]).wait()

    return wait


def keep_and_send(table, block_of, keep_first, keep_second, send):
    core = table[C]
    keep_first[...] = block_of(core)
    keep_second[...] = block_of(2 + core)

    def one(i, _):
        send[i] = block_of(2 * i + 1 - core).astype(bf16)
        return 0

    lax.fori_loop(0, 2, one, 0)


def place_rows(table, pieces, whole):
    x, y, c = table[X], table[Y], table[C]
    tokens = pieces[0].shape[0]
    for dc in range(2):
        for dx in range(2):
            block = 2 * (x + dx - 2 * x * dx) + c + dc - 2 * c * dc
            for dy in range(2):
                at = pl.ds(pl.multiple_of(tokens * (y + dy - 2 * y * dy), tokens), tokens)
                whole[block, at, :] = pieces[4 * dc + 2 * dy + dx][...]


def grad_body(table, *refs):
    place_rows(table, refs[:8], refs[8])


def rows_body(table, *refs):
    rows, gains = refs[:8], refs[8:12]
    raw, normed, inverse, gain_first, gain_second = refs[12:]
    place_rows(table, rows, raw)
    x, c = table[X], table[C]
    for dc in range(2):
        for dx in range(2):
            block = 2 * (x + dx - 2 * x * dx) + c + dc - 2 * c * dc
            gain = gains[2 * dc + dx][...]
            gain_first[block] = gain[0:1]
            gain_second[block] = gain[1:2]

    def square(b, total):
        values = raw[b].astype(f32)
        return total + jnp.sum(values * values, axis=1, keepdims=True)

    count = raw.shape[0]
    total = lax.fori_loop(0, count, square, jnp.zeros((raw.shape[1], 1), f32))
    scale = lax.rsqrt(total / (count * raw.shape[2]) + eps)
    inverse[...] = scale

    def norm(b, _):
        normed[b] = (raw[b].astype(f32) * scale * gain_first[b]).astype(bf16)
        return 0

    lax.fori_loop(0, count, norm, 0)


def turn(values, cosine, sine):
    half = values.shape[0] // 2
    first, second = values[:half], values[half:]
    return jnp.concatenate(
        [first * cosine - second * sine, second * cosine + first * sine], axis=0
    )


def qkv_body(table, normed, cosine, sine, pieces, query, own, weights, acc, sems):
    start_pieces(table, pieces, weights, sems)()
    count = acc.shape[0]
    acc[...] = jnp.zeros_like(acc)

    def one(b, _):
        acc[...] += dims(weights[b, :count], normed[b], 1, 1)
        return 0

    lax.fori_loop(0, normed.shape[0], one, 0)
    flipped = acc[...]
    head = HEAD_DIM
    heads = query.shape[0] // head
    cos, sin = cosine[...], sine[...]
    for h in range(heads):
        at = slice(h * head, (h + 1) * head)
        query[at] = turn(flipped[at], cos, sin).astype(bf16)
    at = slice(heads * head, (heads + 1) * head)
    own[:head] = turn(flipped[at], cos, sin).astype(bf16)
    own[head:] = flipped[(heads + 1) * head :].astype(bf16)


def attend_body(
    table, query, own, *refs
):
    moved = refs[: GROUP - 1]
    weights, attended, attended_low, log_total, far, keep_first, keep_second, send = refs[
        GROUP - 1 :
    ]
    tokens = own.shape[1]
    for place in range(GROUP):

        @pl.when(table[Z_IN] == place)
        def _():
            for slot in range(PROMPTS):
                k = place - slot
                far[:, slot * tokens : (slot + 1) * tokens] = (
                    moved[k - 1][...] if k > 0 else own[...]
                )

    head = HEAD_DIM
    block = tokens // 2
    key_far, value_far = far[:head].T, far[head:]
    key_own = own[:head].T
    total = far.shape[1]
    near_row = lax.broadcasted_iota(jnp.int32, (block, block), 0)
    near_col = lax.broadcasted_iota(jnp.int32, (block, block), 1)
    causal = near_row <= near_col
    row = lax.broadcasted_iota(jnp.int32, (total, block), 0)
    for part in range(2):
        cols = slice(part * block, (part + 1) * block)
        key_near, value_near = key_own[cols], own[head:, cols]
        seen = row < table[COUNT + part] * block

        def one(h, _):
            at = pl.ds(pl.multiple_of(h * head, head), head)
            rows = query[at, cols]
            score_far = jnp.where(seen, dims(key_far, rows, 1, 0) * score_scale, neg_big)
            score_near = jnp.where(causal, dims(key_near, rows, 1, 0) * score_scale, neg_big)
            top = jnp.maximum(
                jnp.max(score_far, axis=0, keepdims=True), jnp.max(score_near, axis=0, keepdims=True)
            )
            weight_far = jnp.exp(score_far - top)
            weight_near = jnp.exp(score_near - top)
            weight = jnp.sum(weight_far, axis=0, keepdims=True) + jnp.sum(
                weight_near, axis=0, keepdims=True
            )
            out = dims(value_far, weight_far.astype(bf16), 1, 0) + dims(
                value_near, weight_near.astype(bf16), 1, 0
            )
            attended[at, cols] = out / weight
            log_total[h, :, cols] = top + jnp.log(weight)
            return 0

        lax.fori_loop(0, query.shape[0] // head, one, 0)
    values = attended[...]
    attended_low[...] = values.astype(bf16)
    flipped = values.T.astype(bf16)
    first = weights.shape[1] - query.shape[0]
    keep_and_send(
        table,
        lambda b: dims(flipped, weights[b, first:], 1, 0),
        keep_first,
        keep_second,
        send,
    )


def hidden_body(
    table, raw, own_first, own_second, other_first, other_second, gain, hidden, normed, inverse
):
    core = table[C]
    summed, other = (own_first, own_second), (other_first, other_second)
    for i in range(2):
        b = 2 * i + core
        hidden[b] = raw[b].astype(f32) + summed[i][...].astype(f32)
        b = 2 * i + 1 - core
        hidden[b] = raw[b].astype(f32) + other[i][...].astype(f32)

    def square(b, total):
        values = hidden[b]
        return total + jnp.sum(values * values, axis=1, keepdims=True)

    count = raw.shape[0]
    total = lax.fori_loop(0, count, square, jnp.zeros((raw.shape[1], 1), f32))
    scale = lax.rsqrt(total / (count * raw.shape[2]) + eps)
    inverse[...] = scale

    def norm(b, _):
        normed[b] = (hidden[b] * scale * gain[b]).astype(bf16)
        return 0

    lax.fori_loop(0, count, norm, 0)


def start_blocks(source, whole, sems):
    def copy(b):
        return pltpu.make_async_copy(source.at[b], whole.at[b], sems.at[b])

    for b in range(source.shape[0]):
        copy(b).start()
    return lambda b: copy(b).wait()


def gate_body(table, normed, pieces, active, gate_slope, up_slope, weights, acc, sems):
    wait = start_blocks(pieces[0], weights, sems)
    width = acc.shape[1]
    acc[...] = jnp.zeros_like(acc)

    def one(b, _):
        wait(b)
        acc[...] += dims(normed[b], weights[b, :width], 1, 1)
        return 0

    lax.fori_loop(0, normed.shape[0], one, 0)
    half = width // 2
    rows = acc.shape[0] // 4

    def part(i, _):
        at = pl.ds(pl.multiple_of(i * rows, rows), rows)
        gate, up = acc[at, :half], acc[at, half:]
        sigmoid = jax.nn.sigmoid(gate)
        active[at] = (gate * sigmoid * up).astype(bf16)
        gate_slope[at] = up * sigmoid * (1.0 + gate * (1.0 - sigmoid))
        up_slope[at] = gate * sigmoid
        return 0

    lax.fori_loop(0, 4, part, 0)


def gate_back_body(
    table,
    grad,
    gate_slope,
    up_slope,
    pieces,
    change,
    keep_first,
    keep_second,
    send,
    weights,
    acc,
    sems,
):
    wait = start_blocks(pieces[0], weights, sems)
    half = acc.shape[1]
    acc[...] = jnp.zeros_like(acc)

    def one(b, _):
        wait(b)
        acc[...] += dims(grad[b], weights[b, 2 * half :], 1, 1)
        return 0

    lax.fori_loop(0, grad.shape[0], one, 0)
    change[:, :half] = (acc[...] * gate_slope[...]).astype(bf16)
    change[:, half:] = (acc[...] * up_slope[...]).astype(bf16)
    values = change[...]
    keep_and_send(
        table, lambda b: dims(values, weights[b, : 2 * half], 1, 0), keep_first, keep_second, send
    )


def forward_parts_body(table, active, grad, normed, change, parts):
    width = change.shape[1]
    flipped = change[...].T
    flipped_active = active[...].T

    def one(b, _):
        parts[b, :width] = dims(flipped, normed[b], 1, 0).astype(bf16)
        parts[b, width:] = dims(flipped_active, grad[b], 1, 0).astype(bf16)
        return 0

    lax.fori_loop(0, grad.shape[0], one, 0)


def down_body(table, active, pieces, keep_first, keep_second, send, weights, sems):
    wait = start_blocks(pieces[0], weights, sems)
    for b in range(weights.shape[0]):
        wait(b)
    values = active[...]
    first = weights.shape[1] - values.shape[1]
    keep_and_send(
        table, lambda b: dims(values, weights[b, first:], 1, 0), keep_first, keep_second, send
    )


def attend_back_body(
    table,
    hidden,
    inverse,
    own_first,
    own_second,
    other_first,
    other_second,
    grad,
    gain,
    weights,
    query,
    own,
    far,
    attended,
    log_total,
    cosine,
    sine,
    through,
    pull,
    query_low,
    own_back,
    *rest,
):
    sends, far_back, change = rest[: GROUP - 1], rest[-2], rest[-1]
    core = table[C]
    count, tokens, model = hidden.shape
    for i, (mine, theirs) in enumerate(((own_first, other_first), (own_second, other_second))):
        change[2 * i + core] = mine[...].astype(f32) * gain[2 * i + core]
        change[2 * i + 1 - core] = theirs[...].astype(f32) * gain[2 * i + 1 - core]

    def product(b, total):
        return total + jnp.sum(change[b] * hidden[b], axis=1, keepdims=True)

    inner = lax.fori_loop(0, count, product, jnp.zeros((tokens, 1), f32))
    scale = inverse[...]
    back = scale * scale * scale * inner / (count * model)
    pull[...] = back

    def rows(b, total):
        values = grad[b].astype(f32) + scale * change[b] - hidden[b] * back
        low = values.astype(bf16)
        through[b] = low
        return total + dims(low, weights[b, first:], 1, 1)

    heads_cols = query.shape[0]
    first = weights.shape[1] - heads_cols
    branch = lax.fori_loop(0, count, rows, jnp.zeros((tokens, heads_cols), f32))
    branch = branch.T.astype(bf16)

    head = HEAD_DIM
    block = tokens // 2
    key_far_t = far[:head]
    key_far, value_far = key_far_t.T, far[head:].T
    key_own, value_own = own[:head].T, own[head:].T
    total = far.shape[1]
    near_row = lax.broadcasted_iota(jnp.int32, (block, block), 0)
    near_col = lax.broadcasted_iota(jnp.int32, (block, block), 1)
    causal = near_row <= near_col
    row = lax.broadcasted_iota(jnp.int32, (total, block), 0)
    far_back[...] = jnp.zeros_like(far_back)
    own_back[...] = jnp.zeros_like(own_back)
    for part in range(2):
        cols = slice(part * block, (part + 1) * block)
        key_near, value_near = key_own[cols], value_own[cols]
        key_near_t = own[:head, cols]
        seen = row < table[COUNT + part] * block
        for h in range(heads_cols // head):
            at = slice(h * head, (h + 1) * head)
            rows_q, rows_grad = query[at, cols], branch[at, cols]
            delta = jnp.sum(
                rows_grad.astype(f32) * attended[at, cols], axis=0, keepdims=True
            )
            logs = log_total[h, :, cols]

            def one(key, value, allowed):
                score = dims(key, rows_q, 1, 0) * score_scale
                prob = jnp.where(allowed, jnp.exp(score - logs), 0.0)
                moved = (prob * (dims(value, rows_grad, 1, 0) - delta)).astype(bf16)
                return prob.astype(bf16), moved

            prob_far, moved_far = one(key_far, value_far, seen)
            prob_near, moved_near = one(key_near, value_near, causal)
            query_back = (
                dims(key_far_t, moved_far, 1, 0) + dims(key_near_t, moved_near, 1, 0)
            ) * score_scale
            query_low[at, cols] = turn(query_back, cosine[:, cols], -sine[:, cols]).astype(bf16)
            far_back[:head] += dims(rows_q, moved_far, 1, 1) * score_scale
            far_back[head:] += dims(rows_grad, prob_far, 1, 1)
            own_back[:head, cols] += dims(rows_q, moved_near, 1, 1) * score_scale
            own_back[head:, cols] += dims(rows_grad, prob_near, 1, 1)
    for slot in range(PROMPTS):

        @pl.when(table[Z_IN] == slot)
        def _():
            own_back[...] += far_back[:, slot * tokens : (slot + 1) * tokens]

    for k in range(1, GROUP):
        sends[k - 1][...] = far_back[:, :tokens].astype(bf16)
        for slot in range(1, PROMPTS):

            @pl.when(table[Z_IN] == slot + k)
            def _():
                sends[k - 1][...] = far_back[:, slot * tokens : (slot + 1) * tokens].astype(bf16)


def query_parts_body(table, query_low, normed, attended_low, through, *parts):
    rows = query_low.shape[0]
    for k, part in enumerate(parts):
        b = table[ORDER + k]
        part[:rows] = dims(query_low[...], normed[b], 1, 0).astype(bf16)
        part[rows:] = dims(attended_low[...], through[b], 1, 0).astype(bf16)


def qkv_back_body(table, own_back, *refs):
    moved, refs = refs[: GROUP - 1], refs[GROUP - 1 :]
    query_low, normed, weights, cosine, sine = refs[:5]
    parts, (keep_first, keep_second, send) = refs[5:-3], refs[-3:]
    head = HEAD_DIM
    total = own_back[...]
    for part in moved:
        total = total + part[...].astype(f32)
    key = turn(total[:head], cosine[...], -sine[...])
    low = jnp.concatenate([key, total[head:]], axis=0)
    low_16 = low.astype(bf16)
    for k, part in enumerate(parts):
        part[...] = dims(low_16, normed[table[ORDER + k]], 1, 0).astype(bf16)
    flipped = jnp.concatenate([query_low[...].T, low.T.astype(bf16)], axis=1)
    width = flipped.shape[1]
    keep_and_send(
        table,
        lambda b: dims(flipped, weights[b, :width], 1, 0),
        keep_first,
        keep_second,
        send,
    )


def halves_of(table, whole):
    half = whole.shape[0] // 2
    low, high = whole[:half], whole[half:]
    flag = table[Y] == 0
    return jnp.where(flag, low, high), jnp.where(flag, high, low)


def split_body(table, *refs):
    count = len(refs) - 2
    mine_ref, other_ref = refs[-2:]
    at = 0
    for i, ref in enumerate(refs[:count]):
        whole = ref[...]
        if i < count - 1:
            whole = whole.T
        mine, other = halves_of(table, whole)
        rows = mine.shape[0]
        mine_ref[at : at + rows] = mine
        other_ref[at : at + rows] = other
        at += rows


def join_body(table, mine, got, *outs, last_turned):
    flag = table[Y] == 0
    at = 0
    for i, out in enumerate(outs):
        turned = last_turned or i < len(outs) - 1
        rows = out.shape[1 if turned else 0] // 2
        parts = mine[at : at + rows].astype(f32), got[at : at + rows].astype(f32)
        at += rows
        low, high = jnp.where(flag, parts[0], parts[1]), jnp.where(flag, parts[1], parts[0])
        if turned:
            out[:, :rows] = low.T
            out[:, rows:] = high.T
        else:
            out[:rows] = low
            out[rows:] = high


def rope_tables(positions, half):
    freq = rope_base ** (-(2.0 * jnp.arange(half, dtype=f32)) / (2.0 * half))
    angle = freq[:, None] * positions.astype(f32)[None, :]
    return (jnp.cos(angle), jnp.sin(angle))


def shards(
    layer_in,
    first_gain,
    query_weight,
    key_matrix,
    value_matrix,
    out_weight,
    second_gain,
    gate_weight,
    up_weight,
    down_weight,
    out_grad,
):
    place = Place()
    n, ny, y, z_in, table = place.n, place.ny, place.y, place.z_in, place.table
    lined = place.lined
    block, width = layer_in.shape
    tokens = 2 * block
    model_width = width * ny
    hidden_dev = gate_weight.shape[1] // 2
    query_rows = query_weight.shape[1] // 2
    kv_rows = key_matrix.shape[1]
    qkv_cols = query_rows + kv_rows
    full = (ny, tokens, width)
    wide = [(full[1:], f32), (full[1:], f32), ((2,) + full[1:], bf16)]

    def pieces_of(*matrices):
        rows = sum(max(m.shape) for m in matrices) // 2
        cols = min(matrices[0].shape)
        mine, other = call(split_body, [((rows, cols), bf16)] * 2, table, matrices)
        return jnp.concatenate(pair(y, mine, place.swap_y(other)), axis=1)

    attend_piece = pieces_of(query_weight, key_matrix, value_matrix, out_weight)
    forward_piece = pieces_of(gate_weight, up_weight, down_weight)
    forward_pieces = [gather_whole(place, forward_piece)]
    if lined:
        attend_pieces = gather_pieces(place, attend_piece)
    else:
        attend_pieces = [gather_whole(place, attend_piece)]
    attend_shape = (ny, qkv_cols + query_rows, width)
    forward_shape = (ny, 3 * hidden_dev, width)
    sems = pltpu.SemaphoreType.DMA((ny,))

    def spread(value):
        by_x = place.swap_x(value)
        four = [value, by_x, place.swap_y(value), place.swap_y(by_x)]
        return four + [place.swap_c(r) for r in four]

    gains = jnp.stack([first_gain, second_gain])
    two = [gains, place.swap_x(gains)]
    gains = two + [place.swap_c(g) for g in two]
    raw, normed_in, inverse_in, gain_in, gain_mid = call(
        rows_body,
        [(full, bf16), (full, bf16), ((tokens, 1), f32)] + [((ny, 1, width), f32)] * 2,
        table,
        spread(layer_in) + gains,
        earlier=[forward_piece],
    )

    within = jnp.arange(block, dtype=jnp.int32)
    positions = jnp.minimum(place.offset, PROMPT_DEV)[:, None] * block + within[None, :]
    cosine, sine = rope_tables(positions.reshape(-1), HEAD_DIM // 2)
    query, own, attend_weights = call(
        qkv_body,
        [((query_rows, tokens), bf16), ((kv_rows, tokens), bf16), (attend_shape, bf16)],
        table,
        [normed_in, cosine, sine],
        [attend_pieces],
        [pltpu.VMEM((qkv_cols, tokens), f32), sems],
    )
    moved = [
        place.send_z(
            own,
            [(s, s + k) for s in range(n) if s % GROUP < PROMPTS and s % GROUP + k < GROUP],
        )
        for k in range(1, GROUP)
    ]
    (grad,) = call(grad_body, [(full, bf16)], table, spread(after(out_grad, normed_in)))
    attended, attended_low, log_total, far, keep_first, keep_second, send = call(
        attend_body,
        [
            ((query_rows, tokens), f32),
            ((query_rows, tokens), bf16),
            ((query_rows // HEAD_DIM, 1, tokens), f32),
            ((kv_rows, PROMPTS * tokens), bf16),
        ]
        + wide,
        table,
        [query, own] + moved + [attend_weights],
        earlier=[grad],
    )
    summed = all_sum(place, (keep_first, keep_second), send)

    hidden, normed_mid, inverse_mid = call(
        hidden_body,
        [(full, f32), (full, bf16), ((tokens, 1), f32)],
        table,
        [raw] + summed + [gain_mid],
    )
    active, gate_slope, up_slope = call(
        gate_body,
        [((tokens, hidden_dev), bf16)] + [((tokens, hidden_dev), f32)] * 2,
        table,
        [normed_mid],
        [forward_pieces],
        [
            pltpu.VMEM(forward_shape, bf16),
            pltpu.VMEM((tokens, 2 * hidden_dev), f32),
            sems,
        ],
    )
    change, keep_first, keep_second, send = call(
        gate_back_body,
        [((tokens, 2 * hidden_dev), bf16)] + wide,
        table,
        [grad, gate_slope, up_slope],
        [forward_pieces],
        [pltpu.VMEM(forward_shape, bf16), pltpu.VMEM((tokens, hidden_dev), f32), sems],
    )
    summed = all_sum(place, (keep_first, keep_second), send)
    (forward_parts,) = call(
        forward_parts_body, [(forward_shape, bf16)], table, [active, grad, normed_mid, change]
    )
    forward_grad = scatter_whole(place, forward_parts)
    keep_first, keep_second, send = call(
        down_body,
        wide,
        table,
        [active],
        [forward_pieces],
        [pltpu.VMEM(forward_shape, bf16), sems],
        earlier=[summed[-1]],
    )
    hidden_own = own_block(place, hidden)
    layer_out = (hidden_own + own_sum(place, (keep_first, keep_second), send)).astype(bf16)
    through, pull, query_low, own_back, *sends = call(
        attend_back_body,
        [
            (full, bf16),
            ((tokens, 1), f32),
            ((query_rows, tokens), bf16),
            ((kv_rows, tokens), f32),
        ]
        + [((kv_rows, tokens), bf16)] * (GROUP - 1),
        table,
        [hidden, inverse_mid]
        + summed
        + [
            grad,
            gain_mid,
            attend_weights,
            query,
            own,
            far,
            attended,
            log_total,
            cosine,
            sine,
        ],
        scratch=[pltpu.VMEM((kv_rows, PROMPTS * tokens), f32), pltpu.VMEM(full, f32)],
    )
    inverse_own, _ = part_of(y, inverse_mid, 0)
    pull_own, _ = part_of(y, pull, 0)
    mid_own = jnp.where(place.x == 0, summed[0], summed[1])
    mid_own = part_of(y, mid_own, 0)[0].astype(f32)
    through_own = (
        out_grad.astype(f32)
        + inverse_own * mid_own * second_gain[None, :]
        - hidden_own * pull_own
    )
    second_term = jnp.sum(mid_own * hidden_own * inverse_own, axis=0)

    query_parts = call(
        query_parts_body,
        [((2 * query_rows, width), bf16)] * ny,
        table,
        [query_low, normed_in, attended_low, through],
    )
    query_grad = scatter_sum(place, query_parts)

    moved = [
        place.send_z(
            sends[k - 1],
            [(s, s - k) for s in range(n) if 0 <= s % GROUP - k < PROMPTS],
        )
        for k in range(1, GROUP)
    ]
    *kv_parts, keep_first, keep_second, send = call(
        qkv_back_body,
        [((kv_rows, width), bf16)] * ny + wide,
        table,
        [own_back] + moved + [query_low, normed_in, attend_weights, cosine, sine],
    )
    kv_grad = scatter_sum(place, kv_parts)
    first_own = own_sum(place, (keep_first, keep_second), send)
    input_own = layer_in.astype(f32)
    inverse_own, _ = part_of(y, inverse_in, 0)
    scaled = first_own * first_gain[None, :]
    inner = jnp.sum(scaled * input_own, axis=1, keepdims=True)
    inner = inner + place.swap_c(inner)
    inner = inner + place.swap_x(inner)
    in_grad = (
        through_own + inverse_own * scaled - input_own * (inverse_own**3 * inner / model_width)
    )
    first_term = jnp.sum(first_own * input_own * inverse_own, axis=0)
    terms = jnp.stack([first_term, second_term])
    bit = 1
    while bit < place.nx:
        terms = terms + place.swap_gx(terms, bit)
        bit *= 2

    def joined(summed_part, outs, last_turned=False):
        mine, other = part_of(y, summed_part, 1)
        got = place.swap_y(other.astype(bf16))
        return call(
            partial(join_body, last_turned=last_turned),
            [(m.shape, f32) for m in outs],
            table,
            [mine, got],
        )

    gate_grad, up_grad, down_grad = joined(forward_grad, (gate_weight, up_weight, down_weight))
    query_out, out_out = joined(query_grad, (query_weight, out_weight))
    key_out, value_out = joined(kv_grad, (key_matrix, value_matrix), True)
    return (
        layer_out,
        in_grad,
        terms[0],
        query_out,
        key_out,
        value_out,
        out_out,
        terms[1],
        gate_grad,
        up_grad,
        down_grad,
    )


def solution(mesh):
    rows, cols, gain = P("gx", "gy"), P("gy", "gx"), P("gy")
    return jax.shard_map(
        shards,
        mesh=mesh,
        in_specs=(rows, gain, rows, rows, rows, cols, gain, rows, rows, cols, rows),
        out_specs=(rows, rows, gain, rows, rows, rows, cols, gain, rows, rows, cols),
        check_vma=False,
    )
```

```python
import jax
import jax.numpy as jnp
from jax import lax
from jax.experimental import pallas as pl
from jax.experimental.pallas import tpu as pltpu
from jax.sharding import PartitionSpec as P

HEAD_DIM = 96
PROMPT_DEV = 4
CONT_DEV = 4
GROUP = (PROMPT_DEV + CONT_DEV) // 2
PROMPTS = PROMPT_DEV // 2

eps = 1e-05
neg_big = -1e30
rope_base = 100000.0
score_scale = HEAD_DIM ** (-0.5)
f32 = jnp.float32
bf16 = jnp.bfloat16


def dims(left, right, left_axis, right_axis):
    return lax.dot_general(
        left, right, (((left_axis,), (right_axis,)), ((), ())), preferred_element_type=f32
    )


class Place:
    def __init__(self):
        self.nx = lax.axis_size("gx")
        self.ny = lax.axis_size("gy")
        assert self.ny == 4 and self.nx % (PROMPT_DEV + CONT_DEV) == 0
        self.n = self.nx // 2
        self.gx = lax.axis_index("gx")
        self.gy = lax.axis_index("gy")
        self.z, self.y = self.gx // 2, self.gx % 2
        self.x, self.c = self.gy // 2, self.gy % 2
        self.z_in = self.z % GROUP
        offset = 2 * self.z_in + jnp.arange(2, dtype=jnp.int32)
        self.offset = offset
        self.lined = self.n == self.ny
        blocks = jnp.arange(self.ny, dtype=jnp.int32)
        first = jnp.stack([self.z, self.y, self.x, self.c, self.z_in]).astype(jnp.int32)
        self.table = jnp.concatenate(
            [first, jnp.minimum(offset, PROMPT_DEV), blocks ^ self.z if self.lined else blocks]
        )

    def swap_gx(self, value, bit):
        return lax.ppermute(value, "gx", [(i, i ^ bit) for i in range(self.nx)])

    def swap_y(self, value):
        return self.swap_gx(value, 1)

    def swap_x(self, value):
        return lax.ppermute(value, "gy", [(i, i ^ 2) for i in range(self.ny)])

    def swap_c(self, value):
        return lax.ppermute(value, "gy", [(i, i ^ 1) for i in range(self.ny)])

    def send_z(self, value, moves):
        pairs = [(2 * s + y, 2 * t + y) for s, t in moves for y in range(2)]
        return lax.ppermute(value, "gx", pairs)

    def by_y(self):
        return [[2 * z + y for z in range(self.n)] for y in range(2)]


def pair(flag, mine, other):
    return jnp.where(flag == 0, mine, other), jnp.where(flag == 0, other, mine)


def part_of(flag, whole, axis):
    low, high = jnp.split(whole, 2, axis)
    return jnp.where(flag == 0, low, high), jnp.where(flag == 0, high, low)


def after(value, *earlier):
    return lax.optimization_barrier((value,) + earlier)[0]


NEAR = [(0, 1), (1, 0), (2, 3), (3, 2)]
SECOND = [(0, 2), (1, 3), (2, 0), (3, 1)]
MIDDLE = [(1, 2), (2, 1)]
INWARD = [(0, 1), (3, 2)]
OUTWARD = [(1, 0), (2, 3)]


def gather_pieces(place, piece, late_middle=False):
    second = place.send_z(piece, SECOND)
    near = place.send_z(piece, NEAR)
    middle = place.send_z(after(piece, second) if late_middle else piece, MIDDLE)
    return [piece, near, second, middle, place.send_z(second, OUTWARD)]


def gather_whole(place, piece):
    every = lax.all_gather(piece, "gx", axis_index_groups=place.by_y())
    inner = place.n // place.ny
    if inner == 1:
        return every
    rows, cols = piece.shape
    every = every.reshape(place.ny, inner, rows, cols)
    return jnp.swapaxes(every, 1, 2).reshape(place.ny, rows, inner * cols)


def scatter_whole(place, parts):
    inner = place.n // place.ny
    if inner > 1:
        count, rows, cols = parts.shape
        parts = jnp.swapaxes(parts.reshape(count, rows, inner, cols // inner), 1, 2)
        parts = parts.reshape(place.n, rows, cols // inner)
    return lax.psum_scatter(parts, "gx", axis_index_groups=place.by_y())


def scatter_sum(place, parts, before_second, before_sum):
    if not place.lined:
        return scatter_whole(place, jnp.stack(parts)).astype(f32)
    own, near, second, third = parts
    far = place.send_z(third, INWARD)
    near = place.send_z(near, NEAR)
    middle = place.send_z(third, MIDDLE)
    second = after(second, *before_second)
    second = place.send_z((second.astype(f32) + far.astype(f32)).astype(bf16), SECOND)
    own = after(own, *before_sum)
    return own.astype(f32) + near.astype(f32) + middle.astype(f32) + second.astype(f32)


def all_sum(place, keep, send):
    got = place.swap_c(send)
    first, second = keep[0] + got[0].astype(f32), keep[1] + got[1].astype(f32)
    first_got = place.swap_x(first.astype(bf16))
    second_got = place.swap_y(second.astype(bf16))
    first, second = first + first_got.astype(f32), second + second_got.astype(f32)
    first_low, second_low = lax.optimization_barrier((first.astype(bf16), second.astype(bf16)))
    first_got = place.swap_y(first_low)
    second_got = place.swap_x(second_low)
    own = [
        (first + first_got.astype(f32)).astype(bf16),
        (second + second_got.astype(f32)).astype(bf16),
    ]
    return own + [place.swap_c(part) for part in own]


def own_sum(place, keep, send):
    got = place.swap_c(send)
    first, second = keep[0] + got[0].astype(f32), keep[1] + got[1].astype(f32)
    mine, other = jnp.where(place.x == 0, first, second), jnp.where(place.x == 0, second, first)
    mine = mine + place.swap_x(other.astype(bf16)).astype(f32)
    mine, other = part_of(place.y, mine, 0)
    return mine + place.swap_y(other.astype(bf16)).astype(f32)


def own_block(place, blocks):
    rows = blocks.shape[1] // 2
    return lax.dynamic_slice(
        blocks, (place.gy, place.y * rows, 0), (1, rows, blocks.shape[2])
    )[0]


Z, Y, X, C, Z_IN, COUNT = range(6)
ORDER = COUNT + 2


def call(body, outs, table, operands, pieces=(), scratch=(), earlier=(), limit=24):
    lengths = [len(p) for p in pieces]
    flat = [a for p in pieces for a in p] + list(earlier)
    vmem = pl.BlockSpec(memory_space=pltpu.VMEM)

    def kernel(table_ref, *refs):
        plain, rest = refs[: len(operands)], refs[len(operands) :]
        lists = []
        for length in lengths:
            lists.append(rest[:length])
            rest = rest[length:]
        rest = rest[len(earlier) :]
        body(table_ref, *plain, *lists, *rest)

    return pl.pallas_call(
        kernel,
        out_shape=[jax.ShapeDtypeStruct(shape, dtype) for shape, dtype in outs],
        in_specs=[pl.BlockSpec(memory_space=pltpu.SMEM)]
        + [vmem] * len(operands)
        + [pl.BlockSpec(memory_space=pl.ANY)] * len(flat),
        out_specs=[vmem] * len(outs),
        scratch_shapes=list(scratch),
        compiler_params=pltpu.CompilerParams(vmem_limit_bytes=limit << 20),
    )(table, *operands, *flat)


def start_pieces(table, pieces, whole, sems, rows=slice(None)):
    count = whole.shape[0]
    block = [table[ORDER + k] for k in range(count)]

    def copy(piece, k):
        source = piece.at[rows] if rows != slice(None) else piece
        return pltpu.make_async_copy(source, whole.at[block[k]], sems.at[k])

    if len(pieces) == 1:
        for k in range(count):
            copy(pieces[0].at[block[k]], k).start()
        return lambda k: copy(pieces[0].at[block[k]], k).wait()
    z = table[Z]
    own, near, second, middle, end = pieces
    for k, piece in enumerate((own, near, second)):
        copy(piece, k).start()
    inside = jnp.logical_or(z == 1, z == 2)

    @pl.when(inside)
    def _():
        copy(middle, 3).start()

    @pl.when(jnp.logical_not(inside))
    def _():
        copy(end, 3).start()

    return lambda k: copy(own, k).wait()


def keep_and_send(table, block_of, keep_first, keep_second, send):
    core = table[C]
    keep_first[...] = block_of(core)
    keep_second[...] = block_of(2 + core)

    def one(i, _):
        send[i] = block_of(2 * i + 1 - core).astype(bf16)
        return 0

    lax.fori_loop(0, 2, one, 0)


def place_rows(table, pieces, whole):
    x, y, c = table[X], table[Y], table[C]
    tokens = whole.shape[1] // 2
    for dc in range(2):
        for dx in range(2):
            block = 2 * (x + dx - 2 * x * dx) + c + dc - 2 * c * dc
            for dy in range(2):
                at = pl.ds(pl.multiple_of(tokens * (y + dy - 2 * y * dy), tokens), tokens)
                array, start = pieces[4 * dc + 2 * dy + dx]
                whole[block, at, :] = array[start : start + tokens]


def stacked_pieces(near, far, tokens, start=0):
    return [(a, start + i * tokens) for a in (near, far) for i in range(4)]


def grad_body(table, near, far, grad):
    place_rows(table, stacked_pieces(near, far, grad.shape[1] // 2), grad)


def norm_rows(raw, gain, normed):
    def square(b, total):
        values = raw[b].astype(f32)
        return total + jnp.sum(values * values, axis=1, keepdims=True)

    count = raw.shape[0]
    total = lax.fori_loop(0, count, square, jnp.zeros((raw.shape[1], 1), f32))
    scale = lax.rsqrt(total / (count * raw.shape[2]) + eps)

    def norm(b, _):
        normed[b] = (raw[b].astype(f32) * scale * gain[b]).astype(bf16)
        return 0

    lax.fori_loop(0, count, norm, 0)
    return scale


def rows_body(table, near, far, *refs):
    gains = refs[:4]
    raw, normed, inverse, gain_first, gain_second = refs[4:]
    place_rows(table, stacked_pieces(near, far, raw.shape[1] // 2), raw)
    x, c = table[X], table[C]
    for dc in range(2):
        for dx in range(2):
            block = 2 * (x + dx - 2 * x * dx) + c + dc - 2 * c * dc
            gain = gains[2 * dc + dx][...]
            gain_first[block] = gain[0:1]
            gain_second[block] = gain[1:2]
    inverse[...] = norm_rows(raw, gain_first, normed)


def prompt_body(table, near, far, gain, normed, slot):
    tokens = slot.shape[1]
    for i in range(PROMPTS):
        at = 4 * i * (tokens // 2)
        place_rows(table, stacked_pieces(near, far, tokens // 2, at), slot)
        norm_rows(slot, gain, normed.at[:, i * tokens : (i + 1) * tokens])


def turn(values, cosine, sine):
    half = values.shape[0] // 2
    first, second = values[:half], values[half:]
    return jnp.concatenate(
        [first * cosine - second * sine, second * cosine + first * sine], axis=0
    )


def qkv_body(
    table,
    normed,
    prompt,
    cosine,
    sine,
    far_cosine,
    far_sine,
    pieces,
    query,
    own,
    far,
    weights,
    acc,
    far_acc,
    sems,
):
    wait = start_pieces(table, pieces, weights, sems)
    count = acc.shape[0]
    far_count = far.shape[0]
    for k in range(weights.shape[0]):
        wait(k)
    acc[...] = jnp.zeros_like(acc)
    far_acc[...] = jnp.zeros_like(far_acc)

    def one(b, _):
        acc[...] += dims(weights[b, :count], normed[b], 1, 1)
        far_acc[...] += dims(weights[b, count - far_count : count], prompt[b], 1, 1)
        return 0

    lax.fori_loop(0, normed.shape[0], one, 0)
    head = HEAD_DIM
    heads = query.shape[0] // head
    cos, sin = cosine[...], sine[...]
    for h in range(heads):
        at = slice(h * head, (h + 1) * head)
        query[at] = turn(acc[at], cos, sin).astype(bf16)
    at = slice(heads * head, (heads + 1) * head)
    own[:head] = turn(acc[at], cos, sin).astype(bf16)
    own[head:] = acc[(heads + 1) * head :].astype(bf16)
    far[:head] = turn(far_acc[:head], far_cosine[...], far_sine[...]).astype(bf16)
    far[head:] = far_acc[head:].astype(bf16)


def attend_body(
    table,
    query,
    own,
    far,
    weights,
    attended,
    attended_low,
    log_total,
    keep_first,
    keep_second,
    send,
):
    tokens = own.shape[1]
    head = HEAD_DIM
    block = tokens // 2
    key_far, value_far = far[:head].T, far[head:]
    key_own = own[:head].T
    total = far.shape[1]
    near_row = lax.broadcasted_iota(jnp.int32, (block, block), 0)
    near_col = lax.broadcasted_iota(jnp.int32, (block, block), 1)
    causal = near_row <= near_col
    row = lax.broadcasted_iota(jnp.int32, (total, block), 0)
    for part in range(2):
        cols = slice(part * block, (part + 1) * block)
        key_near, value_near = key_own[cols], own[head:, cols]
        seen = row < table[COUNT + part] * block

        def one(h, _):
            at = pl.ds(pl.multiple_of(h * head, head), head)
            rows = query[at, cols]
            score_far = jnp.where(seen, dims(key_far, rows, 1, 0) * score_scale, neg_big)
            score_near = jnp.where(causal, dims(key_near, rows, 1, 0) * score_scale, neg_big)
            top = jnp.maximum(
                jnp.max(score_far, axis=0, keepdims=True), jnp.max(score_near, axis=0, keepdims=True)
            )
            weight_far = jnp.exp(score_far - top)
            weight_near = jnp.exp(score_near - top)
            weight = jnp.sum(weight_far, axis=0, keepdims=True) + jnp.sum(
                weight_near, axis=0, keepdims=True
            )
            out = dims(value_far, weight_far.astype(bf16), 1, 0) + dims(
                value_near, weight_near.astype(bf16), 1, 0
            )
            attended[at, cols] = out / weight
            log_total[h, :, cols] = top + jnp.log(weight)
            return 0

        lax.fori_loop(0, query.shape[0] // head, one, 0)
    values = attended[...]
    attended_low[...] = values.astype(bf16)
    flipped = values.T.astype(bf16)
    first = weights.shape[1] - query.shape[0]
    keep_and_send(
        table,
        lambda b: dims(flipped, weights[b, first:], 1, 0),
        keep_first,
        keep_second,
        send,
    )


def hidden_body(
    table, raw, own_first, own_second, other_first, other_second, gain, hidden, normed, inverse
):
    core = table[C]
    summed, other = (own_first, own_second), (other_first, other_second)
    for i in range(2):
        b = 2 * i + core
        hidden[b] = raw[b].astype(f32) + summed[i][...].astype(f32)
        b = 2 * i + 1 - core
        hidden[b] = raw[b].astype(f32) + other[i][...].astype(f32)

    def square(b, total):
        values = hidden[b]
        return total + jnp.sum(values * values, axis=1, keepdims=True)

    count = raw.shape[0]
    total = lax.fori_loop(0, count, square, jnp.zeros((raw.shape[1], 1), f32))
    scale = lax.rsqrt(total / (count * raw.shape[2]) + eps)
    inverse[...] = scale

    def norm(b, _):
        normed[b] = (hidden[b] * scale * gain[b]).astype(bf16)
        return 0

    lax.fori_loop(0, count, norm, 0)


def forward_body(
    table,
    normed,
    grad,
    pieces,
    active,
    change,
    keep_first,
    keep_second,
    send,
    weights,
    acc,
    gate_slope,
    up_slope,
    sems,
):
    wait = start_pieces(table, pieces, weights, sems)
    count, tokens = normed.shape[:2]
    width = acc.shape[1]
    half = width // 2
    for k in range(count):
        b = table[ORDER + k]
        wait(k)
        product = dims(normed[b], weights[b, :width], 1, 1)
        if k == 0:
            acc[...] = product
        else:
            acc[...] += product
    rows = tokens // 4

    def part(i, _):
        at = pl.ds(pl.multiple_of(i * rows, rows), rows)
        gate, up = acc[at, :half], acc[at, half:]
        sigmoid = jax.nn.sigmoid(gate)
        active[at] = (gate * sigmoid * up).astype(bf16)
        gate_slope[at] = up * sigmoid * (1.0 + gate * (1.0 - sigmoid))
        up_slope[at] = gate * sigmoid
        return 0

    lax.fori_loop(0, 4, part, 0)

    def back(b, total):
        return total + dims(grad[b], weights[b, width:], 1, 1)

    slope = lax.fori_loop(0, count, back, jnp.zeros((tokens, half), f32))
    change[:, :half] = (slope * gate_slope[...]).astype(bf16)
    change[:, half:] = (slope * up_slope[...]).astype(bf16)
    values = change[...]
    keep_and_send(
        table, lambda b: dims(values, weights[b, :width], 1, 0), keep_first, keep_second, send
    )


def forward_parts_body(table, active, grad, normed, change, *parts):
    width = change.shape[1]
    flipped = change[...].T
    flipped_active = active[...].T
    for k, part in enumerate(parts):
        b = table[ORDER + k]
        part[:width] = dims(flipped, normed[b], 1, 0).astype(bf16)
        part[width:] = dims(flipped_active, grad[b], 1, 0).astype(bf16)


def down_body(table, active, pieces, keep_first, keep_second, send, weights, sems):
    rows = weights.shape[1]
    wait = start_pieces(table, pieces, weights, sems, slice(2 * rows, 3 * rows))
    for k in range(weights.shape[0]):
        wait(k)
    values = active[...]
    keep_and_send(table, lambda b: dims(values, weights[b], 1, 0), keep_first, keep_second, send)


def attend_back_body(
    table,
    hidden,
    inverse,
    own_first,
    own_second,
    other_first,
    other_second,
    grad,
    gain,
    weights,
    query,
    own,
    far,
    attended,
    log_total,
    cosine,
    sine,
    far_cosine,
    far_sine,
    through,
    pull,
    query_low,
    own_low,
    far_low,
    own_back,
    *rest,
):
    sends, far_back, change = rest[: GROUP - 1], rest[-2], rest[-1]
    core = table[C]
    count, tokens, model = hidden.shape
    for i, (mine, theirs) in enumerate(((own_first, other_first), (own_second, other_second))):
        change[2 * i + core] = mine[...].astype(f32) * gain[2 * i + core]
        change[2 * i + 1 - core] = theirs[...].astype(f32) * gain[2 * i + 1 - core]

    def product(b, total):
        return total + jnp.sum(change[b] * hidden[b], axis=1, keepdims=True)

    inner = lax.fori_loop(0, count, product, jnp.zeros((tokens, 1), f32))
    scale = inverse[...]
    back = scale * scale * scale * inner / (count * model)
    pull[...] = back

    def rows(b, total):
        values = grad[b].astype(f32) + scale * change[b] - hidden[b] * back
        low = values.astype(bf16)
        through[b] = low
        return total + dims(low, weights[b, first:], 1, 1)

    heads_cols = query.shape[0]
    first = weights.shape[1] - heads_cols
    branch = lax.fori_loop(0, count, rows, jnp.zeros((tokens, heads_cols), f32))
    branch = branch.T.astype(bf16)

    head = HEAD_DIM
    block = tokens // 2
    key_far_t = far[:head]
    key_far, value_far = key_far_t.T, far[head:].T
    key_own, value_own = own[:head].T, own[head:].T
    total = far.shape[1]
    near_row = lax.broadcasted_iota(jnp.int32, (block, block), 0)
    near_col = lax.broadcasted_iota(jnp.int32, (block, block), 1)
    causal = near_row <= near_col
    row = lax.broadcasted_iota(jnp.int32, (total, block), 0)
    far_back[...] = jnp.zeros_like(far_back)
    own_back[...] = jnp.zeros_like(own_back)
    for part in range(2):
        cols = slice(part * block, (part + 1) * block)
        key_near, value_near = key_own[cols], value_own[cols]
        key_near_t = own[:head, cols]
        seen = row < table[COUNT + part] * block
        for h in range(heads_cols // head):
            at = slice(h * head, (h + 1) * head)
            rows_q, rows_grad = query[at, cols], branch[at, cols]
            delta = jnp.sum(
                rows_grad.astype(f32) * attended[at, cols], axis=0, keepdims=True
            )
            logs = log_total[h, :, cols]

            def one(key, value, allowed):
                score = dims(key, rows_q, 1, 0) * score_scale
                prob = jnp.where(allowed, jnp.exp(score - logs), 0.0)
                moved = (prob * (dims(value, rows_grad, 1, 0) - delta)).astype(bf16)
                return prob.astype(bf16), moved

            prob_far, moved_far = one(key_far, value_far, seen)
            prob_near, moved_near = one(key_near, value_near, causal)
            query_back = (
                dims(key_far_t, moved_far, 1, 0) + dims(key_near_t, moved_near, 1, 0)
            ) * score_scale
            query_low[at, cols] = turn(query_back, cosine[:, cols], -sine[:, cols]).astype(bf16)
            far_back[:head] += dims(rows_q, moved_far, 1, 1) * score_scale
            far_back[head:] += dims(rows_grad, prob_far, 1, 1)
            own_back[:head, cols] += dims(rows_q, moved_near, 1, 1) * score_scale
            own_back[head:, cols] += dims(rows_grad, prob_near, 1, 1)
    own_low[:head] = turn(own_back[:head], cosine[...], -sine[...]).astype(bf16)
    own_low[head:] = own_back[head:].astype(bf16)
    far_low[:head] = turn(far_back[:head], far_cosine[...], -far_sine[...]).astype(bf16)
    far_low[head:] = far_back[head:].astype(bf16)
    for slot in range(PROMPTS):

        @pl.when(table[Z_IN] == slot)
        def _():
            own_back[...] += far_back[:, slot * tokens : (slot + 1) * tokens]

    for k in range(1, GROUP):
        sends[k - 1][...] = far_back[:, :tokens].astype(bf16)
        for slot in range(1, PROMPTS):

            @pl.when(table[Z_IN] == slot + k)
            def _():
                sends[k - 1][...] = far_back[:, slot * tokens : (slot + 1) * tokens].astype(bf16)


def attend_parts_body(
    table, query_low, own_low, far_low, normed, prompt, attended_low, through, *parts
):
    first = query_low.shape[0]
    second = first + own_low.shape[0]
    for k, part in enumerate(parts):
        b = table[ORDER + k]
        part[:first] = dims(query_low[...], normed[b], 1, 0).astype(bf16)
        part[first:second] = (
            dims(own_low[...], normed[b], 1, 0) + dims(far_low[...], prompt[b], 1, 0)
        ).astype(bf16)
        part[second:] = dims(attended_low[...], through[b], 1, 0).astype(bf16)


def qkv_back_body(table, own_back, *refs):
    moved, refs = refs[: GROUP - 1], refs[GROUP - 1 :]
    query_low, weights, cosine, sine = refs[:4]
    keep_first, keep_second, send = refs[4:]
    head = HEAD_DIM
    total = own_back[...]
    for part in moved:
        total = total + part[...].astype(f32)
    key = turn(total[:head], cosine[...], -sine[...])
    low = jnp.concatenate([key, total[head:]], axis=0)
    flipped = jnp.concatenate([query_low[...].T, low.T.astype(bf16)], axis=1)
    width = flipped.shape[1]
    keep_and_send(
        table,
        lambda b: dims(flipped, weights[b, :width], 1, 0),
        keep_first,
        keep_second,
        send,
    )


def halves_of(table, whole):
    half = whole.shape[0] // 2
    low, high = whole[:half], whole[half:]
    flag = table[Y] == 0
    return jnp.where(flag, low, high), jnp.where(flag, high, low)


def split_body(table, *refs):
    count = len(refs) - 2
    mine_ref, other_ref = refs[-2:]
    at = 0
    for i, ref in enumerate(refs[:count]):
        whole = ref[...]
        if i < count - 1:
            whole = whole.T
        mine, other = halves_of(table, whole)
        rows = mine.shape[0]
        mine_ref[at : at + rows] = mine
        other_ref[at : at + rows] = other
        at += rows


def join_body(table, mine, got, *outs):
    flag = table[Y] == 0
    at = 0
    for i, out in enumerate(outs):
        turned = i < len(outs) - 1
        rows = out.shape[1 if turned else 0] // 2
        parts = mine[at : at + rows].astype(f32), got[at : at + rows].astype(f32)
        at += rows
        low, high = jnp.where(flag, parts[0], parts[1]), jnp.where(flag, parts[1], parts[0])
        if turned:
            out[:, :rows] = low.T
            out[:, rows:] = high.T
        else:
            out[:rows] = low
            out[rows:] = high


def rope_tables(positions, half):
    freq = rope_base ** (-(2.0 * jnp.arange(half, dtype=f32)) / (2.0 * half))
    angle = freq[:, None] * positions.astype(f32)[None, :]
    return (jnp.cos(angle), jnp.sin(angle))


def shards(
    layer_in,
    first_gain,
    query_weight,
    key_matrix,
    value_matrix,
    out_weight,
    second_gain,
    gate_weight,
    up_weight,
    down_weight,
    out_grad,
):
    place = Place()
    n, ny, y, z_in, table = place.n, place.ny, place.y, place.z_in, place.table
    lined = place.lined
    block, width = layer_in.shape
    tokens = 2 * block
    model_width = width * ny
    hidden_dev = gate_weight.shape[1] // 2
    query_rows = query_weight.shape[1] // 2
    kv_rows = key_matrix.shape[1]
    qkv_cols = query_rows + kv_rows
    full = (ny, tokens, width)
    wide = [(full[1:], f32), (full[1:], f32), ((2,) + full[1:], bf16)]

    def halves(*matrices):
        rows = sum(max(m.shape) for m in matrices) // 2
        cols = min(matrices[0].shape)
        return call(split_body, [((rows, cols), bf16)] * 2, table, matrices)

    def whole_piece(mine, got):
        return jnp.concatenate(pair(y, mine, got), axis=1)

    mine, other = halves(query_weight, key_matrix, value_matrix, out_weight)
    attend_got = place.swap_y(other)
    attend_piece = whole_piece(mine, attend_got)
    mine, other = halves(gate_weight, up_weight, down_weight)
    forward_piece = whole_piece(mine, place.swap_y(after(other, attend_got)))
    if lined:
        attend_pieces = gather_pieces(place, attend_piece)
        forward_pieces = gather_pieces(place, after(forward_piece, attend_pieces[-1]), True)
    else:
        attend_pieces = [gather_whole(place, attend_piece)]
        forward_pieces = [gather_whole(place, forward_piece)]
    attend_shape = (ny, qkv_cols + query_rows, width)
    forward_shape = (ny, 3 * hidden_dev, width)
    sems = pltpu.SemaphoreType.DMA((ny,))

    def over_cores(four):
        near = jnp.concatenate(four, axis=0)
        return [near, place.swap_c(near)]

    def spread(value):
        by_x = place.swap_x(value)
        return over_cores([value, by_x, place.swap_y(value), place.swap_y(by_x)])

    gains = jnp.stack([first_gain, second_gain])
    two = [gains, place.swap_x(gains)]
    gains = two + [place.swap_c(g) for g in two]
    raw, normed_in, inverse_in, gain_in, gain_mid = call(
        rows_body,
        [(full, bf16), (full, bf16), ((tokens, 1), f32)] + [((ny, 1, width), f32)] * 2,
        table,
        spread(layer_in) + gains,
    )

    moved = [
        place.send_z(
            layer_in,
            [(s, s + k) for s in range(n) if s % GROUP < PROMPTS and s % GROUP + k < GROUP],
        )
        for k in range(1, GROUP)
    ]
    slots = [layer_in] * PROMPTS
    for i in range(PROMPTS):
        for k in range(1, GROUP):
            slots[i] = jnp.where(z_in == i + k, moved[k - 1], slots[i])
    pieces = []
    for i, slot in enumerate(slots):
        if i % 2 == 0:
            by_x = place.swap_x(slot)
            pieces += [slot, by_x, place.swap_y(slot), place.swap_y(by_x)]
        else:
            by_y = place.swap_y(slot)
            pieces += [slot, place.swap_x(slot), by_y, place.swap_x(by_y)]
    (prompt,) = call(
        prompt_body,
        [((ny, PROMPTS * tokens, width), bf16)],
        table,
        over_cores(pieces) + [gain_in],
        scratch=[pltpu.VMEM(full, bf16)],
    )

    within = jnp.arange(block, dtype=jnp.int32)
    positions = jnp.minimum(place.offset, PROMPT_DEV)[:, None] * block + within[None, :]
    cosine, sine = rope_tables(positions.reshape(-1), HEAD_DIM // 2)
    far_cosine, far_sine = rope_tables(
        jnp.arange(PROMPTS * tokens, dtype=jnp.int32), HEAD_DIM // 2
    )
    tables = [cosine, sine, far_cosine, far_sine]
    query, own, far, attend_weights = call(
        qkv_body,
        [
            ((query_rows, tokens), bf16),
            ((kv_rows, tokens), bf16),
            ((kv_rows, PROMPTS * tokens), bf16),
            (attend_shape, bf16),
        ],
        table,
        [normed_in, prompt] + tables,
        [attend_pieces],
        [
            pltpu.VMEM((qkv_cols, tokens), f32),
            pltpu.VMEM((kv_rows, PROMPTS * tokens), f32),
            sems,
        ],
    )
    (grad,) = call(grad_body, [(full, bf16)], table, spread(after(out_grad, normed_in)))
    attended, attended_low, log_total, keep_first, keep_second, send = call(
        attend_body,
        [
            ((query_rows, tokens), f32),
            ((query_rows, tokens), bf16),
            ((query_rows // HEAD_DIM, 1, tokens), f32),
        ]
        + wide,
        table,
        [query, own, far, attend_weights],
    )
    summed = all_sum(place, (keep_first, keep_second), send)

    hidden, normed_mid, inverse_mid = call(
        hidden_body,
        [(full, f32), (full, bf16), ((tokens, 1), f32)],
        table,
        [raw] + summed + [gain_mid],
    )
    active, change, keep_first, keep_second, send = call(
        forward_body,
        [((tokens, hidden_dev), bf16), ((tokens, 2 * hidden_dev), bf16)] + wide,
        table,
        [normed_mid, grad],
        [forward_pieces],
        [pltpu.VMEM(forward_shape, bf16), pltpu.VMEM((tokens, 2 * hidden_dev), f32)]
        + [pltpu.VMEM((tokens, hidden_dev), f32)] * 2
        + [sems],
    )
    summed = all_sum(place, (keep_first, keep_second), send)
    forward_parts = call(
        forward_parts_body,
        [(forward_shape[1:], bf16)] * ny,
        table,
        [active, grad, normed_mid, change],
    )
    keep_first, keep_second, send = call(
        down_body,
        wide,
        table,
        [active],
        [forward_pieces],
        [pltpu.VMEM((ny, hidden_dev, width), bf16), sems],
        earlier=[summed[-1]],
    )
    hidden_own = own_block(place, hidden)
    layer_out = (hidden_own + own_sum(place, (keep_first, keep_second), send)).astype(bf16)
    through, pull, query_low, own_low, far_low, own_back, *sends = call(
        attend_back_body,
        [
            (full, bf16),
            ((tokens, 1), f32),
            ((query_rows, tokens), bf16),
            ((kv_rows, tokens), bf16),
            ((kv_rows, PROMPTS * tokens), bf16),
            ((kv_rows, tokens), f32),
        ]
        + [((kv_rows, tokens), bf16)] * (GROUP - 1),
        table,
        [hidden, inverse_mid]
        + summed
        + [
            grad,
            gain_mid,
            attend_weights,
            query,
            own,
            far,
            attended,
            log_total,
        ]
        + tables,
        scratch=[pltpu.VMEM((kv_rows, PROMPTS * tokens), f32), pltpu.VMEM(full, f32)],
    )
    inverse_own, _ = part_of(y, inverse_mid, 0)
    pull_own, _ = part_of(y, pull, 0)
    mid_own = jnp.where(place.x == 0, summed[0], summed[1])
    mid_own = part_of(y, mid_own, 0)[0].astype(f32)
    through_own = (
        out_grad.astype(f32)
        + inverse_own * mid_own * second_gain[None, :]
        - hidden_own * pull_own
    )
    second_term = jnp.sum(mid_own * hidden_own * inverse_own, axis=0)

    moved = [
        place.send_z(
            sends[k - 1],
            [(s, s - k) for s in range(n) if 0 <= s % GROUP - k < PROMPTS],
        )
        for k in range(1, GROUP)
    ]
    attend_parts = call(
        attend_parts_body,
        [(attend_shape[1:], bf16)] * ny,
        table,
        [query_low, own_low, far_low, normed_in, prompt, attended_low, through],
    )
    keep_first, keep_second, send = call(
        qkv_back_body,
        wide,
        table,
        [own_back] + moved + [query_low, attend_weights, cosine, sine],
    )
    forward_grad = scatter_sum(place, forward_parts, [send], [send])
    attend_grad = scatter_sum(place, attend_parts, [send], [send])
    first_own = own_sum(place, (keep_first, keep_second), send)
    input_own = layer_in.astype(f32)
    inverse_own, _ = part_of(y, inverse_in, 0)
    scaled = first_own * first_gain[None, :]
    inner = jnp.sum(scaled * input_own, axis=1, keepdims=True)
    inner = inner + place.swap_c(inner)
    inner = inner + place.swap_x(inner)
    in_grad = (
        through_own + inverse_own * scaled - input_own * (inverse_own**3 * inner / model_width)
    )
    first_term = jnp.sum(first_own * input_own * inverse_own, axis=0)
    terms = jnp.stack([first_term, second_term])
    bit = 1
    while bit < place.nx:
        terms = terms + place.swap_gx(terms, bit)
        bit *= 2

    def joined(summed_part, outs):
        mine, other = part_of(y, summed_part, 1)
        got = place.swap_y(other.astype(bf16))
        return call(
            join_body,
            [(m.shape, f32) for m in outs],
            table,
            [mine, got],
        )

    gate_grad, up_grad, down_grad = joined(forward_grad, (gate_weight, up_weight, down_weight))
    query_out, key_out, value_out, out_out = joined(
        attend_grad, (query_weight, key_matrix, value_matrix, out_weight)
    )
    return (
        layer_out,
        in_grad,
        terms[0],
        query_out,
        key_out,
        value_out,
        out_out,
        terms[1],
        gate_grad,
        up_grad,
        down_grad,
    )


def solution(mesh):
    rows, cols, gain = P("gx", "gy"), P("gy", "gx"), P("gy")
    return jax.shard_map(
        shards,
        mesh=mesh,
        in_specs=(rows, gain, rows, rows, rows, cols, gain, rows, rows, cols, rows),
        out_specs=(rows, rows, gain, rows, rows, rows, cols, gain, rows, rows, cols),
        check_vma=False,
    )
```

```python
import jax
import jax.numpy as jnp
from jax import lax
from jax.experimental import pallas as pl
from jax.experimental.pallas import tpu as pltpu
from jax.sharding import PartitionSpec as P

HEAD_DIM = 96
PROMPT_DEV = 4
CONT_DEV = 4
GROUP = (PROMPT_DEV + CONT_DEV) // 2
PROMPTS = PROMPT_DEV // 2

eps = 1e-05
neg_big = -1e30
rope_base = 100000.0
score_scale = HEAD_DIM ** (-0.5)
f32 = jnp.float32
bf16 = jnp.bfloat16


def dims(left, right, left_axis, right_axis):
    return lax.dot_general(
        left, right, (((left_axis,), (right_axis,)), ((), ())), preferred_element_type=f32
    )


class Place:
    def __init__(self):
        self.nx = lax.axis_size("gx")
        self.ny = lax.axis_size("gy")
        assert self.ny == 4 and self.nx % (PROMPT_DEV + CONT_DEV) == 0
        self.n = self.nx // 2
        self.gx = lax.axis_index("gx")
        self.gy = lax.axis_index("gy")
        self.z, self.y = self.gx // 2, self.gx % 2
        self.x, self.c = self.gy // 2, self.gy % 2
        self.z_in = self.z % GROUP
        offset = 2 * self.z_in + jnp.arange(2, dtype=jnp.int32)
        self.offset = offset
        self.lined = self.n == self.ny
        blocks = jnp.arange(self.ny, dtype=jnp.int32)
        first = jnp.stack([self.z, self.y, self.x, self.c, self.z_in]).astype(jnp.int32)
        self.table = jnp.concatenate(
            [first, jnp.minimum(offset, PROMPT_DEV), blocks ^ self.z if self.lined else blocks]
        )

    def swap_gx(self, value, bit):
        return lax.ppermute(value, "gx", [(i, i ^ bit) for i in range(self.nx)])

    def swap_y(self, value):
        return self.swap_gx(value, 1)

    def swap_x(self, value):
        return lax.ppermute(value, "gy", [(i, i ^ 2) for i in range(self.ny)])

    def swap_c(self, value):
        return lax.ppermute(value, "gy", [(i, i ^ 1) for i in range(self.ny)])

    def send_z(self, value, moves):
        pairs = [(2 * s + y, 2 * t + y) for s, t in moves for y in range(2)]
        return lax.ppermute(value, "gx", pairs)

    def by_y(self):
        return [[2 * z + y for z in range(self.n)] for y in range(2)]


def pair(flag, mine, other):
    return jnp.where(flag == 0, mine, other), jnp.where(flag == 0, other, mine)


def part_of(flag, whole, axis):
    low, high = jnp.split(whole, 2, axis)
    return jnp.where(flag == 0, low, high), jnp.where(flag == 0, high, low)


def after(value, *earlier):
    return lax.optimization_barrier((value,) + earlier)[0]


NEAR = [(0, 1), (1, 0), (2, 3), (3, 2)]
SECOND = [(0, 2), (1, 3), (2, 0), (3, 1)]
MIDDLE = [(1, 2), (2, 1)]
INWARD = [(0, 1), (3, 2)]
OUTWARD = [(1, 0), (2, 3)]


def gather_pieces(place, piece, late_middle=False):
    second = place.send_z(piece, SECOND)
    near = place.send_z(piece, NEAR)
    middle = place.send_z(after(piece, second) if late_middle else piece, MIDDLE)
    return [piece, near, second, middle, place.send_z(second, OUTWARD)]


def gather_whole(place, piece):
    every = lax.all_gather(piece, "gx", axis_index_groups=place.by_y())
    inner = place.n // place.ny
    if inner == 1:
        return every
    rows, cols = piece.shape
    every = every.reshape(place.ny, inner, rows, cols)
    return jnp.swapaxes(every, 1, 2).reshape(place.ny, rows, inner * cols)


def scatter_whole(place, parts):
    inner = place.n // place.ny
    if inner > 1:
        count, rows, cols = parts.shape
        parts = jnp.swapaxes(parts.reshape(count, rows, inner, cols // inner), 1, 2)
        parts = parts.reshape(place.n, rows, cols // inner)
    return lax.psum_scatter(parts, "gx", axis_index_groups=place.by_y())


def start_scatter(place, parts):
    if not place.lined:
        return [scatter_whole(place, jnp.stack(parts))]
    own, near, second, third = parts
    far = place.send_z(third, INWARD)
    middle = place.send_z(third, MIDDLE)
    return [own, second, far, place.send_z(near, NEAR), middle]


def second_scatter(place, started, *earlier):
    if not place.lined:
        return None
    second = after(started[1], *earlier)
    return place.send_z((second.astype(f32) + started[2].astype(f32)).astype(bf16), SECOND)


def end_scatter(place, started, second, *earlier):
    if not place.lined:
        return started[0].astype(f32)
    own, near, middle = after(started[0], *earlier), started[3], started[4]
    return own.astype(f32) + near.astype(f32) + middle.astype(f32) + second.astype(f32)


def reduce_core(place, keep, sends):
    return [keep[i] + place.swap_c(send).astype(f32) for i, send in enumerate(sends)]


def all_sum(place, keep, sends, before_first=(), before_second=()):
    first, second = reduce_core(place, keep, sends)
    low = (first.astype(bf16), second.astype(bf16))
    low = lax.optimization_barrier(low + tuple(before_first))
    first, second = (
        first + place.swap_x(low[0]).astype(f32),
        second + place.swap_y(low[1]).astype(f32),
    )
    low = (first.astype(bf16), second.astype(bf16))
    low = lax.optimization_barrier(low + tuple(before_second))
    own = [
        (first + place.swap_y(low[0]).astype(f32)).astype(bf16),
        (second + place.swap_x(low[1]).astype(f32)).astype(bf16),
    ]
    return own + [place.swap_c(part) for part in own]


def own_sum(place, keep, sends):
    first, second = reduce_core(place, keep, sends)
    mine, other = jnp.where(place.x == 0, first, second), jnp.where(place.x == 0, second, first)
    mine = mine + place.swap_x(other.astype(bf16)).astype(f32)
    mine, other = part_of(place.y, mine, 0)
    return mine + place.swap_y(other.astype(bf16)).astype(f32)


def own_block(place, blocks):
    rows = blocks.shape[1] // 2
    return lax.dynamic_slice(
        blocks, (place.gy, place.y * rows, 0), (1, rows, blocks.shape[2])
    )[0]


Z, Y, X, C, Z_IN, COUNT = range(6)
ORDER = COUNT + 2


def call(body, outs, table, operands, pieces=(), scratch=(), earlier=(), limit=24):
    lengths = [len(p) for p in pieces]
    flat = [a for p in pieces for a in p] + list(earlier)
    vmem = pl.BlockSpec(memory_space=pltpu.VMEM)

    def kernel(table_ref, *refs):
        plain, rest = refs[: len(operands)], refs[len(operands) :]
        lists = []
        for length in lengths:
            lists.append(rest[:length])
            rest = rest[length:]
        rest = rest[len(earlier) :]
        body(table_ref, *plain, *lists, *rest)

    return pl.pallas_call(
        kernel,
        out_shape=[jax.ShapeDtypeStruct(shape, dtype) for shape, dtype in outs],
        in_specs=[pl.BlockSpec(memory_space=pltpu.SMEM)]
        + [vmem] * len(operands)
        + [pl.BlockSpec(memory_space=pl.ANY)] * len(flat),
        out_specs=[vmem] * len(outs),
        scratch_shapes=list(scratch),
        compiler_params=pltpu.CompilerParams(vmem_limit_bytes=limit << 20),
    )(table, *operands, *flat)


def start_pieces(table, pieces, whole, sems, rows=slice(None)):
    count = whole.shape[0]
    block = [table[ORDER + k] for k in range(count)]

    def copy(piece, k):
        source = piece.at[rows] if rows != slice(None) else piece
        return pltpu.make_async_copy(source, whole.at[block[k]], sems.at[k])

    def wait(k):
        pltpu.make_async_copy(whole.at[0], whole.at[0], sems.at[k]).wait()

    if len(pieces) == 1:
        for k in range(count):
            copy(pieces[0].at[block[k]], k).start()
        return wait
    z = table[Z]
    own, near, second, middle, end = pieces
    for k, piece in enumerate((own, near, second)):
        copy(piece, k).start()
    inside = jnp.logical_or(z == 1, z == 2)

    @pl.when(inside)
    def _():
        copy(middle, 3).start()

    @pl.when(jnp.logical_not(inside))
    def _():
        copy(end, 3).start()

    return wait


def keep_and_send(table, block_of, keep, sends):
    core = table[C]
    for i, send in enumerate(sends):
        keep[i] = block_of(2 * i + core)
        send[...] = block_of(2 * i + 1 - core).astype(bf16)


def place_rows(table, pieces, whole):
    x, y, c = table[X], table[Y], table[C]
    tokens = whole.shape[1] // 2
    for dc in range(2):
        for dx in range(2):
            block = 2 * (x + dx - 2 * x * dx) + c + dc - 2 * c * dc
            for dy in range(2):
                at = pl.ds(pl.multiple_of(tokens * (y + dy - 2 * y * dy), tokens), tokens)
                array, start = pieces[4 * dc + 2 * dy + dx]
                whole[block, at, :] = array[start : start + tokens]


def stacked_pieces(near, far, stride, start=0):
    return [(a, start + i * stride) for a in (near, far) for i in range(4)]


def norm_rows(raw, gain, normed):
    def square(b, total):
        values = raw[b].astype(f32)
        return total + jnp.sum(values * values, axis=1, keepdims=True)

    count = raw.shape[0]
    total = lax.fori_loop(0, count, square, jnp.zeros((raw.shape[1], 1), f32))
    scale = lax.rsqrt(total / (count * raw.shape[2]) + eps)

    def norm(b, _):
        normed[b] = (raw[b].astype(f32) * scale * gain[b]).astype(bf16)
        return 0

    lax.fori_loop(0, count, norm, 0)
    return scale


def rows_body(table, near, far, *refs):
    gains = refs[:4]
    raw, grad, normed, inverse, gain_first, gain_second = refs[4:]
    tokens = raw.shape[1]
    place_rows(table, stacked_pieces(near, far, tokens), raw)
    place_rows(table, stacked_pieces(near, far, tokens, tokens // 2), grad)
    x, c = table[X], table[C]
    for dc in range(2):
        for dx in range(2):
            block = 2 * (x + dx - 2 * x * dx) + c + dc - 2 * c * dc
            gain = gains[2 * dc + dx][...]
            gain_first[block] = gain[0:1]
            gain_second[block] = gain[1:2]
    inverse[...] = norm_rows(raw, gain_first, normed)


def prompt_body(table, near, far, gain, normed, slot):
    tokens = slot.shape[1]
    for i in range(PROMPTS):
        at = 4 * i * (tokens // 2)
        place_rows(table, stacked_pieces(near, far, tokens // 2, at), slot)
        norm_rows(slot, gain, normed.at[:, i * tokens : (i + 1) * tokens])


def turn(values, cosine, sine):
    half = values.shape[0] // 2
    first, second = values[:half], values[half:]
    return jnp.concatenate(
        [first * cosine - second * sine, second * cosine + first * sine], axis=0
    )


def qkv_body(
    table,
    normed,
    prompt,
    cosine,
    sine,
    far_cosine,
    far_sine,
    pieces,
    query,
    own,
    far,
    weights,
    acc,
    far_acc,
    sems,
):
    wait = start_pieces(table, pieces, weights, sems)
    count = acc.shape[0]
    far_count = far.shape[0]
    for k in range(weights.shape[0]):
        wait(k)
    acc[...] = jnp.zeros_like(acc)
    far_acc[...] = jnp.zeros_like(far_acc)

    def one(b, _):
        acc[...] += dims(weights[b, :count], normed[b], 1, 1)
        far_acc[...] += dims(weights[b, count - far_count : count], prompt[b], 1, 1)
        return 0

    lax.fori_loop(0, normed.shape[0], one, 0)
    head = HEAD_DIM
    heads = query.shape[0] // head
    cos, sin = cosine[...], sine[...]
    for h in range(heads):
        at = slice(h * head, (h + 1) * head)
        query[at] = turn(acc[at], cos, sin).astype(bf16)
    at = slice(heads * head, (heads + 1) * head)
    own[:head] = turn(acc[at], cos, sin).astype(bf16)
    own[head:] = acc[(heads + 1) * head :].astype(bf16)
    far[:head] = turn(far_acc[:head], far_cosine[...], far_sine[...]).astype(bf16)
    far[head:] = far_acc[head:].astype(bf16)


def attend_body(
    table,
    query,
    own,
    far,
    weights,
    attended,
    attended_low,
    log_total,
    keep,
    first_send,
    second_send,
):
    tokens = own.shape[1]
    head = HEAD_DIM
    block = tokens // 2
    key_far, value_far = far[:head].T, far[head:]
    key_own = own[:head].T
    total = far.shape[1]
    near_row = lax.broadcasted_iota(jnp.int32, (block, block), 0)
    near_col = lax.broadcasted_iota(jnp.int32, (block, block), 1)
    causal = near_row <= near_col
    row = lax.broadcasted_iota(jnp.int32, (total, block), 0)
    for part in range(2):
        cols = slice(part * block, (part + 1) * block)
        key_near, value_near = key_own[cols], own[head:, cols]
        seen = row < table[COUNT + part] * block

        def one(h, _):
            at = pl.ds(pl.multiple_of(h * head, head), head)
            rows = query[at, cols]
            score_far = jnp.where(seen, dims(key_far, rows, 1, 0) * score_scale, neg_big)
            score_near = jnp.where(causal, dims(key_near, rows, 1, 0) * score_scale, neg_big)
            top = jnp.maximum(
                jnp.max(score_far, axis=0, keepdims=True), jnp.max(score_near, axis=0, keepdims=True)
            )
            weight_far = jnp.exp(score_far - top)
            weight_near = jnp.exp(score_near - top)
            weight = jnp.sum(weight_far, axis=0, keepdims=True) + jnp.sum(
                weight_near, axis=0, keepdims=True
            )
            out = dims(value_far, weight_far.astype(bf16), 1, 0) + dims(
                value_near, weight_near.astype(bf16), 1, 0
            )
            attended[at, cols] = out / weight
            log_total[h, :, cols] = top + jnp.log(weight)
            return 0

        lax.fori_loop(0, query.shape[0] // head, one, 0)
    values = attended[...]
    attended_low[...] = values.astype(bf16)
    flipped = values.T.astype(bf16)
    first = weights.shape[1] - query.shape[0]
    keep_and_send(
        table,
        lambda b: dims(flipped, weights[b, first:], 1, 0),
        keep,
        (first_send, second_send),
    )


def hidden_body(
    table, raw, own_first, own_second, other_first, other_second, gain, hidden, normed, inverse
):
    core = table[C]
    summed, other = (own_first, own_second), (other_first, other_second)
    for i in range(2):
        b = 2 * i + core
        hidden[b] = raw[b].astype(f32) + summed[i][...].astype(f32)
        b = 2 * i + 1 - core
        hidden[b] = raw[b].astype(f32) + other[i][...].astype(f32)

    def square(b, total):
        values = hidden[b]
        return total + jnp.sum(values * values, axis=1, keepdims=True)

    count = raw.shape[0]
    total = lax.fori_loop(0, count, square, jnp.zeros((raw.shape[1], 1), f32))
    scale = lax.rsqrt(total / (count * raw.shape[2]) + eps)
    inverse[...] = scale

    def norm(b, _):
        normed[b] = (hidden[b] * scale * gain[b]).astype(bf16)
        return 0

    lax.fori_loop(0, count, norm, 0)


def forward_body(
    table,
    normed,
    grad,
    pieces,
    active,
    change,
    keep,
    first_send,
    second_send,
    weights,
    acc,
    gate_slope,
    up_slope,
    sems,
):
    wait = start_pieces(table, pieces, weights, sems)
    count, tokens = normed.shape[:2]
    width = acc.shape[1]
    half = width // 2
    acc[...] = jnp.zeros_like(acc)

    def one(k, _):
        b = table[ORDER + k]
        wait(k)
        acc[...] += dims(normed[b], weights[b, :width], 1, 1)
        return 0

    lax.fori_loop(0, count, one, 0)
    rows = tokens // 4

    def part(i, _):
        at = pl.ds(pl.multiple_of(i * rows, rows), rows)
        gate, up = acc[at, :half], acc[at, half:]
        sigmoid = jax.nn.sigmoid(gate)
        active[at] = (gate * sigmoid * up).astype(bf16)
        gate_slope[at] = up * sigmoid * (1.0 + gate * (1.0 - sigmoid))
        up_slope[at] = gate * sigmoid
        return 0

    lax.fori_loop(0, 4, part, 0)

    def back(b, total):
        return total + dims(grad[b], weights[b, width:], 1, 1)

    slope = lax.fori_loop(0, count, back, jnp.zeros((tokens, half), f32))
    change[:, :half] = (slope * gate_slope[...]).astype(bf16)
    change[:, half:] = (slope * up_slope[...]).astype(bf16)
    values = change[...]
    keep_and_send(
        table,
        lambda b: dims(values, weights[b, :width], 1, 0),
        keep,
        (first_send, second_send),
    )


def forward_parts_body(table, active, grad, normed, change, *refs):
    parts, flipped = refs[:-1], refs[-1]
    width = change.shape[1]
    flipped[:width] = change[...].T
    flipped[width:] = active[...].T
    rows = width // 4

    def fill(first, count, source):
        def one(i, _):
            at = pl.ds(pl.multiple_of((first + i) * rows, rows), rows)
            for k, part in enumerate(parts):
                part[at] = dims(flipped[at], source[table[ORDER + k]], 1, 0).astype(bf16)
            return 0

        lax.fori_loop(0, count, one, 0)

    fill(0, 4, normed)
    fill(4, flipped.shape[0] // rows - 4, grad)


def down_body(table, active, pieces, keep, first_send, second_send, weights, sems):
    rows = weights.shape[1]
    wait = start_pieces(table, pieces, weights, sems, slice(2 * rows, 3 * rows))
    for k in range(weights.shape[0]):
        wait(k)
    values = active[...]
    keep_and_send(
        table, lambda b: dims(values, weights[b], 1, 0), keep, (first_send, second_send)
    )


def attend_back_body(
    table,
    hidden,
    inverse,
    own_first,
    own_second,
    other_first,
    other_second,
    grad,
    gain,
    weights,
    query,
    own,
    far,
    attended,
    log_total,
    cosine,
    sine,
    far_cosine,
    far_sine,
    through,
    pull,
    query_low,
    own_low,
    far_low,
    own_back,
    *rest,
):
    sends, inner_first = rest[: GROUP - 1], rest[GROUP - 1]
    far_back, change, branch = rest[GROUP:]
    core = table[C]
    count, tokens, model = hidden.shape
    for i, (mine, theirs) in enumerate(((own_first, other_first), (own_second, other_second))):
        change[2 * i + core] = mine[...].astype(f32) * gain[2 * i + core]
        change[2 * i + 1 - core] = theirs[...].astype(f32) * gain[2 * i + 1 - core]

    def product(b, total):
        return total + jnp.sum(change[b] * hidden[b], axis=1, keepdims=True)

    inner = lax.fori_loop(0, count, product, jnp.zeros((tokens, 1), f32))
    scale = inverse[...]
    back = scale * scale * scale * inner / (count * model)
    pull[...] = back

    def rows(b, total):
        values = grad[b].astype(f32) + scale * change[b] - hidden[b] * back
        low = values.astype(bf16)
        through[b] = low
        return total + dims(low, weights[b, first:], 1, 1)

    heads_cols = query.shape[0]
    first = weights.shape[1] - heads_cols
    total_rows = lax.fori_loop(0, count, rows, jnp.zeros((tokens, heads_cols), f32))
    branch[...] = total_rows.T.astype(bf16)

    head = HEAD_DIM
    block = tokens // 2
    key_far_t = far[:head]
    key_far, value_far = key_far_t.T, far[head:].T
    key_own, value_own = own[:head].T, own[head:].T
    total = far.shape[1]
    near_row = lax.broadcasted_iota(jnp.int32, (block, block), 0)
    near_col = lax.broadcasted_iota(jnp.int32, (block, block), 1)
    causal = near_row <= near_col
    row = lax.broadcasted_iota(jnp.int32, (total, block), 0)
    far_back[...] = jnp.zeros_like(far_back)
    own_back[...] = jnp.zeros_like(own_back)
    inner_first[...] = jnp.zeros_like(inner_first)
    for part in range(2):
        cols = slice(part * block, (part + 1) * block)
        key_near, value_near = key_own[cols], value_own[cols]
        key_near_t = own[:head, cols]
        seen = row < table[COUNT + part] * block

        def one_head(h, _):
            at = pl.ds(pl.multiple_of(h * head, head), head)
            rows_q, rows_grad = query[at, cols], branch[at, cols]
            delta = jnp.sum(
                rows_grad.astype(f32) * attended[at, cols], axis=0, keepdims=True
            )
            logs = log_total[h, :, cols]

            def one(key, value, allowed):
                score = dims(key, rows_q, 1, 0) * score_scale
                prob = jnp.where(allowed, jnp.exp(score - logs), 0.0)
                moved = (prob * (dims(value, rows_grad, 1, 0) - delta)).astype(bf16)
                return prob.astype(bf16), moved

            prob_far, moved_far = one(key_far, value_far, seen)
            prob_near, moved_near = one(key_near, value_near, causal)
            query_back = (
                dims(key_far_t, moved_far, 1, 0) + dims(key_near_t, moved_near, 1, 0)
            ) * score_scale
            inner_first[:, cols] += jnp.sum(
                query_back * rows_q.astype(f32), axis=0, keepdims=True
            )
            query_low[at, cols] = turn(query_back, cosine[:, cols], -sine[:, cols]).astype(bf16)
            far_back[:head] += dims(rows_q, moved_far, 1, 1) * score_scale
            far_back[head:] += dims(rows_grad, prob_far, 1, 1)
            own_back[:head, cols] += dims(rows_q, moved_near, 1, 1) * score_scale
            own_back[head:, cols] += dims(rows_grad, prob_near, 1, 1)
            return 0

        lax.fori_loop(0, heads_cols // head, one_head, 0)
    own_low[:head] = turn(own_back[:head], cosine[...], -sine[...]).astype(bf16)
    own_low[head:] = own_back[head:].astype(bf16)
    far_low[:head] = turn(far_back[:head], far_cosine[...], -far_sine[...]).astype(bf16)
    far_low[head:] = far_back[head:].astype(bf16)
    for slot in range(PROMPTS):

        @pl.when(table[Z_IN] == slot)
        def _():
            own_back[...] += far_back[:, slot * tokens : (slot + 1) * tokens]

    for k in range(1, GROUP):
        sends[k - 1][...] = far_back[:, :tokens].astype(bf16)
        for slot in range(1, PROMPTS):

            @pl.when(table[Z_IN] == slot + k)
            def _():
                sends[k - 1][...] = far_back[:, slot * tokens : (slot + 1) * tokens].astype(bf16)


def attend_parts_body(
    table, query_low, own_low, far_low, normed, prompt, attended_low, through, *parts
):
    first = query_low.shape[0]
    second = first + own_low.shape[0]
    for k, part in enumerate(parts):
        b = table[ORDER + k]
        part[:first] = dims(query_low[...], normed[b], 1, 0).astype(bf16)
        part[first:second] = (
            dims(own_low[...], normed[b], 1, 0) + dims(far_low[...], prompt[b], 1, 0)
        ).astype(bf16)
        part[second:] = dims(attended_low[...], through[b], 1, 0).astype(bf16)


def qkv_back_body(table, own_back, *refs):
    moved, refs = refs[: GROUP - 1], refs[GROUP - 1 :]
    query_low, weights, cosine, sine, own, inner = refs[:6]
    keep, first_send, second_send, inner_first = refs[6:]
    head = HEAD_DIM
    total = own_back[...]
    for part in moved:
        total = total + part[...].astype(f32)
    inner_first[...] = inner[...] + jnp.sum(total * own[...].astype(f32), axis=0, keepdims=True)
    key = turn(total[:head], cosine[...], -sine[...])
    low = jnp.concatenate([key, total[head:]], axis=0)
    flipped = jnp.concatenate([query_low[...].T, low.T.astype(bf16)], axis=1)
    width = flipped.shape[1]
    keep_and_send(
        table,
        lambda b: dims(flipped, weights[b, :width], 1, 0),
        keep,
        (first_send, second_send),
    )


def halves_of(table, whole):
    half = whole.shape[0] // 2
    low, high = whole[:half], whole[half:]
    flag = table[Y] == 0
    return jnp.where(flag, low, high), jnp.where(flag, high, low)


def split_body(table, *refs):
    count = len(refs) - 2
    mine_ref, other_ref = refs[-2:]
    at = 0
    for i, ref in enumerate(refs[:count]):
        whole = ref[...]
        if i < count - 1:
            whole = whole.T
        mine, other = halves_of(table, whole)
        rows = mine.shape[0]
        mine_ref[at : at + rows] = mine
        other_ref[at : at + rows] = other
        at += rows


def join_body(table, mine, got, *outs):
    flag = table[Y] == 0
    at = 0
    for i, out in enumerate(outs):
        turned = i < len(outs) - 1
        rows = out.shape[1 if turned else 0] // 2
        parts = mine[at : at + rows].astype(f32), got[at : at + rows].astype(f32)
        at += rows
        low, high = jnp.where(flag, parts[0], parts[1]), jnp.where(flag, parts[1], parts[0])
        if turned:
            out[:, :rows] = low.T
            out[:, rows:] = high.T
        else:
            out[:rows] = low
            out[rows:] = high


def rope_tables(positions, half):
    freq = rope_base ** (-(2.0 * jnp.arange(half, dtype=f32)) / (2.0 * half))
    angle = freq[:, None] * positions.astype(f32)[None, :]
    return (jnp.cos(angle), jnp.sin(angle))


def shards(
    layer_in,
    first_gain,
    query_weight,
    key_matrix,
    value_matrix,
    out_weight,
    second_gain,
    gate_weight,
    up_weight,
    down_weight,
    out_grad,
):
    place = Place()
    n, ny, y, z_in, table = place.n, place.ny, place.y, place.z_in, place.table
    lined = place.lined
    block, width = layer_in.shape
    tokens = 2 * block
    model_width = width * ny
    hidden_dev = gate_weight.shape[1] // 2
    query_rows = query_weight.shape[1] // 2
    kv_rows = key_matrix.shape[1]
    qkv_cols = query_rows + kv_rows
    full = (ny, tokens, width)
    wide = [((2,) + full[1:], f32), (full[1:], bf16), (full[1:], bf16)]

    def halves(*matrices):
        rows = sum(max(m.shape) for m in matrices) // 2
        cols = min(matrices[0].shape)
        return call(split_body, [((rows, cols), bf16)] * 2, table, matrices)

    def whole_piece(mine, got):
        return jnp.concatenate(pair(y, mine, got), axis=1)

    mine, other = halves(query_weight, key_matrix, value_matrix, out_weight)
    early_in = after(layer_in, other)
    attend_got = place.swap_y(other)
    attend_piece = whole_piece(mine, attend_got)
    mine, other = halves(gate_weight, up_weight, down_weight)
    forward_piece = whole_piece(mine, place.swap_y(after(other, attend_got)))
    if lined:
        attend_pieces = gather_pieces(place, attend_piece)
        forward_pieces = gather_pieces(place, after(forward_piece, *attend_pieces[1:]), True)
    else:
        attend_pieces = [gather_whole(place, attend_piece)]
        forward_pieces = [gather_whole(place, forward_piece)]
    attend_shape = (ny, qkv_cols + query_rows, width)
    forward_shape = (ny, 3 * hidden_dev, width)
    sems = pltpu.SemaphoreType.DMA((ny,))

    def over_cores(four):
        near = jnp.concatenate(four, axis=0)
        return [near, place.swap_c(near)]

    def spread(value):
        by_x = place.swap_x(value)
        return over_cores([value, by_x, place.swap_y(value), place.swap_y(by_x)])

    gains = jnp.stack([first_gain, second_gain])
    two = [gains, place.swap_x(gains)]
    gains = two + [place.swap_c(g) for g in two]
    raw, grad, normed_in, inverse_in, gain_in, gain_mid = call(
        rows_body,
        [(full, bf16)] * 3 + [((tokens, 1), f32)] + [((ny, 1, width), f32)] * 2,
        table,
        spread(after(jnp.concatenate([layer_in, out_grad], axis=0), attend_got)) + gains,
    )

    attend_hop = attend_pieces[len(attend_pieces) // 2]
    moved = [
        place.send_z(
            early_in,
            [(s, s + k) for s in range(n) if s % GROUP < PROMPTS and s % GROUP + k < GROUP],
        )
        for k in range(1, GROUP)
    ]
    slots = [layer_in] * PROMPTS
    for i in range(PROMPTS):
        for k in range(1, GROUP):
            slots[i] = jnp.where(z_in == i + k, moved[k - 1], slots[i])
    pieces = []
    for i, slot in enumerate(slots):
        slot = after(slot, attend_got)
        if i % 2 == 0:
            by_x = place.swap_x(slot)
            late, late_x = lax.optimization_barrier((slot, by_x, attend_hop))[:2]
            pieces += [slot, by_x, place.swap_y(late), place.swap_y(late_x)]
        else:
            by_y = place.swap_y(slot)
            late, late_y = lax.optimization_barrier((slot, by_y, attend_hop))[:2]
            pieces += [slot, place.swap_x(late), by_y, place.swap_x(late_y)]
    (prompt,) = call(
        prompt_body,
        [((ny, PROMPTS * tokens, width), bf16)],
        table,
        over_cores(pieces) + [gain_in],
        scratch=[pltpu.VMEM(full, bf16)],
    )

    within = jnp.arange(block, dtype=jnp.int32)
    positions = jnp.minimum(place.offset, PROMPT_DEV)[:, None] * block + within[None, :]
    cosine, sine = rope_tables(positions.reshape(-1), HEAD_DIM // 2)
    far_cosine, far_sine = rope_tables(
        jnp.arange(PROMPTS * tokens, dtype=jnp.int32), HEAD_DIM // 2
    )
    tables = [cosine, sine, far_cosine, far_sine]
    query, own, far, attend_weights = call(
        qkv_body,
        [
            ((query_rows, tokens), bf16),
            ((kv_rows, tokens), bf16),
            ((kv_rows, PROMPTS * tokens), bf16),
            (attend_shape, bf16),
        ],
        table,
        [normed_in, prompt] + tables,
        [attend_pieces],
        [
            pltpu.VMEM((qkv_cols, tokens), f32),
            pltpu.VMEM((kv_rows, PROMPTS * tokens), f32),
            sems,
        ],
    )
    attended, attended_low, log_total, keep, *sends = call(
        attend_body,
        [
            ((query_rows, tokens), f32),
            ((query_rows, tokens), bf16),
            ((query_rows // HEAD_DIM, 1, tokens), f32),
        ]
        + wide,
        table,
        [query, own, far, attend_weights],
    )
    summed = all_sum(place, keep, sends, [forward_pieces[len(forward_pieces) // 2]])

    hidden, normed_mid, inverse_mid = call(
        hidden_body,
        [(full, f32), (full, bf16), ((tokens, 1), f32)],
        table,
        [raw] + summed + [gain_mid],
    )
    active, change, keep, *sends = call(
        forward_body,
        [((tokens, hidden_dev), bf16), ((tokens, 2 * hidden_dev), bf16)] + wide,
        table,
        [normed_mid, grad],
        [forward_pieces],
        [pltpu.VMEM(forward_shape, bf16), pltpu.VMEM((tokens, 2 * hidden_dev), f32)]
        + [pltpu.VMEM((tokens, hidden_dev), f32)] * 2
        + [sems],
    )
    forward_parts = call(
        forward_parts_body,
        [(forward_shape[1:], bf16)] * ny,
        table,
        [active, grad, normed_mid, change],
        scratch=[pltpu.VMEM(forward_shape[1:2] + (tokens,), bf16)],
    )
    forward_started = start_scatter(place, forward_parts)
    summed = all_sum(place, keep, sends, before_second=forward_parts[:1])
    forward_second = second_scatter(place, forward_started, summed[-1])
    hidden_own = own_block(place, hidden)
    through, pull, query_low, own_low, far_low, own_back, *returns, inner_first = call(
        attend_back_body,
        [
            (full, bf16),
            ((tokens, 1), f32),
            ((query_rows, tokens), bf16),
            ((kv_rows, tokens), bf16),
            ((kv_rows, PROMPTS * tokens), bf16),
            ((kv_rows, tokens), f32),
        ]
        + [((kv_rows, tokens), bf16)] * (GROUP - 1)
        + [((1, tokens), f32)],
        table,
        [hidden, inverse_mid]
        + summed
        + [
            grad,
            gain_mid,
            attend_weights,
            query,
            own,
            far,
            attended,
            log_total,
        ]
        + tables,
        earlier=forward_started[2:3] + forward_started[4:],
        scratch=[
            pltpu.VMEM((kv_rows, PROMPTS * tokens), f32),
            pltpu.VMEM(full, f32),
            pltpu.VMEM((query_rows, tokens), bf16),
        ],
    )
    keep, *sends = call(
        down_body,
        wide,
        table,
        [active],
        [forward_pieces],
        [pltpu.VMEM((ny, hidden_dev, width), bf16), sems],
        earlier=[through],
    )
    layer_out = (hidden_own + own_sum(place, keep, sends)).astype(bf16)
    inverse_own, _ = part_of(y, inverse_mid, 0)
    pull_own, _ = part_of(y, pull, 0)
    mid_own = jnp.where(place.x == 0, summed[0], summed[1])
    mid_own = part_of(y, mid_own, 0)[0].astype(f32)
    through_own = (
        out_grad.astype(f32)
        + inverse_own * mid_own * second_gain[None, :]
        - hidden_own * pull_own
    )
    second_term = jnp.sum(mid_own * hidden_own * inverse_own, axis=0)

    moved = [
        place.send_z(
            returns[k - 1],
            [(s, s - k) for s in range(n) if 0 <= s % GROUP - k < PROMPTS],
        )
        for k in range(1, GROUP)
    ]
    attend_parts = call(
        attend_parts_body,
        [(attend_shape[1:], bf16)] * ny,
        table,
        [query_low, own_low, far_low, normed_in, prompt, attended_low, through],
    )
    keep, *sends, inner = call(
        qkv_back_body,
        wide + [((1, tokens), f32)],
        table,
        [own_back] + moved + [query_low, attend_weights, cosine, sine, own, inner_first],
        earlier=forward_started[3:4] + ([forward_second] if lined else []),
    )
    attend_started = start_scatter(place, attend_parts)
    if lined:
        attend_second = second_scatter(place, attend_started, forward_second)
    else:
        attend_second = None
    forward_grad = end_scatter(place, forward_started, forward_second, sends[-1])
    attend_grad = end_scatter(place, attend_started, attend_second, sends[-1])
    inner = inner + place.swap_c(inner)
    inner = inner + place.swap_x(inner)
    inner = inner + place.swap_y(inner)
    first_own = own_sum(place, keep, sends)
    input_own = layer_in.astype(f32)
    inverse_own, _ = part_of(y, inverse_in, 0)
    scaled = first_own * first_gain[None, :]
    inner = part_of(y, inner.reshape(tokens, 1), 0)[0]
    in_grad = (
        through_own + inverse_own * scaled - input_own * (inverse_own**2 * inner / model_width)
    )
    first_term = jnp.sum(first_own * input_own * inverse_own, axis=0)
    terms = jnp.stack([first_term, second_term])
    bit = 1
    while bit < place.nx:
        terms = terms + place.swap_gx(terms, bit)
        bit *= 2

    def joined(summed_part, outs):
        mine, other = part_of(y, summed_part, 1)
        got = place.swap_y(other.astype(bf16))
        return call(
            join_body,
            [(m.shape, f32) for m in outs],
            table,
            [mine, got],
        )

    gate_grad, up_grad, down_grad = joined(forward_grad, (gate_weight, up_weight, down_weight))
    query_out, key_out, value_out, out_out = joined(
        attend_grad, (query_weight, key_matrix, value_matrix, out_weight)
    )
    return (
        layer_out,
        in_grad,
        terms[0],
        query_out,
        key_out,
        value_out,
        out_out,
        terms[1],
        gate_grad,
        up_grad,
        down_grad,
    )


def solution(mesh):
    rows, cols, gain = P("gx", "gy"), P("gy", "gx"), P("gy")
    return jax.shard_map(
        shards,
        mesh=mesh,
        in_specs=(rows, gain, rows, rows, rows, cols, gain, rows, rows, cols, rows),
        out_specs=(rows, rows, gain, rows, rows, rows, cols, gain, rows, rows, cols),
        check_vma=False,
    )
```

```python
import jax
import jax.numpy as jnp
from jax import lax
from jax.experimental import pallas as pl
from jax.experimental.pallas import tpu as pltpu
from jax.sharding import PartitionSpec as P

HEAD_DIM = 96
PROMPT_DEV = 4
CONT_DEV = 4
GROUP = (PROMPT_DEV + CONT_DEV) // 2
PROMPTS = PROMPT_DEV // 2

eps = 1e-05
neg_big = -1e30
rope_base = 100000.0
score_scale = HEAD_DIM ** (-0.5)
f32 = jnp.float32
bf16 = jnp.bfloat16


def dims(left, right, left_axis, right_axis):
    return lax.dot_general(
        left, right, (((left_axis,), (right_axis,)), ((), ())), preferred_element_type=f32
    )


class Place:
    def __init__(self):
        self.nx = lax.axis_size("gx")
        self.ny = lax.axis_size("gy")
        assert self.ny == 4 and self.nx % (PROMPT_DEV + CONT_DEV) == 0
        self.n = self.nx // 2
        self.gx = lax.axis_index("gx")
        self.gy = lax.axis_index("gy")
        self.z, self.y = self.gx // 2, self.gx % 2
        self.x, self.c = self.gy // 2, self.gy % 2
        self.z_in = self.z % GROUP
        offset = 2 * self.z_in + jnp.arange(2, dtype=jnp.int32)
        self.offset = offset
        self.lined = self.n == self.ny
        blocks = jnp.arange(self.ny, dtype=jnp.int32)
        first = jnp.stack([self.z, self.y, self.x, self.c, self.z_in]).astype(jnp.int32)
        self.table = jnp.concatenate(
            [first, jnp.minimum(offset, PROMPT_DEV), blocks ^ self.z if self.lined else blocks]
        )

    def swap_gx(self, value, bit):
        return lax.ppermute(value, "gx", [(i, i ^ bit) for i in range(self.nx)])

    def swap_y(self, value):
        return self.swap_gx(value, 1)

    def swap_x(self, value):
        return lax.ppermute(value, "gy", [(i, i ^ 2) for i in range(self.ny)])

    def swap_c(self, value):
        return lax.ppermute(value, "gy", [(i, i ^ 1) for i in range(self.ny)])

    def send_z(self, value, moves):
        pairs = [(2 * s + y, 2 * t + y) for s, t in moves for y in range(2)]
        return lax.ppermute(value, "gx", pairs)

    def by_y(self):
        return [[2 * z + y for z in range(self.n)] for y in range(2)]


def pair(flag, mine, other):
    return jnp.where(flag == 0, mine, other), jnp.where(flag == 0, other, mine)


def part_of(flag, whole, axis):
    low, high = jnp.split(whole, 2, axis)
    return jnp.where(flag == 0, low, high), jnp.where(flag == 0, high, low)


def after(value, *earlier):
    return lax.optimization_barrier((value,) + earlier)[0]


NEAR = [(0, 1), (1, 0), (2, 3), (3, 2)]
SECOND = [(0, 2), (1, 3), (2, 0), (3, 1)]
MIDDLE = [(1, 2), (2, 1)]
INWARD = [(0, 1), (3, 2)]
OUTWARD = [(1, 0), (2, 3)]


def gather_pieces(place, piece, late_middle=False):
    second = place.send_z(piece, SECOND)
    near = place.send_z(piece, NEAR)
    middle = place.send_z(after(piece, second) if late_middle else piece, MIDDLE)
    return [piece, near, second, middle, place.send_z(second, OUTWARD)]


def gather_whole(place, piece):
    every = lax.all_gather(piece, "gx", axis_index_groups=place.by_y())
    inner = place.n // place.ny
    if inner == 1:
        return every
    rows, cols = piece.shape
    every = every.reshape(place.ny, inner, rows, cols)
    return jnp.swapaxes(every, 1, 2).reshape(place.ny, rows, inner * cols)


def scatter_whole(place, parts):
    inner = place.n // place.ny
    if inner > 1:
        count, rows, cols = parts.shape
        parts = jnp.swapaxes(parts.reshape(count, rows, inner, cols // inner), 1, 2)
        parts = parts.reshape(place.n, rows, cols // inner)
    return lax.psum_scatter(parts, "gx", axis_index_groups=place.by_y())


def start_scatter(place, parts):
    if not place.lined:
        return [scatter_whole(place, jnp.stack(parts))]
    own, near, second, third = parts
    far = place.send_z(third, INWARD)
    middle = place.send_z(third, MIDDLE)
    return [own, second, far, place.send_z(near, NEAR), middle]


def second_scatter(place, started, *earlier):
    if not place.lined:
        return None
    second = after(started[1], *earlier)
    return place.send_z((second.astype(f32) + started[2].astype(f32)).astype(bf16), SECOND)


def end_scatter(place, started, second, *earlier):
    if not place.lined:
        return started[0].astype(f32)
    own, near, middle = after(started[0], *earlier), started[3], started[4]
    return own.astype(f32) + near.astype(f32) + middle.astype(f32) + second.astype(f32)


def reduce_core(place, keep, sends):
    return [keep[i] + place.swap_c(send).astype(f32) for i, send in enumerate(sends)]


def all_sum(place, keep, sends, before_first=(), before_second=()):
    first, second = reduce_core(place, keep, sends)
    low = (first.astype(bf16), second.astype(bf16))
    low = lax.optimization_barrier(low + tuple(before_first))
    first, second = (
        first + place.swap_x(low[0]).astype(f32),
        second + place.swap_y(low[1]).astype(f32),
    )
    low = (first.astype(bf16), second.astype(bf16))
    low = lax.optimization_barrier(low + tuple(before_second))
    own = [
        (first + place.swap_y(low[0]).astype(f32)).astype(bf16),
        (second + place.swap_x(low[1]).astype(f32)).astype(bf16),
    ]
    return own + [place.swap_c(part) for part in own]


def own_sum(place, keep, sends):
    first, second = reduce_core(place, keep, sends)
    mine, other = jnp.where(place.x == 0, first, second), jnp.where(place.x == 0, second, first)
    mine = mine + place.swap_x(other.astype(bf16)).astype(f32)
    mine, other = part_of(place.y, mine, 0)
    return mine + place.swap_y(other.astype(bf16)).astype(f32)


def own_block(place, blocks):
    rows = blocks.shape[1] // 2
    return lax.dynamic_slice(
        blocks, (place.gy, place.y * rows, 0), (1, rows, blocks.shape[2])
    )[0]


Z, Y, X, C, Z_IN, COUNT = range(6)
ORDER = COUNT + 2


def call(body, outs, table, operands, pieces=(), scratch=(), earlier=(), limit=24):
    lengths = [len(p) for p in pieces]
    flat = [a for p in pieces for a in p] + list(earlier)
    vmem = pl.BlockSpec(memory_space=pltpu.VMEM)

    def kernel(table_ref, *refs):
        plain, rest = refs[: len(operands)], refs[len(operands) :]
        lists = []
        for length in lengths:
            lists.append(rest[:length])
            rest = rest[length:]
        rest = rest[len(earlier) :]
        body(table_ref, *plain, *lists, *rest)

    return pl.pallas_call(
        kernel,
        out_shape=[jax.ShapeDtypeStruct(shape, dtype) for shape, dtype in outs],
        in_specs=[pl.BlockSpec(memory_space=pltpu.SMEM)]
        + [vmem] * len(operands)
        + [pl.BlockSpec(memory_space=pl.ANY)] * len(flat),
        out_specs=[vmem] * len(outs),
        scratch_shapes=list(scratch),
        compiler_params=pltpu.CompilerParams(vmem_limit_bytes=limit << 20),
    )(table, *operands, *flat)


def start_pieces(table, pieces, whole, sems, rows=slice(None)):
    count = whole.shape[0]
    block = [table[ORDER + k] for k in range(count)]

    def copy(piece, k):
        source = piece.at[rows] if rows != slice(None) else piece
        return pltpu.make_async_copy(source, whole.at[block[k]], sems.at[k])

    def wait(k):
        pltpu.make_async_copy(whole.at[0], whole.at[0], sems.at[k]).wait()

    if len(pieces) == 1:
        for k in range(count):
            copy(pieces[0].at[block[k]], k).start()
        return wait
    z = table[Z]
    own, near, second, middle, end = pieces
    for k, piece in enumerate((own, near, second)):
        copy(piece, k).start()
    inside = jnp.logical_or(z == 1, z == 2)

    @pl.when(inside)
    def _():
        copy(middle, 3).start()

    @pl.when(jnp.logical_not(inside))
    def _():
        copy(end, 3).start()

    return wait


def keep_and_send(table, block_of, keep, sends):
    core = table[C]
    for i, send in enumerate(sends):
        keep[i] = block_of(2 * i + core)
        send[...] = block_of(2 * i + 1 - core).astype(bf16)


def place_rows(table, pieces, whole):
    x, y, c = table[X], table[Y], table[C]
    tokens = pieces[0].shape[0]
    for dc in range(2):
        for dx in range(2):
            block = 2 * (x + dx - 2 * x * dx) + c + dc - 2 * c * dc
            for dy in range(2):
                at = pl.ds(pl.multiple_of(tokens * (y + dy - 2 * y * dy), tokens), tokens)
                whole[block, at, :] = pieces[4 * dc + 2 * dy + dx][...]


def grad_body(table, *refs):
    place_rows(table, refs[:8], refs[8])


def norm_rows(raw, gain, normed):
    def square(b, total):
        values = raw[b].astype(f32)
        return total + jnp.sum(values * values, axis=1, keepdims=True)

    count = raw.shape[0]
    total = lax.fori_loop(0, count, square, jnp.zeros((raw.shape[1], 1), f32))
    scale = lax.rsqrt(total / (count * raw.shape[2]) + eps)

    def norm(b, _):
        normed[b] = (raw[b].astype(f32) * scale * gain[b]).astype(bf16)
        return 0

    lax.fori_loop(0, count, norm, 0)
    return scale


def rows_body(table, *refs):
    gains = refs[8:12]
    raw, normed, inverse, gain_first, gain_second = refs[12:]
    place_rows(table, refs[:8], raw)
    x, c = table[X], table[C]
    for dc in range(2):
        for dx in range(2):
            block = 2 * (x + dx - 2 * x * dx) + c + dc - 2 * c * dc
            gain = gains[2 * dc + dx][...]
            gain_first[block] = gain[0:1]
            gain_second[block] = gain[1:2]
    inverse[...] = norm_rows(raw, gain_first, normed)


def turn(values, cosine, sine):
    half = values.shape[0] // 2
    first, second = values[:half], values[half:]
    return jnp.concatenate(
        [first * cosine - second * sine, second * cosine + first * sine], axis=0
    )


def qkv_body(
    table, normed, cosine, sine, pieces, query, own, weights, acc, sems
):
    wait = start_pieces(table, pieces, weights, sems)
    count = acc.shape[0]
    acc[...] = jnp.zeros_like(acc)

    def one(k, _):
        b = table[ORDER + k]
        wait(k)
        acc[...] += dims(weights[b, :count], normed[b], 1, 1)
        return 0

    lax.fori_loop(0, normed.shape[0], one, 0)
    head = HEAD_DIM
    heads = query.shape[0] // head
    cos, sin = cosine[...], sine[...]
    for h in range(heads):
        at = slice(h * head, (h + 1) * head)
        query[at] = turn(acc[at], cos, sin).astype(bf16)
    at = slice(heads * head, (heads + 1) * head)
    own[:head] = turn(acc[at], cos, sin).astype(bf16)
    own[head:] = acc[(heads + 1) * head :].astype(bf16)


def attend_body(table, query, own, *refs):
    moved, refs = refs[: GROUP - 1], refs[GROUP - 1 :]
    weights, attended, attended_low, log_total, far, keep, first_send, second_send = refs
    tokens = own.shape[1]
    for place in range(GROUP):

        @pl.when(table[Z_IN] == place)
        def _():
            for slot in range(PROMPTS):
                k = place - slot
                far[:, slot * tokens : (slot + 1) * tokens] = (
                    moved[k - 1][...] if k > 0 else own[...]
                )

    head = HEAD_DIM
    block = tokens // 2
    key_far, value_far = far[:head].T, far[head:]
    key_own = own[:head].T
    total = far.shape[1]
    near_row = lax.broadcasted_iota(jnp.int32, (block, block), 0)
    near_col = lax.broadcasted_iota(jnp.int32, (block, block), 1)
    causal = near_row <= near_col
    row = lax.broadcasted_iota(jnp.int32, (total, block), 0)
    for part in range(2):
        cols = slice(part * block, (part + 1) * block)
        key_near, value_near = key_own[cols], own[head:, cols]
        seen = row < table[COUNT + part] * block

        def one(h, _):
            at = pl.ds(pl.multiple_of(h * head, head), head)
            rows = query[at, cols]
            score_far = jnp.where(seen, dims(key_far, rows, 1, 0) * score_scale, neg_big)
            score_near = jnp.where(causal, dims(key_near, rows, 1, 0) * score_scale, neg_big)
            top = jnp.maximum(
                jnp.max(score_far, axis=0, keepdims=True), jnp.max(score_near, axis=0, keepdims=True)
            )
            weight_far = jnp.exp(score_far - top)
            weight_near = jnp.exp(score_near - top)
            weight = jnp.sum(weight_far, axis=0, keepdims=True) + jnp.sum(
                weight_near, axis=0, keepdims=True
            )
            out = dims(value_far, weight_far.astype(bf16), 1, 0) + dims(
                value_near, weight_near.astype(bf16), 1, 0
            )
            attended[at, cols] = out / weight
            log_total[h, :, cols] = top + jnp.log(weight)
            return 0

        lax.fori_loop(0, query.shape[0] // head, one, 0)
    values = attended[...]
    attended_low[...] = values.astype(bf16)
    flipped = values.T.astype(bf16)
    first = weights.shape[1] - query.shape[0]
    keep_and_send(
        table,
        lambda b: dims(flipped, weights[b, first:], 1, 0),
        keep,
        (first_send, second_send),
    )


def hidden_body(
    table, raw, own_first, own_second, other_first, other_second, gain, hidden, normed, inverse
):
    core = table[C]
    summed, other = (own_first, own_second), (other_first, other_second)
    for i in range(2):
        b = 2 * i + core
        hidden[b] = raw[b].astype(f32) + summed[i][...].astype(f32)
        b = 2 * i + 1 - core
        hidden[b] = raw[b].astype(f32) + other[i][...].astype(f32)

    def square(b, total):
        values = hidden[b]
        return total + jnp.sum(values * values, axis=1, keepdims=True)

    count = raw.shape[0]
    total = lax.fori_loop(0, count, square, jnp.zeros((raw.shape[1], 1), f32))
    scale = lax.rsqrt(total / (count * raw.shape[2]) + eps)
    inverse[...] = scale

    def norm(b, _):
        normed[b] = (hidden[b] * scale * gain[b]).astype(bf16)
        return 0

    lax.fori_loop(0, count, norm, 0)


def forward_body(
    table,
    normed,
    grad,
    pieces,
    active,
    change,
    keep,
    first_send,
    second_send,
    weights,
    acc,
    gate_slope,
    up_slope,
    sems,
):
    wait = start_pieces(table, pieces, weights, sems)
    count, tokens = normed.shape[:2]
    width = acc.shape[1]
    half = width // 2
    acc[...] = jnp.zeros_like(acc)

    def one(k, _):
        b = table[ORDER + k]
        wait(k)
        acc[...] += dims(normed[b], weights[b, :width], 1, 1)
        return 0

    lax.fori_loop(0, count, one, 0)
    rows = tokens // 4

    def part(i, _):
        at = pl.ds(pl.multiple_of(i * rows, rows), rows)
        gate, up = acc[at, :half], acc[at, half:]
        sigmoid = jax.nn.sigmoid(gate)
        active[at] = (gate * sigmoid * up).astype(bf16)
        gate_slope[at] = up * sigmoid * (1.0 + gate * (1.0 - sigmoid))
        up_slope[at] = gate * sigmoid
        return 0

    lax.fori_loop(0, 4, part, 0)

    def back(b, total):
        return total + dims(grad[b], weights[b, width:], 1, 1)

    slope = lax.fori_loop(0, count, back, jnp.zeros((tokens, half), f32))
    change[:, :half] = (slope * gate_slope[...]).astype(bf16)
    change[:, half:] = (slope * up_slope[...]).astype(bf16)
    values = change[...]
    keep_and_send(
        table,
        lambda b: dims(values, weights[b, :width], 1, 0),
        keep,
        (first_send, second_send),
    )


def forward_parts_body(table, active, grad, normed, change, *refs):
    parts, flipped = refs[:-1], refs[-1]
    width = change.shape[1]
    flipped[:width] = change[...].T
    flipped[width:] = active[...].T
    rows = width // 4

    def fill(first, count, source):
        def one(i, _):
            at = pl.ds(pl.multiple_of((first + i) * rows, rows), rows)
            for k, part in enumerate(parts):
                part[at] = dims(flipped[at], source[table[ORDER + k]], 1, 0).astype(bf16)
            return 0

        lax.fori_loop(0, count, one, 0)

    fill(0, 4, normed)
    fill(4, flipped.shape[0] // rows - 4, grad)


def down_body(table, active, pieces, keep, first_send, second_send, weights, sems):
    rows = weights.shape[1]
    wait = start_pieces(table, pieces, weights, sems, slice(2 * rows, 3 * rows))
    for k in range(weights.shape[0]):
        wait(k)
    values = active[...]
    keep_and_send(
        table, lambda b: dims(values, weights[b], 1, 0), keep, (first_send, second_send)
    )


def attend_back_body(
    table,
    hidden,
    inverse,
    own_first,
    own_second,
    other_first,
    other_second,
    grad,
    gain,
    weights,
    query,
    own,
    far,
    attended,
    log_total,
    cosine,
    sine,
    through,
    pull,
    query_low,
    own_back,
    *rest,
):
    sends, inner_first = rest[: GROUP - 1], rest[GROUP - 1]
    far_back, change, branch = rest[GROUP:]
    core = table[C]
    count, tokens, model = hidden.shape
    for i, (mine, theirs) in enumerate(((own_first, other_first), (own_second, other_second))):
        change[2 * i + core] = mine[...].astype(f32) * gain[2 * i + core]
        change[2 * i + 1 - core] = theirs[...].astype(f32) * gain[2 * i + 1 - core]

    def product(b, total):
        return total + jnp.sum(change[b] * hidden[b], axis=1, keepdims=True)

    inner = lax.fori_loop(0, count, product, jnp.zeros((tokens, 1), f32))
    scale = inverse[...]
    back = scale * scale * scale * inner / (count * model)
    pull[...] = back

    def rows(b, total):
        values = grad[b].astype(f32) + scale * change[b] - hidden[b] * back
        low = values.astype(bf16)
        through[b] = low
        return total + dims(low, weights[b, first:], 1, 1)

    heads_cols = query.shape[0]
    first = weights.shape[1] - heads_cols
    total_rows = lax.fori_loop(0, count, rows, jnp.zeros((tokens, heads_cols), f32))
    branch[...] = total_rows.T.astype(bf16)

    head = HEAD_DIM
    block = tokens // 2
    key_far_t = far[:head]
    key_far, value_far = key_far_t.T, far[head:].T
    key_own, value_own = own[:head].T, own[head:].T
    total = far.shape[1]
    near_row = lax.broadcasted_iota(jnp.int32, (block, block), 0)
    near_col = lax.broadcasted_iota(jnp.int32, (block, block), 1)
    causal = near_row <= near_col
    row = lax.broadcasted_iota(jnp.int32, (total, block), 0)
    far_back[...] = jnp.zeros_like(far_back)
    own_back[...] = jnp.zeros_like(own_back)
    inner_first[...] = jnp.zeros_like(inner_first)
    for part in range(2):
        cols = slice(part * block, (part + 1) * block)
        key_near, value_near = key_own[cols], value_own[cols]
        key_near_t = own[:head, cols]
        seen = row < table[COUNT + part] * block

        def one_head(h, _):
            at = pl.ds(pl.multiple_of(h * head, head), head)
            rows_q, rows_grad = query[at, cols], branch[at, cols]
            delta = jnp.sum(
                rows_grad.astype(f32) * attended[at, cols], axis=0, keepdims=True
            )
            logs = log_total[h, :, cols]

            def one(key, value, allowed):
                score = dims(key, rows_q, 1, 0) * score_scale
                prob = jnp.where(allowed, jnp.exp(score - logs), 0.0)
                moved = (prob * (dims(value, rows_grad, 1, 0) - delta)).astype(bf16)
                return prob.astype(bf16), moved

            prob_far, moved_far = one(key_far, value_far, seen)
            prob_near, moved_near = one(key_near, value_near, causal)
            query_back = (
                dims(key_far_t, moved_far, 1, 0) + dims(key_near_t, moved_near, 1, 0)
            ) * score_scale
            inner_first[:, cols] += jnp.sum(
                query_back * rows_q.astype(f32), axis=0, keepdims=True
            )
            query_low[at, cols] = turn(query_back, cosine[:, cols], -sine[:, cols]).astype(bf16)
            far_back[:head] += dims(rows_q, moved_far, 1, 1) * score_scale
            far_back[head:] += dims(rows_grad, prob_far, 1, 1)
            own_back[:head, cols] += dims(rows_q, moved_near, 1, 1) * score_scale
            own_back[head:, cols] += dims(rows_grad, prob_near, 1, 1)
            return 0

        lax.fori_loop(0, heads_cols // head, one_head, 0)
    for slot in range(PROMPTS):

        @pl.when(table[Z_IN] == slot)
        def _():
            own_back[...] += far_back[:, slot * tokens : (slot + 1) * tokens]

    for k in range(1, GROUP):
        sends[k - 1][...] = far_back[:, :tokens].astype(bf16)
        for slot in range(1, PROMPTS):

            @pl.when(table[Z_IN] == slot + k)
            def _():
                sends[k - 1][...] = far_back[:, slot * tokens : (slot + 1) * tokens].astype(bf16)


def attend_parts_body(table, query_low, own_low, normed, attended_low, through, *parts):
    first = query_low.shape[0]
    second = first + own_low.shape[0]
    for k, part in enumerate(parts):
        b = table[ORDER + k]
        part[:first] = dims(query_low[...], normed[b], 1, 0).astype(bf16)
        part[first:second] = dims(own_low[...], normed[b], 1, 0).astype(bf16)
        part[second:] = dims(attended_low[...], through[b], 1, 0).astype(bf16)


def qkv_back_body(table, own_back, *refs):
    moved, refs = refs[: GROUP - 1], refs[GROUP - 1 :]
    query_low, weights, cosine, sine, own, inner = refs[:6]
    keep, first_send, second_send, inner_first, own_low = refs[6:]
    head = HEAD_DIM
    total = own_back[...]
    for part in moved:
        total = total + part[...].astype(f32)
    inner_first[...] = inner[...] + jnp.sum(total * own[...].astype(f32), axis=0, keepdims=True)
    key = turn(total[:head], cosine[...], -sine[...])
    low = jnp.concatenate([key, total[head:]], axis=0)
    own_low[...] = low.astype(bf16)
    flipped = jnp.concatenate([query_low[...].T, low.T.astype(bf16)], axis=1)
    width = flipped.shape[1]
    keep_and_send(
        table,
        lambda b: dims(flipped, weights[b, :width], 1, 0),
        keep,
        (first_send, second_send),
    )


def halves_of(table, whole):
    half = whole.shape[0] // 2
    low, high = whole[:half], whole[half:]
    flag = table[Y] == 0
    return jnp.where(flag, low, high), jnp.where(flag, high, low)


def split_body(table, matrices, mine_ref, other_ref, *scratch):
    copies = [
        pltpu.make_async_copy(source, held, scratch[-1].at[i])
        for i, (source, held) in enumerate(zip(matrices, scratch))
    ]
    for copy in copies:
        copy.start()
    at = 0
    for i, copy in enumerate(copies):
        copy.wait()
        whole = scratch[i][...]
        if i < len(copies) - 1:
            whole = whole.T
        mine, other = halves_of(table, whole)
        rows = mine.shape[0]
        mine_ref[at : at + rows] = mine
        other_ref[at : at + rows] = other
        at += rows


def join_body(table, mine, got, *outs):
    flag = table[Y] == 0
    at = 0
    for i, out in enumerate(outs):
        turned = i < len(outs) - 1
        rows = out.shape[1 if turned else 0] // 2
        parts = mine[at : at + rows].astype(f32), got[at : at + rows].astype(f32)
        at += rows
        low, high = jnp.where(flag, parts[0], parts[1]), jnp.where(flag, parts[1], parts[0])
        if turned:
            out[:, :rows] = low.T
            out[:, rows:] = high.T
        else:
            out[:rows] = low
            out[rows:] = high


def rope_tables(positions, half):
    freq = rope_base ** (-(2.0 * jnp.arange(half, dtype=f32)) / (2.0 * half))
    angle = freq[:, None] * positions.astype(f32)[None, :]
    return (jnp.cos(angle), jnp.sin(angle))


def shards(
    layer_in,
    first_gain,
    query_weight,
    key_matrix,
    value_matrix,
    out_weight,
    second_gain,
    gate_weight,
    up_weight,
    down_weight,
    out_grad,
):
    place = Place()
    n, ny, y, z_in, table = place.n, place.ny, place.y, place.z_in, place.table
    lined = place.lined
    block, width = layer_in.shape
    tokens = 2 * block
    model_width = width * ny
    hidden_dev = gate_weight.shape[1] // 2
    query_rows = query_weight.shape[1] // 2
    kv_rows = key_matrix.shape[1]
    qkv_cols = query_rows + kv_rows
    full = (ny, tokens, width)
    wide = [((2,) + full[1:], f32), (full[1:], bf16), (full[1:], bf16)]

    def halves(*matrices):
        rows = sum(max(m.shape) for m in matrices) // 2
        cols = min(matrices[0].shape)
        return call(
            split_body,
            [((rows, cols), bf16)] * 2,
            table,
            [],
            [matrices],
            [pltpu.VMEM(m.shape, bf16) for m in matrices]
            + [pltpu.SemaphoreType.DMA((len(matrices),))],
        )

    def whole_piece(mine, got):
        return jnp.concatenate(pair(y, mine, got), axis=1)

    def spread(value):
        by_x = place.swap_x(value)
        four = [value, by_x, place.swap_y(value), place.swap_y(by_x)]
        return four + [place.swap_c(r) for r in four]

    mine, other = halves(query_weight, key_matrix, value_matrix, out_weight)
    attend_got = place.swap_y(other)
    attend_piece = whole_piece(mine, attend_got)
    input_rows = spread(after(layer_in, other))
    mine, other = halves(gate_weight, up_weight, down_weight)
    forward_piece = whole_piece(mine, place.swap_y(after(other, attend_got, input_rows[3])))
    if lined:
        attend_pieces = gather_pieces(place, attend_piece)
        forward_pieces = gather_pieces(place, after(forward_piece, *attend_pieces[1:]), True)
    else:
        attend_pieces = [gather_whole(place, attend_piece)]
        forward_pieces = [gather_whole(place, forward_piece)]
    attend_shape = (ny, qkv_cols + query_rows, width)
    forward_shape = (ny, 3 * hidden_dev, width)
    sems = pltpu.SemaphoreType.DMA((ny,))

    gains = jnp.stack([first_gain, second_gain])
    two = [gains, place.swap_x(gains)]
    gains = two + [place.swap_c(g) for g in two]
    raw, normed_in, inverse_in, gain_in, gain_mid = call(
        rows_body,
        [(full, bf16)] * 2 + [((tokens, 1), f32)] + [((ny, 1, width), f32)] * 2,
        table,
        input_rows + gains,
    )

    within = jnp.arange(block, dtype=jnp.int32)
    positions = jnp.minimum(place.offset, PROMPT_DEV)[:, None] * block + within[None, :]
    cosine, sine = rope_tables(positions.reshape(-1), HEAD_DIM // 2)
    query, own, attend_weights = call(
        qkv_body,
        [((query_rows, tokens), bf16), ((kv_rows, tokens), bf16), (attend_shape, bf16)],
        table,
        [normed_in, cosine, sine],
        [attend_pieces],
        [pltpu.VMEM((qkv_cols, tokens), f32), sems],
    )
    moved = [
        place.send_z(
            own,
            [(s, s + k) for s in range(n) if s % GROUP < PROMPTS and s % GROUP + k < GROUP],
        )
        for k in range(1, GROUP)
    ]
    (grad,) = call(grad_body, [(full, bf16)], table, spread(after(out_grad, query)))
    attended, attended_low, log_total, far, keep, *sends = call(
        attend_body,
        [
            ((query_rows, tokens), f32),
            ((query_rows, tokens), bf16),
            ((query_rows // HEAD_DIM, 1, tokens), f32),
            ((kv_rows, PROMPTS * tokens), bf16),
        ]
        + wide,
        table,
        [query, own] + moved + [attend_weights],
    )
    summed = all_sum(place, keep, sends, [forward_pieces[len(forward_pieces) // 2]])

    hidden, normed_mid, inverse_mid = call(
        hidden_body,
        [(full, f32), (full, bf16), ((tokens, 1), f32)],
        table,
        [raw] + summed + [gain_mid],
    )
    active, change, keep, *sends = call(
        forward_body,
        [((tokens, hidden_dev), bf16), ((tokens, 2 * hidden_dev), bf16)] + wide,
        table,
        [normed_mid, grad],
        [forward_pieces],
        [pltpu.VMEM(forward_shape, bf16), pltpu.VMEM((tokens, 2 * hidden_dev), f32)]
        + [pltpu.VMEM((tokens, hidden_dev), f32)] * 2
        + [sems],
    )
    forward_parts = call(
        forward_parts_body,
        [(forward_shape[1:], bf16)] * ny,
        table,
        [active, grad, normed_mid, change],
        scratch=[pltpu.VMEM(forward_shape[1:2] + (tokens,), bf16)],
    )
    forward_started = start_scatter(place, forward_parts)
    summed = all_sum(place, keep, sends, before_second=forward_parts[:1])
    forward_second = second_scatter(place, forward_started, summed[-1])
    hidden_own = own_block(place, hidden)
    through, pull, query_low, own_back, *returns, inner_first = call(
        attend_back_body,
        [
            (full, bf16),
            ((tokens, 1), f32),
            ((query_rows, tokens), bf16),
            ((kv_rows, tokens), f32),
        ]
        + [((kv_rows, tokens), bf16)] * (GROUP - 1)
        + [((1, tokens), f32)],
        table,
        [hidden, inverse_mid]
        + summed
        + [
            grad,
            gain_mid,
            attend_weights,
            query,
            own,
            far,
            attended,
            log_total,
            cosine,
            sine,
        ],
        earlier=forward_started[2:3] + forward_started[4:],
        scratch=[
            pltpu.VMEM((kv_rows, PROMPTS * tokens), f32),
            pltpu.VMEM(full, f32),
            pltpu.VMEM((query_rows, tokens), bf16),
        ],
    )
    inverse_own, _ = part_of(y, inverse_mid, 0)
    pull_own, _ = part_of(y, pull, 0)
    mid_own = jnp.where(place.x == 0, summed[0], summed[1])
    mid_own = part_of(y, mid_own, 0)[0].astype(f32)
    through_own = (
        out_grad.astype(f32)
        + inverse_own * mid_own * second_gain[None, :]
        - hidden_own * pull_own
    )
    second_term = jnp.sum(mid_own * hidden_own * inverse_own, axis=0)

    moved = [
        place.send_z(
            returns[k - 1],
            [(s, s - k) for s in range(n) if 0 <= s % GROUP - k < PROMPTS],
        )
        for k in range(1, GROUP)
    ]
    keep, *sends, inner, own_low = call(
        qkv_back_body,
        wide + [((1, tokens), f32), ((kv_rows, tokens), bf16)],
        table,
        [own_back] + moved + [query_low, attend_weights, cosine, sine, own, inner_first],
        earlier=forward_started[3:4] + ([forward_second] if lined else []),
    )
    attend_parts = call(
        attend_parts_body,
        [(attend_shape[1:], bf16)] * ny,
        table,
        [query_low, own_low, normed_in, attended_low, through],
    )
    attend_started = start_scatter(place, attend_parts)
    if lined:
        attend_second = second_scatter(place, attend_started, forward_second)
    else:
        attend_second = None
    forward_grad = end_scatter(place, forward_started, forward_second, own_low)
    attend_grad = end_scatter(place, attend_started, attend_second, own_low)
    inner = inner + place.swap_c(inner)
    inner = inner + place.swap_x(inner)
    inner = inner + place.swap_y(inner)
    first_own = own_sum(place, keep, sends)
    input_own = layer_in.astype(f32)
    inverse_own, _ = part_of(y, inverse_in, 0)
    scaled = first_own * first_gain[None, :]
    inner = part_of(y, inner.reshape(tokens, 1), 0)[0]
    in_grad = (
        through_own + inverse_own * scaled - input_own * (inverse_own**2 * inner / model_width)
    )
    first_term = jnp.sum(first_own * input_own * inverse_own, axis=0)
    terms = jnp.stack([first_term, second_term])
    bit = 1
    while bit < place.nx:
        terms = terms + place.swap_gx(terms, bit)
        bit *= 2

    keep, *sends = call(
        down_body,
        wide,
        table,
        [active],
        [forward_pieces],
        [pltpu.VMEM((ny, hidden_dev, width), bf16), sems],
        earlier=[own_low],
    )
    layer_out = (hidden_own + own_sum(place, keep, sends)).astype(bf16)

    def joined(summed_part, outs):
        mine, other = part_of(y, summed_part, 1)
        got = place.swap_y(other.astype(bf16))
        return call(
            join_body,
            [(m.shape, f32) for m in outs],
            table,
            [mine, got],
        )

    gate_grad, up_grad, down_grad = joined(forward_grad, (gate_weight, up_weight, down_weight))
    query_out, key_out, value_out, out_out = joined(
        attend_grad, (query_weight, key_matrix, value_matrix, out_weight)
    )
    return (
        layer_out,
        in_grad,
        terms[0],
        query_out,
        key_out,
        value_out,
        out_out,
        terms[1],
        gate_grad,
        up_grad,
        down_grad,
    )


def solution(mesh):
    rows, cols, gain = P("gx", "gy"), P("gy", "gx"), P("gy")
    return jax.shard_map(
        shards,
        mesh=mesh,
        in_specs=(rows, gain, rows, rows, rows, cols, gain, rows, rows, cols, rows),
        out_specs=(rows, rows, gain, rows, rows, rows, cols, gain, rows, rows, cols),
        check_vma=False,
    )
```

```python
from functools import partial

import jax
import jax.numpy as jnp
from jax import lax
from jax.experimental import pallas as pl
from jax.experimental.pallas import tpu as pltpu
from jax.sharding import PartitionSpec as P

HEAD_DIM = 96
PROMPT_DEV = 4
CONT_DEV = 4
GROUP = (PROMPT_DEV + CONT_DEV) // 2
PROMPTS = PROMPT_DEV // 2

eps = 1e-05
neg_big = -1e30
rope_base = 100000.0
score_scale = HEAD_DIM ** (-0.5)
f32 = jnp.float32
bf16 = jnp.bfloat16


def dims(left, right, left_axis, right_axis):
    return lax.dot_general(
        left, right, (((left_axis,), (right_axis,)), ((), ())), preferred_element_type=f32
    )


class Place:
    def __init__(self):
        self.nx = lax.axis_size("gx")
        self.ny = lax.axis_size("gy")
        assert self.ny == 4 and self.nx % (PROMPT_DEV + CONT_DEV) == 0
        self.n = self.nx // 2
        self.gx = lax.axis_index("gx")
        self.gy = lax.axis_index("gy")
        self.z, self.y = self.gx // 2, self.gx % 2
        self.x, self.c = self.gy // 2, self.gy % 2
        self.z_in = self.z % GROUP
        offset = 2 * self.z_in + jnp.arange(2, dtype=jnp.int32)
        self.offset = offset
        self.lined = self.n == self.ny
        blocks = jnp.arange(self.ny, dtype=jnp.int32)
        first = jnp.stack([self.z, self.y, self.x, self.c, self.z_in]).astype(jnp.int32)
        self.table = jnp.concatenate(
            [first, jnp.minimum(offset, PROMPT_DEV), blocks ^ self.z if self.lined else blocks]
        )

    def swap_gx(self, value, bit):
        return lax.ppermute(value, "gx", [(i, i ^ bit) for i in range(self.nx)])

    def swap_y(self, value):
        return self.swap_gx(value, 1)

    def swap_x(self, value):
        return lax.ppermute(value, "gy", [(i, i ^ 2) for i in range(self.ny)])

    def swap_c(self, value):
        return lax.ppermute(value, "gy", [(i, i ^ 1) for i in range(self.ny)])

    def send_z(self, value, moves):
        pairs = [(2 * s + y, 2 * t + y) for s, t in moves for y in range(2)]
        return lax.ppermute(value, "gx", pairs)

    def by_y(self):
        return [[2 * z + y for z in range(self.n)] for y in range(2)]


def pair(flag, mine, other):
    return jnp.where(flag == 0, mine, other), jnp.where(flag == 0, other, mine)


def part_of(flag, whole, axis):
    low, high = jnp.split(whole, 2, axis)
    return jnp.where(flag == 0, low, high), jnp.where(flag == 0, high, low)


def after(value, *earlier):
    return lax.optimization_barrier((value,) + earlier)[0]


NEAR = [(0, 1), (1, 0), (2, 3), (3, 2)]
SECOND = [(0, 2), (1, 3), (2, 0), (3, 1)]
MIDDLE = [(1, 2), (2, 1)]
INWARD = [(0, 1), (3, 2)]
OUTWARD = [(1, 0), (2, 3)]


def gather_pieces(place, piece, late_middle=False):
    second = place.send_z(piece, SECOND)
    near = place.send_z(piece, NEAR)
    middle = place.send_z(after(piece, second) if late_middle else piece, MIDDLE)
    return [piece, near, second, middle, place.send_z(second, OUTWARD)]


def gather_whole(place, piece):
    every = lax.all_gather(piece, "gx", axis_index_groups=place.by_y())
    inner = place.n // place.ny
    if inner == 1:
        return every
    rows, cols = piece.shape
    every = every.reshape(place.ny, inner, rows, cols)
    return jnp.swapaxes(every, 1, 2).reshape(place.ny, rows, inner * cols)


def scatter_whole(place, parts):
    inner = place.n // place.ny
    if inner > 1:
        count, rows, cols = parts.shape
        parts = jnp.swapaxes(parts.reshape(count, rows, inner, cols // inner), 1, 2)
        parts = parts.reshape(place.n, rows, cols // inner)
    return lax.psum_scatter(parts, "gx", axis_index_groups=place.by_y())


def start_scatter(place, parts):
    if not place.lined:
        return [scatter_whole(place, jnp.stack(parts))]
    own, near, second, third = parts
    far = place.send_z(third, INWARD)
    middle = place.send_z(third, MIDDLE)
    return [own, second, far, place.send_z(near, NEAR), middle]


def second_scatter(place, started, part, count, *earlier):
    if not place.lined:
        return None
    rows, cols = started[1].shape
    at = slice(part * (rows // count), (part + 1) * (rows // count))
    (summed,) = call(
        partial(add_body, rows=at),
        [((rows // count, cols), bf16)],
        place.table,
        [],
        [started[1:3]],
        [pltpu.VMEM((rows // count, cols), bf16)] * 2 + [pltpu.SemaphoreType.DMA((2,))],
        earlier=[started[4]] + list(earlier),
    )
    return place.send_z(summed, SECOND)


def end_scatter(place, started, seconds, *earlier):
    if not place.lined:
        return started
    return [after(started[0], *earlier), started[3], started[4]] + list(seconds)


def add(left, right):
    return (left.astype(f32) + right.astype(f32)).astype(bf16)


def reduce_core(place, keeps, sends):
    return [add(keep, place.swap_c(send)) for keep, send in zip(keeps, sends)]


def all_sum(place, keeps, sends, before_first=(), before_second=(), before_last=()):
    low = tuple(reduce_core(place, keeps, sends))
    low = lax.optimization_barrier(low + tuple(before_first))
    low = add(low[0], place.swap_x(low[0])), add(low[1], place.swap_y(low[1]))
    low = lax.optimization_barrier(low + tuple(before_second))
    own = (add(low[0], place.swap_y(low[0])), add(low[1], place.swap_x(low[1])))
    if before_last:
        own = lax.optimization_barrier(own + tuple(before_last))[:2]
    own = list(own)
    return own + [place.swap_c(part) for part in own]


def own_sum(place, keeps, sends):
    first, second = reduce_core(place, keeps, sends)
    mine, other = jnp.where(place.x == 0, first, second), jnp.where(place.x == 0, second, first)
    mine = add(mine, place.swap_x(other))
    mine, other = part_of(place.y, mine, 0)
    return mine.astype(f32) + place.swap_y(other).astype(f32)


def own_block(place, blocks):
    rows = blocks.shape[1] // 2
    return lax.dynamic_slice(
        blocks, (place.gy, place.y * rows, 0), (1, rows, blocks.shape[2])
    )[0]


Z, Y, X, C, Z_IN, COUNT = range(6)
ORDER = COUNT + 2


def call(body, outs, table, operands, pieces=(), scratch=(), earlier=(), held=(), alias=0, limit=24):
    lengths = [len(p) for p in pieces]
    flat = [a for p in pieces for a in p] + list(earlier)
    vmem = pl.BlockSpec(memory_space=pltpu.VMEM)
    copied = [pltpu.VMEM(a.shape, a.dtype) for a in held]
    if held:
        copied.append(pltpu.SemaphoreType.DMA((len(held),)))

    def kernel(table_ref, *refs):
        plain, rest = refs[: len(operands)], refs[len(operands) :]
        sources, rest = rest[: len(held)], rest[len(held) :]
        lists = []
        for length in lengths:
            lists.append(rest[:length])
            rest = rest[length:]
        rest = rest[len(earlier) :]
        targets = ()
        if held:
            rest, targets = rest[: -len(copied)], rest[-len(copied) :]
            copies = [
                pltpu.make_async_copy(source, target, targets[-1].at[i])
                for i, (source, target) in enumerate(zip(sources, targets))
            ]
            for copy in copies:
                copy.start()
            for copy in copies:
                copy.wait()
        body(table_ref, *plain, *targets[:-1], *lists, *rest)

    return pl.pallas_call(
        kernel,
        out_shape=[jax.ShapeDtypeStruct(shape, dtype) for shape, dtype in outs],
        in_specs=[pl.BlockSpec(memory_space=pltpu.SMEM)]
        + [pl.BlockSpec(memory_space=pl.ANY)] * alias
        + [vmem] * (len(operands) - alias)
        + [pl.BlockSpec(memory_space=pltpu.HBM)] * len(held)
        + [pl.BlockSpec(memory_space=pl.ANY)] * len(flat),
        out_specs=[pl.BlockSpec(memory_space=pl.ANY)] * alias + [vmem] * (len(outs) - alias),
        scratch_shapes=list(scratch) + copied,
        input_output_aliases={i + 1: i for i in range(alias)},
        compiler_params=pltpu.CompilerParams(vmem_limit_bytes=limit << 20),
    )(table, *operands, *held, *flat)


def start_pieces(table, pieces, whole, sems, rows=slice(None)):
    count = whole.shape[0]
    block = [table[ORDER + k] for k in range(count)]

    def copy(piece, k):
        source = piece.at[rows] if rows != slice(None) else piece
        return pltpu.make_async_copy(source, whole.at[block[k]], sems.at[k])

    def wait(k):
        pltpu.make_async_copy(whole.at[0], whole.at[0], sems.at[k]).wait()

    if len(pieces) == 1:
        for k in range(count):
            copy(pieces[0].at[block[k]], k).start()
        return wait
    z = table[Z]
    own, near, second, middle, end = pieces
    for k, piece in enumerate((own, near, second)):
        copy(piece, k).start()
    inside = jnp.logical_or(z == 1, z == 2)

    @pl.when(inside)
    def _():
        copy(middle, 3).start()

    @pl.when(jnp.logical_not(inside))
    def _():
        copy(end, 3).start()

    return wait


def keep_and_send(table, block_of, outs):
    core = table[C]
    for i in range(2):
        outs[i][...] = block_of(2 * i + core).astype(bf16)
        outs[2 + i][...] = block_of(2 * i + 1 - core).astype(bf16)


def place_rows(table, pieces, raw, grad):
    x, y, c = table[X], table[Y], table[C]
    tokens = raw.shape[1] // 2
    for dc in range(2):
        for dx in range(2):
            block = 2 * (x + dx - 2 * x * dx) + c + dc - 2 * c * dc
            for dy in range(2):
                at = pl.ds(pl.multiple_of(tokens * (y + dy - 2 * y * dy), tokens), tokens)
                piece = pieces[4 * dc + 2 * dy + dx]
                raw[block, at, :] = piece[:tokens]
                grad[block, at, :] = piece[tokens:]


def norm_rows(raw, gain, normed):
    def square(b, total):
        values = raw[b].astype(f32)
        return total + jnp.sum(values * values, axis=1, keepdims=True)

    count = raw.shape[0]
    total = lax.fori_loop(0, count, square, jnp.zeros((raw.shape[1], 1), f32))
    scale = lax.rsqrt(total / (count * raw.shape[2]) + eps)

    def norm(b, _):
        normed[b] = (raw[b].astype(f32) * scale * gain[b]).astype(bf16)
        return 0

    lax.fori_loop(0, count, norm, 0)
    return scale


def rows_body(table, *refs):
    gains = refs[8:12]
    raw, grad, normed, inverse, gain_first, gain_second = refs[12:]
    place_rows(table, refs[:8], raw, grad)
    x, c = table[X], table[C]
    for dc in range(2):
        for dx in range(2):
            block = 2 * (x + dx - 2 * x * dx) + c + dc - 2 * c * dc
            gain = gains[2 * dc + dx][...]
            gain_first[block] = gain[0:1]
            gain_second[block] = gain[1:2]
    inverse[...] = norm_rows(raw, gain_first, normed)


def turn(values, cosine, sine):
    half = values.shape[0] // 2
    first, second = values[:half], values[half:]
    return jnp.concatenate(
        [first * cosine - second * sine, second * cosine + first * sine], axis=0
    )


def qkv_body(
    table, normed, cosine, sine, pieces, query, own, weights, acc, sems
):
    wait = start_pieces(table, pieces, weights, sems)
    count = acc.shape[0]
    acc[...] = jnp.zeros_like(acc)

    def one(k, _):
        b = table[ORDER + k]
        wait(k)
        acc[...] += dims(weights[b, :count], normed[b], 1, 1)
        return 0

    lax.fori_loop(0, normed.shape[0], one, 0)
    head = HEAD_DIM
    heads = query.shape[0] // head
    cos, sin = cosine[...], sine[...]
    for h in range(heads):
        at = slice(h * head, (h + 1) * head)
        query[at] = turn(acc[at], cos, sin).astype(bf16)
    at = slice(heads * head, (heads + 1) * head)
    own[:head] = turn(acc[at], cos, sin).astype(bf16)
    own[head:] = acc[(heads + 1) * head :].astype(bf16)


def attend_body(table, query, own, *refs):
    moved, refs = refs[: GROUP - 1], refs[GROUP - 1 :]
    (weights, attended, attended_low, log_total, far), outs = refs[:5], refs[5:]
    tokens = own.shape[1]
    for place in range(GROUP):

        @pl.when(table[Z_IN] == place)
        def _():
            for slot in range(PROMPTS):
                k = place - slot
                far[:, slot * tokens : (slot + 1) * tokens] = (
                    moved[k - 1][...] if k > 0 else own[...]
                )

    head = HEAD_DIM
    block = tokens // 2
    key_far, value_far = far[:head].T, far[head:]
    key_own = own[:head].T
    total = far.shape[1]
    near_row = lax.broadcasted_iota(jnp.int32, (block, block), 0)
    near_col = lax.broadcasted_iota(jnp.int32, (block, block), 1)
    causal = near_row <= near_col
    row = lax.broadcasted_iota(jnp.int32, (total, block), 0)
    for part in range(2):
        cols = slice(part * block, (part + 1) * block)
        key_near, value_near = key_own[cols], own[head:, cols]
        seen = row < table[COUNT + part] * block

        def one(h, _):
            at = pl.ds(pl.multiple_of(h * head, head), head)
            rows = query[at, cols]
            score_far = jnp.where(seen, dims(key_far, rows, 1, 0) * score_scale, neg_big)
            score_near = jnp.where(causal, dims(key_near, rows, 1, 0) * score_scale, neg_big)
            top = jnp.maximum(
                jnp.max(score_far, axis=0, keepdims=True), jnp.max(score_near, axis=0, keepdims=True)
            )
            weight_far = jnp.exp(score_far - top)
            weight_near = jnp.exp(score_near - top)
            weight = jnp.sum(weight_far, axis=0, keepdims=True) + jnp.sum(
                weight_near, axis=0, keepdims=True
            )
            out = dims(value_far, weight_far.astype(bf16), 1, 0) + dims(
                value_near, weight_near.astype(bf16), 1, 0
            )
            attended[at, cols] = out / weight
            log_total[h, :, cols] = top + jnp.log(weight)
            return 0

        lax.fori_loop(0, query.shape[0] // head, one, 0)
    values = attended[...]
    attended_low[...] = values.astype(bf16)
    flipped = values.T.astype(bf16)
    first = weights.shape[1] - query.shape[0]
    keep_and_send(
        table,
        lambda b: dims(flipped, weights[b, first:], 1, 0),
        outs,
    )


def hidden_body(
    table, own_first, own_second, other_first, other_second, raw, gain, hidden, normed, inverse
):
    core = table[C]
    summed, other = (own_first, own_second), (other_first, other_second)
    for i in range(2):
        b = 2 * i + core
        hidden[b] = raw[b].astype(f32) + summed[i][...].astype(f32)
        b = 2 * i + 1 - core
        hidden[b] = raw[b].astype(f32) + other[i][...].astype(f32)

    def square(b, total):
        values = hidden[b]
        return total + jnp.sum(values * values, axis=1, keepdims=True)

    count = raw.shape[0]
    total = lax.fori_loop(0, count, square, jnp.zeros((raw.shape[1], 1), f32))
    scale = lax.rsqrt(total / (count * raw.shape[2]) + eps)
    inverse[...] = scale

    def norm(b, _):
        normed[b] = (hidden[b] * scale * gain[b]).astype(bf16)
        return 0

    lax.fori_loop(0, count, norm, 0)


def forward_body(
    table,
    normed,
    grad,
    pieces,
    active,
    change,
    *refs,
):
    outs, (weights, acc, gate_slope, up_slope, sems) = refs[:4], refs[4:]
    wait = start_pieces(table, pieces, weights, sems)
    count, tokens = normed.shape[:2]
    width = acc.shape[1]
    half = width // 2
    acc[...] = jnp.zeros_like(acc)

    def one(k, _):
        b = table[ORDER + k]
        wait(k)
        acc[...] += dims(normed[b], weights[b, :width], 1, 1)
        return 0

    lax.fori_loop(0, count, one, 0)
    rows = tokens // 4

    def part(i, _):
        at = pl.ds(pl.multiple_of(i * rows, rows), rows)
        gate, up = acc[at, :half], acc[at, half:]
        sigmoid = jax.nn.sigmoid(gate)
        active[at] = (gate * sigmoid * up).astype(bf16)
        gate_slope[at] = up * sigmoid * (1.0 + gate * (1.0 - sigmoid))
        up_slope[at] = gate * sigmoid
        return 0

    lax.fori_loop(0, 4, part, 0)

    def back(b, total):
        return total + dims(grad[b], weights[b, width:], 1, 1)

    slope = lax.fori_loop(0, count, back, jnp.zeros((tokens, half), f32))
    change[:, :half] = (slope * gate_slope[...]).astype(bf16)
    change[:, half:] = (slope * up_slope[...]).astype(bf16)
    values = change[...]
    keep_and_send(
        table,
        lambda b: dims(values, weights[b, :width], 1, 0),
        outs,
    )


def forward_parts_body(table, active, normed, change, grad, *refs):
    parts, flipped = refs[:-1], refs[-1]
    width = change.shape[1]
    flipped[:width] = change[...].T
    flipped[width:] = active[...].T
    rows = width // 4

    def fill(first, count, source):
        def one(i, _):
            at = pl.ds(pl.multiple_of((first + i) * rows, rows), rows)
            for k, part in enumerate(parts):
                part[at] = dims(flipped[at], source[table[ORDER + k]], 1, 0).astype(bf16)
            return 0

        lax.fori_loop(0, count, one, 0)

    fill(0, 4, normed)
    fill(4, flipped.shape[0] // rows - 4, grad)


def down_body(table, active, pieces, *refs):
    outs, (weights, sems) = refs[:4], refs[4:]
    rows = weights.shape[1]
    wait = start_pieces(table, pieces, weights, sems, slice(2 * rows, 3 * rows))
    for k in range(weights.shape[0]):
        wait(k)
    values = active[...]
    keep_and_send(table, lambda b: dims(values, weights[b], 1, 0), outs)


def attend_back_body(
    table,
    own_first,
    own_second,
    other_first,
    other_second,
    hidden,
    inverse,
    grad,
    gain,
    weights,
    query,
    own,
    far,
    attended,
    log_total,
    cosine,
    sine,
    through,
    pull,
    query_low,
    own_back,
    *rest,
):
    sends, inner_first = rest[: GROUP - 1], rest[GROUP - 1]
    far_back, change, branch = rest[GROUP:]
    core = table[C]
    count, tokens, model = hidden.shape
    for i, (mine, theirs) in enumerate(((own_first, other_first), (own_second, other_second))):
        change[2 * i + core] = mine[...].astype(f32) * gain[2 * i + core]
        change[2 * i + 1 - core] = theirs[...].astype(f32) * gain[2 * i + 1 - core]

    def product(b, total):
        return total + jnp.sum(change[b] * hidden[b], axis=1, keepdims=True)

    inner = lax.fori_loop(0, count, product, jnp.zeros((tokens, 1), f32))
    scale = inverse[...]
    back = scale * scale * scale * inner / (count * model)
    pull[...] = back

    def rows(b, total):
        values = grad[b].astype(f32) + scale * change[b] - hidden[b] * back
        low = values.astype(bf16)
        through[b] = low
        return total + dims(low, weights[b, first:], 1, 1)

    heads_cols = query.shape[0]
    first = weights.shape[1] - heads_cols
    total_rows = lax.fori_loop(0, count, rows, jnp.zeros((tokens, heads_cols), f32))
    branch[...] = total_rows.T.astype(bf16)

    head = HEAD_DIM
    block = tokens // 2
    key_far_t = far[:head]
    key_far, value_far = key_far_t.T, far[head:].T
    key_own, value_own = own[:head].T, own[head:].T
    total = far.shape[1]
    near_row = lax.broadcasted_iota(jnp.int32, (block, block), 0)
    near_col = lax.broadcasted_iota(jnp.int32, (block, block), 1)
    causal = near_row <= near_col
    row = lax.broadcasted_iota(jnp.int32, (total, block), 0)
    far_back[...] = jnp.zeros_like(far_back)
    own_back[...] = jnp.zeros_like(own_back)
    inner_first[...] = jnp.zeros_like(inner_first)
    for part in range(2):
        cols = slice(part * block, (part + 1) * block)
        key_near, value_near = key_own[cols], value_own[cols]
        key_near_t = own[:head, cols]
        seen = row < table[COUNT + part] * block

        def one_head(h, _):
            at = pl.ds(pl.multiple_of(h * head, head), head)
            rows_q, rows_grad = query[at, cols], branch[at, cols]
            delta = jnp.sum(
                rows_grad.astype(f32) * attended[at, cols], axis=0, keepdims=True
            )
            logs = log_total[h, :, cols]

            def one(key, value, allowed):
                score = dims(key, rows_q, 1, 0) * score_scale
                prob = jnp.where(allowed, jnp.exp(score - logs), 0.0)
                moved = (prob * (dims(value, rows_grad, 1, 0) - delta)).astype(bf16)
                return prob.astype(bf16), moved

            prob_far, moved_far = one(key_far, value_far, seen)
            prob_near, moved_near = one(key_near, value_near, causal)
            query_back = (
                dims(key_far_t, moved_far, 1, 0) + dims(key_near_t, moved_near, 1, 0)
            ) * score_scale
            inner_first[:, cols] += jnp.sum(
                query_back * rows_q.astype(f32), axis=0, keepdims=True
            )
            query_low[at, cols] = turn(query_back, cosine[:, cols], -sine[:, cols]).astype(bf16)
            far_back[:head] += dims(rows_q, moved_far, 1, 1) * score_scale
            far_back[head:] += dims(rows_grad, prob_far, 1, 1)
            own_back[:head, cols] += dims(rows_q, moved_near, 1, 1) * score_scale
            own_back[head:, cols] += dims(rows_grad, prob_near, 1, 1)
            return 0

        lax.fori_loop(0, heads_cols // head, one_head, 0)
    for slot in range(PROMPTS):

        @pl.when(table[Z_IN] == slot)
        def _():
            own_back[...] += far_back[:, slot * tokens : (slot + 1) * tokens]

    for k in range(1, GROUP):
        sends[k - 1][...] = far_back[:, :tokens].astype(bf16)
        for slot in range(1, PROMPTS):

            @pl.when(table[Z_IN] == slot + k)
            def _():
                sends[k - 1][...] = far_back[:, slot * tokens : (slot + 1) * tokens].astype(bf16)


def attend_parts_body(table, query_low, through, normed, attended_low, *parts):
    rows = query_low.shape[0]
    for k, part in enumerate(parts):
        b = table[ORDER + k]
        part[:rows] = dims(query_low[...], normed[b], 1, 0).astype(bf16)
        part[-rows:] = dims(attended_low[...], through[b], 1, 0).astype(bf16)


def qkv_back_body(table, *refs):
    count = table.shape[0] - ORDER
    own_back, moved, refs = refs[count], refs[count + 1 : count + GROUP], refs[count + GROUP :]
    query_low, inner, weights, cosine, sine, own, normed = refs[:7]
    parts, outs = refs[7 : 7 + count], refs[7 + count : 11 + count]
    inner_first, own_low, changed, sems = refs[11 + count :]
    head = HEAD_DIM
    total = own_back[...]
    for part in moved:
        total = total + part[...].astype(f32)
    inner_first[...] = inner[...] + jnp.sum(total * own[...].astype(f32), axis=0, keepdims=True)
    key = turn(total[:head], cosine[...], -sine[...])
    low = jnp.concatenate([key, total[head:]], axis=0)
    own_low[...] = low.astype(bf16)
    first = query_low.shape[0]
    copies = []
    for k, part in enumerate(parts):
        changed[k] = dims(own_low[...], normed[table[ORDER + k]], 1, 0).astype(bf16)
        target = part.at[first : first + low.shape[0]]
        copies.append(pltpu.make_async_copy(changed.at[k], target, sems.at[k]))
        copies[k].start()
    flipped = jnp.concatenate([query_low[...].T, low.T.astype(bf16)], axis=1)
    width = flipped.shape[1]
    keep_and_send(table, lambda b: dims(flipped, weights[b, :width], 1, 0), outs)
    for copy in copies:
        copy.wait()


def halves_of(table, whole):
    half = whole.shape[0] // 2
    low, high = whole[:half], whole[half:]
    flag = table[Y] == 0
    return jnp.where(flag, low, high), jnp.where(flag, high, low)


def add_body(table, sources, out, first, second, sems, *, rows):
    copies = [
        pltpu.make_async_copy(source.at[rows], held, sems.at[i])
        for i, (source, held) in enumerate(zip(sources, (first, second)))
    ]
    for copy in copies:
        copy.start()
    for copy in copies:
        copy.wait()
    out[...] = add(first[...], second[...])


def pack(rows, packed):
    half, cols = packed.shape[0], rows.shape[1]
    packed[:, :cols] = rows[:half].astype(packed.dtype)
    packed[:, cols:] = rows[half:].astype(packed.dtype)


def split_body(table, *refs):
    matrices, (mine_ref, other_ref) = refs[:-2], refs[-2:]
    pairs = [halves_of(table, matrix[...].T) for matrix in matrices]
    pack(jnp.concatenate([mine for mine, _ in pairs], axis=0), mine_ref)
    pack(jnp.concatenate([other for _, other in pairs], axis=0), other_ref)


def piece_body(table, mine_ref, got_ref, piece):
    flag = table[Y] == 0
    mine, got = mine_ref[...], got_ref[...]
    low, high = jnp.where(flag, mine, got), jnp.where(flag, got, mine)
    half, cols = mine.shape[0], mine.shape[1] // 2
    for i in range(2):
        piece[i * half : (i + 1) * half, :cols] = low[:, i * cols : (i + 1) * cols]
        piece[i * half : (i + 1) * half, cols:] = high[:, i * cols : (i + 1) * cols]


def sum_body(table, *refs):
    parts, (mine_ref, other_ref) = refs[:-2], refs[-2:]
    whole = [part for part in parts if part.shape == parts[0].shape]
    total = whole[0][...].astype(f32)
    for part in whole[1:]:
        total = total + part[...].astype(f32)
    rest = [part[...].astype(f32) for part in parts if part.shape != parts[0].shape]
    if rest:
        total = total + jnp.concatenate(rest, axis=0)
    cols = total.shape[1] // 2
    low, high = total[:, :cols], total[:, cols:]
    flag = table[Y] == 0
    pack(jnp.where(flag, low, high), mine_ref)
    pack(jnp.where(flag, high, low), other_ref)


def join_body(table, mine_ref, got_ref, *outs):
    flag = table[Y] == 0
    cols = mine_ref.shape[1] // 2

    def unpacked(ref):
        return jnp.concatenate([ref[:, :cols], ref[:, cols:]], axis=0).astype(f32)

    mine, got = unpacked(mine_ref), unpacked(got_ref)
    low, high = jnp.where(flag, mine, got), jnp.where(flag, got, mine)
    at = 0
    for out in outs:
        rows = out.shape[1] // 2
        out[:, :rows] = low[at : at + rows].T
        out[:, rows:] = high[at : at + rows].T
        at += rows


def rope_tables(positions, half):
    freq = rope_base ** (-(2.0 * jnp.arange(half, dtype=f32)) / (2.0 * half))
    angle = freq[:, None] * positions.astype(f32)[None, :]
    return (jnp.cos(angle), jnp.sin(angle))


def shards(
    layer_in,
    first_gain,
    query_weight,
    key_matrix,
    value_matrix,
    out_weight,
    second_gain,
    gate_weight,
    up_weight,
    down_weight,
    out_grad,
):
    place = Place()
    n, ny, y, z_in, table = place.n, place.ny, place.y, place.z_in, place.table
    lined = place.lined
    block, width = layer_in.shape
    tokens = 2 * block
    model_width = width * ny
    hidden_dev = gate_weight.shape[1] // 2
    query_rows = query_weight.shape[1] // 2
    kv_rows = key_matrix.shape[1]
    qkv_cols = query_rows + kv_rows
    full = (ny, tokens, width)
    wide = [(full[1:], bf16)] * 4

    def halves(*matrices, earlier=()):
        rows = sum(m.shape[1] for m in matrices) // 2
        packed = (rows // 2, 2 * matrices[0].shape[0])
        return call(split_body, [(packed, bf16)] * 2, table, [], held=matrices, earlier=earlier)

    def whole_piece(mine, got):
        rows, cols = mine.shape
        (piece,) = call(piece_body, [((2 * rows, cols), bf16)], table, [mine, got])
        return piece

    def spread(value, *before_y):
        by_x = place.swap_x(value)
        late, late_x = lax.optimization_barrier((value, by_x) + before_y)[:2]
        four = [value, by_x, place.swap_y(late), place.swap_y(late_x)]
        return four + [place.swap_c(r) for r in four]

    mine, other = halves(query_weight, key_matrix, value_matrix, out_weight.T)
    attend_got = place.swap_y(other)
    attend_piece = whole_piece(mine, attend_got)
    mine, other = halves(gate_weight, up_weight, down_weight.T, earlier=[attend_got])
    forward_got = place.swap_y(other)
    forward_piece = whole_piece(mine, forward_got)
    rows = jnp.concatenate([layer_in, out_grad], axis=0)
    input_rows = spread(after(rows, attend_got), forward_got)
    if lined:
        attend_pieces = gather_pieces(place, attend_piece)
        forward_pieces = gather_pieces(place, after(forward_piece, *attend_pieces[1:]), True)
    else:
        attend_pieces = [gather_whole(place, attend_piece)]
        forward_pieces = [gather_whole(place, forward_piece)]
    attend_shape = (ny, qkv_cols + query_rows, width)
    forward_shape = (ny, 3 * hidden_dev, width)
    sems = pltpu.SemaphoreType.DMA((ny,))

    gains = jnp.stack([first_gain, second_gain])
    two = [gains, place.swap_x(gains)]
    gains = two + [place.swap_c(g) for g in two]
    raw, grad, normed_in, inverse_in, gain_in, gain_mid = call(
        rows_body,
        [(full, bf16)] * 3 + [((tokens, 1), f32)] + [((ny, 1, width), f32)] * 2,
        table,
        input_rows + gains,
    )

    within = jnp.arange(block, dtype=jnp.int32)
    positions = jnp.minimum(place.offset, PROMPT_DEV)[:, None] * block + within[None, :]
    cosine, sine = rope_tables(positions.reshape(-1), HEAD_DIM // 2)
    query, own, attend_weights = call(
        qkv_body,
        [((query_rows, tokens), bf16), ((kv_rows, tokens), bf16), (attend_shape, bf16)],
        table,
        [normed_in, cosine, sine],
        [attend_pieces],
        [pltpu.VMEM((qkv_cols, tokens), f32), sems],
    )
    moved = [
        place.send_z(
            own,
            [(s, s + k) for s in range(n) if s % GROUP < PROMPTS and s % GROUP + k < GROUP],
        )
        for k in range(1, GROUP)
    ]
    attended, attended_low, log_total, far, *halves_out = call(
        attend_body,
        [
            ((query_rows, tokens), f32),
            ((query_rows, tokens), bf16),
            ((query_rows // HEAD_DIM, 1, tokens), f32),
            ((kv_rows, PROMPTS * tokens), bf16),
        ]
        + wide,
        table,
        [query, own] + moved + [attend_weights],
    )
    summed = all_sum(
        place,
        halves_out[:2],
        halves_out[2:],
        before_first=forward_pieces[1:3] if lined else forward_pieces,
        before_last=forward_pieces[3:],
    )

    hidden, normed_mid, inverse_mid = call(
        hidden_body,
        [(full, f32), (full, bf16), ((tokens, 1), f32)],
        table,
        summed,
        held=[raw, gain_mid],
    )
    active, change, *halves_out = call(
        forward_body,
        [((tokens, hidden_dev), bf16), ((tokens, 2 * hidden_dev), bf16)] + wide,
        table,
        [normed_mid],
        [forward_pieces],
        [pltpu.VMEM(forward_shape, bf16), pltpu.VMEM((tokens, 2 * hidden_dev), f32)]
        + [pltpu.VMEM((tokens, hidden_dev), f32)] * 2
        + [sems],
        held=[grad],
    )
    forward_parts = call(
        forward_parts_body,
        [(forward_shape[1:], bf16)] * ny,
        table,
        [active, normed_mid, change],
        held=[grad],
        scratch=[pltpu.VMEM(forward_shape[1:2] + (tokens,), bf16)],
    )
    forward_started = start_scatter(place, forward_parts)
    summed = all_sum(
        place, halves_out[:2], halves_out[2:], before_second=forward_parts[:1]
    )
    forward_second = second_scatter(place, forward_started, 0, 2, summed[-1])
    hidden_own = own_block(place, hidden)
    through, pull, query_low, own_back, *returns, inner_first = call(
        attend_back_body,
        [
            (full, bf16),
            ((tokens, 1), f32),
            ((query_rows, tokens), bf16),
            ((kv_rows, tokens), f32),
        ]
        + [((kv_rows, tokens), bf16)] * (GROUP - 1)
        + [((1, tokens), f32)],
        table,
        summed,
        held=[
            hidden,
            inverse_mid,
            grad,
            gain_mid,
            attend_weights,
            query,
            own,
            far,
            attended,
            log_total,
            cosine,
            sine,
        ],
        earlier=forward_started[2:3] + forward_started[4:],
        scratch=[
            pltpu.VMEM((kv_rows, PROMPTS * tokens), f32),
            pltpu.VMEM(full, f32),
            pltpu.VMEM((query_rows, tokens), bf16),
        ],
    )
    inverse_own, _ = part_of(y, inverse_mid, 0)
    pull_own, _ = part_of(y, pull, 0)
    mid_own = jnp.where(place.x == 0, summed[0], summed[1])
    mid_own = part_of(y, mid_own, 0)[0].astype(f32)
    through_own = (
        out_grad.astype(f32)
        + inverse_own * mid_own * second_gain[None, :]
        - hidden_own * pull_own
    )
    second_term = jnp.sum(mid_own * hidden_own * inverse_own, axis=0)

    moved = [
        place.send_z(
            returns[k - 1],
            [(s, s - k) for s in range(n) if 0 <= s % GROUP - k < PROMPTS],
        )
        for k in range(1, GROUP)
    ]
    attend_parts = call(
        attend_parts_body,
        [(attend_shape[1:], bf16)] * ny,
        table,
        [query_low, through],
        held=[normed_in, attended_low],
    )
    results = call(
        qkv_back_body,
        [(attend_shape[1:], bf16)] * ny
        + wide
        + [((1, tokens), f32), ((kv_rows, tokens), bf16)],
        table,
        list(attend_parts) + [own_back] + moved + [query_low, inner_first],
        held=[attend_weights, cosine, sine, own, normed_in],
        scratch=[pltpu.VMEM((ny, kv_rows, width), bf16), sems],
        earlier=forward_started[3:4] + ([forward_second] if lined else []),
        alias=ny,
    )
    attend_parts, first_halves, (inner, own_low) = results[:ny], results[ny:-2], results[-2:]
    attend_started = start_scatter(place, attend_parts)
    forward_seconds = [
        forward_second,
        second_scatter(place, forward_started, 1, 2, summed[-1], moved[0]),
    ]
    attend_second = second_scatter(place, attend_started, 0, 1)
    forward_grad = end_scatter(place, forward_started, forward_seconds, own_low)
    attend_grad = end_scatter(place, attend_started, [attend_second], own_low)
    inner = inner + place.swap_c(inner)
    inner = inner + place.swap_x(inner)
    inner = inner + place.swap_y(inner)
    first_own = own_sum(place, first_halves[:2], first_halves[2:])
    input_own = layer_in.astype(f32)
    inverse_own, _ = part_of(y, inverse_in, 0)
    scaled = first_own * first_gain[None, :]
    inner = part_of(y, inner.reshape(tokens, 1), 0)[0]
    in_grad = (
        through_own + inverse_own * scaled - input_own * (inverse_own**2 * inner / model_width)
    )
    first_term = jnp.sum(first_own * input_own * inverse_own, axis=0)
    terms = jnp.stack([first_term, second_term])
    bit = 1
    while bit < place.nx:
        terms = terms + place.swap_gx(terms, bit)
        bit *= 2

    down_halves = call(
        down_body,
        wide,
        table,
        [],
        [forward_pieces],
        [pltpu.VMEM((ny, hidden_dev, width), bf16), sems],
        earlier=[own_low],
        held=[active],
    )
    layer_out = (hidden_own + own_sum(place, down_halves[:2], down_halves[2:])).astype(bf16)

    def joined(parts, outs):
        rows, cols = parts[0].shape
        packed = (rows // 2, cols)
        mine, other = call(sum_body, [(packed, f32), (packed, bf16)], table, parts)
        shapes = [(cols // 2, inner) for inner in outs]
        return call(
            join_body, [(s, f32) for s in shapes], table, [mine, place.swap_y(other)]
        )

    gate_grad, up_grad, down_grad = joined(forward_grad, [2 * hidden_dev] * 3)
    query_out, key_out, value_out, out_out = joined(
        attend_grad, [2 * query_rows, kv_rows, kv_rows, 2 * query_rows]
    )
    return (
        layer_out,
        in_grad,
        terms[0],
        query_out,
        key_out,
        value_out,
        out_out.T,
        terms[1],
        gate_grad,
        up_grad,
        down_grad.T,
    )


def solution(mesh):
    rows, cols, gain = P("gx", "gy"), P("gy", "gx"), P("gy")
    return jax.shard_map(
        shards,
        mesh=mesh,
        in_specs=(rows, gain, rows, rows, rows, cols, gain, rows, rows, cols, rows),
        out_specs=(rows, rows, gain, rows, rows, rows, cols, gain, rows, rows, cols),
        check_vma=False,
    )
```

```python
from functools import partial

import jax
import jax.numpy as jnp
from jax import lax
from jax.experimental import pallas as pl
from jax.experimental.pallas import tpu as pltpu
from jax.sharding import PartitionSpec as P

HEAD_DIM = 96
PROMPT_DEV = 4
CONT_DEV = 4
GROUP = (PROMPT_DEV + CONT_DEV) // 2
PROMPTS = PROMPT_DEV // 2

eps = 1e-05
neg_big = -1e30
rope_base = 100000.0
score_scale = HEAD_DIM ** (-0.5)
f32 = jnp.float32
bf16 = jnp.bfloat16


def dims(left, right, left_axis, right_axis):
    return lax.dot_general(
        left, right, (((left_axis,), (right_axis,)), ((), ())), preferred_element_type=f32
    )


class Place:
    def __init__(self):
        self.nx = lax.axis_size("gx")
        self.ny = lax.axis_size("gy")
        assert self.ny == 4 and self.nx % (PROMPT_DEV + CONT_DEV) == 0
        self.n = self.nx // 2
        self.gx = lax.axis_index("gx")
        self.gy = lax.axis_index("gy")
        self.z, self.y = self.gx // 2, self.gx % 2
        self.x, self.c = self.gy // 2, self.gy % 2
        self.z_in = self.z % GROUP
        offset = 2 * self.z_in + jnp.arange(2, dtype=jnp.int32)
        self.offset = offset
        self.lined = self.n == self.ny
        blocks = jnp.arange(self.ny, dtype=jnp.int32)
        first = jnp.stack([self.z, self.y, self.x, self.c, self.z_in]).astype(jnp.int32)
        self.table = jnp.concatenate(
            [first, jnp.minimum(offset, PROMPT_DEV), blocks ^ self.z if self.lined else blocks]
        )

    def swap_gx(self, value, bit):
        return lax.ppermute(value, "gx", [(i, i ^ bit) for i in range(self.nx)])

    def swap_y(self, value):
        return self.swap_gx(value, 1)

    def swap_x(self, value):
        return lax.ppermute(value, "gy", [(i, i ^ 2) for i in range(self.ny)])

    def swap_c(self, value):
        return lax.ppermute(value, "gy", [(i, i ^ 1) for i in range(self.ny)])

    def send_z(self, value, moves):
        pairs = [(2 * s + y, 2 * t + y) for s, t in moves for y in range(2)]
        return lax.ppermute(value, "gx", pairs)

    def by_y(self):
        return [[2 * z + y for z in range(self.n)] for y in range(2)]


def pair(flag, mine, other):
    return jnp.where(flag == 0, mine, other), jnp.where(flag == 0, other, mine)


def part_of(flag, whole, axis):
    low, high = jnp.split(whole, 2, axis)
    return jnp.where(flag == 0, low, high), jnp.where(flag == 0, high, low)


def after(value, *earlier):
    return lax.optimization_barrier((value,) + earlier)[0]


NEAR = [(0, 1), (1, 0), (2, 3), (3, 2)]
SECOND = [(0, 2), (1, 3), (2, 0), (3, 1)]
MIDDLE = [(1, 2), (2, 1)]
INWARD = [(0, 1), (3, 2)]
OUTWARD = [(1, 0), (2, 3)]


def gather_pieces(place, piece, late_middle=False):
    second = place.send_z(piece, SECOND)
    near = place.send_z(piece, NEAR)
    middle = place.send_z(after(piece, second) if late_middle else piece, MIDDLE)
    return [piece, near, second, middle, place.send_z(second, OUTWARD)]


def gather_whole(place, piece):
    every = lax.all_gather(piece, "gx", axis_index_groups=place.by_y())
    inner = place.n // place.ny
    if inner == 1:
        return every
    rows, cols = piece.shape
    every = every.reshape(place.ny, inner, rows, cols)
    return jnp.swapaxes(every, 1, 2).reshape(place.ny, rows, inner * cols)


def scatter_whole(place, parts):
    inner = place.n // place.ny
    if inner > 1:
        count, rows, cols = parts.shape
        parts = jnp.swapaxes(parts.reshape(count, rows, inner, cols // inner), 1, 2)
        parts = parts.reshape(place.n, rows, cols // inner)
    return lax.psum_scatter(parts, "gx", axis_index_groups=place.by_y())


def start_scatter(place, parts):
    if not place.lined:
        return [scatter_whole(place, jnp.stack(parts))]
    own, near, second, third = parts
    far = place.send_z(third, INWARD)
    middle = place.send_z(third, MIDDLE)
    return [own, second, far, place.send_z(near, NEAR), middle]


def second_scatter(place, started, part, count, *earlier):
    if not place.lined:
        return None, None
    rows, cols = started[1].shape
    at = slice(part * (rows // count), (part + 1) * (rows // count))
    (summed,) = call(
        partial(add_body, rows=at),
        [((rows // count, cols), bf16)],
        place.table,
        [],
        [started[1:3]],
        [pltpu.VMEM((rows // count, cols), bf16)] * 2 + [pltpu.SemaphoreType.DMA((2,))],
        earlier=[started[4]] + list(earlier),
    )
    return summed, place.send_z(summed, SECOND)


def end_scatter(place, started, seconds, *earlier):
    if not place.lined:
        return started
    return [after(started[0], *earlier), started[3], started[4]] + list(seconds)


def add(left, right):
    return (left.astype(f32) + right.astype(f32)).astype(bf16)


def reduce_core(place, keeps, sends):
    return [add(keep, place.swap_c(send)) for keep, send in zip(keeps, sends)]


def all_sum(place, keeps, sends, before_first=(), before_second=(), before_last=()):
    low = tuple(reduce_core(place, keeps, sends))
    low = lax.optimization_barrier(low + tuple(before_first))
    low = add(low[0], place.swap_x(low[0])), add(low[1], place.swap_y(low[1]))
    low = lax.optimization_barrier(low + tuple(before_second))
    own = (add(low[0], place.swap_y(low[0])), add(low[1], place.swap_x(low[1])))
    if before_last:
        own = lax.optimization_barrier(own + tuple(before_last))[:2]
    own = list(own)
    return own + [place.swap_c(part) for part in own]


def own_sum(place, keeps, sends, before_x=(), before_y=()):
    first, second = reduce_core(place, keeps, sends)
    if before_x:
        first, second = lax.optimization_barrier((first, second) + tuple(before_x))[:2]
    mine, other = jnp.where(place.x == 0, first, second), jnp.where(place.x == 0, second, first)
    mine = add(mine, place.swap_x(other))
    mine = after(mine, *before_y) if before_y else mine
    mine, other = part_of(place.y, mine, 0)
    return mine.astype(f32) + place.swap_y(other).astype(f32)


def own_block(place, blocks):
    rows = blocks.shape[1] // 2
    return lax.dynamic_slice(
        blocks, (place.gy, place.y * rows, 0), (1, rows, blocks.shape[2])
    )[0]


Z, Y, X, C, Z_IN, COUNT = range(6)
ORDER = COUNT + 2


def call(body, outs, table, operands, pieces=(), scratch=(), earlier=(), held=(), alias=0, limit=24):
    lengths = [len(p) for p in pieces]
    flat = [a for p in pieces for a in p] + list(earlier)
    vmem = pl.BlockSpec(memory_space=pltpu.VMEM)
    copied = [pltpu.VMEM(a.shape, a.dtype) for a in held]
    if held:
        copied.append(pltpu.SemaphoreType.DMA((len(held),)))

    def kernel(table_ref, *refs):
        plain, rest = refs[: len(operands)], refs[len(operands) :]
        sources, rest = rest[: len(held)], rest[len(held) :]
        lists = []
        for length in lengths:
            lists.append(rest[:length])
            rest = rest[length:]
        rest = rest[len(earlier) :]
        targets = ()
        if held:
            rest, targets = rest[: -len(copied)], rest[-len(copied) :]
            copies = [
                pltpu.make_async_copy(source, target, targets[-1].at[i])
                for i, (source, target) in enumerate(zip(sources, targets))
            ]
            for copy in copies:
                copy.start()
            for copy in copies:
                copy.wait()
        body(table_ref, *plain, *targets[:-1], *lists, *rest)

    return pl.pallas_call(
        kernel,
        out_shape=[jax.ShapeDtypeStruct(shape, dtype) for shape, dtype in outs],
        in_specs=[pl.BlockSpec(memory_space=pltpu.SMEM)]
        + [pl.BlockSpec(memory_space=pl.ANY)] * alias
        + [vmem] * (len(operands) - alias)
        + [pl.BlockSpec(memory_space=pltpu.HBM)] * len(held)
        + [pl.BlockSpec(memory_space=pl.ANY)] * len(flat),
        out_specs=[pl.BlockSpec(memory_space=pl.ANY)] * alias + [vmem] * (len(outs) - alias),
        scratch_shapes=list(scratch) + copied,
        input_output_aliases={i + 1: i for i in range(alias)},
        compiler_params=pltpu.CompilerParams(vmem_limit_bytes=limit << 20),
    )(table, *operands, *held, *flat)


def start_pieces(table, pieces, whole, sems, rows=slice(None)):
    count = whole.shape[0]
    block = [table[ORDER + k] for k in range(count)]

    def copy(piece, k):
        source = piece.at[rows] if rows != slice(None) else piece
        return pltpu.make_async_copy(source, whole.at[block[k]], sems.at[k])

    def wait(k):
        pltpu.make_async_copy(whole.at[0], whole.at[0], sems.at[k]).wait()

    if len(pieces) == 1:
        for k in range(count):
            copy(pieces[0].at[block[k]], k).start()
        return wait
    z = table[Z]
    own, near, second, middle, end = pieces
    for k, piece in enumerate((own, near, second)):
        copy(piece, k).start()
    inside = jnp.logical_or(z == 1, z == 2)

    @pl.when(inside)
    def _():
        copy(middle, 3).start()

    @pl.when(jnp.logical_not(inside))
    def _():
        copy(end, 3).start()

    return wait


def keep_and_send(table, block_of, outs):
    core = table[C]
    for i in range(2):
        outs[i][...] = block_of(2 * i + core).astype(bf16)
        outs[2 + i][...] = block_of(2 * i + 1 - core).astype(bf16)


def place_rows(table, pieces, raw, grad):
    x, y, c = table[X], table[Y], table[C]
    tokens = raw.shape[1] // 2
    for dc in range(2):
        for dx in range(2):
            block = 2 * (x + dx - 2 * x * dx) + c + dc - 2 * c * dc
            for dy in range(2):
                at = pl.ds(pl.multiple_of(tokens * (y + dy - 2 * y * dy), tokens), tokens)
                piece = pieces[4 * dc + 2 * dy + dx]
                raw[block, at, :] = piece[:tokens]
                grad[block, at, :] = piece[tokens:]


def norm_rows(raw, gain, normed):
    def square(b, total):
        values = raw[b].astype(f32)
        return total + jnp.sum(values * values, axis=1, keepdims=True)

    count = raw.shape[0]
    total = lax.fori_loop(0, count, square, jnp.zeros((raw.shape[1], 1), f32))
    scale = lax.rsqrt(total / (count * raw.shape[2]) + eps)

    def norm(b, _):
        normed[b] = (raw[b].astype(f32) * scale * gain[b]).astype(bf16)
        return 0

    lax.fori_loop(0, count, norm, 0)
    return scale


def rows_body(table, *refs):
    gains = refs[8:12]
    raw, grad, normed, inverse, gain_first, gain_second = refs[12:]
    place_rows(table, refs[:8], raw, grad)
    x, c = table[X], table[C]
    for dc in range(2):
        for dx in range(2):
            block = 2 * (x + dx - 2 * x * dx) + c + dc - 2 * c * dc
            gain = gains[2 * dc + dx][...]
            gain_first[block] = gain[0:1]
            gain_second[block] = gain[1:2]
    inverse[...] = norm_rows(raw, gain_first, normed)


def turn(values, cosine, sine):
    half = values.shape[0] // 2
    first, second = values[:half], values[half:]
    return jnp.concatenate(
        [first * cosine - second * sine, second * cosine + first * sine], axis=0
    )


def qkv_body(
    table, normed, cosine, sine, pieces, query, own, weights, acc, sems
):
    wait = start_pieces(table, pieces, weights, sems)
    count = acc.shape[0]
    acc[...] = jnp.zeros_like(acc)

    def one(k, _):
        b = table[ORDER + k]
        wait(k)
        acc[...] += dims(weights[b, :count], normed[b], 1, 1)
        return 0

    lax.fori_loop(0, normed.shape[0], one, 0)
    head = HEAD_DIM
    heads = query.shape[0] // head
    cos, sin = cosine[...], sine[...]
    for h in range(heads):
        at = slice(h * head, (h + 1) * head)
        query[at] = turn(acc[at], cos, sin).astype(bf16)
    at = slice(heads * head, (heads + 1) * head)
    own[:head] = turn(acc[at], cos, sin).astype(bf16)
    own[head:] = acc[(heads + 1) * head :].astype(bf16)


def attend_body(table, query, own, *refs):
    moved, refs = refs[: GROUP - 1], refs[GROUP - 1 :]
    (weights, attended, attended_low, log_total, far), outs = refs[:5], refs[5:]
    tokens = own.shape[1]
    for place in range(GROUP):

        @pl.when(table[Z_IN] == place)
        def _():
            for slot in range(PROMPTS):
                k = place - slot
                far[:, slot * tokens : (slot + 1) * tokens] = (
                    moved[k - 1][...] if k > 0 else own[...]
                )

    head = HEAD_DIM
    block = tokens // 2
    key_far, value_far = far[:head].T, far[head:]
    key_own = own[:head].T
    total = far.shape[1]
    near_row = lax.broadcasted_iota(jnp.int32, (block, block), 0)
    near_col = lax.broadcasted_iota(jnp.int32, (block, block), 1)
    causal = near_row <= near_col
    row = lax.broadcasted_iota(jnp.int32, (total, block), 0)
    for part in range(2):
        cols = slice(part * block, (part + 1) * block)
        key_near, value_near = key_own[cols], own[head:, cols]
        seen = row < table[COUNT + part] * block

        def one(h, _):
            at = pl.ds(pl.multiple_of(h * head, head), head)
            rows = query[at, cols]
            score_far = jnp.where(seen, dims(key_far, rows, 1, 0) * score_scale, neg_big)
            score_near = jnp.where(causal, dims(key_near, rows, 1, 0) * score_scale, neg_big)
            top = jnp.maximum(
                jnp.max(score_far, axis=0, keepdims=True), jnp.max(score_near, axis=0, keepdims=True)
            )
            weight_far = jnp.exp(score_far - top)
            weight_near = jnp.exp(score_near - top)
            weight = jnp.sum(weight_far, axis=0, keepdims=True) + jnp.sum(
                weight_near, axis=0, keepdims=True
            )
            out = dims(value_far, weight_far.astype(bf16), 1, 0) + dims(
                value_near, weight_near.astype(bf16), 1, 0
            )
            attended[at, cols] = out / weight
            log_total[h, :, cols] = top + jnp.log(weight)
            return 0

        lax.fori_loop(0, query.shape[0] // head, one, 0)
    values = attended[...]
    attended_low[...] = values.astype(bf16)
    flipped = values.T.astype(bf16)
    first = weights.shape[1] - query.shape[0]
    keep_and_send(
        table,
        lambda b: dims(flipped, weights[b, first:], 1, 0),
        outs,
    )


def hidden_body(
    table, own_first, own_second, other_first, other_second, raw, gain, hidden, normed, inverse
):
    core = table[C]
    summed, other = (own_first, own_second), (other_first, other_second)
    for i in range(2):
        b = 2 * i + core
        hidden[b] = raw[b].astype(f32) + summed[i][...].astype(f32)
        b = 2 * i + 1 - core
        hidden[b] = raw[b].astype(f32) + other[i][...].astype(f32)

    def square(b, total):
        values = hidden[b]
        return total + jnp.sum(values * values, axis=1, keepdims=True)

    count = raw.shape[0]
    total = lax.fori_loop(0, count, square, jnp.zeros((raw.shape[1], 1), f32))
    scale = lax.rsqrt(total / (count * raw.shape[2]) + eps)
    inverse[...] = scale

    def norm(b, _):
        normed[b] = (hidden[b] * scale * gain[b]).astype(bf16)
        return 0

    lax.fori_loop(0, count, norm, 0)


def forward_body(
    table,
    normed,
    grad,
    pieces,
    active,
    change,
    *refs,
):
    outs, (down, weights, acc, gate_slope, up_slope, sems, down_sems) = refs[:4], refs[4:]
    split = weights.shape[1]
    wait = start_pieces(table, pieces, weights, sems, slice(0, split))
    down_wait = start_pieces(
        table, pieces, down, down_sems, slice(split, split + down.shape[1])
    )
    count, tokens = normed.shape[:2]
    width = acc.shape[1]
    half = width // 2
    acc[...] = jnp.zeros_like(acc)

    def one(k, _):
        b = table[ORDER + k]
        wait(k)
        acc[...] += dims(normed[b], weights[b, :width], 1, 1)
        return 0

    lax.fori_loop(0, count, one, 0)
    rows = tokens // 4

    def part(i, _):
        at = pl.ds(pl.multiple_of(i * rows, rows), rows)
        gate, up = acc[at, :half], acc[at, half:]
        sigmoid = jax.nn.sigmoid(gate)
        active[at] = (gate * sigmoid * up).astype(bf16)
        gate_slope[at] = up * sigmoid * (1.0 + gate * (1.0 - sigmoid))
        up_slope[at] = gate * sigmoid
        return 0

    lax.fori_loop(0, 4, part, 0)

    def back(k, total):
        b = table[ORDER + k]
        down_wait(k)
        return total + dims(grad[b], down[b], 1, 1)

    slope = lax.fori_loop(0, count, back, jnp.zeros((tokens, half), f32))
    change[:, :half] = (slope * gate_slope[...]).astype(bf16)
    change[:, half:] = (slope * up_slope[...]).astype(bf16)
    values = change[...]
    keep_and_send(
        table,
        lambda b: dims(values, weights[b, :width], 1, 0),
        outs,
    )


def forward_third_body(table, active, normed, change, grad, third, both):
    width = change.shape[1]
    both[:width] = change[...].T
    both[width:] = active[...].T
    b = table[ORDER + 3]
    third[:width] = dims(both[:width], normed[b], 1, 0).astype(bf16)
    third[width:] = dims(both[width:], grad[b], 1, 0).astype(bf16)


def forward_parts_body(table, both, normed, grad, *parts):
    rows = both.shape[0] // 6

    def fill(first, count, source):
        def one(i, _):
            at = pl.ds(pl.multiple_of((first + i) * rows, rows), rows)
            for k, part in enumerate(parts):
                part[at] = dims(both[at], source[table[ORDER + k]], 1, 0).astype(bf16)
            return 0

        lax.fori_loop(0, count, one, 0)

    fill(0, 4, normed)
    fill(4, 2, grad)


def down_body(table, active, weights, *outs):
    values = active[...]
    keep_and_send(table, lambda b: dims(values, weights[b], 1, 0), outs)


def attend_back_body(
    table,
    own_first,
    own_second,
    other_first,
    other_second,
    hidden,
    inverse,
    grad,
    gain,
    weights,
    query,
    own,
    far,
    attended,
    log_total,
    cosine,
    sine,
    through,
    pull,
    query_low,
    own_back,
    *rest,
):
    sends, inner_first = rest[: GROUP - 1], rest[GROUP - 1]
    far_back, change, branch = rest[GROUP:]
    core = table[C]
    count, tokens, model = hidden.shape
    for i, (mine, theirs) in enumerate(((own_first, other_first), (own_second, other_second))):
        change[2 * i + core] = mine[...].astype(f32) * gain[2 * i + core]
        change[2 * i + 1 - core] = theirs[...].astype(f32) * gain[2 * i + 1 - core]

    def product(b, total):
        return total + jnp.sum(change[b] * hidden[b], axis=1, keepdims=True)

    inner = lax.fori_loop(0, count, product, jnp.zeros((tokens, 1), f32))
    scale = inverse[...]
    back = scale * scale * scale * inner / (count * model)
    pull[...] = back

    def rows(b, total):
        values = grad[b].astype(f32) + scale * change[b] - hidden[b] * back
        low = values.astype(bf16)
        through[b] = low
        return total + dims(low, weights[b, first:], 1, 1)

    heads_cols = query.shape[0]
    first = weights.shape[1] - heads_cols
    total_rows = lax.fori_loop(0, count, rows, jnp.zeros((tokens, heads_cols), f32))
    branch[...] = total_rows.T.astype(bf16)

    head = HEAD_DIM
    block = tokens // 2
    key_far_t = far[:head]
    key_far, value_far = key_far_t.T, far[head:].T
    key_own, value_own = own[:head].T, own[head:].T
    total = far.shape[1]
    near_row = lax.broadcasted_iota(jnp.int32, (block, block), 0)
    near_col = lax.broadcasted_iota(jnp.int32, (block, block), 1)
    causal = near_row <= near_col
    row = lax.broadcasted_iota(jnp.int32, (total, block), 0)
    far_back[...] = jnp.zeros_like(far_back)
    own_back[...] = jnp.zeros_like(own_back)
    inner_first[...] = jnp.zeros_like(inner_first)
    for part in range(2):
        cols = slice(part * block, (part + 1) * block)
        key_near, value_near = key_own[cols], value_own[cols]
        key_near_t = own[:head, cols]
        seen = row < table[COUNT + part] * block

        def one_head(h, _):
            at = pl.ds(pl.multiple_of(h * head, head), head)
            rows_q, rows_grad = query[at, cols], branch[at, cols]
            delta = jnp.sum(
                rows_grad.astype(f32) * attended[at, cols], axis=0, keepdims=True
            )
            logs = log_total[h, :, cols]

            def one(key, value, allowed):
                score = dims(key, rows_q, 1, 0) * score_scale
                prob = jnp.where(allowed, jnp.exp(score - logs), 0.0)
                moved = (prob * (dims(value, rows_grad, 1, 0) - delta)).astype(bf16)
                return prob.astype(bf16), moved

            prob_far, moved_far = one(key_far, value_far, seen)
            prob_near, moved_near = one(key_near, value_near, causal)
            query_back = (
                dims(key_far_t, moved_far, 1, 0) + dims(key_near_t, moved_near, 1, 0)
            ) * score_scale
            inner_first[:, cols] += jnp.sum(
                query_back * rows_q.astype(f32), axis=0, keepdims=True
            )
            query_low[at, cols] = turn(query_back, cosine[:, cols], -sine[:, cols]).astype(bf16)
            far_back[:head] += dims(rows_q, moved_far, 1, 1) * score_scale
            far_back[head:] += dims(rows_grad, prob_far, 1, 1)
            own_back[:head, cols] += dims(rows_q, moved_near, 1, 1) * score_scale
            own_back[head:, cols] += dims(rows_grad, prob_near, 1, 1)
            return 0

        lax.fori_loop(0, heads_cols // head, one_head, 0)
    for slot in range(PROMPTS):

        @pl.when(table[Z_IN] == slot)
        def _():
            own_back[...] += far_back[:, slot * tokens : (slot + 1) * tokens]

    for k in range(1, GROUP):
        sends[k - 1][...] = far_back[:, :tokens].astype(bf16)
        for slot in range(1, PROMPTS):

            @pl.when(table[Z_IN] == slot + k)
            def _():
                sends[k - 1][...] = far_back[:, slot * tokens : (slot + 1) * tokens].astype(bf16)


def attend_parts_body(table, query_low, through, normed, attended_low, *parts):
    rows = query_low.shape[0]
    for k, part in enumerate(parts):
        b = table[ORDER + k]
        part[:rows] = dims(query_low[...], normed[b], 1, 0).astype(bf16)
        part[-rows:] = dims(attended_low[...], through[b], 1, 0).astype(bf16)


def qkv_back_body(table, *refs):
    count = table.shape[0] - ORDER
    own_back, moved, refs = refs[count], refs[count + 1 : count + GROUP], refs[count + GROUP :]
    query_low, inner, weights, cosine, sine, own, normed = refs[:7]
    parts, outs = refs[7 : 7 + count], refs[7 + count : 11 + count]
    inner_first, own_low, changed, sems = refs[11 + count :]
    head = HEAD_DIM
    total = own_back[...]
    for part in moved:
        total = total + part[...].astype(f32)
    inner_first[...] = inner[...] + jnp.sum(total * own[...].astype(f32), axis=0, keepdims=True)
    key = turn(total[:head], cosine[...], -sine[...])
    low = jnp.concatenate([key, total[head:]], axis=0)
    own_low[...] = low.astype(bf16)
    first = query_low.shape[0]
    copies = []
    for k, part in enumerate(parts):
        changed[k] = dims(own_low[...], normed[table[ORDER + k]], 1, 0).astype(bf16)
        target = part.at[first : first + low.shape[0]]
        copies.append(pltpu.make_async_copy(changed.at[k], target, sems.at[k]))
        copies[k].start()
    flipped = jnp.concatenate([query_low[...].T, low.T.astype(bf16)], axis=1)
    width = flipped.shape[1]
    keep_and_send(table, lambda b: dims(flipped, weights[b, :width], 1, 0), outs)
    for copy in copies:
        copy.wait()


def halves_of(table, whole):
    half = whole.shape[0] // 2
    low, high = whole[:half], whole[half:]
    flag = table[Y] == 0
    return jnp.where(flag, low, high), jnp.where(flag, high, low)


def add_body(table, sources, out, first, second, sems, *, rows):
    copies = [
        pltpu.make_async_copy(source.at[rows], held, sems.at[i])
        for i, (source, held) in enumerate(zip(sources, (first, second)))
    ]
    for copy in copies:
        copy.start()
    for copy in copies:
        copy.wait()
    out[...] = add(first[...], second[...])


def pack(rows, packed):
    half, cols = packed.shape[0], rows.shape[1]
    packed[:, :cols] = rows[:half].astype(packed.dtype)
    packed[:, cols:] = rows[half:].astype(packed.dtype)


def split_body(table, *refs):
    matrices, (mine_ref, other_ref) = refs[:-2], refs[-2:]
    pairs = [halves_of(table, matrix[...].T) for matrix in matrices]
    pack(jnp.concatenate([mine for mine, _ in pairs], axis=0), mine_ref)
    pack(jnp.concatenate([other for _, other in pairs], axis=0), other_ref)


def piece_body(table, mine_ref, got_ref, piece):
    flag = table[Y] == 0
    mine, got = mine_ref[...], got_ref[...]
    low, high = jnp.where(flag, mine, got), jnp.where(flag, got, mine)
    half, cols = mine.shape[0], mine.shape[1] // 2
    for i in range(2):
        piece[i * half : (i + 1) * half, :cols] = low[:, i * cols : (i + 1) * cols]
        piece[i * half : (i + 1) * half, cols:] = high[:, i * cols : (i + 1) * cols]


def sum_body(table, *refs):
    parts, (mine_ref, other_ref) = refs[:-2], refs[-2:]
    whole = [part for part in parts if part.shape == parts[0].shape]
    total = whole[0][...].astype(f32)
    for part in whole[1:]:
        total = total + part[...].astype(f32)
    rest = [part[...].astype(f32) for part in parts if part.shape != parts[0].shape]
    if rest:
        total = total + jnp.concatenate(rest, axis=0)
    cols = total.shape[1] // 2
    low, high = total[:, :cols], total[:, cols:]
    flag = table[Y] == 0
    pack(jnp.where(flag, low, high), mine_ref)
    pack(jnp.where(flag, high, low), other_ref)


def join_body(table, mine_ref, got_ref, *outs):
    flag = table[Y] == 0
    cols = mine_ref.shape[1] // 2

    def unpacked(ref):
        return jnp.concatenate([ref[:, :cols], ref[:, cols:]], axis=0).astype(f32)

    mine, got = unpacked(mine_ref), unpacked(got_ref)
    low, high = jnp.where(flag, mine, got), jnp.where(flag, got, mine)
    at = 0
    for out in outs:
        rows = out.shape[1] // 2
        out[:, :rows] = low[at : at + rows].T
        out[:, rows:] = high[at : at + rows].T
        at += rows


def rope_tables(positions, half):
    freq = rope_base ** (-(2.0 * jnp.arange(half, dtype=f32)) / (2.0 * half))
    angle = freq[:, None] * positions.astype(f32)[None, :]
    return (jnp.cos(angle), jnp.sin(angle))


def shards(
    layer_in,
    first_gain,
    query_weight,
    key_matrix,
    value_matrix,
    out_weight,
    second_gain,
    gate_weight,
    up_weight,
    down_weight,
    out_grad,
):
    place = Place()
    n, ny, y, z_in, table = place.n, place.ny, place.y, place.z_in, place.table
    lined = place.lined
    block, width = layer_in.shape
    tokens = 2 * block
    model_width = width * ny
    hidden_dev = gate_weight.shape[1] // 2
    query_rows = query_weight.shape[1] // 2
    kv_rows = key_matrix.shape[1]
    qkv_cols = query_rows + kv_rows
    full = (ny, tokens, width)
    wide = [(full[1:], bf16)] * 4

    def halves(*matrices, earlier=()):
        rows = sum(m.shape[1] for m in matrices) // 2
        packed = (rows // 2, 2 * matrices[0].shape[0])
        return call(split_body, [(packed, bf16)] * 2, table, [], held=matrices, earlier=earlier)

    def whole_piece(mine, got):
        rows, cols = mine.shape
        (piece,) = call(piece_body, [((2 * rows, cols), bf16)], table, [mine, got])
        return piece

    def spread(value, *before_y):
        by_x = place.swap_x(value)
        late, late_x = lax.optimization_barrier((value, by_x) + before_y)[:2]
        four = [value, by_x, place.swap_y(late), place.swap_y(late_x)]
        return four + [place.swap_c(r) for r in four]

    mine, other = halves(query_weight, key_matrix, value_matrix, out_weight.T)
    attend_got = place.swap_y(other)
    attend_piece = whole_piece(mine, attend_got)
    mine, other = halves(gate_weight, up_weight, down_weight.T, earlier=[attend_piece])
    forward_got = place.swap_y(other)
    forward_piece = whole_piece(mine, forward_got)
    rows = jnp.concatenate([layer_in, out_grad], axis=0)
    input_rows = spread(after(rows, attend_piece), forward_got)
    if lined:
        attend_pieces = gather_pieces(place, attend_piece)
        forward_pieces = gather_pieces(place, after(forward_piece, *attend_pieces[1:]), True)
    else:
        attend_pieces = [gather_whole(place, attend_piece)]
        forward_pieces = [gather_whole(place, forward_piece)]
    attend_shape = (ny, qkv_cols + query_rows, width)
    forward_shape = (ny, 3 * hidden_dev, width)
    sems = pltpu.SemaphoreType.DMA((ny,))

    gains = jnp.stack([first_gain, second_gain])
    two = [gains, place.swap_x(gains)]
    gains = two + [place.swap_c(g) for g in two]
    raw, grad, normed_in, inverse_in, gain_in, gain_mid = call(
        rows_body,
        [(full, bf16)] * 3 + [((tokens, 1), f32)] + [((ny, 1, width), f32)] * 2,
        table,
        input_rows + gains,
    )

    within = jnp.arange(block, dtype=jnp.int32)
    positions = jnp.minimum(place.offset, PROMPT_DEV)[:, None] * block + within[None, :]
    cosine, sine = rope_tables(positions.reshape(-1), HEAD_DIM // 2)
    query, own, attend_weights = call(
        qkv_body,
        [((query_rows, tokens), bf16), ((kv_rows, tokens), bf16), (attend_shape, bf16)],
        table,
        [normed_in, cosine, sine],
        [attend_pieces],
        [pltpu.VMEM((qkv_cols, tokens), f32), sems],
    )
    moved = [
        place.send_z(
            own,
            [(s, s + k) for s in range(n) if s % GROUP < PROMPTS and s % GROUP + k < GROUP],
        )
        for k in range(1, GROUP)
    ]
    attended, attended_low, log_total, far, *halves_out = call(
        attend_body,
        [
            ((query_rows, tokens), f32),
            ((query_rows, tokens), bf16),
            ((query_rows // HEAD_DIM, 1, tokens), f32),
            ((kv_rows, PROMPTS * tokens), bf16),
        ]
        + wide,
        table,
        [query, own] + moved + [attend_weights],
    )
    summed = all_sum(
        place,
        halves_out[:2],
        halves_out[2:],
        before_first=forward_pieces[1:3] if lined else forward_pieces,
        before_last=forward_pieces[3:],
    )

    hidden, normed_mid, inverse_mid = call(
        hidden_body,
        [(full, f32), (full, bf16), ((tokens, 1), f32)],
        table,
        summed,
        held=[raw, gain_mid],
    )
    active, change, *halves_out, down_whole = call(
        forward_body,
        [((tokens, hidden_dev), bf16), ((tokens, 2 * hidden_dev), bf16)]
        + wide
        + [((ny, hidden_dev, width), bf16)],
        table,
        [normed_mid],
        [forward_pieces],
        [
            pltpu.VMEM((ny, 2 * hidden_dev, width), bf16),
            pltpu.VMEM((tokens, 2 * hidden_dev), f32),
        ]
        + [pltpu.VMEM((tokens, hidden_dev), f32)] * 2
        + [sems, sems],
        held=[grad],
    )
    third, both = call(
        forward_third_body,
        [(forward_shape[1:], bf16), (forward_shape[1:2] + (tokens,), bf16)],
        table,
        [active, normed_mid, change],
        held=[grad],
    )
    forward_parts = call(
        forward_parts_body,
        [(forward_shape[1:], bf16)] * 3,
        table,
        [both, normed_mid],
        held=[grad],
    )
    forward_parts = list(forward_parts) + [third]
    forward_started = start_scatter(place, forward_parts)
    down_halves = call(
        down_body, wide, table, [active, down_whole], earlier=[forward_parts[0]]
    )
    summed = all_sum(
        place,
        halves_out[:2],
        halves_out[2:],
        before_second=forward_parts[:1],
        before_last=list(down_halves[:1]) + forward_started[2:3] + forward_started[4:],
    )
    _, forward_second = second_scatter(place, forward_started, 0, 2, summed[-1])
    hidden_own = own_block(place, hidden)
    through, pull, query_low, own_back, *returns, inner_first = call(
        attend_back_body,
        [
            (full, bf16),
            ((tokens, 1), f32),
            ((query_rows, tokens), bf16),
            ((kv_rows, tokens), f32),
        ]
        + [((kv_rows, tokens), bf16)] * (GROUP - 1)
        + [((1, tokens), f32)],
        table,
        summed,
        held=[
            hidden,
            inverse_mid,
            grad,
            gain_mid,
            attend_weights,
            query,
            own,
            far,
            attended,
            log_total,
            cosine,
            sine,
        ],
        earlier=forward_started[2:3] + forward_started[4:],
        scratch=[
            pltpu.VMEM((kv_rows, PROMPTS * tokens), f32),
            pltpu.VMEM(full, f32),
            pltpu.VMEM((query_rows, tokens), bf16),
        ],
    )
    down_sends = lax.optimization_barrier(tuple(down_halves[2:]) + (through,))[:2]
    layer_out = (hidden_own + own_sum(place, down_halves[:2], down_sends)).astype(bf16)
    inverse_own, _ = part_of(y, inverse_mid, 0)
    pull_own, _ = part_of(y, pull, 0)
    mid_own = jnp.where(place.x == 0, summed[0], summed[1])
    mid_own = part_of(y, mid_own, 0)[0].astype(f32)
    through_own = (
        out_grad.astype(f32)
        + inverse_own * mid_own * second_gain[None, :]
        - hidden_own * pull_own
    )
    second_term = jnp.sum(mid_own * hidden_own * inverse_own, axis=0)

    moved = [
        place.send_z(
            returns[k - 1],
            [(s, s - k) for s in range(n) if 0 <= s % GROUP - k < PROMPTS],
        )
        for k in range(1, GROUP)
    ]
    attend_parts = call(
        attend_parts_body,
        [(attend_shape[1:], bf16)] * ny,
        table,
        [query_low, through],
        held=[normed_in, attended_low],
    )
    results = call(
        qkv_back_body,
        [(attend_shape[1:], bf16)] * ny
        + wide
        + [((1, tokens), f32), ((kv_rows, tokens), bf16)],
        table,
        list(attend_parts) + [own_back] + moved + [query_low, inner_first],
        held=[attend_weights, cosine, sine, own, normed_in],
        scratch=[pltpu.VMEM((ny, kv_rows, width), bf16), sems],
        earlier=forward_started[3:4] + ([forward_second] if lined else []),
        alias=ny,
    )
    attend_parts, first_halves = results[:ny], results[ny:-2]
    inner, own_low = results[-2:]
    attend_started = start_scatter(place, attend_parts)
    forward_seconds = [
        forward_second,
        second_scatter(place, forward_started, 1, 2, summed[-1], moved[0])[1],
    ]
    attend_sent, attend_second = second_scatter(place, attend_started, 0, 1)
    attend_grad = end_scatter(place, attend_started, [attend_second], own_low)
    inner = inner + place.swap_c(inner)
    inner = inner + place.swap_x(inner)
    inner = inner + place.swap_y(inner)
    first_own = own_sum(
        place,
        first_halves[:2],
        first_halves[2:],
        before_y=[attend_sent] if lined else [],
    )
    forward_grad = end_scatter(
        place, forward_started, forward_seconds, *([attend_sent] if lined else [])
    )
    input_own = layer_in.astype(f32)
    inverse_own, _ = part_of(y, inverse_in, 0)
    scaled = first_own * first_gain[None, :]
    inner = part_of(y, inner.reshape(tokens, 1), 0)[0]
    in_grad = (
        through_own + inverse_own * scaled - input_own * (inverse_own**2 * inner / model_width)
    )
    first_term = jnp.sum(first_own * input_own * inverse_own, axis=0)
    terms = jnp.stack([first_term, second_term])
    bit = 1
    while bit < place.nx:
        terms = terms + place.swap_gx(terms, bit)
        bit *= 2

    def joined(parts, outs):
        rows, cols = parts[0].shape
        packed = (rows // 2, cols)
        mine, other = call(sum_body, [(packed, f32), (packed, bf16)], table, parts)
        shapes = [(cols // 2, inner) for inner in outs]
        return call(
            join_body, [(s, f32) for s in shapes], table, [mine, place.swap_y(other)]
        )

    gate_grad, up_grad, down_grad = joined(forward_grad, [2 * hidden_dev] * 3)
    query_out, key_out, value_out, out_out = joined(
        attend_grad, [2 * query_rows, kv_rows, kv_rows, 2 * query_rows]
    )
    return (
        layer_out,
        in_grad,
        terms[0],
        query_out,
        key_out,
        value_out,
        out_out.T,
        terms[1],
        gate_grad,
        up_grad,
        down_grad.T,
    )


def solution(mesh):
    rows, cols, gain = P("gx", "gy"), P("gy", "gx"), P("gy")
    return jax.shard_map(
        shards,
        mesh=mesh,
        in_specs=(rows, gain, rows, rows, rows, cols, gain, rows, rows, cols, rows),
        out_specs=(rows, rows, gain, rows, rows, rows, cols, gain, rows, rows, cols),
        check_vma=False,
    )
```

```python
from functools import partial

import jax
import jax.numpy as jnp
from jax import lax
from jax.experimental import pallas as pl
from jax.experimental.pallas import tpu as pltpu
from jax.sharding import PartitionSpec as P

HEAD_DIM = 96
PROMPT_DEV = 4
CONT_DEV = 4
GROUP = (PROMPT_DEV + CONT_DEV) // 2
PROMPTS = PROMPT_DEV // 2

eps = 1e-05
neg_big = -1e30
rope_base = 100000.0
score_scale = HEAD_DIM ** (-0.5)
f32 = jnp.float32
bf16 = jnp.bfloat16


def dims(left, right, left_axis, right_axis):
    return lax.dot_general(
        left, right, (((left_axis,), (right_axis,)), ((), ())), preferred_element_type=f32
    )


class Place:
    def __init__(self):
        self.nx = lax.axis_size("gx")
        self.ny = lax.axis_size("gy")
        assert self.ny == 4 and self.nx % (PROMPT_DEV + CONT_DEV) == 0
        self.n = self.nx // 2
        self.gx = lax.axis_index("gx")
        self.gy = lax.axis_index("gy")
        self.z, self.y = self.gx // 2, self.gx % 2
        self.x, self.c = self.gy // 2, self.gy % 2
        self.z_in = self.z % GROUP
        offset = 2 * self.z_in + jnp.arange(2, dtype=jnp.int32)
        self.offset = offset
        self.lined = self.n == self.ny
        blocks = jnp.arange(self.ny, dtype=jnp.int32)
        first = jnp.stack([self.z, self.y, self.x, self.c, self.z_in]).astype(jnp.int32)
        self.table = jnp.concatenate(
            [first, jnp.minimum(offset, PROMPT_DEV), blocks ^ self.z if self.lined else blocks]
        )

    def swap_gx(self, value, bit):
        return lax.ppermute(value, "gx", [(i, i ^ bit) for i in range(self.nx)])

    def swap_y(self, value):
        return self.swap_gx(value, 1)

    def swap_x(self, value):
        return lax.ppermute(value, "gy", [(i, i ^ 2) for i in range(self.ny)])

    def swap_c(self, value):
        return lax.ppermute(value, "gy", [(i, i ^ 1) for i in range(self.ny)])

    def send_z(self, value, moves):
        pairs = [(2 * s + y, 2 * t + y) for s, t in moves for y in range(2)]
        return lax.ppermute(value, "gx", pairs)

    def by_y(self):
        return [[2 * z + y for z in range(self.n)] for y in range(2)]


def pair(flag, mine, other):
    return jnp.where(flag == 0, mine, other), jnp.where(flag == 0, other, mine)


def part_of(flag, whole, axis):
    low, high = jnp.split(whole, 2, axis)
    return jnp.where(flag == 0, low, high), jnp.where(flag == 0, high, low)


def after(value, *earlier):
    return lax.optimization_barrier((value,) + earlier)[0]


NEAR = [(0, 1), (1, 0), (2, 3), (3, 2)]
SECOND = [(0, 2), (1, 3), (2, 0), (3, 1)]
MIDDLE = [(1, 2), (2, 1)]
INWARD = [(0, 1), (3, 2)]
OUTWARD = [(1, 0), (2, 3)]


def gather_pieces(place, piece, late_middle=False):
    second = place.send_z(piece, SECOND)
    near = place.send_z(piece, NEAR)
    middle = place.send_z(after(piece, second) if late_middle else piece, MIDDLE)
    return [piece, near, second, middle, place.send_z(second, OUTWARD)]


def gather_whole(place, piece):
    every = lax.all_gather(piece, "gx", axis_index_groups=place.by_y())
    inner = place.n // place.ny
    if inner == 1:
        return every
    rows, cols = piece.shape
    every = every.reshape(place.ny, inner, rows, cols)
    return jnp.swapaxes(every, 1, 2).reshape(place.ny, rows, inner * cols)


def scatter_whole(place, parts):
    inner = place.n // place.ny
    if inner > 1:
        count, rows, cols = parts.shape
        parts = jnp.swapaxes(parts.reshape(count, rows, inner, cols // inner), 1, 2)
        parts = parts.reshape(place.n, rows, cols // inner)
    return lax.psum_scatter(parts, "gx", axis_index_groups=place.by_y())


def start_scatter(place, parts):
    if not place.lined:
        return [scatter_whole(place, jnp.stack(parts))]
    own, near, second, third = parts
    far = place.send_z(third, INWARD)
    middle = place.send_z(third, MIDDLE)
    return [own, second, far, place.send_z(near, NEAR), middle]


def second_scatter(place, started, part, count, *earlier):
    if not place.lined:
        return None, None
    rows, cols = started[1].shape
    at = slice(part * (rows // count), (part + 1) * (rows // count))
    (summed,) = call(
        partial(add_body, rows=at),
        [((rows // count, cols), bf16)],
        place.table,
        [],
        [started[1:3]],
        [pltpu.VMEM((rows // count, cols), bf16)] * 2 + [pltpu.SemaphoreType.DMA((2,))],
        earlier=[started[4]] + list(earlier),
    )
    return summed, place.send_z(summed, SECOND)


def end_scatter(place, started, seconds, *earlier):
    if not place.lined:
        return started
    return [after(started[0], *earlier), started[3], started[4]] + list(seconds)


def add(left, right):
    return (left.astype(f32) + right.astype(f32)).astype(bf16)


def reduce_core(place, keeps, sends):
    return [add(keep, place.swap_c(send)) for keep, send in zip(keeps, sends)]


def all_sum(place, keeps, sends, before_first=(), before_second=(), before_last=()):
    low = tuple(reduce_core(place, keeps, sends))
    low = lax.optimization_barrier(low + tuple(before_first))
    low = add(low[0], place.swap_x(low[0])), add(low[1], place.swap_y(low[1]))
    low = lax.optimization_barrier(low + tuple(before_second))
    own = (add(low[0], place.swap_y(low[0])), add(low[1], place.swap_x(low[1])))
    if before_last:
        own = lax.optimization_barrier(own + tuple(before_last))[:2]
    own = list(own)
    return own + [place.swap_c(part) for part in own]


def own_sum(place, keeps, sends, before_x=(), before_y=()):
    first, second = reduce_core(place, keeps, sends)
    if before_x:
        first, second = lax.optimization_barrier((first, second) + tuple(before_x))[:2]
    mine, other = jnp.where(place.x == 0, first, second), jnp.where(place.x == 0, second, first)
    mine = add(mine, place.swap_x(other))
    mine = after(mine, *before_y) if before_y else mine
    mine, other = part_of(place.y, mine, 0)
    return mine.astype(f32) + place.swap_y(other).astype(f32)


def own_block(place, blocks):
    rows = blocks.shape[1] // 2
    return lax.dynamic_slice(
        blocks, (place.gy, place.y * rows, 0), (1, rows, blocks.shape[2])
    )[0]


Z, Y, X, C, Z_IN, COUNT = range(6)
ORDER = COUNT + 2


def call(body, outs, table, operands, pieces=(), scratch=(), earlier=(), held=(), alias=0, limit=24):
    lengths = [len(p) for p in pieces]
    flat = [a for p in pieces for a in p] + list(earlier)
    vmem = pl.BlockSpec(memory_space=pltpu.VMEM)
    copied = [pltpu.VMEM(a.shape, a.dtype) for a in held]
    if held:
        copied.append(pltpu.SemaphoreType.DMA((len(held),)))

    def kernel(table_ref, *refs):
        plain, rest = refs[: len(operands)], refs[len(operands) :]
        sources, rest = rest[: len(held)], rest[len(held) :]
        lists = []
        for length in lengths:
            lists.append(rest[:length])
            rest = rest[length:]
        rest = rest[len(earlier) :]
        targets = ()
        if held:
            rest, targets = rest[: -len(copied)], rest[-len(copied) :]
            copies = [
                pltpu.make_async_copy(source, target, targets[-1].at[i])
                for i, (source, target) in enumerate(zip(sources, targets))
            ]
            for copy in copies:
                copy.start()
            for copy in copies:
                copy.wait()
        body(table_ref, *plain, *targets[:-1], *lists, *rest)

    return pl.pallas_call(
        kernel,
        out_shape=[jax.ShapeDtypeStruct(shape, dtype) for shape, dtype in outs],
        in_specs=[pl.BlockSpec(memory_space=pltpu.SMEM)]
        + [pl.BlockSpec(memory_space=pl.ANY)] * alias
        + [vmem] * (len(operands) - alias)
        + [pl.BlockSpec(memory_space=pltpu.HBM)] * len(held)
        + [pl.BlockSpec(memory_space=pl.ANY)] * len(flat),
        out_specs=[pl.BlockSpec(memory_space=pl.ANY)] * alias + [vmem] * (len(outs) - alias),
        scratch_shapes=list(scratch) + copied,
        input_output_aliases={i + 1: i for i in range(alias)},
        compiler_params=pltpu.CompilerParams(vmem_limit_bytes=limit << 20),
    )(table, *operands, *held, *flat)


def start_pieces(table, pieces, whole, sems, rows=slice(None)):
    count = whole.shape[0]
    block = [table[ORDER + k] for k in range(count)]

    def copy(piece, k):
        source = piece.at[rows] if rows != slice(None) else piece
        return pltpu.make_async_copy(source, whole.at[block[k]], sems.at[k])

    def wait(k):
        pltpu.make_async_copy(whole.at[0], whole.at[0], sems.at[k]).wait()

    if len(pieces) == 1:
        for k in range(count):
            copy(pieces[0].at[block[k]], k).start()
        return wait
    z = table[Z]
    own, near, second, middle, end = pieces
    for k, piece in enumerate((own, near, second)):
        copy(piece, k).start()
    inside = jnp.logical_or(z == 1, z == 2)

    @pl.when(inside)
    def _():
        copy(middle, 3).start()

    @pl.when(jnp.logical_not(inside))
    def _():
        copy(end, 3).start()

    return wait


def keep_and_send(table, block_of, outs):
    core = table[C]
    for i in range(2):
        outs[i][...] = block_of(2 * i + core).astype(bf16)
        outs[2 + i][...] = block_of(2 * i + 1 - core).astype(bf16)


def place_rows(table, pieces, raw, grad):
    x, y, c = table[X], table[Y], table[C]
    tokens = raw.shape[1] // 2
    for dc in range(2):
        for dx in range(2):
            block = 2 * (x + dx - 2 * x * dx) + c + dc - 2 * c * dc
            for dy in range(2):
                at = pl.ds(pl.multiple_of(tokens * (y + dy - 2 * y * dy), tokens), tokens)
                piece = pieces[4 * dc + 2 * dy + dx]
                raw[block, at, :] = piece[:tokens]
                grad[block, at, :] = piece[tokens:]


def norm_rows(raw, gain, normed):
    def square(b, total):
        values = raw[b].astype(f32)
        return total + jnp.sum(values * values, axis=1, keepdims=True)

    count = raw.shape[0]
    total = lax.fori_loop(0, count, square, jnp.zeros((raw.shape[1], 1), f32))
    scale = lax.rsqrt(total / (count * raw.shape[2]) + eps)

    def norm(b, _):
        normed[b] = (raw[b].astype(f32) * scale * gain[b]).astype(bf16)
        return 0

    lax.fori_loop(0, count, norm, 0)
    return scale


def rows_body(table, *refs):
    gains = refs[8:12]
    raw, grad, normed, inverse, gain_first, gain_second = refs[12:]
    place_rows(table, refs[:8], raw, grad)
    x, c = table[X], table[C]
    for dc in range(2):
        for dx in range(2):
            block = 2 * (x + dx - 2 * x * dx) + c + dc - 2 * c * dc
            gain = gains[2 * dc + dx][...]
            gain_first[block] = gain[0:1]
            gain_second[block] = gain[1:2]
    inverse[...] = norm_rows(raw, gain_first, normed)


def turn(values, cosine, sine):
    half = values.shape[0] // 2
    first, second = values[:half], values[half:]
    return jnp.concatenate(
        [first * cosine - second * sine, second * cosine + first * sine], axis=0
    )


def qkv_body(
    table, normed, cosine, sine, pieces, query, own, weights, acc, sems
):
    wait = start_pieces(table, pieces, weights, sems)
    count = acc.shape[0]
    acc[...] = jnp.zeros_like(acc)

    def one(k, _):
        b = table[ORDER + k]
        wait(k)
        acc[...] += dims(weights[b, :count], normed[b], 1, 1)
        return 0

    lax.fori_loop(0, normed.shape[0], one, 0)
    head = HEAD_DIM
    heads = query.shape[0] // head
    cos, sin = cosine[...], sine[...]
    for h in range(heads):
        at = slice(h * head, (h + 1) * head)
        query[at] = turn(acc[at], cos, sin).astype(bf16)
    at = slice(heads * head, (heads + 1) * head)
    own[:head] = turn(acc[at], cos, sin).astype(bf16)
    own[head:] = acc[(heads + 1) * head :].astype(bf16)


def attend_body(table, query, own, *refs):
    moved, refs = refs[: GROUP - 1], refs[GROUP - 1 :]
    (weights, attended, attended_low, log_total, far), outs = refs[:5], refs[5:]
    tokens = own.shape[1]
    for place in range(GROUP):

        @pl.when(table[Z_IN] == place)
        def _():
            for slot in range(PROMPTS):
                k = place - slot
                far[:, slot * tokens : (slot + 1) * tokens] = (
                    moved[k - 1][...] if k > 0 else own[...]
                )

    head = HEAD_DIM
    block = tokens // 2
    key_far, value_far = far[:head].T, far[head:]
    key_own = own[:head].T
    total = far.shape[1]
    near_row = lax.broadcasted_iota(jnp.int32, (block, block), 0)
    near_col = lax.broadcasted_iota(jnp.int32, (block, block), 1)
    causal = near_row <= near_col
    row = lax.broadcasted_iota(jnp.int32, (total, block), 0)
    for part in range(2):
        cols = slice(part * block, (part + 1) * block)
        key_near, value_near = key_own[cols], own[head:, cols]
        seen = row < table[COUNT + part] * block

        def one(h, _):
            at = pl.ds(pl.multiple_of(h * head, head), head)
            rows = query[at, cols]
            score_far = jnp.where(seen, dims(key_far, rows, 1, 0) * score_scale, neg_big)
            score_near = jnp.where(causal, dims(key_near, rows, 1, 0) * score_scale, neg_big)
            top = jnp.maximum(
                jnp.max(score_far, axis=0, keepdims=True), jnp.max(score_near, axis=0, keepdims=True)
            )
            weight_far = jnp.exp(score_far - top)
            weight_near = jnp.exp(score_near - top)
            weight = jnp.sum(weight_far, axis=0, keepdims=True) + jnp.sum(
                weight_near, axis=0, keepdims=True
            )
            out = dims(value_far, weight_far.astype(bf16), 1, 0) + dims(
                value_near, weight_near.astype(bf16), 1, 0
            )
            attended[at, cols] = out / weight
            log_total[h, :, cols] = top + jnp.log(weight)
            return 0

        lax.fori_loop(0, query.shape[0] // head, one, 0)
    values = attended[...]
    attended_low[...] = values.astype(bf16)
    flipped = values.T.astype(bf16)
    first = weights.shape[1] - query.shape[0]
    keep_and_send(
        table,
        lambda b: dims(flipped, weights[b, first:], 1, 0),
        outs,
    )


def hidden_body(
    table, own_first, own_second, other_first, other_second, raw, gain, hidden, normed, inverse
):
    core = table[C]
    summed, other = (own_first, own_second), (other_first, other_second)
    for i in range(2):
        b = 2 * i + core
        hidden[b] = raw[b].astype(f32) + summed[i][...].astype(f32)
        b = 2 * i + 1 - core
        hidden[b] = raw[b].astype(f32) + other[i][...].astype(f32)

    def square(b, total):
        values = hidden[b]
        return total + jnp.sum(values * values, axis=1, keepdims=True)

    count = raw.shape[0]
    total = lax.fori_loop(0, count, square, jnp.zeros((raw.shape[1], 1), f32))
    scale = lax.rsqrt(total / (count * raw.shape[2]) + eps)
    inverse[...] = scale

    def norm(b, _):
        normed[b] = (hidden[b] * scale * gain[b]).astype(bf16)
        return 0

    lax.fori_loop(0, count, norm, 0)


def forward_body(
    table,
    normed,
    grad,
    pieces,
    active,
    change,
    *refs,
):
    outs, (down, weights, acc, gate_slope, up_slope, sems, down_sems) = refs[:4], refs[4:]
    split = weights.shape[1]
    wait = start_pieces(table, pieces, weights, sems, slice(0, split))
    down_wait = start_pieces(
        table, pieces, down, down_sems, slice(split, split + down.shape[1])
    )
    count, tokens = normed.shape[:2]
    width = acc.shape[1]
    half = width // 2
    acc[...] = jnp.zeros_like(acc)

    def one(k, _):
        b = table[ORDER + k]
        wait(k)
        acc[...] += dims(normed[b], weights[b, :width], 1, 1)
        return 0

    lax.fori_loop(0, count, one, 0)
    rows = tokens // 4

    def part(i, _):
        at = pl.ds(pl.multiple_of(i * rows, rows), rows)
        gate, up = acc[at, :half], acc[at, half:]
        sigmoid = jax.nn.sigmoid(gate)
        active[at] = (gate * sigmoid * up).astype(bf16)
        gate_slope[at] = up * sigmoid * (1.0 + gate * (1.0 - sigmoid))
        up_slope[at] = gate * sigmoid
        return 0

    lax.fori_loop(0, 4, part, 0)

    def back(k, total):
        b = table[ORDER + k]
        down_wait(k)
        return total + dims(grad[b], down[b], 1, 1)

    slope = lax.fori_loop(0, count, back, jnp.zeros((tokens, half), f32))
    change[:, :half] = (slope * gate_slope[...]).astype(bf16)
    change[:, half:] = (slope * up_slope[...]).astype(bf16)
    values = change[...]
    keep_and_send(
        table,
        lambda b: dims(values, weights[b, :width], 1, 0),
        outs,
    )


def forward_third_body(table, active, normed, change, grad, third, both):
    width = change.shape[1]
    both[:width] = change[...].T
    both[width:] = active[...].T
    b = table[ORDER + 3]
    third[:width] = dims(both[:width], normed[b], 1, 0).astype(bf16)
    third[width:] = dims(both[width:], grad[b], 1, 0).astype(bf16)


def forward_parts_body(table, both, normed, grad, *parts):
    rows = both.shape[0] // 6

    def fill(first, count, source):
        def one(i, _):
            at = pl.ds(pl.multiple_of((first + i) * rows, rows), rows)
            for k, part in enumerate(parts):
                part[at] = dims(both[at], source[table[ORDER + k]], 1, 0).astype(bf16)
            return 0

        lax.fori_loop(0, count, one, 0)

    fill(0, 4, normed)
    fill(4, 2, grad)


def down_body(table, active, weights, *outs):
    values = active[...]
    keep_and_send(table, lambda b: dims(values, weights[b], 1, 0), outs)


def attend_back_body(
    table,
    own_first,
    own_second,
    other_first,
    other_second,
    hidden,
    inverse,
    grad,
    gain,
    weights,
    query,
    own,
    far,
    attended,
    log_total,
    cosine,
    sine,
    through,
    pull,
    query_low,
    own_back,
    *rest,
):
    sends, inner_first = rest[: GROUP - 1], rest[GROUP - 1]
    far_back, change, branch = rest[GROUP:]
    core = table[C]
    count, tokens, model = hidden.shape
    for i, (mine, theirs) in enumerate(((own_first, other_first), (own_second, other_second))):
        change[2 * i + core] = mine[...].astype(f32) * gain[2 * i + core]
        change[2 * i + 1 - core] = theirs[...].astype(f32) * gain[2 * i + 1 - core]

    def product(b, total):
        return total + jnp.sum(change[b] * hidden[b], axis=1, keepdims=True)

    inner = lax.fori_loop(0, count, product, jnp.zeros((tokens, 1), f32))
    scale = inverse[...]
    back = scale * scale * scale * inner / (count * model)
    pull[...] = back

    def rows(b, total):
        values = grad[b].astype(f32) + scale * change[b] - hidden[b] * back
        low = values.astype(bf16)
        through[b] = low
        return total + dims(low, weights[b, first:], 1, 1)

    heads_cols = query.shape[0]
    first = weights.shape[1] - heads_cols
    total_rows = lax.fori_loop(0, count, rows, jnp.zeros((tokens, heads_cols), f32))
    branch[...] = total_rows.T.astype(bf16)

    head = HEAD_DIM
    block = tokens // 2
    key_far_t = far[:head]
    key_far, value_far = key_far_t.T, far[head:].T
    key_own, value_own = own[:head].T, own[head:].T
    total = far.shape[1]
    near_row = lax.broadcasted_iota(jnp.int32, (block, block), 0)
    near_col = lax.broadcasted_iota(jnp.int32, (block, block), 1)
    causal = near_row <= near_col
    row = lax.broadcasted_iota(jnp.int32, (total, block), 0)
    far_back[...] = jnp.zeros_like(far_back)
    own_back[...] = jnp.zeros_like(own_back)
    inner_first[...] = jnp.zeros_like(inner_first)
    for part in range(2):
        cols = slice(part * block, (part + 1) * block)
        key_near, value_near = key_own[cols], value_own[cols]
        key_near_t = own[:head, cols]
        seen = row < table[COUNT + part] * block

        def one_head(h, _):
            at = pl.ds(pl.multiple_of(h * head, head), head)
            rows_q, rows_grad = query[at, cols], branch[at, cols]
            delta = jnp.sum(
                rows_grad.astype(f32) * attended[at, cols], axis=0, keepdims=True
            )
            logs = log_total[h, :, cols]

            def one(key, value, allowed):
                score = dims(key, rows_q, 1, 0) * score_scale
                prob = jnp.where(allowed, jnp.exp(score - logs), 0.0)
                moved = (prob * (dims(value, rows_grad, 1, 0) - delta)).astype(bf16)
                return prob.astype(bf16), moved

            prob_far, moved_far = one(key_far, value_far, seen)
            prob_near, moved_near = one(key_near, value_near, causal)
            query_back = (
                dims(key_far_t, moved_far, 1, 0) + dims(key_near_t, moved_near, 1, 0)
            ) * score_scale
            inner_first[:, cols] += jnp.sum(
                query_back * rows_q.astype(f32), axis=0, keepdims=True
            )
            query_low[at, cols] = turn(query_back, cosine[:, cols], -sine[:, cols]).astype(bf16)
            far_back[:head] += dims(rows_q, moved_far, 1, 1) * score_scale
            far_back[head:] += dims(rows_grad, prob_far, 1, 1)
            own_back[:head, cols] += dims(rows_q, moved_near, 1, 1) * score_scale
            own_back[head:, cols] += dims(rows_grad, prob_near, 1, 1)
            return 0

        lax.fori_loop(0, heads_cols // head, one_head, 0)
    for slot in range(PROMPTS):

        @pl.when(table[Z_IN] == slot)
        def _():
            own_back[...] += far_back[:, slot * tokens : (slot + 1) * tokens]

    for k in range(1, GROUP):
        sends[k - 1][...] = far_back[:, :tokens].astype(bf16)
        for slot in range(1, PROMPTS):

            @pl.when(table[Z_IN] == slot + k)
            def _():
                sends[k - 1][...] = far_back[:, slot * tokens : (slot + 1) * tokens].astype(bf16)


def attend_parts_body(table, query_low, through, normed, attended_low, *parts):
    rows = query_low.shape[0]
    for k, part in enumerate(parts):
        b = table[ORDER + k]
        part[:rows] = dims(query_low[...], normed[b], 1, 0).astype(bf16)
        part[-rows:] = dims(attended_low[...], through[b], 1, 0).astype(bf16)


def qkv_back_body(table, *refs):
    count = table.shape[0] - ORDER
    own_back, moved, refs = refs[count], refs[count + 1 : count + GROUP], refs[count + GROUP :]
    query_low, inner, weights, cosine, sine, own, normed = refs[:7]
    parts, outs = refs[7 : 7 + count], refs[7 + count : 11 + count]
    inner_first, own_low, changed, sems = refs[11 + count :]
    head = HEAD_DIM
    total = own_back[...]
    for part in moved:
        total = total + part[...].astype(f32)
    inner_first[...] = inner[...] + jnp.sum(total * own[...].astype(f32), axis=0, keepdims=True)
    key = turn(total[:head], cosine[...], -sine[...])
    low = jnp.concatenate([key, total[head:]], axis=0)
    own_low[...] = low.astype(bf16)
    first = query_low.shape[0]
    copies = []
    for k, part in enumerate(parts):
        changed[k] = dims(own_low[...], normed[table[ORDER + k]], 1, 0).astype(bf16)
        target = part.at[first : first + low.shape[0]]
        copies.append(pltpu.make_async_copy(changed.at[k], target, sems.at[k]))
        copies[k].start()
    flipped = jnp.concatenate([query_low[...].T, low.T.astype(bf16)], axis=1)
    width = flipped.shape[1]
    keep_and_send(table, lambda b: dims(flipped, weights[b, :width], 1, 0), outs)
    for copy in copies:
        copy.wait()


def halves_of(table, whole):
    half = whole.shape[0] // 2
    low, high = whole[:half], whole[half:]
    flag = table[Y] == 0
    return jnp.where(flag, low, high), jnp.where(flag, high, low)


def add_body(table, sources, out, first, second, sems, *, rows):
    copies = [
        pltpu.make_async_copy(source.at[rows], held, sems.at[i])
        for i, (source, held) in enumerate(zip(sources, (first, second)))
    ]
    for copy in copies:
        copy.start()
    for copy in copies:
        copy.wait()
    out[...] = add(first[...], second[...])


def pack(rows, packed):
    half, cols = packed.shape[0], rows.shape[1]
    packed[:, :cols] = rows[:half].astype(packed.dtype)
    packed[:, cols:] = rows[half:].astype(packed.dtype)


def split_body(table, *refs):
    matrices, (mine_ref, other_ref) = refs[:-2], refs[-2:]
    pairs = [halves_of(table, matrix[...].T) for matrix in matrices]
    pack(jnp.concatenate([mine for mine, _ in pairs], axis=0), mine_ref)
    pack(jnp.concatenate([other for _, other in pairs], axis=0), other_ref)


def piece_body(table, mine_ref, got_ref, piece):
    flag = table[Y] == 0
    mine, got = mine_ref[...], got_ref[...]
    low, high = jnp.where(flag, mine, got), jnp.where(flag, got, mine)
    half, cols = mine.shape[0], mine.shape[1] // 2
    for i in range(2):
        piece[i * half : (i + 1) * half, :cols] = low[:, i * cols : (i + 1) * cols]
        piece[i * half : (i + 1) * half, cols:] = high[:, i * cols : (i + 1) * cols]


def sum_body(table, *refs):
    parts, (mine_ref, other_ref) = refs[:-2], refs[-2:]
    whole = [part for part in parts if part.shape == parts[0].shape]
    total = whole[0][...].astype(f32)
    for part in whole[1:]:
        total = total + part[...].astype(f32)
    rest = [part[...].astype(f32) for part in parts if part.shape != parts[0].shape]
    if rest:
        total = total + jnp.concatenate(rest, axis=0)
    cols = total.shape[1] // 2
    low, high = total[:, :cols], total[:, cols:]
    flag = table[Y] == 0
    pack(jnp.where(flag, low, high), mine_ref)
    pack(jnp.where(flag, high, low), other_ref)


def join_body(table, mine_ref, got_ref, *outs):
    flag = table[Y] == 0
    cols = mine_ref.shape[1] // 2

    def unpacked(ref):
        return jnp.concatenate([ref[:, :cols], ref[:, cols:]], axis=0).astype(f32)

    mine, got = unpacked(mine_ref), unpacked(got_ref)
    low, high = jnp.where(flag, mine, got), jnp.where(flag, got, mine)
    at = 0
    for out in outs:
        rows = out.shape[1] // 2
        out[:, :rows] = low[at : at + rows].T
        out[:, rows:] = high[at : at + rows].T
        at += rows


def rope_tables(positions, half):
    freq = rope_base ** (-(2.0 * jnp.arange(half, dtype=f32)) / (2.0 * half))
    angle = freq[:, None] * positions.astype(f32)[None, :]
    return (jnp.cos(angle), jnp.sin(angle))


def shards(
    layer_in,
    first_gain,
    query_weight,
    key_matrix,
    value_matrix,
    out_weight,
    second_gain,
    gate_weight,
    up_weight,
    down_weight,
    out_grad,
):
    place = Place()
    n, ny, y, z_in, table = place.n, place.ny, place.y, place.z_in, place.table
    lined = place.lined
    block, width = layer_in.shape
    tokens = 2 * block
    model_width = width * ny
    hidden_dev = gate_weight.shape[1] // 2
    query_rows = query_weight.shape[1] // 2
    kv_rows = key_matrix.shape[1]
    qkv_cols = query_rows + kv_rows
    full = (ny, tokens, width)
    wide = [(full[1:], bf16)] * 4

    def halves(*matrices, earlier=()):
        rows = sum(m.shape[1] for m in matrices) // 2
        packed = (rows // 2, 2 * matrices[0].shape[0])
        return call(split_body, [(packed, bf16)] * 2, table, [], held=matrices, earlier=earlier)

    def whole_piece(mine, got):
        rows, cols = mine.shape
        (piece,) = call(piece_body, [((2 * rows, cols), bf16)], table, [mine, got])
        return piece

    def spread(value, *before_y):
        by_x = place.swap_x(value)
        late, late_x = lax.optimization_barrier((value, by_x) + before_y)[:2]
        four = [value, by_x, place.swap_y(late), place.swap_y(late_x)]
        return four + [place.swap_c(r) for r in four]

    mine, other = halves(query_weight, key_matrix, value_matrix, out_weight.T)
    attend_got = place.swap_y(other)
    attend_piece = whole_piece(mine, attend_got)
    mine, other = halves(gate_weight, up_weight, down_weight.T, earlier=[attend_piece])
    forward_got = place.swap_y(other)
    forward_piece = whole_piece(mine, forward_got)
    rows = jnp.concatenate([layer_in, out_grad], axis=0)
    input_rows = spread(after(rows, attend_piece), forward_got)
    if lined:
        attend_pieces = gather_pieces(place, attend_piece)
        forward_pieces = gather_pieces(place, after(forward_piece, *attend_pieces[1:]), True)
    else:
        attend_pieces = [gather_whole(place, attend_piece)]
        forward_pieces = [gather_whole(place, forward_piece)]
    attend_shape = (ny, qkv_cols + query_rows, width)
    forward_shape = (ny, 3 * hidden_dev, width)
    sems = pltpu.SemaphoreType.DMA((ny,))

    gains = jnp.stack([first_gain, second_gain])
    two = [gains, place.swap_x(gains)]
    gains = two + [place.swap_c(g) for g in two]
    raw, grad, normed_in, inverse_in, gain_in, gain_mid = call(
        rows_body,
        [(full, bf16)] * 3 + [((tokens, 1), f32)] + [((ny, 1, width), f32)] * 2,
        table,
        input_rows + gains,
    )

    within = jnp.arange(block, dtype=jnp.int32)
    positions = jnp.minimum(place.offset, PROMPT_DEV)[:, None] * block + within[None, :]
    cosine, sine = rope_tables(positions.reshape(-1), HEAD_DIM // 2)
    query, own, attend_weights = call(
        qkv_body,
        [((query_rows, tokens), bf16), ((kv_rows, tokens), bf16), (attend_shape, bf16)],
        table,
        [normed_in, cosine, sine],
        [attend_pieces],
        [pltpu.VMEM((qkv_cols, tokens), f32), sems],
    )
    moved = [
        place.send_z(
            own,
            [(s, s + k) for s in range(n) if s % GROUP < PROMPTS and s % GROUP + k < GROUP],
        )
        for k in range(1, GROUP)
    ]
    attended, attended_low, log_total, far, *halves_out = call(
        attend_body,
        [
            ((query_rows, tokens), f32),
            ((query_rows, tokens), bf16),
            ((query_rows // HEAD_DIM, 1, tokens), f32),
            ((kv_rows, PROMPTS * tokens), bf16),
        ]
        + wide,
        table,
        [query, own] + moved + [attend_weights],
        earlier=forward_pieces[1:3],
    )
    summed = all_sum(
        place,
        halves_out[:2],
        halves_out[2:],
        before_first=forward_pieces[1:3] if lined else forward_pieces,
        before_last=forward_pieces[3:],
    )

    hidden, normed_mid, inverse_mid = call(
        hidden_body,
        [(full, f32), (full, bf16), ((tokens, 1), f32)],
        table,
        summed,
        held=[raw, gain_mid],
    )
    active, change, *halves_out, down_whole = call(
        forward_body,
        [((tokens, hidden_dev), bf16), ((tokens, 2 * hidden_dev), bf16)]
        + wide
        + [((ny, hidden_dev, width), bf16)],
        table,
        [normed_mid],
        [forward_pieces],
        [
            pltpu.VMEM((ny, 2 * hidden_dev, width), bf16),
            pltpu.VMEM((tokens, 2 * hidden_dev), f32),
        ]
        + [pltpu.VMEM((tokens, hidden_dev), f32)] * 2
        + [sems, sems],
        held=[grad],
    )
    third, both = call(
        forward_third_body,
        [(forward_shape[1:], bf16), (forward_shape[1:2] + (tokens,), bf16)],
        table,
        [active, normed_mid, change],
        held=[grad],
    )
    forward_parts = call(
        forward_parts_body,
        [(forward_shape[1:], bf16)] * 3,
        table,
        [both, normed_mid],
        held=[grad],
    )
    forward_parts = list(forward_parts) + [third]
    forward_started = start_scatter(place, forward_parts)
    down_halves = call(
        down_body, wide, table, [active, down_whole], earlier=[forward_parts[0]]
    )
    summed = all_sum(
        place,
        halves_out[:2],
        halves_out[2:],
        before_second=forward_parts[:1],
        before_last=list(down_halves[:1]) + forward_started[2:3] + forward_started[4:],
    )
    _, forward_second = second_scatter(place, forward_started, 0, 2, summed[-1])
    hidden_own = own_block(place, hidden)
    through, pull, query_low, own_back, *returns, inner_first = call(
        attend_back_body,
        [
            (full, bf16),
            ((tokens, 1), f32),
            ((query_rows, tokens), bf16),
            ((kv_rows, tokens), f32),
        ]
        + [((kv_rows, tokens), bf16)] * (GROUP - 1)
        + [((1, tokens), f32)],
        table,
        summed,
        held=[
            hidden,
            inverse_mid,
            grad,
            gain_mid,
            attend_weights,
            query,
            own,
            far,
            attended,
            log_total,
            cosine,
            sine,
        ],
        earlier=forward_started[2:3] + forward_started[4:],
        scratch=[
            pltpu.VMEM((kv_rows, PROMPTS * tokens), f32),
            pltpu.VMEM(full, f32),
            pltpu.VMEM((query_rows, tokens), bf16),
        ],
    )
    down_sends = lax.optimization_barrier(tuple(down_halves[2:]) + (through,))[:2]
    layer_out = (hidden_own + own_sum(place, down_halves[:2], down_sends)).astype(bf16)
    inverse_own, _ = part_of(y, inverse_mid, 0)
    pull_own, _ = part_of(y, pull, 0)
    mid_own = jnp.where(place.x == 0, summed[0], summed[1])
    mid_own = part_of(y, mid_own, 0)[0].astype(f32)
    through_own = (
        out_grad.astype(f32)
        + inverse_own * mid_own * second_gain[None, :]
        - hidden_own * pull_own
    )
    second_term = jnp.sum(mid_own * hidden_own * inverse_own, axis=0)

    moved = [
        place.send_z(
            returns[k - 1],
            [(s, s - k) for s in range(n) if 0 <= s % GROUP - k < PROMPTS],
        )
        for k in range(1, GROUP)
    ]
    attend_parts = call(
        attend_parts_body,
        [(attend_shape[1:], bf16)] * ny,
        table,
        [query_low, through],
        held=[normed_in, attended_low],
    )
    results = call(
        qkv_back_body,
        [(attend_shape[1:], bf16)] * ny
        + wide
        + [((1, tokens), f32), ((kv_rows, tokens), bf16)],
        table,
        list(attend_parts) + [own_back] + moved + [query_low, inner_first],
        held=[attend_weights, cosine, sine, own, normed_in],
        scratch=[pltpu.VMEM((ny, kv_rows, width), bf16), sems],
        earlier=forward_started[3:4] + ([forward_second] if lined else []),
        alias=ny,
    )
    attend_parts, first_halves = results[:ny], results[ny:-2]
    inner, own_low = results[-2:]
    attend_started = start_scatter(place, attend_parts)
    forward_seconds = [
        forward_second,
        second_scatter(place, forward_started, 1, 2, summed[-1], moved[0])[1],
    ]
    attend_sent, attend_second = second_scatter(place, attend_started, 0, 1)
    attend_grad = end_scatter(place, attend_started, [attend_second], own_low)
    inner = inner + place.swap_c(inner)
    inner = inner + place.swap_x(inner)
    inner = inner + place.swap_y(inner)
    first_own = own_sum(
        place,
        first_halves[:2],
        first_halves[2:],
        before_y=[attend_sent] if lined else [],
    )
    forward_grad = end_scatter(
        place, forward_started, forward_seconds, *([attend_sent] if lined else [])
    )
    input_own = layer_in.astype(f32)
    inverse_own, _ = part_of(y, inverse_in, 0)
    scaled = first_own * first_gain[None, :]
    inner = part_of(y, inner.reshape(tokens, 1), 0)[0]
    in_grad = (
        through_own + inverse_own * scaled - input_own * (inverse_own**2 * inner / model_width)
    )
    first_term = jnp.sum(first_own * input_own * inverse_own, axis=0)
    terms = jnp.stack([first_term, second_term])
    bit = 1
    while bit < place.nx:
        terms = terms + place.swap_gx(terms, bit)
        bit *= 2

    def joined(parts, outs):
        rows, cols = parts[0].shape
        packed = (rows // 2, cols)
        mine, other = call(sum_body, [(packed, f32), (packed, bf16)], table, parts)
        shapes = [(cols // 2, inner) for inner in outs]
        return call(
            join_body, [(s, f32) for s in shapes], table, [mine, place.swap_y(other)]
        )

    gate_grad, up_grad, down_grad = joined(forward_grad, [2 * hidden_dev] * 3)
    query_out, key_out, value_out, out_out = joined(
        attend_grad, [2 * query_rows, kv_rows, kv_rows, 2 * query_rows]
    )
    return (
        layer_out,
        in_grad,
        terms[0],
        query_out,
        key_out,
        value_out,
        out_out.T,
        terms[1],
        gate_grad,
        up_grad,
        down_grad.T,
    )


def solution(mesh):
    rows, cols, gain = P("gx", "gy"), P("gy", "gx"), P("gy")
    return jax.shard_map(
        shards,
        mesh=mesh,
        in_specs=(rows, gain, rows, rows, rows, cols, gain, rows, rows, cols, rows),
        out_specs=(rows, rows, gain, rows, rows, rows, cols, gain, rows, rows, cols),
        check_vma=False,
    )
```

```python
from functools import partial

import jax
import jax.numpy as jnp
from jax import lax
from jax.experimental import pallas as pl
from jax.experimental.pallas import tpu as pltpu
from jax.sharding import PartitionSpec as P

HEAD_DIM = 96
PROMPT_DEV = 4
CONT_DEV = 4
GROUP = (PROMPT_DEV + CONT_DEV) // 2
PROMPTS = PROMPT_DEV // 2

eps = 1e-05
neg_big = -1e30
rope_base = 100000.0
score_scale = HEAD_DIM ** (-0.5)
f32 = jnp.float32
bf16 = jnp.bfloat16


def dims(left, right, left_axis, right_axis):
    return lax.dot_general(
        left, right, (((left_axis,), (right_axis,)), ((), ())), preferred_element_type=f32
    )


class Place:
    def __init__(self):
        self.nx = lax.axis_size("gx")
        self.ny = lax.axis_size("gy")
        assert self.ny == 4 and self.nx % (PROMPT_DEV + CONT_DEV) == 0
        self.n = self.nx // 2
        self.gx = lax.axis_index("gx")
        self.gy = lax.axis_index("gy")
        self.z, self.y = self.gx // 2, self.gx % 2
        self.x, self.c = self.gy // 2, self.gy % 2
        self.z_in = self.z % GROUP
        offset = 2 * self.z_in + jnp.arange(2, dtype=jnp.int32)
        self.offset = offset
        self.lined = self.n == self.ny
        blocks = jnp.arange(self.ny, dtype=jnp.int32)
        first = jnp.stack([self.z, self.y, self.x, self.c, self.z_in]).astype(jnp.int32)
        self.table = jnp.concatenate(
            [first, jnp.minimum(offset, PROMPT_DEV), blocks ^ self.z if self.lined else blocks]
        )

    def swap_gx(self, value, bit):
        return lax.ppermute(value, "gx", [(i, i ^ bit) for i in range(self.nx)])

    def swap_y(self, value):
        return self.swap_gx(value, 1)

    def swap_x(self, value):
        return lax.ppermute(value, "gy", [(i, i ^ 2) for i in range(self.ny)])

    def swap_c(self, value):
        return lax.ppermute(value, "gy", [(i, i ^ 1) for i in range(self.ny)])

    def send_z(self, value, moves):
        pairs = [(2 * s + y, 2 * t + y) for s, t in moves for y in range(2)]
        return lax.ppermute(value, "gx", pairs)

    def by_y(self):
        return [[2 * z + y for z in range(self.n)] for y in range(2)]


def pair(flag, mine, other):
    return jnp.where(flag == 0, mine, other), jnp.where(flag == 0, other, mine)


def part_of(flag, whole, axis):
    low, high = jnp.split(whole, 2, axis)
    return jnp.where(flag == 0, low, high), jnp.where(flag == 0, high, low)


def after(value, *earlier):
    return lax.optimization_barrier((value,) + earlier)[0]


NEAR = [(0, 1), (1, 0), (2, 3), (3, 2)]
SECOND = [(0, 2), (1, 3), (2, 0), (3, 1)]
MIDDLE = [(1, 2), (2, 1)]
INWARD = [(0, 1), (3, 2)]
OUTWARD = [(1, 0), (2, 3)]


def gather_pieces(place, piece, late_middle=False):
    second = place.send_z(piece, SECOND)
    near = place.send_z(piece, NEAR)
    middle = place.send_z(after(piece, second) if late_middle else piece, MIDDLE)
    return [piece, near, second, middle, place.send_z(second, OUTWARD)]


def gather_whole(place, piece):
    every = lax.all_gather(piece, "gx", axis_index_groups=place.by_y())
    inner = place.n // place.ny
    if inner == 1:
        return every
    rows, cols = piece.shape
    every = every.reshape(place.ny, inner, rows, cols)
    return jnp.swapaxes(every, 1, 2).reshape(place.ny, rows, inner * cols)


def scatter_whole(place, parts):
    inner = place.n // place.ny
    if inner > 1:
        count, rows, cols = parts.shape
        parts = jnp.swapaxes(parts.reshape(count, rows, inner, cols // inner), 1, 2)
        parts = parts.reshape(place.n, rows, cols // inner)
    return lax.psum_scatter(parts, "gx", axis_index_groups=place.by_y())


def start_scatter(place, parts):
    if not place.lined:
        return [scatter_whole(place, jnp.stack(parts))]
    own, near, second, third = parts
    far = place.send_z(third, INWARD)
    middle = place.send_z(third, MIDDLE)
    return [own, second, far, place.send_z(near, NEAR), middle]


def second_scatter(place, started, part, count, *earlier):
    if not place.lined:
        return None, None
    rows, cols = started[1].shape
    at = slice(part * (rows // count), (part + 1) * (rows // count))
    (summed,) = call(
        partial(add_body, rows=at),
        [((rows // count, cols), bf16)],
        place.table,
        [],
        [started[1:3]],
        [pltpu.VMEM((rows // count, cols), bf16)] * 2 + [pltpu.SemaphoreType.DMA((2,))],
        earlier=[started[4]] + list(earlier),
    )
    return summed, place.send_z(summed, SECOND)


def end_scatter(place, started, seconds, *earlier):
    if not place.lined:
        return started
    return [after(started[0], *earlier), started[3], started[4]] + list(seconds)


def add(left, right):
    return (left.astype(f32) + right.astype(f32)).astype(bf16)


def reduce_core(place, keeps, sends):
    return [add(keep, place.swap_c(send)) for keep, send in zip(keeps, sends)]


def all_sum(place, keeps, sends, before_first=(), before_second=(), before_last=()):
    low = tuple(reduce_core(place, keeps, sends))
    low = lax.optimization_barrier(low + tuple(before_first))
    low = add(low[0], place.swap_x(low[0])), add(low[1], place.swap_y(low[1]))
    low = lax.optimization_barrier(low + tuple(before_second))
    own = (add(low[0], place.swap_y(low[0])), add(low[1], place.swap_x(low[1])))
    if before_last:
        own = lax.optimization_barrier(own + tuple(before_last))[:2]
    own = list(own)
    return own + [place.swap_c(part) for part in own]


def own_sum(place, keeps, sends, before_x=(), before_y=()):
    first, second = reduce_core(place, keeps, sends)
    if before_x:
        first, second = lax.optimization_barrier((first, second) + tuple(before_x))[:2]
    mine, other = jnp.where(place.x == 0, first, second), jnp.where(place.x == 0, second, first)
    mine = add(mine, place.swap_x(other))
    mine = after(mine, *before_y) if before_y else mine
    mine, other = part_of(place.y, mine, 0)
    return mine.astype(f32) + place.swap_y(other).astype(f32)


def own_block(place, blocks):
    rows = blocks.shape[1] // 2
    return lax.dynamic_slice(
        blocks, (place.gy, place.y * rows, 0), (1, rows, blocks.shape[2])
    )[0]


Z, Y, X, C, Z_IN, COUNT = range(6)
ORDER = COUNT + 2


def call(body, outs, table, operands, pieces=(), scratch=(), earlier=(), held=(), alias=0, limit=24):
    if operands:
        operands, held = list(operands) + list(held), ()
    lengths = [len(p) for p in pieces]
    flat = [a for p in pieces for a in p] + list(earlier)
    vmem = pl.BlockSpec(memory_space=pltpu.VMEM)
    copied = [pltpu.VMEM(a.shape, a.dtype) for a in held]
    if held:
        copied.append(pltpu.SemaphoreType.DMA((len(held),)))

    def kernel(table_ref, *refs):
        plain, rest = refs[: len(operands)], refs[len(operands) :]
        sources, rest = rest[: len(held)], rest[len(held) :]
        lists = []
        for length in lengths:
            lists.append(rest[:length])
            rest = rest[length:]
        rest = rest[len(earlier) :]
        targets = ()
        if held:
            rest, targets = rest[: -len(copied)], rest[-len(copied) :]
            copies = [
                pltpu.make_async_copy(source, target, targets[-1].at[i])
                for i, (source, target) in enumerate(zip(sources, targets))
            ]
            for copy in copies:
                copy.start()
            for copy in copies:
                copy.wait()
        body(table_ref, *plain, *targets[:-1], *lists, *rest)

    return pl.pallas_call(
        kernel,
        out_shape=[jax.ShapeDtypeStruct(shape, dtype) for shape, dtype in outs],
        in_specs=[pl.BlockSpec(memory_space=pltpu.SMEM)]
        + [pl.BlockSpec(memory_space=pl.ANY)] * alias
        + [vmem] * (len(operands) - alias)
        + [pl.BlockSpec(memory_space=pltpu.HBM)] * len(held)
        + [pl.BlockSpec(memory_space=pl.ANY)] * len(flat),
        out_specs=[pl.BlockSpec(memory_space=pl.ANY)] * alias + [vmem] * (len(outs) - alias),
        scratch_shapes=list(scratch) + copied,
        input_output_aliases={i + 1: i for i in range(alias)},
        compiler_params=pltpu.CompilerParams(vmem_limit_bytes=limit << 20),
    )(table, *operands, *held, *flat)


def start_pieces(table, pieces, whole, sems, rows=slice(None)):
    count = whole.shape[0]
    block = [table[ORDER + k] for k in range(count)]

    def copy(piece, k):
        source = piece.at[rows] if rows != slice(None) else piece
        return pltpu.make_async_copy(source, whole.at[block[k]], sems.at[k])

    def wait(k):
        pltpu.make_async_copy(whole.at[0], whole.at[0], sems.at[k]).wait()

    if len(pieces) == 1:
        for k in range(count):
            copy(pieces[0].at[block[k]], k).start()
        return wait
    z = table[Z]
    own, near, second, middle, end = pieces
    for k, piece in enumerate((own, near, second)):
        copy(piece, k).start()
    inside = jnp.logical_or(z == 1, z == 2)

    @pl.when(inside)
    def _():
        copy(middle, 3).start()

    @pl.when(jnp.logical_not(inside))
    def _():
        copy(end, 3).start()

    return wait


def keep_and_send(table, block_of, outs):
    core = table[C]
    for i in range(2):
        outs[i][...] = block_of(2 * i + core).astype(bf16)
        outs[2 + i][...] = block_of(2 * i + 1 - core).astype(bf16)


def place_rows(table, pieces, raw, grad):
    x, y, c = table[X], table[Y], table[C]
    tokens = raw.shape[1] // 2
    for dc in range(2):
        for dx in range(2):
            block = 2 * (x + dx - 2 * x * dx) + c + dc - 2 * c * dc
            for dy in range(2):
                at = pl.ds(pl.multiple_of(tokens * (y + dy - 2 * y * dy), tokens), tokens)
                piece = pieces[4 * dc + 2 * dy + dx]
                raw[block, at, :] = piece[:tokens]
                grad[block, at, :] = piece[tokens:]


def norm_rows(raw, gain, normed):
    def square(b, total):
        values = raw[b].astype(f32)
        return total + jnp.sum(values * values, axis=1, keepdims=True)

    count = raw.shape[0]
    total = lax.fori_loop(0, count, square, jnp.zeros((raw.shape[1], 1), f32))
    scale = lax.rsqrt(total / (count * raw.shape[2]) + eps)

    def norm(b, _):
        normed[b] = (raw[b].astype(f32) * scale * gain[b]).astype(bf16)
        return 0

    lax.fori_loop(0, count, norm, 0)
    return scale


def rows_body(table, *refs):
    gains = refs[8:12]
    raw, grad, normed, inverse, gain_first, gain_second = refs[12:]
    place_rows(table, refs[:8], raw, grad)
    x, c = table[X], table[C]
    for dc in range(2):
        for dx in range(2):
            block = 2 * (x + dx - 2 * x * dx) + c + dc - 2 * c * dc
            gain = gains[2 * dc + dx][...]
            gain_first[block] = gain[0:1]
            gain_second[block] = gain[1:2]
    inverse[...] = norm_rows(raw, gain_first, normed)


def turn(values, cosine, sine):
    half = values.shape[0] // 2
    first, second = values[:half], values[half:]
    return jnp.concatenate(
        [first * cosine - second * sine, second * cosine + first * sine], axis=0
    )


def qkv_body(
    table, normed, cosine, sine, pieces, query, own, weights, acc, sems
):
    wait = start_pieces(table, pieces, weights, sems)
    count = acc.shape[0]
    acc[...] = jnp.zeros_like(acc)

    def one(k, _):
        b = table[ORDER + k]
        wait(k)
        acc[...] += dims(weights[b, :count], normed[b], 1, 1)
        return 0

    lax.fori_loop(0, normed.shape[0], one, 0)
    head = HEAD_DIM
    heads = query.shape[0] // head
    cos, sin = cosine[...], sine[...]
    for h in range(heads):
        at = slice(h * head, (h + 1) * head)
        query[at] = turn(acc[at], cos, sin).astype(bf16)
    at = slice(heads * head, (heads + 1) * head)
    own[:head] = turn(acc[at], cos, sin).astype(bf16)
    own[head:] = acc[(heads + 1) * head :].astype(bf16)


def attend_body(table, query, own, *refs):
    moved, refs = refs[: GROUP - 1], refs[GROUP - 1 :]
    (weights, attended, attended_low, log_total, far), outs = refs[:5], refs[5:]
    tokens = own.shape[1]
    for place in range(GROUP):

        @pl.when(table[Z_IN] == place)
        def _():
            for slot in range(PROMPTS):
                k = place - slot
                far[:, slot * tokens : (slot + 1) * tokens] = (
                    moved[k - 1][...] if k > 0 else own[...]
                )

    head = HEAD_DIM
    block = tokens // 2
    key_far, value_far = far[:head].T, far[head:]
    key_own = own[:head].T
    total = far.shape[1]
    near_row = lax.broadcasted_iota(jnp.int32, (block, block), 0)
    near_col = lax.broadcasted_iota(jnp.int32, (block, block), 1)
    causal = near_row <= near_col
    row = lax.broadcasted_iota(jnp.int32, (total, block), 0)
    for part in range(2):
        cols = slice(part * block, (part + 1) * block)
        key_near, value_near = key_own[cols], own[head:, cols]
        seen = row < table[COUNT + part] * block

        def one(h, _):
            at = pl.ds(pl.multiple_of(h * head, head), head)
            rows = query[at, cols]
            score_far = jnp.where(seen, dims(key_far, rows, 1, 0) * score_scale, neg_big)
            score_near = jnp.where(causal, dims(key_near, rows, 1, 0) * score_scale, neg_big)
            top = jnp.maximum(
                jnp.max(score_far, axis=0, keepdims=True), jnp.max(score_near, axis=0, keepdims=True)
            )
            weight_far = jnp.exp(score_far - top)
            weight_near = jnp.exp(score_near - top)
            weight = jnp.sum(weight_far, axis=0, keepdims=True) + jnp.sum(
                weight_near, axis=0, keepdims=True
            )
            out = dims(value_far, weight_far.astype(bf16), 1, 0) + dims(
                value_near, weight_near.astype(bf16), 1, 0
            )
            attended[at, cols] = out / weight
            log_total[h, :, cols] = top + jnp.log(weight)
            return 0

        lax.fori_loop(0, query.shape[0] // head, one, 0)
    values = attended[...]
    attended_low[...] = values.astype(bf16)
    flipped = values.T.astype(bf16)
    first = weights.shape[1] - query.shape[0]
    keep_and_send(
        table,
        lambda b: dims(flipped, weights[b, first:], 1, 0),
        outs,
    )


def hidden_body(
    table, own_first, own_second, other_first, other_second, raw, gain, hidden, normed, inverse
):
    core = table[C]
    summed, other = (own_first, own_second), (other_first, other_second)
    for i in range(2):
        b = 2 * i + core
        hidden[b] = raw[b].astype(f32) + summed[i][...].astype(f32)
        b = 2 * i + 1 - core
        hidden[b] = raw[b].astype(f32) + other[i][...].astype(f32)

    def square(b, total):
        values = hidden[b]
        return total + jnp.sum(values * values, axis=1, keepdims=True)

    count = raw.shape[0]
    total = lax.fori_loop(0, count, square, jnp.zeros((raw.shape[1], 1), f32))
    scale = lax.rsqrt(total / (count * raw.shape[2]) + eps)
    inverse[...] = scale

    def norm(b, _):
        normed[b] = (hidden[b] * scale * gain[b]).astype(bf16)
        return 0

    lax.fori_loop(0, count, norm, 0)


def forward_body(
    table,
    normed,
    grad,
    pieces,
    active,
    change,
    *refs,
):
    outs, (down, weights, acc, gate_slope, up_slope, sems, down_sems) = refs[:4], refs[4:]
    split = weights.shape[1]
    wait = start_pieces(table, pieces, weights, sems, slice(0, split))
    down_wait = start_pieces(
        table, pieces, down, down_sems, slice(split, split + down.shape[1])
    )
    count, tokens = normed.shape[:2]
    width = acc.shape[1]
    half = width // 2
    acc[...] = jnp.zeros_like(acc)

    def one(k, _):
        b = table[ORDER + k]
        wait(k)
        acc[...] += dims(normed[b], weights[b, :width], 1, 1)
        return 0

    lax.fori_loop(0, count, one, 0)
    rows = tokens // 4

    def part(i, _):
        at = pl.ds(pl.multiple_of(i * rows, rows), rows)
        gate, up = acc[at, :half], acc[at, half:]
        sigmoid = jax.nn.sigmoid(gate)
        active[at] = (gate * sigmoid * up).astype(bf16)
        gate_slope[at] = up * sigmoid * (1.0 + gate * (1.0 - sigmoid))
        up_slope[at] = gate * sigmoid
        return 0

    lax.fori_loop(0, 4, part, 0)

    def back(k, total):
        b = table[ORDER + k]
        down_wait(k)
        return total + dims(grad[b], down[b], 1, 1)

    slope = lax.fori_loop(0, count, back, jnp.zeros((tokens, half), f32))
    change[:, :half] = (slope * gate_slope[...]).astype(bf16)
    change[:, half:] = (slope * up_slope[...]).astype(bf16)
    values = change[...]
    keep_and_send(
        table,
        lambda b: dims(values, weights[b, :width], 1, 0),
        outs,
    )


def forward_third_body(table, active, normed, change, grad, third, both):
    width = change.shape[1]
    both[:width] = change[...].T
    both[width:] = active[...].T
    b = table[ORDER + 3]
    third[:width] = dims(both[:width], normed[b], 1, 0).astype(bf16)
    third[width:] = dims(both[width:], grad[b], 1, 0).astype(bf16)


def forward_parts_body(table, both, normed, grad, *parts):
    rows = both.shape[0] // 6

    def fill(first, count, source):
        def one(i, _):
            at = pl.ds(pl.multiple_of((first + i) * rows, rows), rows)
            for k, part in enumerate(parts):
                part[at] = dims(both[at], source[table[ORDER + k]], 1, 0).astype(bf16)
            return 0

        lax.fori_loop(0, count, one, 0)

    fill(0, 4, normed)
    fill(4, 2, grad)


def down_body(table, active, weights, *outs):
    values = active[...]
    keep_and_send(table, lambda b: dims(values, weights[b], 1, 0), outs)


def attend_back_body(
    table,
    own_first,
    own_second,
    other_first,
    other_second,
    hidden,
    inverse,
    grad,
    gain,
    weights,
    query,
    own,
    far,
    attended,
    log_total,
    cosine,
    sine,
    through,
    pull,
    query_low,
    own_back,
    *rest,
):
    sends, inner_first = rest[: GROUP - 1], rest[GROUP - 1]
    far_back, change, branch = rest[GROUP:]
    core = table[C]
    count, tokens, model = hidden.shape
    for i, (mine, theirs) in enumerate(((own_first, other_first), (own_second, other_second))):
        change[2 * i + core] = mine[...].astype(f32) * gain[2 * i + core]
        change[2 * i + 1 - core] = theirs[...].astype(f32) * gain[2 * i + 1 - core]

    def product(b, total):
        return total + jnp.sum(change[b] * hidden[b], axis=1, keepdims=True)

    inner = lax.fori_loop(0, count, product, jnp.zeros((tokens, 1), f32))
    scale = inverse[...]
    back = scale * scale * scale * inner / (count * model)
    pull[...] = back

    def rows(b, total):
        values = grad[b].astype(f32) + scale * change[b] - hidden[b] * back
        low = values.astype(bf16)
        through[b] = low
        return total + dims(low, weights[b, first:], 1, 1)

    heads_cols = query.shape[0]
    first = weights.shape[1] - heads_cols
    total_rows = lax.fori_loop(0, count, rows, jnp.zeros((tokens, heads_cols), f32))
    branch[...] = total_rows.T.astype(bf16)

    head = HEAD_DIM
    block = tokens // 2
    key_far_t = far[:head]
    key_far, value_far = key_far_t.T, far[head:].T
    key_own, value_own = own[:head].T, own[head:].T
    total = far.shape[1]
    near_row = lax.broadcasted_iota(jnp.int32, (block, block), 0)
    near_col = lax.broadcasted_iota(jnp.int32, (block, block), 1)
    causal = near_row <= near_col
    row = lax.broadcasted_iota(jnp.int32, (total, block), 0)
    far_back[...] = jnp.zeros_like(far_back)
    own_back[...] = jnp.zeros_like(own_back)
    inner_first[...] = jnp.zeros_like(inner_first)
    for part in range(2):
        cols = slice(part * block, (part + 1) * block)
        key_near, value_near = key_own[cols], value_own[cols]
        key_near_t = own[:head, cols]
        seen = row < table[COUNT + part] * block

        def one_head(h, _):
            at = pl.ds(pl.multiple_of(h * head, head), head)
            rows_q, rows_grad = query[at, cols], branch[at, cols]
            delta = jnp.sum(
                rows_grad.astype(f32) * attended[at, cols], axis=0, keepdims=True
            )
            logs = log_total[h, :, cols]

            def one(key, value, allowed):
                score = dims(key, rows_q, 1, 0) * score_scale
                prob = jnp.where(allowed, jnp.exp(score - logs), 0.0)
                moved = (prob * (dims(value, rows_grad, 1, 0) - delta)).astype(bf16)
                return prob.astype(bf16), moved

            prob_far, moved_far = one(key_far, value_far, seen)
            prob_near, moved_near = one(key_near, value_near, causal)
            query_back = (
                dims(key_far_t, moved_far, 1, 0) + dims(key_near_t, moved_near, 1, 0)
            ) * score_scale
            inner_first[:, cols] += jnp.sum(
                query_back * rows_q.astype(f32), axis=0, keepdims=True
            )
            query_low[at, cols] = turn(query_back, cosine[:, cols], -sine[:, cols]).astype(bf16)
            far_back[:head] += dims(rows_q, moved_far, 1, 1) * score_scale
            far_back[head:] += dims(rows_grad, prob_far, 1, 1)
            own_back[:head, cols] += dims(rows_q, moved_near, 1, 1) * score_scale
            own_back[head:, cols] += dims(rows_grad, prob_near, 1, 1)
            return 0

        lax.fori_loop(0, heads_cols // head, one_head, 0)
    for slot in range(PROMPTS):

        @pl.when(table[Z_IN] == slot)
        def _():
            own_back[...] += far_back[:, slot * tokens : (slot + 1) * tokens]

    for k in range(1, GROUP):
        sends[k - 1][...] = far_back[:, :tokens].astype(bf16)
        for slot in range(1, PROMPTS):

            @pl.when(table[Z_IN] == slot + k)
            def _():
                sends[k - 1][...] = far_back[:, slot * tokens : (slot + 1) * tokens].astype(bf16)


def attend_parts_body(table, query_low, through, normed, attended_low, *parts):
    rows = query_low.shape[0]
    for k, part in enumerate(parts):
        b = table[ORDER + k]
        part[:rows] = dims(query_low[...], normed[b], 1, 0).astype(bf16)
        part[-rows:] = dims(attended_low[...], through[b], 1, 0).astype(bf16)


def qkv_back_body(table, *refs):
    count = table.shape[0] - ORDER
    own_back, moved, refs = refs[count], refs[count + 1 : count + GROUP], refs[count + GROUP :]
    query_low, inner, weights, cosine, sine, own, normed = refs[:7]
    parts, outs = refs[7 : 7 + count], refs[7 + count : 11 + count]
    inner_first, own_low, changed, sems = refs[11 + count :]
    head = HEAD_DIM
    total = own_back[...]
    for part in moved:
        total = total + part[...].astype(f32)
    inner_first[...] = inner[...] + jnp.sum(total * own[...].astype(f32), axis=0, keepdims=True)
    key = turn(total[:head], cosine[...], -sine[...])
    low = jnp.concatenate([key, total[head:]], axis=0)
    own_low[...] = low.astype(bf16)
    first = query_low.shape[0]
    copies = []
    for k, part in enumerate(parts):
        changed[k] = dims(own_low[...], normed[table[ORDER + k]], 1, 0).astype(bf16)
        target = part.at[first : first + low.shape[0]]
        copies.append(pltpu.make_async_copy(changed.at[k], target, sems.at[k]))
        copies[k].start()
    flipped = jnp.concatenate([query_low[...].T, low.T.astype(bf16)], axis=1)
    width = flipped.shape[1]
    keep_and_send(table, lambda b: dims(flipped, weights[b, :width], 1, 0), outs)
    for copy in copies:
        copy.wait()


def halves_of(table, whole):
    half = whole.shape[0] // 2
    low, high = whole[:half], whole[half:]
    flag = table[Y] == 0
    return jnp.where(flag, low, high), jnp.where(flag, high, low)


def add_body(table, sources, out, first, second, sems, *, rows):
    copies = [
        pltpu.make_async_copy(source.at[rows], held, sems.at[i])
        for i, (source, held) in enumerate(zip(sources, (first, second)))
    ]
    for copy in copies:
        copy.start()
    for copy in copies:
        copy.wait()
    out[...] = add(first[...], second[...])


def pack(rows, packed):
    half, cols = packed.shape[0], rows.shape[1]
    packed[:, :cols] = rows[:half].astype(packed.dtype)
    packed[:, cols:] = rows[half:].astype(packed.dtype)


def split_body(table, *refs):
    matrices, (mine_ref, other_ref) = refs[:-2], refs[-2:]
    pairs = [halves_of(table, matrix[...].T) for matrix in matrices]
    pack(jnp.concatenate([mine for mine, _ in pairs], axis=0), mine_ref)
    pack(jnp.concatenate([other for _, other in pairs], axis=0), other_ref)


def piece_body(table, mine_ref, got_ref, piece):
    flag = table[Y] == 0
    mine, got = mine_ref[...], got_ref[...]
    low, high = jnp.where(flag, mine, got), jnp.where(flag, got, mine)
    half, cols = mine.shape[0], mine.shape[1] // 2
    for i in range(2):
        piece[i * half : (i + 1) * half, :cols] = low[:, i * cols : (i + 1) * cols]
        piece[i * half : (i + 1) * half, cols:] = high[:, i * cols : (i + 1) * cols]


def sum_body(table, *refs):
    parts, (mine_ref, other_ref) = refs[:-2], refs[-2:]
    whole = [part for part in parts if part.shape == parts[0].shape]
    total = whole[0][...].astype(f32)
    for part in whole[1:]:
        total = total + part[...].astype(f32)
    rest = [part[...].astype(f32) for part in parts if part.shape != parts[0].shape]
    if rest:
        total = total + jnp.concatenate(rest, axis=0)
    cols = total.shape[1] // 2
    low, high = total[:, :cols], total[:, cols:]
    flag = table[Y] == 0
    pack(jnp.where(flag, low, high), mine_ref)
    pack(jnp.where(flag, high, low), other_ref)


def join_body(table, mine_ref, got_ref, *outs):
    flag = table[Y] == 0
    cols = mine_ref.shape[1] // 2

    def unpacked(ref):
        return jnp.concatenate([ref[:, :cols], ref[:, cols:]], axis=0).astype(f32)

    mine, got = unpacked(mine_ref), unpacked(got_ref)
    low, high = jnp.where(flag, mine, got), jnp.where(flag, got, mine)
    at = 0
    for out in outs:
        rows = out.shape[1] // 2
        out[:, :rows] = low[at : at + rows].T
        out[:, rows:] = high[at : at + rows].T
        at += rows


def rope_tables(positions, half):
    freq = rope_base ** (-(2.0 * jnp.arange(half, dtype=f32)) / (2.0 * half))
    angle = freq[:, None] * positions.astype(f32)[None, :]
    return (jnp.cos(angle), jnp.sin(angle))


def shards(
    layer_in,
    first_gain,
    query_weight,
    key_matrix,
    value_matrix,
    out_weight,
    second_gain,
    gate_weight,
    up_weight,
    down_weight,
    out_grad,
):
    place = Place()
    n, ny, y, z_in, table = place.n, place.ny, place.y, place.z_in, place.table
    lined = place.lined
    block, width = layer_in.shape
    tokens = 2 * block
    model_width = width * ny
    hidden_dev = gate_weight.shape[1] // 2
    query_rows = query_weight.shape[1] // 2
    kv_rows = key_matrix.shape[1]
    qkv_cols = query_rows + kv_rows
    full = (ny, tokens, width)
    wide = [(full[1:], bf16)] * 4

    def halves(*matrices, earlier=()):
        rows = sum(m.shape[1] for m in matrices) // 2
        packed = (rows // 2, 2 * matrices[0].shape[0])
        return call(split_body, [(packed, bf16)] * 2, table, [], held=matrices, earlier=earlier)

    def whole_piece(mine, got):
        rows, cols = mine.shape
        (piece,) = call(piece_body, [((2 * rows, cols), bf16)], table, [mine, got])
        return piece

    def spread(value, *before_y):
        by_x = place.swap_x(value)
        late, late_x = lax.optimization_barrier((value, by_x) + before_y)[:2]
        four = [value, by_x, place.swap_y(late), place.swap_y(late_x)]
        return four + [place.swap_c(r) for r in four]

    mine, other = halves(query_weight, key_matrix, value_matrix, out_weight.T)
    attend_got = place.swap_y(other)
    attend_piece = whole_piece(mine, attend_got)
    mine, other = halves(gate_weight, up_weight, down_weight.T, earlier=[attend_piece])
    forward_got = place.swap_y(other)
    forward_piece = whole_piece(mine, forward_got)
    rows = jnp.concatenate([layer_in, out_grad], axis=0)
    input_rows = spread(after(rows, attend_got), forward_got)
    if lined:
        attend_pieces = gather_pieces(place, attend_piece)
        forward_pieces = gather_pieces(place, after(forward_piece, *attend_pieces[1:]), True)
    else:
        attend_pieces = [gather_whole(place, attend_piece)]
        forward_pieces = [gather_whole(place, forward_piece)]
    attend_shape = (ny, qkv_cols + query_rows, width)
    forward_shape = (ny, 3 * hidden_dev, width)
    sems = pltpu.SemaphoreType.DMA((ny,))

    gains = jnp.stack([first_gain, second_gain])
    two = [gains, place.swap_x(gains)]
    gains = two + [place.swap_c(g) for g in two]
    raw, grad, normed_in, inverse_in, gain_in, gain_mid = call(
        rows_body,
        [(full, bf16)] * 3 + [((tokens, 1), f32)] + [((ny, 1, width), f32)] * 2,
        table,
        input_rows + gains,
    )

    within = jnp.arange(block, dtype=jnp.int32)
    positions = jnp.minimum(place.offset, PROMPT_DEV)[:, None] * block + within[None, :]
    cosine, sine = rope_tables(positions.reshape(-1), HEAD_DIM // 2)
    query, own, attend_weights = call(
        qkv_body,
        [((query_rows, tokens), bf16), ((kv_rows, tokens), bf16), (attend_shape, bf16)],
        table,
        [normed_in, cosine, sine],
        [attend_pieces],
        [pltpu.VMEM((qkv_cols, tokens), f32), sems],
    )
    moved = [
        place.send_z(
            own,
            [(s, s + k) for s in range(n) if s % GROUP < PROMPTS and s % GROUP + k < GROUP],
        )
        for k in range(1, GROUP)
    ]
    attended, attended_low, log_total, far, *halves_out = call(
        attend_body,
        [
            ((query_rows, tokens), f32),
            ((query_rows, tokens), bf16),
            ((query_rows // HEAD_DIM, 1, tokens), f32),
            ((kv_rows, PROMPTS * tokens), bf16),
        ]
        + wide,
        table,
        [query, own] + moved + [attend_weights],
        earlier=forward_pieces[1:3],
    )
    summed = all_sum(
        place,
        halves_out[:2],
        halves_out[2:],
        before_first=forward_pieces[1:3] if lined else forward_pieces,
        before_last=forward_pieces[3:],
    )

    hidden, normed_mid, inverse_mid = call(
        hidden_body,
        [(full, f32), (full, bf16), ((tokens, 1), f32)],
        table,
        summed,
        held=[raw, gain_mid],
    )
    active, change, *halves_out, down_whole = call(
        forward_body,
        [((tokens, hidden_dev), bf16), ((tokens, 2 * hidden_dev), bf16)]
        + wide
        + [((ny, hidden_dev, width), bf16)],
        table,
        [normed_mid],
        [forward_pieces],
        [
            pltpu.VMEM((ny, 2 * hidden_dev, width), bf16),
            pltpu.VMEM((tokens, 2 * hidden_dev), f32),
        ]
        + [pltpu.VMEM((tokens, hidden_dev), f32)] * 2
        + [sems, sems],
        held=[grad],
    )
    third, both = call(
        forward_third_body,
        [(forward_shape[1:], bf16), (forward_shape[1:2] + (tokens,), bf16)],
        table,
        [active, normed_mid, change],
        held=[grad],
    )
    forward_parts = call(
        forward_parts_body,
        [(forward_shape[1:], bf16)] * 3,
        table,
        [both, normed_mid],
        held=[grad],
    )
    forward_parts = list(forward_parts) + [third]
    forward_started = start_scatter(place, forward_parts)
    down_halves = call(
        down_body, wide, table, [active, down_whole], earlier=[forward_parts[0]]
    )
    summed = all_sum(
        place,
        halves_out[:2],
        halves_out[2:],
        before_second=forward_parts[:1],
        before_last=list(down_halves[:1]) + forward_started[2:3] + forward_started[4:],
    )
    _, forward_second = second_scatter(place, forward_started, 0, 2, summed[-1])
    hidden_own = own_block(place, hidden)
    through, pull, query_low, own_back, *returns, inner_first = call(
        attend_back_body,
        [
            (full, bf16),
            ((tokens, 1), f32),
            ((query_rows, tokens), bf16),
            ((kv_rows, tokens), f32),
        ]
        + [((kv_rows, tokens), bf16)] * (GROUP - 1)
        + [((1, tokens), f32)],
        table,
        summed,
        held=[
            hidden,
            inverse_mid,
            grad,
            gain_mid,
            attend_weights,
            query,
            own,
            far,
            attended,
            log_total,
            cosine,
            sine,
        ],
        earlier=forward_started[2:3] + forward_started[4:],
        scratch=[
            pltpu.VMEM((kv_rows, PROMPTS * tokens), f32),
            pltpu.VMEM(full, f32),
            pltpu.VMEM((query_rows, tokens), bf16),
        ],
    )
    down_sends = lax.optimization_barrier(tuple(down_halves[2:]) + (through,))[:2]
    layer_out = (hidden_own + own_sum(place, down_halves[:2], down_sends)).astype(bf16)
    inverse_own, _ = part_of(y, inverse_mid, 0)
    pull_own, _ = part_of(y, pull, 0)
    mid_own = jnp.where(place.x == 0, summed[0], summed[1])
    mid_own = part_of(y, mid_own, 0)[0].astype(f32)
    through_own = (
        out_grad.astype(f32)
        + inverse_own * mid_own * second_gain[None, :]
        - hidden_own * pull_own
    )
    second_term = jnp.sum(mid_own * hidden_own * inverse_own, axis=0)

    moved = [
        place.send_z(
            returns[k - 1],
            [(s, s - k) for s in range(n) if 0 <= s % GROUP - k < PROMPTS],
        )
        for k in range(1, GROUP)
    ]
    attend_parts = call(
        attend_parts_body,
        [(attend_shape[1:], bf16)] * ny,
        table,
        [query_low, through],
        held=[normed_in, attended_low],
    )
    results = call(
        qkv_back_body,
        [(attend_shape[1:], bf16)] * ny
        + wide
        + [((1, tokens), f32), ((kv_rows, tokens), bf16)],
        table,
        list(attend_parts) + [own_back] + moved + [query_low, inner_first],
        held=[attend_weights, cosine, sine, own, normed_in],
        scratch=[pltpu.VMEM((ny, kv_rows, width), bf16), sems],
        earlier=forward_started[3:4] + ([forward_second] if lined else []),
        alias=ny,
    )
    attend_parts, first_halves = results[:ny], results[ny:-2]
    inner, own_low = results[-2:]
    attend_started = start_scatter(place, attend_parts)
    forward_seconds = [
        forward_second,
        second_scatter(place, forward_started, 1, 2, summed[-1], moved[0])[1],
    ]
    attend_sent, attend_second = second_scatter(place, attend_started, 0, 1)
    attend_grad = end_scatter(place, attend_started, [attend_second], own_low)
    inner = inner + place.swap_c(inner)
    inner = inner + place.swap_x(inner)
    inner = inner + place.swap_y(inner)
    first_own = own_sum(
        place,
        first_halves[:2],
        first_halves[2:],
        before_y=[attend_sent] if lined else [],
    )
    forward_grad = end_scatter(
        place, forward_started, forward_seconds, *([attend_sent] if lined else [])
    )
    input_own = layer_in.astype(f32)
    inverse_own, _ = part_of(y, inverse_in, 0)
    scaled = first_own * first_gain[None, :]
    inner = part_of(y, inner.reshape(tokens, 1), 0)[0]
    in_grad = (
        through_own + inverse_own * scaled - input_own * (inverse_own**2 * inner / model_width)
    )
    first_term = jnp.sum(first_own * input_own * inverse_own, axis=0)
    terms = jnp.stack([first_term, second_term])
    bit = 1
    while bit < place.nx:
        terms = terms + place.swap_gx(terms, bit)
        bit *= 2

    def joined(parts, outs):
        rows, cols = parts[0].shape
        packed = (rows // 2, cols)
        mine, other = call(sum_body, [(packed, f32), (packed, bf16)], table, parts)
        shapes = [(cols // 2, inner) for inner in outs]
        return call(
            join_body, [(s, f32) for s in shapes], table, [mine, place.swap_y(other)]
        )

    gate_grad, up_grad, down_grad = joined(forward_grad, [2 * hidden_dev] * 3)
    query_out, key_out, value_out, out_out = joined(
        attend_grad, [2 * query_rows, kv_rows, kv_rows, 2 * query_rows]
    )
    return (
        layer_out,
        in_grad,
        terms[0],
        query_out,
        key_out,
        value_out,
        out_out.T,
        terms[1],
        gate_grad,
        up_grad,
        down_grad.T,
    )


def solution(mesh):
    rows, cols, gain = P("gx", "gy"), P("gy", "gx"), P("gy")
    return jax.shard_map(
        shards,
        mesh=mesh,
        in_specs=(rows, gain, rows, rows, rows, cols, gain, rows, rows, cols, rows),
        out_specs=(rows, rows, gain, rows, rows, rows, cols, gain, rows, rows, cols),
        check_vma=False,
    )
```

```python
from functools import partial

import jax
import jax.numpy as jnp
from jax import lax
from jax.experimental import pallas as pl
from jax.experimental.pallas import tpu as pltpu
from jax.sharding import PartitionSpec as P

HEAD_DIM = 96
PROMPT_DEV = 4
CONT_DEV = 4
GROUP = (PROMPT_DEV + CONT_DEV) // 2
PROMPTS = PROMPT_DEV // 2

eps = 1e-05
neg_big = -1e30
rope_base = 100000.0
score_scale = HEAD_DIM ** (-0.5)
f32 = jnp.float32
bf16 = jnp.bfloat16


def dims(left, right, left_axis, right_axis):
    return lax.dot_general(
        left, right, (((left_axis,), (right_axis,)), ((), ())), preferred_element_type=f32
    )


class Place:
    def __init__(self):
        self.nx = lax.axis_size("gx")
        self.ny = lax.axis_size("gy")
        assert self.ny == 4 and self.nx % (PROMPT_DEV + CONT_DEV) == 0
        self.n = self.nx // 2
        self.gx = lax.axis_index("gx")
        self.gy = lax.axis_index("gy")
        self.z, self.y = self.gx // 2, self.gx % 2
        self.x, self.c = self.gy // 2, self.gy % 2
        self.z_in = self.z % GROUP
        offset = 2 * self.z_in + jnp.arange(2, dtype=jnp.int32)
        self.offset = offset
        self.lined = self.n == self.ny
        blocks = jnp.arange(self.ny, dtype=jnp.int32)
        first = jnp.stack([self.z, self.y, self.x, self.c, self.z_in]).astype(jnp.int32)
        self.table = jnp.concatenate(
            [first, jnp.minimum(offset, PROMPT_DEV), blocks ^ self.z if self.lined else blocks]
        )

    def swap_gx(self, value, bit):
        return lax.ppermute(value, "gx", [(i, i ^ bit) for i in range(self.nx)])

    def swap_y(self, value):
        return self.swap_gx(value, 1)

    def swap_x(self, value):
        return lax.ppermute(value, "gy", [(i, i ^ 2) for i in range(self.ny)])

    def swap_c(self, value):
        return lax.ppermute(value, "gy", [(i, i ^ 1) for i in range(self.ny)])

    def send_z(self, value, moves):
        pairs = [(2 * s + y, 2 * t + y) for s, t in moves for y in range(2)]
        return lax.ppermute(value, "gx", pairs)

    def by_y(self):
        return [[2 * z + y for z in range(self.n)] for y in range(2)]


def pair(flag, mine, other):
    return jnp.where(flag == 0, mine, other), jnp.where(flag == 0, other, mine)


def part_of(flag, whole, axis):
    low, high = jnp.split(whole, 2, axis)
    return jnp.where(flag == 0, low, high), jnp.where(flag == 0, high, low)


def after(value, *earlier):
    return lax.optimization_barrier((value,) + earlier)[0]


NEAR = [(0, 1), (1, 0), (2, 3), (3, 2)]
SECOND = [(0, 2), (1, 3), (2, 0), (3, 1)]
MIDDLE = [(1, 2), (2, 1)]
INWARD = [(0, 1), (3, 2)]
OUTWARD = [(1, 0), (2, 3)]


def gather_pieces(place, piece, late_middle=False):
    second = place.send_z(piece, SECOND)
    near = place.send_z(piece, NEAR)
    middle = place.send_z(after(piece, second) if late_middle else piece, MIDDLE)
    return [piece, near, second, middle, place.send_z(second, OUTWARD)]


def gather_whole(place, piece):
    every = lax.all_gather(piece, "gx", axis_index_groups=place.by_y())
    inner = place.n // place.ny
    if inner == 1:
        return every
    rows, cols = piece.shape
    every = every.reshape(place.ny, inner, rows, cols)
    return jnp.swapaxes(every, 1, 2).reshape(place.ny, rows, inner * cols)


def scatter_whole(place, parts):
    inner = place.n // place.ny
    if inner > 1:
        count, rows, cols = parts.shape
        parts = jnp.swapaxes(parts.reshape(count, rows, inner, cols // inner), 1, 2)
        parts = parts.reshape(place.n, rows, cols // inner)
    return lax.psum_scatter(parts, "gx", axis_index_groups=place.by_y())


def start_scatter(place, parts):
    if not place.lined:
        return [scatter_whole(place, jnp.stack(parts))]
    own, near, second, third = parts
    far = place.send_z(third, INWARD)
    middle = place.send_z(third, MIDDLE)
    return [own, second, far, place.send_z(near, NEAR), middle]


def second_scatter(place, started, part, count, *earlier):
    if not place.lined:
        return None, None
    rows, cols = started[1].shape
    cut = rows if count == 1 else rows * 2 // 3
    at = slice(0, cut) if part == 0 else slice(cut, rows)
    size = at.stop - at.start
    (summed,) = call(
        partial(add_body, rows=at),
        [((size, cols), bf16)],
        place.table,
        [],
        [started[1:3]],
        [pltpu.VMEM((size, cols), bf16)] * 2 + [pltpu.SemaphoreType.DMA((2,))],
        earlier=[started[4]] + list(earlier),
    )
    return summed, place.send_z(summed, SECOND)


def end_scatter(place, started, seconds, *earlier):
    if not place.lined:
        return started
    return [after(started[0], *earlier), started[3], started[4]] + list(seconds)


def add(left, right):
    return (left.astype(f32) + right.astype(f32)).astype(bf16)


def reduce_core(place, keeps, sends):
    return [add(keep, place.swap_c(send)) for keep, send in zip(keeps, sends)]


def all_sum(place, keeps, sends, before_first=(), before_second=(), before_last=()):
    low = tuple(reduce_core(place, keeps, sends))
    low = lax.optimization_barrier(low + tuple(before_first))
    low = add(low[0], place.swap_x(low[0])), add(low[1], place.swap_y(low[1]))
    low = lax.optimization_barrier(low + tuple(before_second))
    own = (add(low[0], place.swap_y(low[0])), add(low[1], place.swap_x(low[1])))
    if before_last:
        own = lax.optimization_barrier(own + tuple(before_last))[:2]
    own = list(own)
    return own + [place.swap_c(part) for part in own]


def own_sum(place, keeps, sends, before_x=(), before_y=()):
    first, second = reduce_core(place, keeps, sends)
    if before_x:
        first, second = lax.optimization_barrier((first, second) + tuple(before_x))[:2]
    mine, other = jnp.where(place.x == 0, first, second), jnp.where(place.x == 0, second, first)
    mine = add(mine, place.swap_x(other))
    mine = after(mine, *before_y) if before_y else mine
    mine, other = part_of(place.y, mine, 0)
    return mine.astype(f32) + place.swap_y(other).astype(f32)


def own_block(place, blocks):
    rows = blocks.shape[1] // 2
    return lax.dynamic_slice(
        blocks, (place.gy, place.y * rows, 0), (1, rows, blocks.shape[2])
    )[0]


Z, Y, X, C, Z_IN, COUNT = range(6)
ORDER = COUNT + 2


def call(body, outs, table, operands, pieces=(), scratch=(), earlier=(), held=(), alias=0, limit=24):
    if operands:
        operands, held = list(operands) + list(held), ()
    lengths = [len(p) for p in pieces]
    flat = [a for p in pieces for a in p] + list(earlier)
    vmem = pl.BlockSpec(memory_space=pltpu.VMEM)
    copied = [pltpu.VMEM(a.shape, a.dtype) for a in held]
    if held:
        copied.append(pltpu.SemaphoreType.DMA((len(held),)))

    def kernel(table_ref, *refs):
        plain, rest = refs[: len(operands)], refs[len(operands) :]
        sources, rest = rest[: len(held)], rest[len(held) :]
        lists = []
        for length in lengths:
            lists.append(rest[:length])
            rest = rest[length:]
        rest = rest[len(earlier) :]
        targets = ()
        if held:
            rest, targets = rest[: -len(copied)], rest[-len(copied) :]
            copies = [
                pltpu.make_async_copy(source, target, targets[-1].at[i])
                for i, (source, target) in enumerate(zip(sources, targets))
            ]
            for copy in copies:
                copy.start()
            for copy in copies:
                copy.wait()
        body(table_ref, *plain, *targets[:-1], *lists, *rest)

    return pl.pallas_call(
        kernel,
        out_shape=[jax.ShapeDtypeStruct(shape, dtype) for shape, dtype in outs],
        in_specs=[pl.BlockSpec(memory_space=pltpu.SMEM)]
        + [pl.BlockSpec(memory_space=pl.ANY)] * alias
        + [vmem] * (len(operands) - alias)
        + [pl.BlockSpec(memory_space=pltpu.HBM)] * len(held)
        + [pl.BlockSpec(memory_space=pl.ANY)] * len(flat),
        out_specs=[pl.BlockSpec(memory_space=pl.ANY)] * alias + [vmem] * (len(outs) - alias),
        scratch_shapes=list(scratch) + copied,
        input_output_aliases={i + 1: i for i in range(alias)},
        compiler_params=pltpu.CompilerParams(vmem_limit_bytes=limit << 20),
    )(table, *operands, *held, *flat)


def start_pieces(table, pieces, whole, sems, rows=slice(None)):
    count = whole.shape[0]
    block = [table[ORDER + k] for k in range(count)]

    def copy(piece, k):
        source = piece.at[rows] if rows != slice(None) else piece
        return pltpu.make_async_copy(source, whole.at[block[k]], sems.at[k])

    def wait(k):
        pltpu.make_async_copy(whole.at[0], whole.at[0], sems.at[k]).wait()

    if len(pieces) == 1:
        for k in range(count):
            copy(pieces[0].at[block[k]], k).start()
        return wait
    z = table[Z]
    own, near, second, middle, end = pieces
    for k, piece in enumerate((own, near, second)):
        copy(piece, k).start()
    inside = jnp.logical_or(z == 1, z == 2)

    @pl.when(inside)
    def _():
        copy(middle, 3).start()

    @pl.when(jnp.logical_not(inside))
    def _():
        copy(end, 3).start()

    return wait


def keep_and_send(table, block_of, outs):
    core = table[C]
    for i in range(2):
        outs[i][...] = block_of(2 * i + core).astype(bf16)
        outs[2 + i][...] = block_of(2 * i + 1 - core).astype(bf16)


def place_rows(table, pieces, raw, grad):
    x, y, c = table[X], table[Y], table[C]
    tokens = raw.shape[1] // 2
    for dc in range(2):
        for dx in range(2):
            block = 2 * (x + dx - 2 * x * dx) + c + dc - 2 * c * dc
            for dy in range(2):
                at = pl.ds(pl.multiple_of(tokens * (y + dy - 2 * y * dy), tokens), tokens)
                piece = pieces[4 * dc + 2 * dy + dx]
                raw[block, at, :] = piece[:tokens]
                grad[block, at, :] = piece[tokens:]


def norm_rows(raw, gain, normed):
    def square(b, total):
        values = raw[b].astype(f32)
        return total + jnp.sum(values * values, axis=1, keepdims=True)

    count = raw.shape[0]
    total = lax.fori_loop(0, count, square, jnp.zeros((raw.shape[1], 1), f32))
    scale = lax.rsqrt(total / (count * raw.shape[2]) + eps)

    def norm(b, _):
        normed[b] = (raw[b].astype(f32) * scale * gain[b]).astype(bf16)
        return 0

    lax.fori_loop(0, count, norm, 0)
    return scale


def rows_body(table, *refs):
    gains = refs[8:12]
    raw, grad, normed, inverse, gain_first, gain_second = refs[12:]
    place_rows(table, refs[:8], raw, grad)
    x, c = table[X], table[C]
    for dc in range(2):
        for dx in range(2):
            block = 2 * (x + dx - 2 * x * dx) + c + dc - 2 * c * dc
            gain = gains[2 * dc + dx][...]
            gain_first[block] = gain[0:1]
            gain_second[block] = gain[1:2]
    inverse[...] = norm_rows(raw, gain_first, normed)


def turn(values, cosine, sine):
    half = values.shape[0] // 2
    first, second = values[:half], values[half:]
    return jnp.concatenate(
        [first * cosine - second * sine, second * cosine + first * sine], axis=0
    )


def qkv_body(
    table, normed, cosine, sine, pieces, query, own, weights, acc, sems
):
    wait = start_pieces(table, pieces, weights, sems)
    count = acc.shape[0]
    acc[...] = jnp.zeros_like(acc)

    def one(k, _):
        b = table[ORDER + k]
        wait(k)
        acc[...] += dims(weights[b, :count], normed[b], 1, 1)
        return 0

    lax.fori_loop(0, normed.shape[0], one, 0)
    head = HEAD_DIM
    heads = query.shape[0] // head
    cos, sin = cosine[...], sine[...]
    for h in range(heads):
        at = slice(h * head, (h + 1) * head)
        query[at] = turn(acc[at], cos, sin).astype(bf16)
    at = slice(heads * head, (heads + 1) * head)
    own[:head] = turn(acc[at], cos, sin).astype(bf16)
    own[head:] = acc[(heads + 1) * head :].astype(bf16)


def attend_body(table, query, own, *refs):
    moved, refs = refs[: GROUP - 1], refs[GROUP - 1 :]
    (weights, attended, attended_low, log_total, far), outs = refs[:5], refs[5:]
    tokens = own.shape[1]
    for place in range(GROUP):

        @pl.when(table[Z_IN] == place)
        def _():
            for slot in range(PROMPTS):
                k = place - slot
                far[:, slot * tokens : (slot + 1) * tokens] = (
                    moved[k - 1][...] if k > 0 else own[...]
                )

    head = HEAD_DIM
    block = tokens // 2
    key_far, value_far = far[:head].T, far[head:]
    key_own = own[:head].T
    total = far.shape[1]
    near_row = lax.broadcasted_iota(jnp.int32, (block, block), 0)
    near_col = lax.broadcasted_iota(jnp.int32, (block, block), 1)
    causal = near_row <= near_col
    row = lax.broadcasted_iota(jnp.int32, (total, block), 0)
    for part in range(2):
        cols = slice(part * block, (part + 1) * block)
        key_near, value_near = key_own[cols], own[head:, cols]
        seen = row < table[COUNT + part] * block

        def one(h, _):
            at = pl.ds(pl.multiple_of(h * head, head), head)
            rows = query[at, cols]
            score_far = jnp.where(seen, dims(key_far, rows, 1, 0) * score_scale, neg_big)
            score_near = jnp.where(causal, dims(key_near, rows, 1, 0) * score_scale, neg_big)
            top = jnp.maximum(
                jnp.max(score_far, axis=0, keepdims=True), jnp.max(score_near, axis=0, keepdims=True)
            )
            weight_far = jnp.exp(score_far - top)
            weight_near = jnp.exp(score_near - top)
            weight = jnp.sum(weight_far, axis=0, keepdims=True) + jnp.sum(
                weight_near, axis=0, keepdims=True
            )
            out = dims(value_far, weight_far.astype(bf16), 1, 0) + dims(
                value_near, weight_near.astype(bf16), 1, 0
            )
            attended[at, cols] = out / weight
            log_total[h, :, cols] = top + jnp.log(weight)
            return 0

        lax.fori_loop(0, query.shape[0] // head, one, 0)
    values = attended[...]
    attended_low[...] = values.astype(bf16)
    flipped = values.T.astype(bf16)
    first = weights.shape[1] - query.shape[0]
    keep_and_send(
        table,
        lambda b: dims(flipped, weights[b, first:], 1, 0),
        outs,
    )


def hidden_body(
    table, own_first, own_second, other_first, other_second, raw, gain, hidden, normed, inverse
):
    core = table[C]
    summed, other = (own_first, own_second), (other_first, other_second)
    for i in range(2):
        b = 2 * i + core
        hidden[b] = raw[b].astype(f32) + summed[i][...].astype(f32)
        b = 2 * i + 1 - core
        hidden[b] = raw[b].astype(f32) + other[i][...].astype(f32)

    def square(b, total):
        values = hidden[b]
        return total + jnp.sum(values * values, axis=1, keepdims=True)

    count = raw.shape[0]
    total = lax.fori_loop(0, count, square, jnp.zeros((raw.shape[1], 1), f32))
    scale = lax.rsqrt(total / (count * raw.shape[2]) + eps)
    inverse[...] = scale

    def norm(b, _):
        normed[b] = (hidden[b] * scale * gain[b]).astype(bf16)
        return 0

    lax.fori_loop(0, count, norm, 0)


def forward_body(
    table,
    normed,
    grad,
    pieces,
    active,
    change,
    *refs,
):
    outs, (down, weights, acc, gate_slope, up_slope, sems, down_sems) = refs[:4], refs[4:]
    split = weights.shape[1]
    wait = start_pieces(table, pieces, weights, sems, slice(0, split))
    down_wait = start_pieces(
        table, pieces, down, down_sems, slice(split, split + down.shape[1])
    )
    count, tokens = normed.shape[:2]
    width = acc.shape[1]
    half = width // 2
    acc[...] = jnp.zeros_like(acc)

    def one(k, _):
        b = table[ORDER + k]
        wait(k)
        acc[...] += dims(normed[b], weights[b, :width], 1, 1)
        return 0

    lax.fori_loop(0, count, one, 0)
    rows = tokens // 4

    def part(i, _):
        at = pl.ds(pl.multiple_of(i * rows, rows), rows)
        gate, up = acc[at, :half], acc[at, half:]
        sigmoid = jax.nn.sigmoid(gate)
        active[at] = (gate * sigmoid * up).astype(bf16)
        gate_slope[at] = up * sigmoid * (1.0 + gate * (1.0 - sigmoid))
        up_slope[at] = gate * sigmoid
        return 0

    lax.fori_loop(0, 4, part, 0)

    def back(k, total):
        b = table[ORDER + k]
        down_wait(k)
        return total + dims(grad[b], down[b], 1, 1)

    slope = lax.fori_loop(0, count, back, jnp.zeros((tokens, half), f32))
    change[:, :half] = (slope * gate_slope[...]).astype(bf16)
    change[:, half:] = (slope * up_slope[...]).astype(bf16)
    values = change[...]
    keep_and_send(
        table,
        lambda b: dims(values, weights[b, :width], 1, 0),
        outs,
    )


def forward_third_body(table, active, normed, change, grad, third, both):
    width = change.shape[1]
    both[:width] = change[...].T
    both[width:] = active[...].T
    b = table[ORDER + 3]
    third[:width] = dims(both[:width], normed[b], 1, 0).astype(bf16)
    third[width:] = dims(both[width:], grad[b], 1, 0).astype(bf16)


def forward_parts_body(table, both, normed, grad, *parts):
    rows = both.shape[0] // 6

    def fill(first, count, source):
        def one(i, _):
            at = pl.ds(pl.multiple_of((first + i) * rows, rows), rows)
            for k, part in enumerate(parts):
                part[at] = dims(both[at], source[table[ORDER + k]], 1, 0).astype(bf16)
            return 0

        lax.fori_loop(0, count, one, 0)

    fill(0, 4, normed)
    fill(4, 2, grad)


def down_body(table, active, weights, *outs):
    values = active[...]
    keep_and_send(table, lambda b: dims(values, weights[b], 1, 0), outs)


def attend_back_body(
    table,
    own_first,
    own_second,
    other_first,
    other_second,
    hidden,
    inverse,
    grad,
    gain,
    weights,
    query,
    own,
    far,
    attended,
    log_total,
    cosine,
    sine,
    through,
    pull,
    query_low,
    own_back,
    *rest,
):
    sends, inner_first = rest[: GROUP - 1], rest[GROUP - 1]
    far_back, change, branch = rest[GROUP:]
    core = table[C]
    count, tokens, model = hidden.shape
    for i, (mine, theirs) in enumerate(((own_first, other_first), (own_second, other_second))):
        change[2 * i + core] = mine[...].astype(f32) * gain[2 * i + core]
        change[2 * i + 1 - core] = theirs[...].astype(f32) * gain[2 * i + 1 - core]

    def product(b, total):
        return total + jnp.sum(change[b] * hidden[b], axis=1, keepdims=True)

    inner = lax.fori_loop(0, count, product, jnp.zeros((tokens, 1), f32))
    scale = inverse[...]
    back = scale * scale * scale * inner / (count * model)
    pull[...] = back

    def rows(b, total):
        values = grad[b].astype(f32) + scale * change[b] - hidden[b] * back
        low = values.astype(bf16)
        through[b] = low
        return total + dims(low, weights[b, first:], 1, 1)

    heads_cols = query.shape[0]
    first = weights.shape[1] - heads_cols
    total_rows = lax.fori_loop(0, count, rows, jnp.zeros((tokens, heads_cols), f32))
    branch[...] = total_rows.T.astype(bf16)

    head = HEAD_DIM
    block = tokens // 2
    key_far_t = far[:head]
    key_far, value_far = key_far_t.T, far[head:].T
    key_own, value_own = own[:head].T, own[head:].T
    total = far.shape[1]
    near_row = lax.broadcasted_iota(jnp.int32, (block, block), 0)
    near_col = lax.broadcasted_iota(jnp.int32, (block, block), 1)
    causal = near_row <= near_col
    row = lax.broadcasted_iota(jnp.int32, (total, block), 0)
    far_back[...] = jnp.zeros_like(far_back)
    own_back[...] = jnp.zeros_like(own_back)
    inner_first[...] = jnp.zeros_like(inner_first)
    for part in range(2):
        cols = slice(part * block, (part + 1) * block)
        key_near, value_near = key_own[cols], value_own[cols]
        key_near_t = own[:head, cols]
        seen = row < table[COUNT + part] * block

        def one_head(h, _):
            at = pl.ds(pl.multiple_of(h * head, head), head)
            rows_q, rows_grad = query[at, cols], branch[at, cols]
            delta = jnp.sum(
                rows_grad.astype(f32) * attended[at, cols], axis=0, keepdims=True
            )
            logs = log_total[h, :, cols]

            def one(key, value, allowed):
                score = dims(key, rows_q, 1, 0) * score_scale
                prob = jnp.where(allowed, jnp.exp(score - logs), 0.0)
                moved = (prob * (dims(value, rows_grad, 1, 0) - delta)).astype(bf16)
                return prob.astype(bf16), moved

            prob_far, moved_far = one(key_far, value_far, seen)
            prob_near, moved_near = one(key_near, value_near, causal)
            query_back = (
                dims(key_far_t, moved_far, 1, 0) + dims(key_near_t, moved_near, 1, 0)
            ) * score_scale
            inner_first[:, cols] += jnp.sum(
                query_back * rows_q.astype(f32), axis=0, keepdims=True
            )
            query_low[at, cols] = turn(query_back, cosine[:, cols], -sine[:, cols]).astype(bf16)
            far_back[:head] += dims(rows_q, moved_far, 1, 1) * score_scale
            far_back[head:] += dims(rows_grad, prob_far, 1, 1)
            own_back[:head, cols] += dims(rows_q, moved_near, 1, 1) * score_scale
            own_back[head:, cols] += dims(rows_grad, prob_near, 1, 1)
            return 0

        lax.fori_loop(0, heads_cols // head, one_head, 0)
    for slot in range(PROMPTS):

        @pl.when(table[Z_IN] == slot)
        def _():
            own_back[...] += far_back[:, slot * tokens : (slot + 1) * tokens]

    for k in range(1, GROUP):
        sends[k - 1][...] = far_back[:, :tokens].astype(bf16)
        for slot in range(1, PROMPTS):

            @pl.when(table[Z_IN] == slot + k)
            def _():
                sends[k - 1][...] = far_back[:, slot * tokens : (slot + 1) * tokens].astype(bf16)


def attend_parts_body(table, query_low, through, normed, attended_low, *parts):
    rows = query_low.shape[0]
    for k, part in enumerate(parts):
        b = table[ORDER + k]
        part[:rows] = dims(query_low[...], normed[b], 1, 0).astype(bf16)
        part[-rows:] = dims(attended_low[...], through[b], 1, 0).astype(bf16)


def qkv_back_body(table, *refs):
    count = table.shape[0] - ORDER
    own_back, moved, refs = refs[count], refs[count + 1 : count + GROUP], refs[count + GROUP :]
    query_low, inner, weights, cosine, sine, own, normed = refs[:7]
    parts, outs = refs[7 : 7 + count], refs[7 + count : 11 + count]
    inner_first, own_low, changed, sems = refs[11 + count :]
    head = HEAD_DIM
    total = own_back[...]
    for part in moved:
        total = total + part[...].astype(f32)
    inner_first[...] = inner[...] + jnp.sum(total * own[...].astype(f32), axis=0, keepdims=True)
    key = turn(total[:head], cosine[...], -sine[...])
    low = jnp.concatenate([key, total[head:]], axis=0)
    own_low[...] = low.astype(bf16)
    first = query_low.shape[0]
    copies = []
    for k, part in enumerate(parts):
        changed[k] = dims(own_low[...], normed[table[ORDER + k]], 1, 0).astype(bf16)
        target = part.at[first : first + low.shape[0]]
        copies.append(pltpu.make_async_copy(changed.at[k], target, sems.at[k]))
        copies[k].start()
    flipped = jnp.concatenate([query_low[...].T, low.T.astype(bf16)], axis=1)
    width = flipped.shape[1]
    keep_and_send(table, lambda b: dims(flipped, weights[b, :width], 1, 0), outs)
    for copy in copies:
        copy.wait()


def halves_of(table, whole):
    half = whole.shape[0] // 2
    low, high = whole[:half], whole[half:]
    flag = table[Y] == 0
    return jnp.where(flag, low, high), jnp.where(flag, high, low)


def add_body(table, sources, out, first, second, sems, *, rows):
    copies = [
        pltpu.make_async_copy(source.at[rows], held, sems.at[i])
        for i, (source, held) in enumerate(zip(sources, (first, second)))
    ]
    for copy in copies:
        copy.start()
    for copy in copies:
        copy.wait()
    out[...] = add(first[...], second[...])


def pack(rows, packed):
    half, cols = packed.shape[0], rows.shape[1]
    packed[:, :cols] = rows[:half].astype(packed.dtype)
    packed[:, cols:] = rows[half:].astype(packed.dtype)


def split_body(table, *refs):
    matrices, (mine_ref, other_ref) = refs[:-2], refs[-2:]
    pairs = [halves_of(table, matrix[...].T) for matrix in matrices]
    pack(jnp.concatenate([mine for mine, _ in pairs], axis=0), mine_ref)
    pack(jnp.concatenate([other for _, other in pairs], axis=0), other_ref)


def piece_body(table, mine_ref, got_ref, piece):
    flag = table[Y] == 0
    mine, got = mine_ref[...], got_ref[...]
    low, high = jnp.where(flag, mine, got), jnp.where(flag, got, mine)
    half, cols = mine.shape[0], mine.shape[1] // 2
    for i in range(2):
        piece[i * half : (i + 1) * half, :cols] = low[:, i * cols : (i + 1) * cols]
        piece[i * half : (i + 1) * half, cols:] = high[:, i * cols : (i + 1) * cols]


def sum_body(table, *refs):
    parts, (mine_ref, other_ref) = refs[:-2], refs[-2:]
    whole = [part for part in parts if part.shape == parts[0].shape]
    total = whole[0][...].astype(f32)
    for part in whole[1:]:
        total = total + part[...].astype(f32)
    rest = [part[...].astype(f32) for part in parts if part.shape != parts[0].shape]
    if rest:
        total = total + jnp.concatenate(rest, axis=0)
    cols = total.shape[1] // 2
    low, high = total[:, :cols], total[:, cols:]
    flag = table[Y] == 0
    pack(jnp.where(flag, low, high), mine_ref)
    pack(jnp.where(flag, high, low), other_ref)


def join_body(table, mine_ref, got_ref, *outs):
    flag = table[Y] == 0
    cols = mine_ref.shape[1] // 2

    def unpacked(ref):
        return jnp.concatenate([ref[:, :cols], ref[:, cols:]], axis=0).astype(f32)

    mine, got = unpacked(mine_ref), unpacked(got_ref)
    low, high = jnp.where(flag, mine, got), jnp.where(flag, got, mine)
    at = 0
    for out in outs:
        rows = out.shape[1] // 2
        out[:, :rows] = low[at : at + rows].T
        out[:, rows:] = high[at : at + rows].T
        at += rows


def rope_tables(positions, half):
    freq = rope_base ** (-(2.0 * jnp.arange(half, dtype=f32)) / (2.0 * half))
    angle = freq[:, None] * positions.astype(f32)[None, :]
    return (jnp.cos(angle), jnp.sin(angle))


def shards(
    layer_in,
    first_gain,
    query_weight,
    key_matrix,
    value_matrix,
    out_weight,
    second_gain,
    gate_weight,
    up_weight,
    down_weight,
    out_grad,
):
    place = Place()
    n, ny, y, z_in, table = place.n, place.ny, place.y, place.z_in, place.table
    lined = place.lined
    block, width = layer_in.shape
    tokens = 2 * block
    model_width = width * ny
    hidden_dev = gate_weight.shape[1] // 2
    query_rows = query_weight.shape[1] // 2
    kv_rows = key_matrix.shape[1]
    qkv_cols = query_rows + kv_rows
    full = (ny, tokens, width)
    wide = [(full[1:], bf16)] * 4

    def halves(*matrices, earlier=()):
        rows = sum(m.shape[1] for m in matrices) // 2
        packed = (rows // 2, 2 * matrices[0].shape[0])
        return call(split_body, [(packed, bf16)] * 2, table, [], held=matrices, earlier=earlier)

    def whole_piece(mine, got):
        rows, cols = mine.shape
        (piece,) = call(piece_body, [((2 * rows, cols), bf16)], table, [mine, got])
        return piece

    def spread(value, *before_y):
        by_x = place.swap_x(value)
        late, late_x = lax.optimization_barrier((value, by_x) + before_y)[:2]
        four = [value, by_x, place.swap_y(late), place.swap_y(late_x)]
        return four + [place.swap_c(r) for r in four]

    mine, other = halves(query_weight, key_matrix, value_matrix, out_weight.T)
    attend_got = place.swap_y(other)
    attend_piece = whole_piece(mine, attend_got)
    mine, other = halves(gate_weight, up_weight, down_weight.T, earlier=[attend_piece])
    forward_got = place.swap_y(other)
    forward_piece = whole_piece(mine, forward_got)
    rows = jnp.concatenate([layer_in, out_grad], axis=0)
    input_rows = spread(after(rows, attend_got), forward_got)
    if lined:
        attend_pieces = gather_pieces(place, attend_piece)
        forward_pieces = gather_pieces(place, after(forward_piece, *attend_pieces[1:]), True)
    else:
        attend_pieces = [gather_whole(place, attend_piece)]
        forward_pieces = [gather_whole(place, forward_piece)]
    attend_shape = (ny, qkv_cols + query_rows, width)
    forward_shape = (ny, 3 * hidden_dev, width)
    sems = pltpu.SemaphoreType.DMA((ny,))

    gains = jnp.stack([first_gain, second_gain])
    two = [gains, place.swap_x(gains)]
    gains = two + [place.swap_c(g) for g in two]
    raw, grad, normed_in, inverse_in, gain_in, gain_mid = call(
        rows_body,
        [(full, bf16)] * 3 + [((tokens, 1), f32)] + [((ny, 1, width), f32)] * 2,
        table,
        input_rows + gains,
    )

    within = jnp.arange(block, dtype=jnp.int32)
    positions = jnp.minimum(place.offset, PROMPT_DEV)[:, None] * block + within[None, :]
    cosine, sine = rope_tables(positions.reshape(-1), HEAD_DIM // 2)
    query, own, attend_weights = call(
        qkv_body,
        [((query_rows, tokens), bf16), ((kv_rows, tokens), bf16), (attend_shape, bf16)],
        table,
        [normed_in, cosine, sine],
        [attend_pieces],
        [pltpu.VMEM((qkv_cols, tokens), f32), sems],
    )
    moved = [
        place.send_z(
            own,
            [(s, s + k) for s in range(n) if s % GROUP < PROMPTS and s % GROUP + k < GROUP],
        )
        for k in range(1, GROUP)
    ]
    attended, attended_low, log_total, far, *halves_out = call(
        attend_body,
        [
            ((query_rows, tokens), f32),
            ((query_rows, tokens), bf16),
            ((query_rows // HEAD_DIM, 1, tokens), f32),
            ((kv_rows, PROMPTS * tokens), bf16),
        ]
        + wide,
        table,
        [query, own] + moved + [attend_weights],
        earlier=forward_pieces[1:3],
    )
    summed = all_sum(
        place,
        halves_out[:2],
        halves_out[2:],
        before_first=forward_pieces[1:3] if lined else forward_pieces,
        before_last=forward_pieces[3:],
    )

    hidden, normed_mid, inverse_mid = call(
        hidden_body,
        [(full, f32), (full, bf16), ((tokens, 1), f32)],
        table,
        summed,
        held=[raw, gain_mid],
    )
    active, change, *halves_out, down_whole = call(
        forward_body,
        [((tokens, hidden_dev), bf16), ((tokens, 2 * hidden_dev), bf16)]
        + wide
        + [((ny, hidden_dev, width), bf16)],
        table,
        [normed_mid],
        [forward_pieces],
        [
            pltpu.VMEM((ny, 2 * hidden_dev, width), bf16),
            pltpu.VMEM((tokens, 2 * hidden_dev), f32),
        ]
        + [pltpu.VMEM((tokens, hidden_dev), f32)] * 2
        + [sems, sems],
        held=[grad],
    )
    third, both = call(
        forward_third_body,
        [(forward_shape[1:], bf16), (forward_shape[1:2] + (tokens,), bf16)],
        table,
        [active, normed_mid, change],
        held=[grad],
    )
    forward_parts = call(
        forward_parts_body,
        [(forward_shape[1:], bf16)] * 3,
        table,
        [both, normed_mid],
        held=[grad],
    )
    forward_parts = list(forward_parts) + [third]
    forward_started = start_scatter(place, forward_parts)
    down_halves = call(
        down_body, wide, table, [active, down_whole], earlier=[forward_parts[0]]
    )
    summed = all_sum(
        place,
        halves_out[:2],
        halves_out[2:],
        before_second=forward_parts[:1],
        before_last=list(down_halves[:1]) + forward_started[2:3] + forward_started[4:],
    )
    _, forward_second = second_scatter(place, forward_started, 0, 2, summed[-1])
    hidden_own = own_block(place, hidden)
    through, pull, query_low, own_back, *returns, inner_first = call(
        attend_back_body,
        [
            (full, bf16),
            ((tokens, 1), f32),
            ((query_rows, tokens), bf16),
            ((kv_rows, tokens), f32),
        ]
        + [((kv_rows, tokens), bf16)] * (GROUP - 1)
        + [((1, tokens), f32)],
        table,
        summed,
        held=[
            hidden,
            inverse_mid,
            grad,
            gain_mid,
            attend_weights,
            query,
            own,
            far,
            attended,
            log_total,
            cosine,
            sine,
        ],
        earlier=forward_started[2:3] + forward_started[4:],
        scratch=[
            pltpu.VMEM((kv_rows, PROMPTS * tokens), f32),
            pltpu.VMEM(full, f32),
            pltpu.VMEM((query_rows, tokens), bf16),
        ],
    )
    down_sends = lax.optimization_barrier(tuple(down_halves[2:]) + (through,))[:2]
    layer_out = (hidden_own + own_sum(place, down_halves[:2], down_sends)).astype(bf16)
    inverse_own, _ = part_of(y, inverse_mid, 0)
    pull_own, _ = part_of(y, pull, 0)
    mid_own = jnp.where(place.x == 0, summed[0], summed[1])
    mid_own = part_of(y, mid_own, 0)[0].astype(f32)
    through_own = (
        out_grad.astype(f32)
        + inverse_own * mid_own * second_gain[None, :]
        - hidden_own * pull_own
    )
    second_term = jnp.sum(mid_own * hidden_own * inverse_own, axis=0)

    moved = [
        place.send_z(
            returns[k - 1],
            [(s, s - k) for s in range(n) if 0 <= s % GROUP - k < PROMPTS],
        )
        for k in range(1, GROUP)
    ]
    attend_parts = call(
        attend_parts_body,
        [(attend_shape[1:], bf16)] * ny,
        table,
        [query_low, through],
        held=[normed_in, attended_low],
    )
    results = call(
        qkv_back_body,
        [(attend_shape[1:], bf16)] * ny
        + wide
        + [((1, tokens), f32), ((kv_rows, tokens), bf16)],
        table,
        list(attend_parts) + [own_back] + moved + [query_low, inner_first],
        held=[attend_weights, cosine, sine, own, normed_in],
        scratch=[pltpu.VMEM((ny, kv_rows, width), bf16), sems],
        earlier=forward_started[3:4] + ([forward_second] if lined else []),
        alias=ny,
    )
    attend_parts, first_halves = results[:ny], results[ny:-2]
    inner, own_low = results[-2:]
    attend_started = start_scatter(place, attend_parts)
    forward_seconds = [
        forward_second,
        second_scatter(place, forward_started, 1, 2, summed[-1], moved[0])[1],
    ]
    attend_sent, attend_second = second_scatter(place, attend_started, 0, 1)
    attend_grad = end_scatter(place, attend_started, [attend_second], own_low)
    inner = inner + place.swap_c(inner)
    inner = inner + place.swap_x(inner)
    inner = inner + place.swap_y(inner)
    first_own = own_sum(
        place,
        first_halves[:2],
        first_halves[2:],
        before_y=[attend_sent] if lined else [],
    )
    forward_grad = end_scatter(
        place, forward_started, forward_seconds, *([attend_sent] if lined else [])
    )
    input_own = layer_in.astype(f32)
    inverse_own, _ = part_of(y, inverse_in, 0)
    scaled = first_own * first_gain[None, :]
    inner = part_of(y, inner.reshape(tokens, 1), 0)[0]
    in_grad = (
        through_own + inverse_own * scaled - input_own * (inverse_own**2 * inner / model_width)
    )
    first_term = jnp.sum(first_own * input_own * inverse_own, axis=0)
    terms = jnp.stack([first_term, second_term])
    bit = 1
    while bit < place.nx:
        terms = terms + place.swap_gx(terms, bit)
        bit *= 2

    def joined(parts, outs):
        rows, cols = parts[0].shape
        packed = (rows // 2, cols)
        mine, other = call(sum_body, [(packed, f32), (packed, bf16)], table, parts)
        shapes = [(cols // 2, inner) for inner in outs]
        return call(
            join_body, [(s, f32) for s in shapes], table, [mine, place.swap_y(other)]
        )

    gate_grad, up_grad, down_grad = joined(forward_grad, [2 * hidden_dev] * 3)
    query_out, key_out, value_out, out_out = joined(
        attend_grad, [2 * query_rows, kv_rows, kv_rows, 2 * query_rows]
    )
    return (
        layer_out,
        in_grad,
        terms[0],
        query_out,
        key_out,
        value_out,
        out_out.T,
        terms[1],
        gate_grad,
        up_grad,
        down_grad.T,
    )


def solution(mesh):
    rows, cols, gain = P("gx", "gy"), P("gy", "gx"), P("gy")
    return jax.shard_map(
        shards,
        mesh=mesh,
        in_specs=(rows, gain, rows, rows, rows, cols, gain, rows, rows, cols, rows),
        out_specs=(rows, rows, gain, rows, rows, rows, cols, gain, rows, rows, cols),
        check_vma=False,
    )
```

```python
from functools import partial

import jax
import jax.numpy as jnp
from jax import lax
from jax.experimental import pallas as pl
from jax.experimental.pallas import tpu as pltpu
from jax.sharding import PartitionSpec as P

HEAD_DIM = 96
PROMPT_DEV = 4
CONT_DEV = 4
GROUP = (PROMPT_DEV + CONT_DEV) // 2
PROMPTS = PROMPT_DEV // 2

eps = 1e-05
neg_big = -1e30
rope_base = 100000.0
score_scale = HEAD_DIM ** (-0.5)
f32 = jnp.float32
bf16 = jnp.bfloat16


def dims(left, right, left_axis, right_axis):
    return lax.dot_general(
        left, right, (((left_axis,), (right_axis,)), ((), ())), preferred_element_type=f32
    )


class Place:
    def __init__(self):
        self.nx = lax.axis_size("gx")
        self.ny = lax.axis_size("gy")
        assert self.ny == 4 and self.nx % (PROMPT_DEV + CONT_DEV) == 0
        self.n = self.nx // 2
        self.gx = lax.axis_index("gx")
        self.gy = lax.axis_index("gy")
        self.z, self.y = self.gx // 2, self.gx % 2
        self.x, self.c = self.gy // 2, self.gy % 2
        self.z_in = self.z % GROUP
        offset = 2 * self.z_in + jnp.arange(2, dtype=jnp.int32)
        self.offset = offset
        self.lined = self.n == self.ny
        blocks = jnp.arange(self.ny, dtype=jnp.int32)
        first = jnp.stack([self.z, self.y, self.x, self.c, self.z_in]).astype(jnp.int32)
        self.table = jnp.concatenate(
            [first, jnp.minimum(offset, PROMPT_DEV), blocks ^ self.z if self.lined else blocks]
        )

    def swap_gx(self, value, bit):
        return lax.ppermute(value, "gx", [(i, i ^ bit) for i in range(self.nx)])

    def swap_y(self, value):
        return self.swap_gx(value, 1)

    def swap_x(self, value):
        return lax.ppermute(value, "gy", [(i, i ^ 2) for i in range(self.ny)])

    def swap_c(self, value):
        return lax.ppermute(value, "gy", [(i, i ^ 1) for i in range(self.ny)])

    def send_z(self, value, moves):
        pairs = [(2 * s + y, 2 * t + y) for s, t in moves for y in range(2)]
        return lax.ppermute(value, "gx", pairs)

    def by_y(self):
        return [[2 * z + y for z in range(self.n)] for y in range(2)]


def pair(flag, mine, other):
    return jnp.where(flag == 0, mine, other), jnp.where(flag == 0, other, mine)


def part_of(flag, whole, axis):
    low, high = jnp.split(whole, 2, axis)
    return jnp.where(flag == 0, low, high), jnp.where(flag == 0, high, low)


def after(value, *earlier):
    return lax.optimization_barrier((value,) + earlier)[0]


NEAR = [(0, 1), (1, 0), (2, 3), (3, 2)]
SECOND = [(0, 2), (1, 3), (2, 0), (3, 1)]
MIDDLE = [(1, 2), (2, 1)]
INWARD = [(0, 1), (3, 2)]
OUTWARD = [(1, 0), (2, 3)]


def gather_pieces(place, piece, late_middle=False):
    second = place.send_z(piece, SECOND)
    near = place.send_z(piece, NEAR)
    middle = place.send_z(after(piece, second) if late_middle else piece, MIDDLE)
    return [piece, near, second, middle, place.send_z(second, OUTWARD)]


def gather_whole(place, piece):
    every = lax.all_gather(piece, "gx", axis_index_groups=place.by_y())
    inner = place.n // place.ny
    if inner == 1:
        return every
    rows, cols = piece.shape
    every = every.reshape(place.ny, inner, rows, cols)
    return jnp.swapaxes(every, 1, 2).reshape(place.ny, rows, inner * cols)


def scatter_whole(place, parts):
    inner = place.n // place.ny
    if inner > 1:
        count, rows, cols = parts.shape
        parts = jnp.swapaxes(parts.reshape(count, rows, inner, cols // inner), 1, 2)
        parts = parts.reshape(place.n, rows, cols // inner)
    return lax.psum_scatter(parts, "gx", axis_index_groups=place.by_y())


def start_scatter(place, parts):
    if not place.lined:
        return [scatter_whole(place, jnp.stack(parts))]
    own, near, second, third = parts
    far = place.send_z(third, INWARD)
    middle = place.send_z(third, MIDDLE)
    return [own, second, far, place.send_z(near, NEAR), middle]


def second_scatter(place, started, part, count, *earlier):
    if not place.lined:
        return None, None
    rows, cols = started[1].shape
    cut = rows if count == 1 else rows * 5 // 8
    at = slice(0, cut) if part == 0 else slice(cut, rows)
    size = at.stop - at.start
    (summed,) = call(
        partial(add_body, rows=at),
        [((size, cols), bf16)],
        place.table,
        [],
        [started[1:3]],
        [pltpu.VMEM((size, cols), bf16)] * 2 + [pltpu.SemaphoreType.DMA((2,))],
        earlier=[started[4]] + list(earlier),
    )
    return summed, place.send_z(summed, SECOND)


def end_scatter(place, started, seconds, *earlier):
    if not place.lined:
        return started
    return [after(started[0], *earlier), started[3], started[4]] + list(seconds)


def add(left, right):
    return (left.astype(f32) + right.astype(f32)).astype(bf16)


def reduce_core(place, keeps, sends):
    return [add(keep, place.swap_c(send)) for keep, send in zip(keeps, sends)]


def all_sum(place, keeps, sends, before_first=(), before_second=(), before_last=()):
    low = tuple(reduce_core(place, keeps, sends))
    low = lax.optimization_barrier(low + tuple(before_first))
    low = add(low[0], place.swap_x(low[0])), add(low[1], place.swap_y(low[1]))
    low = lax.optimization_barrier(low + tuple(before_second))
    own = (add(low[0], place.swap_y(low[0])), add(low[1], place.swap_x(low[1])))
    if before_last:
        own = lax.optimization_barrier(own + tuple(before_last))[:2]
    own = list(own)
    return own + [place.swap_c(part) for part in own]


def own_sum(place, keeps, sends, before_x=(), before_y=()):
    first, second = reduce_core(place, keeps, sends)
    if before_x:
        first, second = lax.optimization_barrier((first, second) + tuple(before_x))[:2]
    mine, other = jnp.where(place.x == 0, first, second), jnp.where(place.x == 0, second, first)
    mine = add(mine, place.swap_x(other))
    mine = after(mine, *before_y) if before_y else mine
    mine, other = part_of(place.y, mine, 0)
    return mine.astype(f32) + place.swap_y(other).astype(f32)


def own_block(place, blocks):
    rows = blocks.shape[1] // 2
    return lax.dynamic_slice(
        blocks, (place.gy, place.y * rows, 0), (1, rows, blocks.shape[2])
    )[0]


Z, Y, X, C, Z_IN, COUNT = range(6)
ORDER = COUNT + 2


def call(body, outs, table, operands, pieces=(), scratch=(), earlier=(), held=(), alias=0, limit=24):
    if operands:
        operands, held = list(operands) + list(held), ()
    lengths = [len(p) for p in pieces]
    flat = [a for p in pieces for a in p] + list(earlier)
    vmem = pl.BlockSpec(memory_space=pltpu.VMEM)
    copied = [pltpu.VMEM(a.shape, a.dtype) for a in held]
    if held:
        copied.append(pltpu.SemaphoreType.DMA((len(held),)))

    def kernel(table_ref, *refs):
        plain, rest = refs[: len(operands)], refs[len(operands) :]
        sources, rest = rest[: len(held)], rest[len(held) :]
        lists = []
        for length in lengths:
            lists.append(rest[:length])
            rest = rest[length:]
        rest = rest[len(earlier) :]
        targets = ()
        if held:
            rest, targets = rest[: -len(copied)], rest[-len(copied) :]
            copies = [
                pltpu.make_async_copy(source, target, targets[-1].at[i])
                for i, (source, target) in enumerate(zip(sources, targets))
            ]
            for copy in copies:
                copy.start()
            for copy in copies:
                copy.wait()
        body(table_ref, *plain, *targets[:-1], *lists, *rest)

    return pl.pallas_call(
        kernel,
        out_shape=[jax.ShapeDtypeStruct(shape, dtype) for shape, dtype in outs],
        in_specs=[pl.BlockSpec(memory_space=pltpu.SMEM)]
        + [pl.BlockSpec(memory_space=pl.ANY)] * alias
        + [vmem] * (len(operands) - alias)
        + [pl.BlockSpec(memory_space=pltpu.HBM)] * len(held)
        + [pl.BlockSpec(memory_space=pl.ANY)] * len(flat),
        out_specs=[pl.BlockSpec(memory_space=pl.ANY)] * alias + [vmem] * (len(outs) - alias),
        scratch_shapes=list(scratch) + copied,
        input_output_aliases={i + 1: i for i in range(alias)},
        compiler_params=pltpu.CompilerParams(vmem_limit_bytes=limit << 20),
    )(table, *operands, *held, *flat)


def start_pieces(table, pieces, whole, sems, rows=slice(None)):
    count = whole.shape[0]
    block = [table[ORDER + k] for k in range(count)]

    def copy(piece, k):
        source = piece.at[rows] if rows != slice(None) else piece
        return pltpu.make_async_copy(source, whole.at[block[k]], sems.at[k])

    def wait(k):
        pltpu.make_async_copy(whole.at[0], whole.at[0], sems.at[k]).wait()

    if len(pieces) == 1:
        for k in range(count):
            copy(pieces[0].at[block[k]], k).start()
        return wait
    z = table[Z]
    own, near, second, middle, end = pieces
    for k, piece in enumerate((own, near, second)):
        copy(piece, k).start()
    inside = jnp.logical_or(z == 1, z == 2)

    @pl.when(inside)
    def _():
        copy(middle, 3).start()

    @pl.when(jnp.logical_not(inside))
    def _():
        copy(end, 3).start()

    return wait


def keep_and_send(table, block_of, outs):
    core = table[C]
    for i in range(2):
        outs[i][...] = block_of(2 * i + core).astype(bf16)
        outs[2 + i][...] = block_of(2 * i + 1 - core).astype(bf16)


def place_rows(table, pieces, raw, grad):
    x, y, c = table[X], table[Y], table[C]
    tokens = raw.shape[1] // 2
    for dc in range(2):
        for dx in range(2):
            block = 2 * (x + dx - 2 * x * dx) + c + dc - 2 * c * dc
            for dy in range(2):
                at = pl.ds(pl.multiple_of(tokens * (y + dy - 2 * y * dy), tokens), tokens)
                piece = pieces[4 * dc + 2 * dy + dx]
                raw[block, at, :] = piece[:tokens]
                grad[block, at, :] = piece[tokens:]


def norm_rows(raw, gain, normed):
    def square(b, total):
        values = raw[b].astype(f32)
        return total + jnp.sum(values * values, axis=1, keepdims=True)

    count = raw.shape[0]
    total = lax.fori_loop(0, count, square, jnp.zeros((raw.shape[1], 1), f32))
    scale = lax.rsqrt(total / (count * raw.shape[2]) + eps)

    def norm(b, _):
        normed[b] = (raw[b].astype(f32) * scale * gain[b]).astype(bf16)
        return 0

    lax.fori_loop(0, count, norm, 0)
    return scale


def rows_body(table, *refs):
    gains = refs[8:12]
    raw, grad, normed, inverse, gain_first, gain_second = refs[12:]
    place_rows(table, refs[:8], raw, grad)
    x, c = table[X], table[C]
    for dc in range(2):
        for dx in range(2):
            block = 2 * (x + dx - 2 * x * dx) + c + dc - 2 * c * dc
            gain = gains[2 * dc + dx][...]
            gain_first[block] = gain[0:1]
            gain_second[block] = gain[1:2]
    inverse[...] = norm_rows(raw, gain_first, normed)


def turn(values, cosine, sine):
    half = values.shape[0] // 2
    first, second = values[:half], values[half:]
    return jnp.concatenate(
        [first * cosine - second * sine, second * cosine + first * sine], axis=0
    )


def qkv_body(
    table, normed, cosine, sine, pieces, query, own, weights, acc, sems
):
    wait = start_pieces(table, pieces, weights, sems)
    count = acc.shape[0]
    acc[...] = jnp.zeros_like(acc)

    def one(k, _):
        b = table[ORDER + k]
        wait(k)
        acc[...] += dims(weights[b, :count], normed[b], 1, 1)
        return 0

    lax.fori_loop(0, normed.shape[0], one, 0)
    head = HEAD_DIM
    heads = query.shape[0] // head
    cos, sin = cosine[...], sine[...]
    for h in range(heads):
        at = slice(h * head, (h + 1) * head)
        query[at] = turn(acc[at], cos, sin).astype(bf16)
    at = slice(heads * head, (heads + 1) * head)
    own[:head] = turn(acc[at], cos, sin).astype(bf16)
    own[head:] = acc[(heads + 1) * head :].astype(bf16)


def attend_body(table, query, own, *refs):
    moved, refs = refs[: GROUP - 1], refs[GROUP - 1 :]
    (weights, attended, attended_low, log_total, far), outs = refs[:5], refs[5:]
    tokens = own.shape[1]
    for place in range(GROUP):

        @pl.when(table[Z_IN] == place)
        def _():
            for slot in range(PROMPTS):
                k = place - slot
                far[:, slot * tokens : (slot + 1) * tokens] = (
                    moved[k - 1][...] if k > 0 else own[...]
                )

    head = HEAD_DIM
    block = tokens // 2
    key_far, value_far = far[:head].T, far[head:]
    key_own = own[:head].T
    total = far.shape[1]
    near_row = lax.broadcasted_iota(jnp.int32, (block, block), 0)
    near_col = lax.broadcasted_iota(jnp.int32, (block, block), 1)
    causal = near_row <= near_col
    row = lax.broadcasted_iota(jnp.int32, (total, block), 0)
    for part in range(2):
        cols = slice(part * block, (part + 1) * block)
        key_near, value_near = key_own[cols], own[head:, cols]
        seen = row < table[COUNT + part] * block

        def one(h, _):
            at = pl.ds(pl.multiple_of(h * head, head), head)
            rows = query[at, cols]
            score_far = jnp.where(seen, dims(key_far, rows, 1, 0) * score_scale, neg_big)
            score_near = jnp.where(causal, dims(key_near, rows, 1, 0) * score_scale, neg_big)
            top = jnp.maximum(
                jnp.max(score_far, axis=0, keepdims=True), jnp.max(score_near, axis=0, keepdims=True)
            )
            weight_far = jnp.exp(score_far - top)
            weight_near = jnp.exp(score_near - top)
            weight = jnp.sum(weight_far, axis=0, keepdims=True) + jnp.sum(
                weight_near, axis=0, keepdims=True
            )
            out = dims(value_far, weight_far.astype(bf16), 1, 0) + dims(
                value_near, weight_near.astype(bf16), 1, 0
            )
            attended[at, cols] = out / weight
            log_total[h, :, cols] = top + jnp.log(weight)
            return 0

        lax.fori_loop(0, query.shape[0] // head, one, 0)
    values = attended[...]
    attended_low[...] = values.astype(bf16)
    flipped = values.T.astype(bf16)
    first = weights.shape[1] - query.shape[0]
    keep_and_send(
        table,
        lambda b: dims(flipped, weights[b, first:], 1, 0),
        outs,
    )


def hidden_body(
    table, own_first, own_second, other_first, other_second, raw, gain, hidden, normed, inverse
):
    core = table[C]
    summed, other = (own_first, own_second), (other_first, other_second)
    for i in range(2):
        b = 2 * i + core
        hidden[b] = raw[b].astype(f32) + summed[i][...].astype(f32)
        b = 2 * i + 1 - core
        hidden[b] = raw[b].astype(f32) + other[i][...].astype(f32)

    def square(b, total):
        values = hidden[b]
        return total + jnp.sum(values * values, axis=1, keepdims=True)

    count = raw.shape[0]
    total = lax.fori_loop(0, count, square, jnp.zeros((raw.shape[1], 1), f32))
    scale = lax.rsqrt(total / (count * raw.shape[2]) + eps)
    inverse[...] = scale

    def norm(b, _):
        normed[b] = (hidden[b] * scale * gain[b]).astype(bf16)
        return 0

    lax.fori_loop(0, count, norm, 0)


def forward_body(
    table,
    normed,
    grad,
    pieces,
    active,
    change,
    *refs,
):
    outs, (down, weights, acc, gate_slope, up_slope, sems, down_sems) = refs[:4], refs[4:]
    split = weights.shape[1]
    wait = start_pieces(table, pieces, weights, sems, slice(0, split))
    down_wait = start_pieces(
        table, pieces, down, down_sems, slice(split, split + down.shape[1])
    )
    count, tokens = normed.shape[:2]
    width = acc.shape[1]
    half = width // 2
    acc[...] = jnp.zeros_like(acc)

    def one(k, _):
        b = table[ORDER + k]
        wait(k)
        acc[...] += dims(normed[b], weights[b, :width], 1, 1)
        return 0

    lax.fori_loop(0, count, one, 0)
    rows = tokens // 4

    def part(i, _):
        at = pl.ds(pl.multiple_of(i * rows, rows), rows)
        gate, up = acc[at, :half], acc[at, half:]
        sigmoid = jax.nn.sigmoid(gate)
        active[at] = (gate * sigmoid * up).astype(bf16)
        gate_slope[at] = up * sigmoid * (1.0 + gate * (1.0 - sigmoid))
        up_slope[at] = gate * sigmoid
        return 0

    lax.fori_loop(0, 4, part, 0)

    def back(k, total):
        b = table[ORDER + k]
        down_wait(k)
        return total + dims(grad[b], down[b], 1, 1)

    slope = lax.fori_loop(0, count, back, jnp.zeros((tokens, half), f32))
    change[:, :half] = (slope * gate_slope[...]).astype(bf16)
    change[:, half:] = (slope * up_slope[...]).astype(bf16)
    values = change[...]
    keep_and_send(
        table,
        lambda b: dims(values, weights[b, :width], 1, 0),
        outs,
    )


def forward_third_body(table, active, normed, change, grad, third, both):
    width = change.shape[1]
    both[:width] = change[...].T
    both[width:] = active[...].T
    b = table[ORDER + 3]
    third[:width] = dims(both[:width], normed[b], 1, 0).astype(bf16)
    third[width:] = dims(both[width:], grad[b], 1, 0).astype(bf16)


def forward_parts_body(table, both, normed, grad, *parts):
    rows = both.shape[0] // 6

    def fill(first, count, source):
        def one(i, _):
            at = pl.ds(pl.multiple_of((first + i) * rows, rows), rows)
            for k, part in enumerate(parts):
                part[at] = dims(both[at], source[table[ORDER + k]], 1, 0).astype(bf16)
            return 0

        lax.fori_loop(0, count, one, 0)

    fill(0, 4, normed)
    fill(4, 2, grad)


def down_body(table, active, weights, *outs):
    values = active[...]
    keep_and_send(table, lambda b: dims(values, weights[b], 1, 0), outs)


def attend_back_body(
    table,
    own_first,
    own_second,
    other_first,
    other_second,
    hidden,
    inverse,
    grad,
    gain,
    weights,
    query,
    own,
    far,
    attended,
    log_total,
    cosine,
    sine,
    through,
    pull,
    query_low,
    own_back,
    *rest,
):
    sends, inner_first = rest[: GROUP - 1], rest[GROUP - 1]
    far_back, change, branch = rest[GROUP:]
    core = table[C]
    count, tokens, model = hidden.shape
    for i, (mine, theirs) in enumerate(((own_first, other_first), (own_second, other_second))):
        change[2 * i + core] = mine[...].astype(f32) * gain[2 * i + core]
        change[2 * i + 1 - core] = theirs[...].astype(f32) * gain[2 * i + 1 - core]

    def product(b, total):
        return total + jnp.sum(change[b] * hidden[b], axis=1, keepdims=True)

    inner = lax.fori_loop(0, count, product, jnp.zeros((tokens, 1), f32))
    scale = inverse[...]
    back = scale * scale * scale * inner / (count * model)
    pull[...] = back

    def rows(b, total):
        values = grad[b].astype(f32) + scale * change[b] - hidden[b] * back
        low = values.astype(bf16)
        through[b] = low
        return total + dims(low, weights[b, first:], 1, 1)

    heads_cols = query.shape[0]
    first = weights.shape[1] - heads_cols
    total_rows = lax.fori_loop(0, count, rows, jnp.zeros((tokens, heads_cols), f32))
    branch[...] = total_rows.T.astype(bf16)

    head = HEAD_DIM
    block = tokens // 2
    key_far_t = far[:head]
    key_far, value_far = key_far_t.T, far[head:].T
    key_own, value_own = own[:head].T, own[head:].T
    total = far.shape[1]
    near_row = lax.broadcasted_iota(jnp.int32, (block, block), 0)
    near_col = lax.broadcasted_iota(jnp.int32, (block, block), 1)
    causal = near_row <= near_col
    row = lax.broadcasted_iota(jnp.int32, (total, block), 0)
    far_back[...] = jnp.zeros_like(far_back)
    own_back[...] = jnp.zeros_like(own_back)
    inner_first[...] = jnp.zeros_like(inner_first)
    for part in range(2):
        cols = slice(part * block, (part + 1) * block)
        key_near, value_near = key_own[cols], value_own[cols]
        key_near_t = own[:head, cols]
        seen = row < table[COUNT + part] * block

        def one_head(h, _):
            at = pl.ds(pl.multiple_of(h * head, head), head)
            rows_q, rows_grad = query[at, cols], branch[at, cols]
            delta = jnp.sum(
                rows_grad.astype(f32) * attended[at, cols], axis=0, keepdims=True
            )
            logs = log_total[h, :, cols]

            def one(key, value, allowed):
                score = dims(key, rows_q, 1, 0) * score_scale
                prob = jnp.where(allowed, jnp.exp(score - logs), 0.0)
                moved = (prob * (dims(value, rows_grad, 1, 0) - delta)).astype(bf16)
                return prob.astype(bf16), moved

            prob_far, moved_far = one(key_far, value_far, seen)
            prob_near, moved_near = one(key_near, value_near, causal)
            query_back = (
                dims(key_far_t, moved_far, 1, 0) + dims(key_near_t, moved_near, 1, 0)
            ) * score_scale
            inner_first[:, cols] += jnp.sum(
                query_back * rows_q.astype(f32), axis=0, keepdims=True
            )
            query_low[at, cols] = turn(query_back, cosine[:, cols], -sine[:, cols]).astype(bf16)
            far_back[:head] += dims(rows_q, moved_far, 1, 1) * score_scale
            far_back[head:] += dims(rows_grad, prob_far, 1, 1)
            own_back[:head, cols] += dims(rows_q, moved_near, 1, 1) * score_scale
            own_back[head:, cols] += dims(rows_grad, prob_near, 1, 1)
            return 0

        lax.fori_loop(0, heads_cols // head, one_head, 0)
    for slot in range(PROMPTS):

        @pl.when(table[Z_IN] == slot)
        def _():
            own_back[...] += far_back[:, slot * tokens : (slot + 1) * tokens]

    for k in range(1, GROUP):
        sends[k - 1][...] = far_back[:, :tokens].astype(bf16)
        for slot in range(1, PROMPTS):

            @pl.when(table[Z_IN] == slot + k)
            def _():
                sends[k - 1][...] = far_back[:, slot * tokens : (slot + 1) * tokens].astype(bf16)


def attend_parts_body(table, query_low, through, normed, attended_low, *parts):
    rows = query_low.shape[0]
    for k, part in enumerate(parts):
        b = table[ORDER + k]
        part[:rows] = dims(query_low[...], normed[b], 1, 0).astype(bf16)
        part[-rows:] = dims(attended_low[...], through[b], 1, 0).astype(bf16)


def qkv_back_body(table, *refs):
    count = table.shape[0] - ORDER
    own_back, moved, refs = refs[count], refs[count + 1 : count + GROUP], refs[count + GROUP :]
    query_low, inner, weights, cosine, sine, own, normed = refs[:7]
    parts, outs = refs[7 : 7 + count], refs[7 + count : 11 + count]
    inner_first, own_low, changed, sems = refs[11 + count :]
    head = HEAD_DIM
    total = own_back[...]
    for part in moved:
        total = total + part[...].astype(f32)
    inner_first[...] = inner[...] + jnp.sum(total * own[...].astype(f32), axis=0, keepdims=True)
    key = turn(total[:head], cosine[...], -sine[...])
    low = jnp.concatenate([key, total[head:]], axis=0)
    own_low[...] = low.astype(bf16)
    first = query_low.shape[0]
    copies = []
    for k, part in enumerate(parts):
        changed[k] = dims(own_low[...], normed[table[ORDER + k]], 1, 0).astype(bf16)
        target = part.at[first : first + low.shape[0]]
        copies.append(pltpu.make_async_copy(changed.at[k], target, sems.at[k]))
        copies[k].start()
    flipped = jnp.concatenate([query_low[...].T, low.T.astype(bf16)], axis=1)
    width = flipped.shape[1]
    keep_and_send(table, lambda b: dims(flipped, weights[b, :width], 1, 0), outs)
    for copy in copies:
        copy.wait()


def halves_of(table, whole):
    half = whole.shape[0] // 2
    low, high = whole[:half], whole[half:]
    flag = table[Y] == 0
    return jnp.where(flag, low, high), jnp.where(flag, high, low)


def add_body(table, sources, out, first, second, sems, *, rows):
    copies = [
        pltpu.make_async_copy(source.at[rows], held, sems.at[i])
        for i, (source, held) in enumerate(zip(sources, (first, second)))
    ]
    for copy in copies:
        copy.start()
    for copy in copies:
        copy.wait()
    out[...] = add(first[...], second[...])


def pack(rows, packed):
    half, cols = packed.shape[0], rows.shape[1]
    packed[:, :cols] = rows[:half].astype(packed.dtype)
    packed[:, cols:] = rows[half:].astype(packed.dtype)


def split_body(table, *refs):
    matrices, (mine_ref, other_ref) = refs[:-2], refs[-2:]
    pairs = [halves_of(table, matrix[...].T) for matrix in matrices]
    pack(jnp.concatenate([mine for mine, _ in pairs], axis=0), mine_ref)
    pack(jnp.concatenate([other for _, other in pairs], axis=0), other_ref)


def piece_body(table, mine_ref, got_ref, piece):
    flag = table[Y] == 0
    mine, got = mine_ref[...], got_ref[...]
    low, high = jnp.where(flag, mine, got), jnp.where(flag, got, mine)
    half, cols = mine.shape[0], mine.shape[1] // 2
    for i in range(2):
        piece[i * half : (i + 1) * half, :cols] = low[:, i * cols : (i + 1) * cols]
        piece[i * half : (i + 1) * half, cols:] = high[:, i * cols : (i + 1) * cols]


def sum_body(table, *refs):
    parts, (mine_ref, other_ref) = refs[:-2], refs[-2:]
    whole = [part for part in parts if part.shape == parts[0].shape]
    total = whole[0][...].astype(f32)
    for part in whole[1:]:
        total = total + part[...].astype(f32)
    rest = [part[...].astype(f32) for part in parts if part.shape != parts[0].shape]
    if rest:
        total = total + jnp.concatenate(rest, axis=0)
    cols = total.shape[1] // 2
    low, high = total[:, :cols], total[:, cols:]
    flag = table[Y] == 0
    pack(jnp.where(flag, low, high), mine_ref)
    pack(jnp.where(flag, high, low), other_ref)


def join_body(table, mine_ref, got_ref, *outs):
    flag = table[Y] == 0
    cols = mine_ref.shape[1] // 2

    def unpacked(ref):
        return jnp.concatenate([ref[:, :cols], ref[:, cols:]], axis=0).astype(f32)

    mine, got = unpacked(mine_ref), unpacked(got_ref)
    low, high = jnp.where(flag, mine, got), jnp.where(flag, got, mine)
    at = 0
    for out in outs:
        rows = out.shape[1] // 2
        out[:, :rows] = low[at : at + rows].T
        out[:, rows:] = high[at : at + rows].T
        at += rows


def rope_tables(positions, half):
    freq = rope_base ** (-(2.0 * jnp.arange(half, dtype=f32)) / (2.0 * half))
    angle = freq[:, None] * positions.astype(f32)[None, :]
    return (jnp.cos(angle), jnp.sin(angle))


def shards(
    layer_in,
    first_gain,
    query_weight,
    key_matrix,
    value_matrix,
    out_weight,
    second_gain,
    gate_weight,
    up_weight,
    down_weight,
    out_grad,
):
    place = Place()
    n, ny, y, z_in, table = place.n, place.ny, place.y, place.z_in, place.table
    lined = place.lined
    block, width = layer_in.shape
    tokens = 2 * block
    model_width = width * ny
    hidden_dev = gate_weight.shape[1] // 2
    query_rows = query_weight.shape[1] // 2
    kv_rows = key_matrix.shape[1]
    qkv_cols = query_rows + kv_rows
    full = (ny, tokens, width)
    wide = [(full[1:], bf16)] * 4

    def halves(*matrices, earlier=()):
        rows = sum(m.shape[1] for m in matrices) // 2
        packed = (rows // 2, 2 * matrices[0].shape[0])
        return call(split_body, [(packed, bf16)] * 2, table, [], held=matrices, earlier=earlier)

    def whole_piece(mine, got):
        rows, cols = mine.shape
        (piece,) = call(piece_body, [((2 * rows, cols), bf16)], table, [mine, got])
        return piece

    def spread(value, *before_y):
        by_x = place.swap_x(value)
        late, late_x = lax.optimization_barrier((value, by_x) + before_y)[:2]
        four = [value, by_x, place.swap_y(late), place.swap_y(late_x)]
        return four + [place.swap_c(r) for r in four]

    mine, other = halves(query_weight, key_matrix, value_matrix, out_weight.T)
    attend_got = place.swap_y(other)
    attend_piece = whole_piece(mine, attend_got)
    mine, other = halves(gate_weight, up_weight, down_weight.T, earlier=[attend_piece])
    forward_got = place.swap_y(other)
    forward_piece = whole_piece(mine, forward_got)
    rows = jnp.concatenate([layer_in, out_grad], axis=0)
    input_rows = spread(after(rows, attend_got), forward_got)
    if lined:
        attend_pieces = gather_pieces(place, attend_piece)
        forward_pieces = gather_pieces(place, after(forward_piece, *attend_pieces[1:]), True)
    else:
        attend_pieces = [gather_whole(place, attend_piece)]
        forward_pieces = [gather_whole(place, forward_piece)]
    attend_shape = (ny, qkv_cols + query_rows, width)
    forward_shape = (ny, 3 * hidden_dev, width)
    sems = pltpu.SemaphoreType.DMA((ny,))

    gains = jnp.stack([first_gain, second_gain])
    two = [gains, place.swap_x(gains)]
    gains = two + [place.swap_c(g) for g in two]
    raw, grad, normed_in, inverse_in, gain_in, gain_mid = call(
        rows_body,
        [(full, bf16)] * 3 + [((tokens, 1), f32)] + [((ny, 1, width), f32)] * 2,
        table,
        input_rows + gains,
    )

    within = jnp.arange(block, dtype=jnp.int32)
    positions = jnp.minimum(place.offset, PROMPT_DEV)[:, None] * block + within[None, :]
    cosine, sine = rope_tables(positions.reshape(-1), HEAD_DIM // 2)
    query, own, attend_weights = call(
        qkv_body,
        [((query_rows, tokens), bf16), ((kv_rows, tokens), bf16), (attend_shape, bf16)],
        table,
        [normed_in, cosine, sine],
        [attend_pieces],
        [pltpu.VMEM((qkv_cols, tokens), f32), sems],
    )
    moved = [
        place.send_z(
            own,
            [(s, s + k) for s in range(n) if s % GROUP < PROMPTS and s % GROUP + k < GROUP],
        )
        for k in range(1, GROUP)
    ]
    attended, attended_low, log_total, far, *halves_out = call(
        attend_body,
        [
            ((query_rows, tokens), f32),
            ((query_rows, tokens), bf16),
            ((query_rows // HEAD_DIM, 1, tokens), f32),
            ((kv_rows, PROMPTS * tokens), bf16),
        ]
        + wide,
        table,
        [query, own] + moved + [attend_weights],
        earlier=forward_pieces[1:3],
    )
    summed = all_sum(
        place,
        halves_out[:2],
        halves_out[2:],
        before_first=forward_pieces[1:3] if lined else forward_pieces,
        before_last=forward_pieces[3:],
    )

    hidden, normed_mid, inverse_mid = call(
        hidden_body,
        [(full, f32), (full, bf16), ((tokens, 1), f32)],
        table,
        summed,
        held=[raw, gain_mid],
    )
    active, change, *halves_out, down_whole = call(
        forward_body,
        [((tokens, hidden_dev), bf16), ((tokens, 2 * hidden_dev), bf16)]
        + wide
        + [((ny, hidden_dev, width), bf16)],
        table,
        [normed_mid],
        [forward_pieces],
        [
            pltpu.VMEM((ny, 2 * hidden_dev, width), bf16),
            pltpu.VMEM((tokens, 2 * hidden_dev), f32),
        ]
        + [pltpu.VMEM((tokens, hidden_dev), f32)] * 2
        + [sems, sems],
        held=[grad],
    )
    third, both = call(
        forward_third_body,
        [(forward_shape[1:], bf16), (forward_shape[1:2] + (tokens,), bf16)],
        table,
        [active, normed_mid, change],
        held=[grad],
    )
    forward_parts = call(
        forward_parts_body,
        [(forward_shape[1:], bf16)] * 3,
        table,
        [both, normed_mid],
        held=[grad],
    )
    forward_parts = list(forward_parts) + [third]
    forward_started = start_scatter(place, forward_parts)
    down_halves = call(
        down_body, wide, table, [active, down_whole], earlier=[forward_parts[0]]
    )
    summed = all_sum(
        place,
        halves_out[:2],
        halves_out[2:],
        before_second=forward_parts[:1],
        before_last=list(down_halves[:1]) + forward_started[2:3] + forward_started[4:],
    )
    _, forward_second = second_scatter(place, forward_started, 0, 2, summed[-1])
    hidden_own = own_block(place, hidden)
    through, pull, query_low, own_back, *returns, inner_first = call(
        attend_back_body,
        [
            (full, bf16),
            ((tokens, 1), f32),
            ((query_rows, tokens), bf16),
            ((kv_rows, tokens), f32),
        ]
        + [((kv_rows, tokens), bf16)] * (GROUP - 1)
        + [((1, tokens), f32)],
        table,
        summed,
        held=[
            hidden,
            inverse_mid,
            grad,
            gain_mid,
            attend_weights,
            query,
            own,
            far,
            attended,
            log_total,
            cosine,
            sine,
        ],
        earlier=forward_started[2:3] + forward_started[4:],
        scratch=[
            pltpu.VMEM((kv_rows, PROMPTS * tokens), f32),
            pltpu.VMEM(full, f32),
            pltpu.VMEM((query_rows, tokens), bf16),
        ],
    )
    down_sends = lax.optimization_barrier(tuple(down_halves[2:]) + (through,))[:2]
    layer_out = (hidden_own + own_sum(place, down_halves[:2], down_sends)).astype(bf16)
    inverse_own, _ = part_of(y, inverse_mid, 0)
    pull_own, _ = part_of(y, pull, 0)
    mid_own = jnp.where(place.x == 0, summed[0], summed[1])
    mid_own = part_of(y, mid_own, 0)[0].astype(f32)
    through_own = (
        out_grad.astype(f32)
        + inverse_own * mid_own * second_gain[None, :]
        - hidden_own * pull_own
    )
    second_term = jnp.sum(mid_own * hidden_own * inverse_own, axis=0)

    moved = [
        place.send_z(
            returns[k - 1],
            [(s, s - k) for s in range(n) if 0 <= s % GROUP - k < PROMPTS],
        )
        for k in range(1, GROUP)
    ]
    attend_parts = call(
        attend_parts_body,
        [(attend_shape[1:], bf16)] * ny,
        table,
        [query_low, through],
        held=[normed_in, attended_low],
    )
    results = call(
        qkv_back_body,
        [(attend_shape[1:], bf16)] * ny
        + wide
        + [((1, tokens), f32), ((kv_rows, tokens), bf16)],
        table,
        list(attend_parts) + [own_back] + moved + [query_low, inner_first],
        held=[attend_weights, cosine, sine, own, normed_in],
        scratch=[pltpu.VMEM((ny, kv_rows, width), bf16), sems],
        earlier=forward_started[3:4] + ([forward_second] if lined else []),
        alias=ny,
    )
    attend_parts, first_halves = results[:ny], results[ny:-2]
    inner, own_low = results[-2:]
    attend_started = start_scatter(place, attend_parts)
    forward_seconds = [
        forward_second,
        second_scatter(place, forward_started, 1, 2, summed[-1], moved[0])[1],
    ]
    attend_sent, attend_second = second_scatter(place, attend_started, 0, 1)
    attend_grad = end_scatter(place, attend_started, [attend_second], own_low)
    inner = inner + place.swap_c(inner)
    inner = inner + place.swap_x(inner)
    inner = inner + place.swap_y(inner)
    first_own = own_sum(
        place,
        first_halves[:2],
        first_halves[2:],
        before_y=[attend_sent] if lined else [],
    )
    forward_grad = end_scatter(
        place, forward_started, forward_seconds, *([attend_sent] if lined else [])
    )
    input_own = layer_in.astype(f32)
    inverse_own, _ = part_of(y, inverse_in, 0)
    scaled = first_own * first_gain[None, :]
    inner = part_of(y, inner.reshape(tokens, 1), 0)[0]
    in_grad = (
        through_own + inverse_own * scaled - input_own * (inverse_own**2 * inner / model_width)
    )
    first_term = jnp.sum(first_own * input_own * inverse_own, axis=0)
    terms = jnp.stack([first_term, second_term])
    bit = 1
    while bit < place.nx:
        terms = terms + place.swap_gx(terms, bit)
        bit *= 2

    def joined(parts, outs):
        rows, cols = parts[0].shape
        packed = (rows // 2, cols)
        mine, other = call(sum_body, [(packed, f32), (packed, bf16)], table, parts)
        shapes = [(cols // 2, inner) for inner in outs]
        return call(
            join_body, [(s, f32) for s in shapes], table, [mine, place.swap_y(other)]
        )

    gate_grad, up_grad, down_grad = joined(forward_grad, [2 * hidden_dev] * 3)
    query_out, key_out, value_out, out_out = joined(
        attend_grad, [2 * query_rows, kv_rows, kv_rows, 2 * query_rows]
    )
    return (
        layer_out,
        in_grad,
        terms[0],
        query_out,
        key_out,
        value_out,
        out_out.T,
        terms[1],
        gate_grad,
        up_grad,
        down_grad.T,
    )


def solution(mesh):
    rows, cols, gain = P("gx", "gy"), P("gy", "gx"), P("gy")
    return jax.shard_map(
        shards,
        mesh=mesh,
        in_specs=(rows, gain, rows, rows, rows, cols, gain, rows, rows, cols, rows),
        out_specs=(rows, rows, gain, rows, rows, rows, cols, gain, rows, rows, cols),
        check_vma=False,
    )
```
